32 devices in a mesh: seq: 16 (over z, y, x), head: 2 (over core).
Axes of the slice: x: 2, y: 2, z: 4, core: 2. Of those that a mesh axis runs over, the one named last changes fastest.
Arguments:
- block_in: bfloat16 [8192, 768], P(('seq', 'head')), may hold values from -6 to 6
- grad_out: bfloat16 [8192, 768], P(('seq', 'head')), may hold values from -6 to 6
- lengths: int32 [2], replicated, may hold values from 1024 to 4096, as said below
- norm_gain: float32 [768], replicated, may hold values from 0.25 to 1.75
- w_in: bfloat16 [768, 3352], replicated, may hold values from -0.21875 to 0.21875
- conv_w: float32 [4, 1792], replicated, may hold values from -3 to 3
- conv_b: float32 [1792], replicated, may hold values from -0.5 to 0.5
- dt_bias: float32 [24], replicated, may hold values from -6 to -3.5
- a_log: float32 [24], replicated, may hold values from -10.5 to 1.4
- d_skip: float32 [24], replicated, may hold values from 0.5 to 2
- gate_gain: float32 [1536], replicated, may hold values from 0.25 to 1.75
- w_out: bfloat16 [1536, 768], replicated, may hold values from -0.15625 to 0.15625
Outputs:
- block_out: bfloat16 [8192, 768], P(('seq', 'head'))
- grad_in: float32 [8192, 768], P(('seq', 'head'))
- grad_norm_gain: float32 [768], replicated
- grad_w_in: float32 [768, 3352], replicated
- grad_conv_w: float32 [4, 1792], replicated
- grad_conv_b: float32 [1792], replicated
- grad_dt_bias: float32 [24], replicated
- grad_a_log: float32 [24], replicated
- grad_d_skip: float32 [24], replicated
- grad_gate_gain: float32 [1536], replicated
- grad_w_out: float32 [1536, 768], replicated
The draws below stay inside these ranges and needn't reach their ends.
Inputs may be any that keep to these rules, and one draw needn't show every extreme that they name: lengths[s] counts the valid slots at the start of sequence s, the rest being padding; at least one sequence is valid in all 4096 slots.
All inputs are finite; a program needn't handle non-finite values.
Results may differ from the reference program's by a relative error of at most 0.012.
The reference program's roundings to bfloat16 on the way count: a program that leaves them out, or rounds other values in their place, can miss the bound.
Values may be sent and summed in bfloat16 or wider, within the bound.
A program may use at most 320 MiB of HBM per device.

```python
from functools import partial
import jax
import jax.numpy as jnp
from jax import lax

D = 768
INNER = 1536
HEADS = 24
HEAD_DIM = 64
STATE = 128
CONV = 4
BLOCK = 256
TOK_DEV = 256
SEQS = 2
LENGTH = 4096
TOKENS = 8192
XBC = 1792
PROJ = 3352
N_HEAD = 2


def draw_lengths(key, part):
    first_key = jax.random.fold_in(key, 11)
    second_key = jax.random.fold_in(key, 23)
    counts = jax.random.randint(first_key, (SEQS,), LENGTH // 4, LENGTH + 1)
    full_one = jax.random.randint(second_key, (), 0, SEQS)
    return jnp.where(jnp.arange(SEQS) == full_one, LENGTH, counts).astype(jnp.int32)


def level_of(own_key, extent, split, smallest, top_value):
    def one(dim, parts):
        heights = jax.random.uniform(jax.random.fold_in(jax.random.fold_in(own_key, 6), dim), (parts,), jnp.float32, smallest / len(split), top_value / len(split))
        return jnp.repeat(jnp.exp(heights), extent[dim] // parts).reshape((-1,) + (1,) * (len(extent) - dim - 1))

    factor_of = one(*split[0])
    for cut in split[1:]:
        factor_of = factor_of * one(*cut)
    return factor_of


def gaussian(key, shape, deviation, reach, cuts=(), held_as=jnp.bfloat16):
    values = jax.random.normal(key, shape, jnp.float32) * deviation
    if len(cuts) > 0:
        values = level_of(key, shape, cuts, -0.22, 0.18) * values
    return jnp.clip(values, min=-reach, max=reach).astype(held_as)


def setup_inputs(seed: int = 0) -> dict:
    seeds = jax.random.split(jax.random.key(seed), 13)
    block_in = gaussian(seeds[0], (TOKENS, D), 1.0, 6.0, ((0, 32),))
    grad_out = gaussian(seeds[1], (TOKENS, D), 1.0, 6.0, ((0, 32),))
    lengths = draw_lengths(jax.random.fold_in(seeds[12], 71), 0)
    norm_gain = jnp.clip(1.0 + 0.15 * jax.random.normal(seeds[3], (D,), jnp.float32), 0.25, 1.75)
    w_in = gaussian(seeds[4], (D, PROJ), D ** -0.5, 0.21875)
    conv_w = gaussian(seeds[5], (CONV, XBC), CONV ** -0.5, 3.0, (), jnp.float32)
    conv_b = jnp.clip(jax.random.uniform(seeds[6], (XBC,), jnp.float32, -0.5, 0.5), -0.5, 0.5)
    dt_bias = jnp.clip(jax.random.uniform(seeds[7], (HEADS,), jnp.float32, -6.0, -3.5), -6.0, -3.5)
    a_log = jnp.clip(jax.random.uniform(seeds[8], (HEADS,), jnp.float32, -10.5, 1.4), -10.5, 1.4)
    d_skip = jnp.clip(jax.random.uniform(seeds[9], (HEADS,), jnp.float32, 0.5, 2.0), 0.5, 2.0)
    gate_gain = jnp.clip(1.0 + 0.15 * jax.random.normal(seeds[10], (INNER,), jnp.float32), 0.25, 1.75)
    w_out = gaussian(seeds[11], (INNER, D), INNER ** -0.5, 0.15625)
    return {"block_in": block_in, "grad_out": grad_out, "lengths": lengths, "norm_gain": norm_gain, "w_in": w_in, "conv_w": conv_w, "conv_b": conv_b, "dt_bias": dt_bias, "a_log": a_log, "d_skip": d_skip, "gate_gain": gate_gain, "w_out": w_out}


@jax.custom_vjp
def low(v):
    return lax.optimization_barrier(v.astype(jnp.bfloat16)).astype(jnp.float32)

@jax.custom_vjp
def low_back(v):
    return v

def low_keep(v):
    return (low(v), None)

def low_pass(kept, grad):
    return (grad,)

def back_keep(v):
    return (v, None)

def back_low(kept, grad):
    return (low(grad),)
low.defvjp(low_keep, low_pass)
low_back.defvjp(back_keep, back_low)
eps_norm = 1e-05
best = lax.Precision.HIGHEST

def block_step(rates, carry_state, inputs):
    x_heads, b_rows, c_rows, dt_rows = inputs
    block_len = dt_rows.shape[1]
    cumulative = jnp.cumsum(dt_rows, axis=1) * rates
    indices = jnp.arange(block_len)
    causal = (indices[:, None] >= indices[None, :])[None, :, :, None]
    spread = cumulative[:, :, None, :] - cumulative[:, None, :, :]
    decays = jnp.where(causal, jnp.exp(jnp.where(causal, spread, 0.0)), 0.0)
    scores = jnp.einsum('stn,sun->stu', c_rows, b_rows, precision=best)
    weight = decays * scores[..., None] * dt_rows[:, None, :, :]
    inner_part = jnp.einsum('stuh,suhp->sthp', weight, x_heads, precision=best)
    carried = jnp.exp(cumulative)[..., None] * jnp.einsum('stn,shpn->sthp', c_rows, carry_state, precision=best)
    to_end = jnp.exp(cumulative[:, -1:, :] - cumulative) * dt_rows
    fresh_state = jnp.einsum('suh,suhp,sun->shpn', to_end, x_heads, b_rows, precision=best)
    carry_state = jnp.exp(cumulative[:, -1, :])[..., None, None] * carry_state + fresh_state
    return (carry_state, inner_part + carried)

def state_space(x_heads, b_rows, c_rows, dt_rows, rates):
    blocks_count = LENGTH // BLOCK

    def blocks(values):
        return jnp.moveaxis(values.reshape((SEQS, blocks_count, BLOCK) + values.shape[2:]), 1, 0)
    stepper = jax.checkpoint(partial(block_step, rates))
    start_state = jnp.zeros((SEQS, HEADS, HEAD_DIM, STATE), jnp.float32)
    final_state, outputs = lax.scan(stepper, start_state, (blocks(x_heads), blocks(b_rows), blocks(c_rows), blocks(dt_rows)))
    return jnp.moveaxis(outputs, 0, 1).reshape(SEQS * LENGTH, INNER)

def layer(valid_mask, source, norm_gain, w_in, conv_w, conv_b, dt_bias, a_log, d_skip, gate_gain, w_out):
    in_scale = lax.rsqrt(lax.optimization_barrier(jnp.mean(source * source, axis=-1, keepdims=True)) + eps_norm)
    normed = low(source * in_scale * norm_gain)
    projected = low_back(low(jnp.dot(normed, w_in, precision=best)))
    gate_in = projected[:, :INNER]
    conv_in = projected[:, INNER:2 * INNER + 2 * STATE].reshape(SEQS, LENGTH, INNER + 2 * STATE)
    dt_in = projected[:, 2 * INNER + 2 * STATE:].reshape(SEQS, LENGTH, HEADS)
    padded = jnp.pad(conv_in, ((0, 0), (CONV - 1, 0), (0, 0)))
    running = conv_b + padded[:, 0:LENGTH] * conv_w[0]
    for position in range(1, CONV):
        running = running + padded[:, position:position + LENGTH] * conv_w[position]
    activated = jax.nn.silu(running)
    keep_mask = valid_mask[..., None]
    x_heads = (activated[..., :INNER] * keep_mask).reshape(SEQS, LENGTH, HEADS, HEAD_DIM)
    b_rows = activated[..., INNER:INNER + STATE]
    c_rows = activated[..., INNER + STATE:]
    dt_rows = jax.nn.softplus(dt_in + dt_bias) * keep_mask
    rates = -jnp.exp(a_log)
    skipped = (x_heads * d_skip[:, None]).reshape(SEQS * LENGTH, INNER)
    mixed = low_back(low(state_space(x_heads, b_rows, c_rows, dt_rows, rates) + skipped))
    gated = mixed * jax.nn.silu(gate_in)
    gate_scale = lax.rsqrt(lax.optimization_barrier(jnp.mean(gated * gated, axis=-1, keepdims=True)) + eps_norm)
    gnormed = low(gated * gate_scale * gate_gain)
    branch = jnp.dot(gnormed, w_out, precision=best)
    return source + valid_mask.reshape(-1, 1) * branch

def to_sequences(rows):
    piece_len = TOK_DEV * N_HEAD
    pieces = LENGTH // piece_len
    return jnp.swapaxes(rows.reshape(pieces, SEQS, piece_len, rows.shape[-1]), 0, 1).reshape(SEQS * LENGTH, rows.shape[-1])

def to_pieces(rows):
    piece_len = TOK_DEV * N_HEAD
    pieces = LENGTH // piece_len
    return jnp.swapaxes(rows.reshape(SEQS, pieces, piece_len, rows.shape[-1]), 0, 1).reshape(SEQS * LENGTH, rows.shape[-1])

def reference(block_in, grad_out, lengths, norm_gain, w_in, conv_w, conv_b, dt_bias, a_log, d_skip, gate_gain, w_out):
    valid_mask = (jnp.arange(LENGTH)[None, :] < lengths[:, None]).astype(jnp.float32)
    operands = (to_sequences(block_in.astype(jnp.float32)), norm_gain, w_in.astype(jnp.float32), conv_w, conv_b, dt_bias, a_log, d_skip, gate_gain, w_out.astype(jnp.float32))
    result, pull_back = jax.vjp(partial(layer, valid_mask), *operands)
    grads = pull_back(to_sequences(grad_out.astype(jnp.float32)))
    return (to_pieces(result).astype(jnp.bfloat16), to_pieces(grads[0]), grads[1], grads[2], grads[3], grads[4], grads[5], grads[6], grads[7], grads[8], grads[9])
```

```python
from functools import partial

import jax
import jax.numpy as jnp
from jax import lax
from jax.experimental import pallas as pl
from jax.experimental.pallas import tpu as pltpu
from jax.sharding import PartitionSpec as P

D = 768
INNER = 1536
HEADS = 24
HEAD_DIM = 64
STATE = 128
CONV = 4
SEQS = 2
XBC = INNER + 2 * STATE
PROJ = 2 * INNER + 2 * STATE + HEADS
PAIRS = HEADS // 2
EPS = 1e-05
LOG2E = 1.4426950408889634

f32 = jnp.float32
bf16 = jnp.bfloat16
MESH = pl.DeviceIdType.MESH
VMEM = pl.BlockSpec(memory_space=pltpu.VMEM)
SMEM = pl.BlockSpec(memory_space=pltpu.SMEM)
NN = ((1,), (0,))
NT = ((1,), (1,))
TN = ((0,), (0,))


def dot(a, b, dims=NN):
    return lax.dot_general(a, b, (dims, ((), ())), preferred_element_type=f32)


def split_dot(a, pick, terms=3):
    total = None
    for _ in range(terms):
        part = a.astype(bf16)
        a = a - part.astype(f32)
        term = dot(part, pick)
        total = term if total is None else total + term
    return total


def split_dot_left(pick, a, terms=3):
    total = None
    for _ in range(terms):
        part = a.astype(bf16)
        a = a - part.astype(f32)
        term = dot(pick, part)
        total = term if total is None else total + term
    return total


def iota(shape, dim):
    return lax.broadcasted_iota(jnp.int32, shape, dim)


def one_hot(cond):
    return jnp.where(cond, 1.0, 0.0).astype(bf16)


def sigmoid(v):
    return 1.0 / (1.0 + jnp.exp(-v))


def lanes(start, size):
    return pl.ds(pl.multiple_of(start, 128), size)


def valid_rows(lengths_ref, per_row, rows, width):
    place = lax.axis_index("seq")
    first = (place // SEQS) * (rows * lax.axis_size("head")) + lax.axis_index("head") * rows
    limit = lengths_ref[place % SEQS]
    return jnp.where(iota((rows, width), 0) + first < limit, 1.0, 0.0)


def call(body, outs, args, scratch=(), smem=(), vmem=56 << 20, cost=None, **params):
    return pl.pallas_call(
        body,
        out_shape=[jax.ShapeDtypeStruct(s, d) for s, d in outs],
        in_specs=[SMEM if i in smem else VMEM for i in range(len(args))],
        out_specs=[VMEM] * len(outs),
        scratch_shapes=list(scratch),
        compiler_params=pltpu.CompilerParams(vmem_limit_bytes=vmem, **params),
    )(*args)


def front_kernel(
    lengths_ref,
    blk,
    edge,
    gain,
    w_in,
    conv_w,
    conv_b,
    heads_ref,
    normed_out,
    gate_out,
    pad_out,
    run_out,
    x_out,
    xd_out,
    xde_out,
    b_out,
    c_out,
    head_out,
    cumt_out,
    cumb_out,
    rows_out,
    state_out,
):
    rows = blk.shape[0]

    def norm(v):
        v = v.astype(f32)
        scale = lax.rsqrt(jnp.mean(v * v, axis=-1, keepdims=True) + EPS)
        return (v * scale * gain[...]).astype(bf16)

    normed = norm(blk[...])
    normed_out[...] = normed
    gate_out[...] = dot(normed, w_in[:INNER, :], NT).astype(bf16)
    ahead = norm(edge[...])
    pad_out[0:16, :] = dot(ahead, w_in[INNER : INNER + XBC, :], NT).astype(bf16).astype(f32)
    pad_out[16 : 16 + rows, :] = dot(normed, w_in[INNER : INNER + XBC, :], NT).astype(bf16).astype(f32)
    keep = valid_rows(lengths_ref, None, rows, 128)
    head_out[3] = jnp.zeros((rows, 128), f32)
    head_out[3, :, 0:HEADS] = dot(normed, w_in[INNER + XBC :, :], NT).astype(bf16).astype(f32)
    lane = iota((rows, 128), 1)
    shifted = head_out[3] + heads_ref[0:1, :]
    soft = jnp.maximum(shifted, 0.0) + jnp.log1p(jnp.exp(-jnp.abs(shifted)))
    dt = jnp.where(lane < HEADS, soft * keep, 0.0)
    rates = -jnp.exp(heads_ref[1:2, :])
    below = one_hot(iota((rows, rows), 0) >= iota((rows, rows), 1))
    cum = split_dot_left(below, dt) * rates
    cum2 = cum * LOG2E
    head_out[0] = dt
    head_out[1] = cum
    head_out[2] = sigmoid(shifted) * keep
    head_out[3] = cum2
    cumt_out[...] = cum2.T
    pick_lane = iota((128, 256), 1)
    pick_head = iota((128, 256), 0)

    def spread(i, carry):
        cumb_out[:, lanes(i * 256, 256)] = split_dot(
            head_out[3], one_hot((pick_lane >> 7) + 2 * i == pick_head)
        )
        return carry

    lax.fori_loop(0, PAIRS, spread, 0)

    def convolve(i):
        cols = lanes(i * 256, 256)
        running = conv_b[:, cols] + pad_out[13 : 13 + rows, cols] * conv_w[0:1, cols]
        for tap in range(1, CONV):
            running = running + pad_out[13 + tap : 13 + tap + rows, cols] * conv_w[tap : tap + 1, cols]
        run_out[:, cols] = running
        return running * sigmoid(running)

    act = convolve(INNER // 256)
    b_out[...] = act[:, :STATE].astype(bf16)
    c_out[...] = act[:, STATE:].astype(bf16)
    keep2 = valid_rows(lengths_ref, None, rows, 256)

    def channels(i, carry):
        cols = lanes(i * 256, 256)
        pick = one_hot((pick_lane >> 6) + 4 * i == pick_head)
        x = convolve(i) * keep2
        x_out[:, cols] = x
        xd = x * split_dot(head_out[0], pick)
        xd_out[:, cols] = xd.astype(bf16)
        wide = split_dot(head_out[3], pick)
        last = wide[rows - 1 : rows, :]
        xde_out[:, cols] = (xd * jnp.exp2(last - wide)).astype(bf16)
        rows_out[0:8, cols] = jnp.broadcast_to(jnp.exp2(last), (8, 256))
        rows_out[8:16, cols] = split_dot(jnp.broadcast_to(heads_ref[2:3, :], (8, 128)), pick)
        return carry

    lax.fori_loop(0, INNER // 256, channels, 0)
    state_out[...] = dot(b_out[...], xde_out[...], TN)


def front(lengths, blk, edge, gain, w_in, conv_w, conv_b, heads):
    t = blk.shape[0]
    outs = [
        ((t, D), bf16),
        ((t, INNER), bf16),
        ((t + 16, XBC), f32),
        ((t, XBC), f32),
        ((t, INNER), f32),
        ((t, INNER), bf16),
        ((t, INNER), bf16),
        ((t, STATE), bf16),
        ((t, STATE), bf16),
        ((4, t, 128), f32),
        ((128, t), f32),
        ((t, HEADS * 128), f32),
        ((16, INNER), f32),
        ((STATE, INNER), f32),
    ]
    return call(front_kernel, outs, (lengths, blk, edge, gain, w_in, conv_w, conv_b, heads), smem=(0,))


def exchange_kernel(reverse, state, decay, out, sib_state, sib_decay, mine, total, got, got_decay, back, back_got, ssem, rsem):
    half = INNER // 2
    chips = lax.axis_size("seq") // SEQS
    rows = STATE // chips
    place = lax.axis_index("seq")
    core = lax.axis_index("head")
    chip = place // SEQS
    which = place % SEQS
    sibling = (place, 1 - core)
    rank = 1 - core if reverse else core
    barrier = pltpu.get_barrier_semaphore()
    pl.semaphore_signal(barrier, inc=1, device_id=sibling, device_id_type=MESH)

    def peer(k):
        return (lax.rem(chip + k, chips) * SEQS + which, core)

    for k in range(1, chips):
        pl.semaphore_signal(barrier, inc=1, device_id=peer(k), device_id_type=MESH)
    pl.semaphore_wait(barrier, chips)
    own_cols = lanes(core * half, half)
    sib_cols = lanes((1 - core) * half, half)

    def copy(src, dst, n, to):
        return pltpu.make_async_remote_copy(
            src_ref=src, dst_ref=dst, send_sem=ssem.at[n], recv_sem=rsem.at[n], device_id=to, device_id_type=MESH
        )

    first = [
        copy(state.at[:, sib_cols], sib_state, 0, sibling),
        copy(decay.at[:, sib_cols], sib_decay, 1, sibling),
    ]
    for c in first:
        c.start()
    for c in first:
        c.wait()
    own = state[:, own_cols]
    own_decay = decay[0:1, own_cols]
    other = sib_state[...]
    other_decay = sib_decay[0:1, :]
    later = rank == 1
    late_decay = jnp.where(later, own_decay, other_decay)
    early_decay = jnp.where(later, other_decay, own_decay)
    early = jnp.where(later, other, own)
    late = jnp.where(later, own, other)
    mine[...] = (late_decay * early + late).astype(bf16)
    total[...] = jnp.broadcast_to(own_decay * other_decay, total.shape)
    second = []
    for k in range(1, chips):
        to = lax.rem(chip + k, chips)
        piece = pl.ds(pl.multiple_of(to * rows, rows), rows)
        second.append(copy(mine.at[piece], got.at[k], 2 * k, peer(k)))
        second.append(copy(total, got_decay.at[k], 2 * k + 1, peer(k)))
    for c in second:
        c.start()
    got[0] = mine[pl.ds(pl.multiple_of(chip * rows, rows), rows), :]
    got_decay[0] = total[...]
    for c in second:
        c.wait()

    def scan(i, carry):
        source = chips - 1 - i if reverse else i
        slot = lax.rem(chip - source + chips, chips)
        to = lax.rem(source - chip + chips, chips)
        back[pl.ds(to, 1)] = carry.astype(bf16)[None]
        return got_decay[pl.ds(slot, 1)][0, 0:1, :] * carry + got[pl.ds(slot, 1)][0].astype(f32)

    lax.fori_loop(0, chips, scan, jnp.zeros((rows, half), f32))
    third = []
    here = pl.ds(pl.multiple_of(chip * rows, rows), rows)
    base = 2 * chips
    for k in range(1, chips):
        third.append(copy(back.at[k], back_got.at[here], base + k, peer(k)))
    for c in third:
        c.start()
    back_got[here, :] = back[0]
    for c in third:
        c.wait()
    enter = back_got[...].astype(f32)
    second_enter = early_decay * enter + early
    for_own = jnp.where(later, second_enter, enter).astype(bf16)
    for_sib = jnp.where(later, enter, second_enter).astype(bf16)
    out[:, own_cols] = for_own
    mine[...] = for_sib
    last = copy(mine, out.at[:, own_cols], base, sibling)
    last.start()
    last.wait()


def exchange(state, decay, reverse):
    half = INNER // 2
    chips = lax.axis_size("seq") // SEQS
    rows = STATE // chips
    n = 3 * chips
    scratch = [
        pltpu.VMEM((STATE, half), f32),
        pltpu.VMEM((8, half), f32),
        pltpu.VMEM((STATE, half), bf16),
        pltpu.VMEM((8, half), f32),
        pltpu.VMEM((chips, rows, half), bf16),
        pltpu.VMEM((chips, 8, half), f32),
        pltpu.VMEM((chips, rows, half), bf16),
        pltpu.VMEM((STATE, half), bf16),
        pltpu.SemaphoreType.DMA((n,)),
        pltpu.SemaphoreType.DMA((n,)),
    ]
    return call(
        partial(exchange_kernel, reverse),
        [((STATE, INNER), bf16)],
        (state, decay),
        scratch,
        collective_id=1 if reverse else 0,
        has_side_effects=True,
    )[0]


def exchange_plain(state, decay, reverse):
    groups = lax.axis_size("head")
    count = lax.axis_size("seq") * groups
    place = lax.axis_index("seq")
    states = lax.all_gather(state.astype(bf16), ("seq", "head"), axis=0)
    decays = lax.all_gather(decay[0:1], ("seq", "head"), axis=0)
    blocks = count // SEQS
    block = place // SEQS * groups + lax.axis_index("head")

    def one(i, carry):
        source = blocks - 1 - i if reverse else i
        index = (source // groups * SEQS + place % SEQS) * groups + source % groups
        new = lax.dynamic_index_in_dim(decays, index, 0, False) * carry
        return new + lax.dynamic_index_in_dim(states, index, 0, False).astype(f32)

    ahead = blocks - 1 - block if reverse else block
    return lax.fori_loop(0, ahead, one, jnp.zeros(state.shape, f32)).astype(bf16)


def middle_kernel(
    lengths_ref,
    blk,
    gout,
    normed,
    gate,
    x_in,
    xd_in,
    b_in,
    c_in,
    cumt,
    cumb,
    rows_in,
    enter,
    gain,
    w_out,
    y_out,
    block_out,
    dy_out,
    dye_out,
    dgate_out,
    ggain_out,
    adj_out,
    grads_out,
    scores,
    mixed,
    gated_s,
    gn_s,
    scale_s,
    dgn_s,
    db_s,
):
    rows = blk.shape[0]
    causal = iota((rows, rows), 0) >= iota((rows, rows), 1)
    scores[...] = jnp.where(causal, dot(c_in[...], b_in[...], NT), 0.0)
    lane = iota((rows, 128), 1)
    left = one_hot(iota((1, 128), 1) < HEAD_DIM)
    right = one_hot(iota((1, 128), 1) >= HEAD_DIM)

    def pair(i, carry):
        cols = lanes(i * 128, 128)
        c0 = cumb[:, lanes(i * 256, 128)]
        c1 = cumb[:, lanes(i * 256 + 128, 128)]
        xd = xd_in[:, cols]
        y = None
        for cc, part, mask in ((c0, 0, left), (c1, 1, right)):
            row = cumt[pl.ds(2 * i + part, 1), :]
            decay = jnp.exp2(jnp.minimum(jnp.concatenate([cc] * (rows // 128), axis=1) - row, 0.0))
            term = dot((decay * scores[...]).astype(bf16), xd * mask)
            y = term if y is None else y + term
        grow = jnp.exp2(jnp.where(lane < HEAD_DIM, c0, c1))
        y = y + grow * dot(c_in[...], enter[:, cols])
        y_out[:, cols] = y
        mixed[:, cols] = (y + rows_in[8:9, cols] * x_in[:, cols]).astype(bf16).astype(f32)
        return carry

    lax.fori_loop(0, PAIRS, pair, 0)
    step = 32

    def gating(i, carry):
        r = pl.ds(pl.multiple_of(i * step, step), step)
        g = gate[r, :].astype(f32)
        gated = mixed[r, :] * g * sigmoid(g)
        scale = lax.rsqrt(jnp.mean(gated * gated, axis=-1, keepdims=True) + EPS)
        gated_s[r, :] = gated
        scale_s[r, :] = jnp.broadcast_to(scale, (step, 128))
        gn_s[r, :] = (gated * scale * gain[...]).astype(bf16)
        return carry

    lax.fori_loop(0, rows // step, gating, 0)
    keep = valid_rows(lengths_ref, None, rows, D)
    db_s[...] = (gout[...].astype(f32) * keep).astype(bf16)
    dgn_s[...] = dot(db_s[...], w_out[...], NT)
    block_out[...] = (blk[...].astype(f32) + keep * dot(gn_s[...], w_out[...])).astype(bf16)
    ggain_out[...] = jnp.zeros_like(ggain_out)

    def ungating(i, carry):
        r = pl.ds(pl.multiple_of(i * step, step), step)
        g = gate[r, :].astype(f32)
        sg = sigmoid(g)
        gated = gated_s[r, :]
        scale = scale_s[r, 0:1]
        dgn = dgn_s[r, :]
        ggain_out[...] += jnp.sum((dgn * gated * scale).reshape(step // 8, 8, INNER), axis=0)
        weighted = dgn * gain[...]
        average = jnp.mean(weighted * gated, axis=-1, keepdims=True)
        d_gated = scale * weighted - gated * (scale * scale * scale) * average
        dy_out[r, :] = (d_gated * g * sg).astype(bf16)
        dgate_out[r, :] = (d_gated * mixed[r, :] * sg * (1.0 + g * (1.0 - sg))).astype(bf16)
        return carry

    lax.fori_loop(0, rows // step, ungating, 0)

    def weigh(i, carry):
        cols = lanes(i * 128, 128)
        grow = jnp.exp2(jnp.where(lane < HEAD_DIM, cumb[:, lanes(i * 256, 128)], cumb[:, lanes(i * 256 + 128, 128)]))
        dye_out[:, cols] = (dy_out[:, cols].astype(f32) * grow).astype(bf16)
        return carry

    lax.fori_loop(0, PAIRS, weigh, 0)
    adj_out[...] = dot(c_in[...], dye_out[...], TN)
    grads_out[:INNER, :] = dot(dgate_out[...], normed[...], TN).astype(bf16)
    grads_out[INNER:, :] = dot(gn_s[...], db_s[...], TN).astype(bf16)


def middle(lengths, blk, gout, normed, gate, x, xd, b, c, cumt, cumb, rows_in, enter, gain, w_out):
    t = blk.shape[0]
    outs = [
        ((t, INNER), f32),
        ((t, D), bf16),
        ((t, INNER), bf16),
        ((t, INNER), bf16),
        ((t, INNER), bf16),
        ((8, INNER), f32),
        ((STATE, INNER), f32),
        ((2 * INNER, D), bf16),
    ]
    scratch = [
        pltpu.VMEM((t, t), f32),
        pltpu.VMEM((t, INNER), f32),
        pltpu.VMEM((t, INNER), f32),
        pltpu.VMEM((t, INNER), bf16),
        pltpu.VMEM((t, 128), f32),
        pltpu.VMEM((t, INNER), f32),
        pltpu.VMEM((t, D), bf16),
    ]
    args = (lengths, blk, gout, normed, gate, x, xd, b, c, cumt, cumb, rows_in, enter, gain, w_out)
    return call(middle_kernel, outs, args, scratch, smem=(0,))


def back_kernel(
    lengths_ref,
    y_in,
    dy_in,
    dye_in,
    x_in,
    xd_in,
    xde_in,
    b_in,
    c_in,
    run_in,
    cumt,
    cumb,
    head_in,
    rows_in,
    heads_ref,
    enter,
    own,
    leave,
    drun_out,
    dz_out,
    small_out,
    scores,
    dscores,
    skip_s,
    q_s,
    ry_s,
):
    rows = y_in.shape[0]
    causal = iota((rows, rows), 1) >= iota((rows, rows), 0)
    scores[...] = jnp.where(causal, dot(b_in[...], c_in[...], NT), 0.0)
    dscores[...] = jnp.zeros_like(dscores)
    q_s[...] = jnp.zeros_like(q_s)
    ry_s[...] = jnp.zeros_like(ry_s)
    lane = iota((rows, 128), 1)
    keep = valid_rows(lengths_ref, None, rows, 128)
    left = one_hot(iota((1, 128), 1) < HEAD_DIM)
    right = one_hot(iota((1, 128), 1) >= HEAD_DIM)
    pick_lane = iota((128, 128), 0)
    pick_head = iota((128, 128), 1)

    def dsilu(cols):
        running = run_in[:, cols]
        sg = sigmoid(running)
        return sg * (1.0 + running * (1.0 - sg))

    def pair(i, carry):
        cols = lanes(i * 128, 128)
        c0 = cumb[:, lanes(i * 256, 128)]
        c1 = cumb[:, lanes(i * 256 + 128, 128)]
        xd = xd_in[:, cols]
        dy = dy_in[:, cols]
        v = None
        for cc, part, mask in ((c0, 0, left), (c1, 1, right)):
            row = cumt[pl.ds(2 * i + part, 1), :]
            decay = jnp.exp2(jnp.minimum(row - jnp.concatenate([cc] * (rows // 128), axis=1), 0.0))
            masked = dy * mask
            term = dot((decay * scores[...]).astype(bf16), masked)
            v = term if v is None else v + term
            dscores[...] += decay * dot(xd, masked, NT)
        c01 = jnp.where(lane < HEAD_DIM, c0, c1)
        v = v + jnp.exp2(c01[rows - 1 : rows, :] - c01) * dot(b_in[...], leave[:, cols])
        pick = one_hot((pick_lane >> 6) + 2 * i == pick_head)
        dtw = split_dot(head_in[0], one_hot((pick_head >> 6) + 2 * i == pick_lane))
        x = x_in[:, cols]
        dyf = dy.astype(f32)
        q_s[...] += split_dot(x * v, pick)
        ry_s[...] += split_dot(dyf * y_in[:, cols], pick)
        skip_s[:, cols] = jnp.sum((dyf * x).reshape(rows // 8, 8, 128), axis=0)
        dx = dtw * v + rows_in[8:9, cols] * dyf
        drun_out[:, cols] = dx * keep * dsilu(cols)
        return carry

    lax.fori_loop(0, PAIRS, pair, 0)
    dsc = jnp.where(causal, dscores[...], 0.0).astype(bf16)
    d_b = dot(dsc, c_in[...]) + dot(xde_in[...], leave[...], NT)
    d_c = dot(dsc, b_in[...], TN) + dot(dye_in[...], enter[...], NT)
    drun_out[:, INNER : INNER + STATE] = d_b * dsilu(slice(INNER, INNER + STATE))
    drun_out[:, INNER + STATE :] = d_c * dsilu(slice(INNER + STATE, XBC))
    full_pick = one_hot((iota((INNER, 128), 0) >> 6) == iota((INNER, 128), 1))
    out_state = rows_in[0:1, :] * enter[...].astype(f32) + own[...]
    d_last = split_dot(
        jnp.sum((leave[...].astype(f32) * out_state).reshape(STATE // 8, 8, INNER), axis=0), full_pick
    )
    d_last = jnp.sum(d_last, axis=0, keepdims=True)
    dt = head_in[0]
    q = q_s[...]
    d_cum = ry_s[...] - dt * q + jnp.where(iota((rows, 128), 0) == rows - 1, d_last, 0.0)
    rates = -jnp.exp(heads_ref[1:2, :])
    above = one_hot(iota((rows, rows), 0) <= iota((rows, rows), 1))
    d_dt = q + split_dot_left(above, d_cum * rates)
    dz = d_dt * head_in[2]
    dz_out[...] = dz
    small_out[0:1, :] = jnp.sum(dz, axis=0, keepdims=True)
    small_out[1:2, :] = jnp.sum(d_cum * head_in[1], axis=0, keepdims=True)
    small_out[2:3, :] = jnp.sum(split_dot(skip_s[...], full_pick), axis=0, keepdims=True)
    small_out[3:8, :] = jnp.zeros((5, 128), f32)


def back(lengths, y, dy, dye, x, xd, xde, b, c, run, cumt, cumb, head, rows_in, heads, enter, own, leave):
    t = y.shape[0]
    outs = [((t, XBC), f32), ((t, 128), f32), ((8, 128), f32)]
    scratch = [
        pltpu.VMEM((t, t), f32),
        pltpu.VMEM((t, t), f32),
        pltpu.VMEM((8, INNER), f32),
        pltpu.VMEM((t, 128), f32),
        pltpu.VMEM((t, 128), f32),
    ]
    args = (lengths, y, dy, dye, x, xd, xde, b, c, run, cumt, cumb, head, rows_in, heads, enter, own, leave)
    return call(back_kernel, outs, args, scratch, smem=(0,))


VEC_ROW = XBC + 128
REST_ROWS = 2048


def last_kernel(
    blk,
    gout,
    normed,
    gain,
    w_in,
    conv_w,
    pad_in,
    drun_in,
    edge,
    dz_in,
    dgate,
    ggain,
    small_in,
    gin_out,
    grads_out,
    ext,
    dproj,
    vec,
    sums,
):
    rows = blk.shape[0]
    ext[0:rows, :] = drun_in[...]
    ext[rows : rows + 8, :] = edge[...]
    vec[...] = jnp.zeros_like(vec)

    def channels(i, carry):
        cols = lanes(i * 128, 128)
        drun = ext[0:rows, cols]
        total = drun * conv_w[CONV - 1 : CONV, cols]
        for tap in range(CONV - 1):
            ahead = CONV - 1 - tap
            total = total + ext[ahead : ahead + rows, cols] * conv_w[tap : tap + 1, cols]
        dproj[:, cols] = total.astype(bf16)
        for tap in range(CONV):
            sums[tap : tap + 1, cols] = jnp.sum(
                drun * pad_in[13 + tap : 13 + tap + rows, cols], axis=0, keepdims=True
            )
        sums[CONV : CONV + 1, cols] = jnp.sum(drun, axis=0, keepdims=True)
        return carry

    lax.fori_loop(0, XBC // 128, channels, 0)
    for v in range(CONV + 1):
        for part in range(3):
            width = min(D, XBC - part * D)
            vec[3 * v + part : 3 * v + part + 1, 0:width] = sums[v : v + 1, part * D : part * D + width]
    dz = dz_in[...].astype(bf16)
    d_normed = dot(dgate[...], w_in[:INNER, :])
    d_normed = d_normed + dot(dproj[...], w_in[INNER : INNER + XBC, :])
    d_normed = d_normed + dot(dz[:, :HEADS], w_in[INNER + XBC :, :])
    src = blk[...].astype(f32)
    scale = lax.rsqrt(jnp.mean(src * src, axis=-1, keepdims=True) + EPS)
    vec[15:16, :] = jnp.sum(d_normed * src * scale, axis=0, keepdims=True)
    gate_gain = jnp.sum(ggain[...], axis=0, keepdims=True)
    vec[16:17, :] = gate_gain[:, :D]
    vec[17:18, :] = gate_gain[:, D:]
    vec[18:21, 0:128] = small_in[0:3, :]
    weighted = d_normed * gain[...]
    average = jnp.mean(weighted * src, axis=-1, keepdims=True)
    gin_out[...] = gout[...].astype(f32) + scale * weighted - src * (scale * scale * scale) * average
    grads_out[:XBC, :] = dot(dproj[...], normed[...], TN).astype(bf16)
    grads_out[XBC:VEC_ROW, :] = dot(dz, normed[...], TN).astype(bf16)
    grads_out[VEC_ROW : VEC_ROW + 32, :] = vec[...].astype(bf16)
    grads_out[VEC_ROW + 32 :, :] = jnp.zeros((REST_ROWS - VEC_ROW - 32, D), bf16)


def last(blk, gout, normed, gain, w_in, conv_w, pad, drun, edge, dz, dgate, ggain, small):
    t = blk.shape[0]
    outs = [((t, D), f32), ((REST_ROWS, D), bf16)]
    scratch = [pltpu.VMEM((t + 8, XBC), f32), pltpu.VMEM((t, XBC), bf16), pltpu.VMEM((32, D), f32), pltpu.VMEM((8, XBC), f32)]
    args = (blk, gout, normed, gain, w_in, conv_w, pad, drun, edge, dz, dgate, ggain, small)
    return call(last_kernel, outs, args, scratch)


ORDERS = (("x", "y", "z1", "z2"), ("y", "x", "z1", "z2"), ("z1", "z2", "x", "y"))
STAGES = 9


def sum_kernel(waves, *refs):
    n = len(waves)
    count = 1 + max(array for array, _, _ in waves)
    ins = [refs[array].at[start : start + rows] for array, start, rows in waves]
    outs = [refs[count + array].at[start : start + rows] for array, start, rows in waves]
    acc, got = refs[2 * count : 2 * count + n], refs[2 * count + n : 2 * count + 2 * n]
    ssem, rsem = refs[2 * count + 2 * n :]
    place = lax.axis_index("seq")
    core = lax.axis_index("head")
    bits = {"c": core, "x": place % 2, "y": place // 2 % 2, "z1": place // 4 % 2, "z2": place // 8}
    steps = {"x": 1, "y": 2, "z1": 4, "z2": 8}

    def partner(d):
        if d == "c":
            return (place, 1 - core)
        return (place + steps[d] * (1 - 2 * bits[d]), core)

    barrier = pltpu.get_barrier_semaphore()
    for d in bits:
        pl.semaphore_signal(barrier, inc=1, device_id=partner(d), device_id_type=MESH)
    pl.semaphore_wait(barrier, len(bits))

    def stream(w, s):
        rows = waves[w][2]
        cols = slice(s * 256, (s + 1) * 256)
        order = ("c",) + ORDERS[s]
        index = w * 3 + s
        keeps, sends = [], []
        off, size = 0, rows
        for d in order[:4]:
            size //= 2
            keeps.append(off + bits[d] * size)
            sends.append(off + (1 - bits[d]) * size)
            off = keeps[-1]
        unit = rows // 16
        base = core * (rows // 2)
        sizes = [rows // 2, rows // 4, rows // 8, unit, unit]
        slots = [0, rows // 2, rows // 2 + rows // 4, rows - 2 * unit, rows - unit]

        def at(start, size):
            return pl.ds(pl.multiple_of(start, 16), size)

        def copy(stage):
            if stage < 5:
                d = order[stage]
                where = sends[stage] if stage < 4 else off
                size = sizes[stage]
                src = ins[w].at[at(where, size), cols] if stage == 0 else acc[w].at[at(where - base, size), cols]
                dst = got[w].at[slice(slots[stage], slots[stage] + size), cols]
            else:
                level = 8 - stage
                d = order[level]
                rows_here = at(keeps[level], sizes[level])
                src = outs[w].at[rows_here, cols]
                dst = outs[w].at[rows_here, cols]
            return pltpu.make_async_remote_copy(
                src_ref=src,
                dst_ref=dst,
                send_sem=ssem.at[index, stage],
                recv_sem=rsem.at[index, stage],
                device_id=partner(d),
                device_id_type=MESH,
            )

        def add(stage):
            where = keeps[stage] if stage < 4 else off
            size = sizes[stage]

            @pl.loop(0, size // unit)
            def _(i):
                here = at(where + i * unit, unit)
                local = at(where - base + i * unit, unit)
                term = got[w][slice(slots[stage], slots[stage] + size), cols] if size == unit else got[w][at(slots[stage] + i * unit, unit), cols]
                if stage == 0:
                    acc[w][local, cols] = ins[w][here, cols] + term
                elif stage < 4:
                    acc[w][local, cols] = acc[w][local, cols] + term
                else:
                    outs[w][here, cols] = acc[w][local, cols] + term

        return copy, add

    streams = {(w, s): stream(w, s) for w in range(n) for s in range(3)}
    for tick in range(STAGES + n):
        for w in range(n):
            stage = tick - w
            for s in range(3):
                copy, add = streams[w, s]
                if 0 < stage <= STAGES:
                    copy(stage - 1).wait()
                    if stage - 1 < 5:
                        add(stage - 1)
                if 0 <= stage < STAGES:
                    copy(stage).start()


def sum_over_devices(*arrays):
    waves = [(k, start, a.shape[0] // 2) for k, a in enumerate(arrays) for start in (0, a.shape[0] // 2)]
    n = len(waves)
    scratch = [pltpu.VMEM((r // 2, D), bf16) for _, _, r in waves] + [pltpu.VMEM((r, D), bf16) for _, _, r in waves]
    scratch += [pltpu.SemaphoreType.DMA((n * 3, STAGES)), pltpu.SemaphoreType.DMA((n * 3, STAGES))]
    return call(
        partial(sum_kernel, waves),
        [(a.shape, bf16) for a in arrays],
        arrays,
        scratch,
        collective_id=2,
        has_side_effects=True,
    )


def shifted(value, ahead):
    groups = lax.axis_size("head")
    count = lax.axis_size("seq") * groups
    moves = []
    for source in range(count):
        piece, half = source // groups, source % groups
        half += ahead
        if half == groups:
            half, piece = 0, piece + SEQS
        elif half < 0:
            half, piece = groups - 1, piece - SEQS
        if 0 <= piece * groups + half < count:
            moves.append((source, piece * groups + half))
    return lax.ppermute(value, ("seq", "head"), moves)


def local(block_in, grad_out, lengths, norm_gain, w_in, conv_w, conv_b, dt_bias, a_log, d_skip, gate_gain, w_out):
    fast = lax.axis_size("seq") == 16 and lax.axis_size("head") == 2
    swap = exchange if fast else exchange_plain
    total = sum_over_devices if fast else lambda *a: lax.psum(a, ("seq", "head"))
    w_in = w_in.T
    heads = jnp.pad(jnp.stack([dt_bias, a_log, d_skip]), ((0, 5), (0, 128 - HEADS)))
    gain = norm_gain.reshape(1, D)
    edge = shifted(block_in[-16:], 1)
    (normed, gate, pad, run, x, xd, xde, b, c, head, cumt, cumb, rows, own) = front(
        lengths, block_in, edge, gain, w_in, conv_w, conv_b.reshape(1, XBC), heads
    )
    enter = swap(own, rows[0:8], False)
    (y, block_out, dy, dye, dgate, ggain, adj, grads_a) = middle(
        lengths, block_in, grad_out, normed, gate, x, xd, b, c, cumt, cumb, rows, enter, gate_gain.reshape(1, INNER), w_out
    )
    leave = swap(adj, rows[0:8], True)
    drun, dz, small = back(
        lengths, y, dy, dye, x, xd, xde, b, c, run, cumt, cumb, head, rows, heads, enter, own, leave
    )
    edge_back = shifted(drun[0:8], -1)
    grad_in, grads_b = last(
        block_in, grad_out, normed, gain, w_in, conv_w, pad, drun, edge_back, dz, dgate, ggain, small
    )
    grads_a, grads_b = total(grads_a, grads_b)
    grad_w_in = jnp.concatenate([grads_a[:INNER], grads_b[: PROJ - INNER]], axis=0).astype(f32).T
    grad_w_out = grads_a[INNER:].astype(f32)
    vec = grads_b[VEC_ROW : VEC_ROW + 32].astype(f32)
    grad_conv = vec[0:12].reshape(CONV, 3 * D)[:, :XBC]
    grad_bias = vec[12:15].reshape(3 * D)[:XBC]
    grad_norm = vec[15]
    grad_gate = vec[16:18].reshape(INNER)
    grad_dt = vec[18, :HEADS]
    grad_alog = vec[19, :HEADS]
    grad_skip = vec[20, :HEADS]
    return (
        block_out,
        grad_in,
        grad_norm,
        grad_w_in,
        grad_conv,
        grad_bias,
        grad_dt,
        grad_alog,
        grad_skip,
        grad_gate,
        grad_w_out,
    )


def solution(mesh):
    rows = P(("seq", "head"), None)
    return jax.shard_map(
        local,
        mesh=mesh,
        in_specs=(rows, rows) + (P(),) * 10,
        out_specs=(rows, rows) + (P(),) * 9,
        check_vma=False,
    )
```

```python
from functools import partial

import jax
import jax.numpy as jnp
from jax import lax
from jax.experimental import pallas as pl
from jax.experimental.pallas import tpu as pltpu
from jax.sharding import PartitionSpec as P

D = 768
INNER = 1536
HEADS = 24
HEAD_DIM = 64
STATE = 128
CONV = 4
SEQS = 2
XBC = INNER + 2 * STATE
PROJ = 2 * INNER + 2 * STATE + HEADS
PAIRS = HEADS // 2
EPS = 1e-05
LOG2E = 1.4426950408889634

f32 = jnp.float32
bf16 = jnp.bfloat16
MESH = pl.DeviceIdType.MESH
VMEM = pl.BlockSpec(memory_space=pltpu.VMEM)
SMEM = pl.BlockSpec(memory_space=pltpu.SMEM)
NN = ((1,), (0,))
NT = ((1,), (1,))
TN = ((0,), (0,))


def dot(a, b, dims=NN):
    return lax.dot_general(a, b, (dims, ((), ())), preferred_element_type=f32)


def split_dot(a, pick, terms=3):
    total = None
    for _ in range(terms):
        part = a.astype(bf16)
        a = a - part.astype(f32)
        term = dot(part, pick)
        total = term if total is None else total + term
    return total


def split_dot_left(pick, a, terms=3):
    total = None
    for _ in range(terms):
        part = a.astype(bf16)
        a = a - part.astype(f32)
        term = dot(pick, part)
        total = term if total is None else total + term
    return total


def iota(shape, dim):
    return lax.broadcasted_iota(jnp.int32, shape, dim)


def one_hot(cond):
    return jnp.where(cond, 1.0, 0.0).astype(bf16)


def sigmoid(v):
    return 1.0 / (1.0 + jnp.exp(-v))


def lanes(start, size):
    return pl.ds(pl.multiple_of(start, 128), size)


def valid_rows(lengths_ref, rows, width):
    place = lax.axis_index("seq")
    first = (place // SEQS) * (rows * lax.axis_size("head")) + lax.axis_index("head") * rows
    limit = lengths_ref[place % SEQS]
    return jnp.where(iota((rows, width), 0) + first < limit, 1.0, 0.0)


def call(body, outs, args, scratch=(), smem=(), vmem=56 << 20, cost=None, **params):
    return pl.pallas_call(
        body,
        out_shape=[jax.ShapeDtypeStruct(s, d) for s, d in outs],
        in_specs=[SMEM if i in smem else VMEM for i in range(len(args))],
        out_specs=[VMEM] * len(outs),
        scratch_shapes=list(scratch),
        compiler_params=pltpu.CompilerParams(vmem_limit_bytes=vmem, **params),
    )(*args)


VEC_ROW = XBC + 128
REST_ROWS = 2048
FIRST_ROWS = 2 * INNER
WAVES = 4


def front_kernel(
    lengths_ref,
    blk,
    edge,
    gain,
    w_in,
    conv_w,
    conv_b,
    heads_ref,
    normed_out,
    gate_out,
    pad_out,
    run_out,
    x_out,
    xd_out,
    xde_out,
    b_out,
    c_out,
    head_out,
    cumt_out,
    cumb_out,
    rows_out,
    state_out,
):
    rows = blk.shape[0]

    def norm(v):
        v = v.astype(f32)
        scale = lax.rsqrt(jnp.mean(v * v, axis=-1, keepdims=True) + EPS)
        return (v * scale * gain[...]).astype(bf16)

    normed = norm(blk[...])
    normed_out[...] = normed
    gate_out[...] = dot(normed, w_in[:INNER, :], NT).astype(bf16)
    ahead = norm(edge[...])
    pad_out[0:16, :] = dot(ahead, w_in[INNER : INNER + XBC, :], NT).astype(bf16).astype(f32)
    pad_out[16 : 16 + rows, :] = dot(normed, w_in[INNER : INNER + XBC, :], NT).astype(bf16).astype(f32)
    keep = valid_rows(lengths_ref, rows, 128)
    head_out[3] = jnp.zeros((rows, 128), f32)
    head_out[3, :, 0:HEADS] = dot(normed, w_in[INNER + XBC :, :], NT).astype(bf16).astype(f32)
    lane = iota((rows, 128), 1)
    shifted = head_out[3] + heads_ref[0:1, :]
    soft = jnp.maximum(shifted, 0.0) + jnp.log1p(jnp.exp(-jnp.abs(shifted)))
    dt = jnp.where(lane < HEADS, soft * keep, 0.0)
    rates = -jnp.exp(heads_ref[1:2, :])
    below = one_hot(iota((rows, rows), 0) >= iota((rows, rows), 1))
    cum = split_dot_left(below, dt) * rates
    cum2 = cum * LOG2E
    head_out[0] = dt
    head_out[1] = cum
    head_out[2] = sigmoid(shifted) * keep
    head_out[3] = cum2
    cumt_out[...] = cum2.T
    pick_lane = iota((128, 256), 1)
    pick_head = iota((128, 256), 0)

    def spread(i, carry):
        cumb_out[:, lanes(i * 256, 256)] = split_dot(
            head_out[3], one_hot((pick_lane >> 7) + 2 * i == pick_head)
        )
        return carry

    lax.fori_loop(0, PAIRS, spread, 0)

    def convolve(i):
        cols = lanes(i * 256, 256)
        running = conv_b[:, cols] + pad_out[13 : 13 + rows, cols] * conv_w[0:1, cols]
        for tap in range(1, CONV):
            running = running + pad_out[13 + tap : 13 + tap + rows, cols] * conv_w[tap : tap + 1, cols]
        run_out[:, cols] = running
        return running * sigmoid(running)

    act = convolve(INNER // 256)
    b_out[...] = act[:, :STATE].astype(bf16)
    c_out[...] = act[:, STATE:].astype(bf16)
    keep2 = valid_rows(lengths_ref, rows, 256)

    def channels(i, carry):
        cols = lanes(i * 256, 256)
        pick = one_hot((pick_lane >> 6) + 4 * i == pick_head)
        x = convolve(i) * keep2
        x_out[:, cols] = x
        xd = x * split_dot(head_out[0], pick)
        xd_out[:, cols] = xd.astype(bf16)
        wide = split_dot(head_out[3], pick)
        last = wide[rows - 1 : rows, :]
        xde_out[:, cols] = (xd * jnp.exp2(last - wide)).astype(bf16)
        rows_out[0:8, cols] = jnp.broadcast_to(jnp.exp2(last), (8, 256))
        rows_out[8:16, cols] = split_dot(jnp.broadcast_to(heads_ref[2:3, :], (8, 128)), pick)
        return carry

    lax.fori_loop(0, INNER // 256, channels, 0)
    state_out[...] = dot(b_out[...], xde_out[...], TN)


def front(lengths, blk, edge, gain, w_in, conv_w, conv_b, heads):
    t = blk.shape[0]
    outs = [
        ((t, D), bf16),
        ((t, INNER), bf16),
        ((t + 16, XBC), f32),
        ((t, XBC), f32),
        ((t, INNER), f32),
        ((t, INNER), bf16),
        ((t, INNER), bf16),
        ((t, STATE), bf16),
        ((t, STATE), bf16),
        ((4, t, 128), f32),
        ((128, t), f32),
        ((t, HEADS * 128), f32),
        ((16, INNER), f32),
        ((STATE, INNER), f32),
    ]
    return call(front_kernel, outs, (lengths, blk, edge, gain, w_in, conv_w, conv_b, heads), smem=(0,))


def exchange_plain(state, decay, reverse):
    groups = lax.axis_size("head")
    count = lax.axis_size("seq") * groups
    place = lax.axis_index("seq")
    states = lax.all_gather(state.astype(bf16), ("seq", "head"), axis=0)
    decays = lax.all_gather(decay[0:1], ("seq", "head"), axis=0)
    blocks = count // SEQS
    block = place // SEQS * groups + lax.axis_index("head")

    def one(i, carry):
        source = blocks - 1 - i if reverse else i
        index = (source // groups * SEQS + place % SEQS) * groups + source % groups
        new = lax.dynamic_index_in_dim(decays, index, 0, False) * carry
        return new + lax.dynamic_index_in_dim(states, index, 0, False).astype(f32)

    ahead = blocks - 1 - block if reverse else block
    return lax.fori_loop(0, ahead, one, jnp.zeros(state.shape, f32)).astype(bf16)


def middle_kernel(
    lengths_ref,
    blk,
    gout,
    normed,
    gate,
    x_in,
    xd_in,
    b_in,
    c_in,
    cumt,
    cumb,
    rows_in,
    enter,
    gain,
    w_out,
    y_out,
    block_out,
    dy_out,
    dye_out,
    dgate_out,
    ggain_out,
    adj_out,
    grads_out,
    scores,
    mixed,
    gated_s,
    gn_s,
    scale_s,
    dgn_s,
    db_s,
):
    rows = blk.shape[0]
    causal = iota((rows, rows), 0) >= iota((rows, rows), 1)
    scores[...] = jnp.where(causal, dot(c_in[...], b_in[...], NT), 0.0)
    lane = iota((rows, 128), 1)
    left = one_hot(iota((1, 128), 1) < HEAD_DIM)
    right = one_hot(iota((1, 128), 1) >= HEAD_DIM)

    def pair(i, carry):
        cols = lanes(i * 128, 128)
        c0 = cumb[:, lanes(i * 256, 128)]
        c1 = cumb[:, lanes(i * 256 + 128, 128)]
        xd = xd_in[:, cols]
        y = None
        for cc, part, mask in ((c0, 0, left), (c1, 1, right)):
            row = cumt[pl.ds(2 * i + part, 1), :]
            decay = jnp.exp2(jnp.minimum(jnp.concatenate([cc] * (rows // 128), axis=1) - row, 0.0))
            term = dot((decay * scores[...]).astype(bf16), xd * mask)
            y = term if y is None else y + term
        grow = jnp.exp2(jnp.where(lane < HEAD_DIM, c0, c1))
        y = y + grow * dot(c_in[...], enter[:, cols])
        y_out[:, cols] = y
        mixed[:, cols] = (y + rows_in[8:9, cols] * x_in[:, cols]).astype(bf16).astype(f32)
        return carry

    lax.fori_loop(0, PAIRS, pair, 0)
    step = 32

    def gating(i, carry):
        r = pl.ds(pl.multiple_of(i * step, step), step)
        g = gate[r, :].astype(f32)
        gated = mixed[r, :] * g * sigmoid(g)
        scale = lax.rsqrt(jnp.mean(gated * gated, axis=-1, keepdims=True) + EPS)
        gated_s[r, :] = gated
        scale_s[r, :] = jnp.broadcast_to(scale, (step, 128))
        gn_s[r, :] = (gated * scale * gain[...]).astype(bf16)
        return carry

    lax.fori_loop(0, rows // step, gating, 0)
    keep = valid_rows(lengths_ref, rows, D)
    db_s[...] = (gout[...].astype(f32) * keep).astype(bf16)
    dgn_s[...] = dot(db_s[...], w_out[...], NT)
    block_out[...] = (blk[...].astype(f32) + keep * dot(gn_s[...], w_out[...])).astype(bf16)
    ggain_out[...] = jnp.zeros_like(ggain_out)

    def ungating(i, carry):
        r = pl.ds(pl.multiple_of(i * step, step), step)
        g = gate[r, :].astype(f32)
        sg = sigmoid(g)
        gated = gated_s[r, :]
        scale = scale_s[r, 0:1]
        dgn = dgn_s[r, :]
        ggain_out[...] += jnp.sum((dgn * gated * scale).reshape(step // 8, 8, INNER), axis=0)
        weighted = dgn * gain[...]
        average = jnp.mean(weighted * gated, axis=-1, keepdims=True)
        d_gated = scale * weighted - gated * (scale * scale * scale) * average
        dy_out[r, :] = (d_gated * g * sg).astype(bf16)
        dgate_out[r, :] = (d_gated * mixed[r, :] * sg * (1.0 + g * (1.0 - sg))).astype(bf16)
        return carry

    lax.fori_loop(0, rows // step, ungating, 0)

    def weigh(i, carry):
        cols = lanes(i * 128, 128)
        grow = jnp.exp2(jnp.where(lane < HEAD_DIM, cumb[:, lanes(i * 256, 128)], cumb[:, lanes(i * 256 + 128, 128)]))
        dye_out[:, cols] = (dy_out[:, cols].astype(f32) * grow).astype(bf16)
        return carry

    lax.fori_loop(0, PAIRS, weigh, 0)
    adj_out[...] = dot(c_in[...], dye_out[...], TN)
    grads_out[:INNER, :] = dot(dgate_out[...], normed[...], TN).astype(bf16)
    grads_out[INNER:, :] = dot(gn_s[...], db_s[...], TN).astype(bf16)


def middle(lengths, blk, gout, normed, gate, x, xd, b, c, cumt, cumb, rows_in, enter, gain, w_out):
    t = blk.shape[0]
    outs = [
        ((t, INNER), f32),
        ((t, D), bf16),
        ((t, INNER), bf16),
        ((t, INNER), bf16),
        ((t, INNER), bf16),
        ((8, INNER), f32),
        ((STATE, INNER), f32),
        ((2 * INNER, D), bf16),
    ]
    scratch = [
        pltpu.VMEM((t, t), f32),
        pltpu.VMEM((t, INNER), f32),
        pltpu.VMEM((t, INNER), f32),
        pltpu.VMEM((t, INNER), bf16),
        pltpu.VMEM((t, 128), f32),
        pltpu.VMEM((t, INNER), f32),
        pltpu.VMEM((t, D), bf16),
    ]
    args = (lengths, blk, gout, normed, gate, x, xd, b, c, cumt, cumb, rows_in, enter, gain, w_out)
    return call(middle_kernel, outs, args, scratch, smem=(0,))


def back_kernel(
    lengths_ref,
    y_in,
    dy_in,
    dye_in,
    x_in,
    xd_in,
    xde_in,
    b_in,
    c_in,
    run_in,
    cumt,
    cumb,
    head_in,
    rows_in,
    heads_ref,
    enter,
    own,
    leave,
    drun_out,
    dz_out,
    small_out,
    scores,
    dscores,
    skip_s,
    q_s,
    ry_s,
):
    rows = y_in.shape[0]
    causal = iota((rows, rows), 1) >= iota((rows, rows), 0)
    scores[...] = jnp.where(causal, dot(b_in[...], c_in[...], NT), 0.0)
    dscores[...] = jnp.zeros_like(dscores)
    q_s[...] = jnp.zeros_like(q_s)
    ry_s[...] = jnp.zeros_like(ry_s)
    lane = iota((rows, 128), 1)
    keep = valid_rows(lengths_ref, rows, 128)
    left = one_hot(iota((1, 128), 1) < HEAD_DIM)
    right = one_hot(iota((1, 128), 1) >= HEAD_DIM)
    pick_lane = iota((128, 128), 0)
    pick_head = iota((128, 128), 1)

    def dsilu(cols):
        running = run_in[:, cols]
        sg = sigmoid(running)
        return sg * (1.0 + running * (1.0 - sg))

    def pair(i, carry):
        cols = lanes(i * 128, 128)
        c0 = cumb[:, lanes(i * 256, 128)]
        c1 = cumb[:, lanes(i * 256 + 128, 128)]
        xd = xd_in[:, cols]
        dy = dy_in[:, cols]
        v = None
        for cc, part, mask in ((c0, 0, left), (c1, 1, right)):
            row = cumt[pl.ds(2 * i + part, 1), :]
            decay = jnp.exp2(jnp.minimum(row - jnp.concatenate([cc] * (rows // 128), axis=1), 0.0))
            masked = dy * mask
            term = dot((decay * scores[...]).astype(bf16), masked)
            v = term if v is None else v + term
            dscores[...] += decay * dot(xd, masked, NT)
        c01 = jnp.where(lane < HEAD_DIM, c0, c1)
        v = v + jnp.exp2(c01[rows - 1 : rows, :] - c01) * dot(b_in[...], leave[:, cols])
        pick = one_hot((pick_lane >> 6) + 2 * i == pick_head)
        dtw = split_dot(head_in[0], one_hot((pick_head >> 6) + 2 * i == pick_lane))
        x = x_in[:, cols]
        dyf = dy.astype(f32)
        q_s[...] += split_dot(x * v, pick)
        ry_s[...] += split_dot(dyf * y_in[:, cols], pick)
        skip_s[:, cols] = jnp.sum((dyf * x).reshape(rows // 8, 8, 128), axis=0)
        dx = dtw * v + rows_in[8:9, cols] * dyf
        drun_out[:, cols] = dx * keep * dsilu(cols)
        return carry

    lax.fori_loop(0, PAIRS, pair, 0)
    dsc = jnp.where(causal, dscores[...], 0.0).astype(bf16)
    d_b = dot(dsc, c_in[...]) + dot(xde_in[...], leave[...], NT)
    d_c = dot(dsc, b_in[...], TN) + dot(dye_in[...], enter[...], NT)
    drun_out[:, INNER : INNER + STATE] = d_b * dsilu(slice(INNER, INNER + STATE))
    drun_out[:, INNER + STATE :] = d_c * dsilu(slice(INNER + STATE, XBC))
    full_pick = one_hot((iota((INNER, 128), 0) >> 6) == iota((INNER, 128), 1))
    out_state = rows_in[0:1, :] * enter[...].astype(f32) + own[...]
    d_last = split_dot(
        jnp.sum((leave[...].astype(f32) * out_state).reshape(STATE // 8, 8, INNER), axis=0), full_pick
    )
    d_last = jnp.sum(d_last, axis=0, keepdims=True)
    dt = head_in[0]
    q = q_s[...]
    d_cum = ry_s[...] - dt * q + jnp.where(iota((rows, 128), 0) == rows - 1, d_last, 0.0)
    rates = -jnp.exp(heads_ref[1:2, :])
    above = one_hot(iota((rows, rows), 0) <= iota((rows, rows), 1))
    d_dt = q + split_dot_left(above, d_cum * rates)
    dz = d_dt * head_in[2]
    dz_out[...] = dz
    small_out[0:1, :] = jnp.sum(dz, axis=0, keepdims=True)
    small_out[1:2, :] = jnp.sum(d_cum * head_in[1], axis=0, keepdims=True)
    small_out[2:3, :] = jnp.sum(split_dot(skip_s[...], full_pick), axis=0, keepdims=True)
    small_out[3:8, :] = jnp.zeros((5, 128), f32)


def back(lengths, y, dy, dye, x, xd, xde, b, c, run, cumt, cumb, head, rows_in, heads, enter, own, leave):
    t = y.shape[0]
    outs = [((t, XBC), f32), ((t, 128), f32), ((8, 128), f32)]
    scratch = [
        pltpu.VMEM((t, t), f32),
        pltpu.VMEM((t, t), f32),
        pltpu.VMEM((8, INNER), f32),
        pltpu.VMEM((t, 128), f32),
        pltpu.VMEM((t, 128), f32),
    ]
    args = (lengths, y, dy, dye, x, xd, xde, b, c, run, cumt, cumb, head, rows_in, heads, enter, own, leave)
    return call(back_kernel, outs, args, scratch, smem=(0,))


def last_kernel(
    blk,
    gout,
    normed,
    gain,
    w_in,
    conv_w,
    pad_in,
    drun_in,
    edge,
    dz_in,
    dgate,
    ggain,
    small_in,
    gin_out,
    grads_out,
    ext,
    dproj,
    vec,
    sums,
):
    rows = blk.shape[0]
    ext[0:rows, :] = drun_in[...]
    ext[rows : rows + 8, :] = edge[...]
    vec[...] = jnp.zeros_like(vec)

    def channels(i, carry):
        cols = lanes(i * 128, 128)
        drun = ext[0:rows, cols]
        total = drun * conv_w[CONV - 1 : CONV, cols]
        for tap in range(CONV - 1):
            ahead = CONV - 1 - tap
            total = total + ext[ahead : ahead + rows, cols] * conv_w[tap : tap + 1, cols]
        dproj[:, cols] = total.astype(bf16)
        for tap in range(CONV):
            sums[tap : tap + 1, cols] = jnp.sum(
                drun * pad_in[13 + tap : 13 + tap + rows, cols], axis=0, keepdims=True
            )
        sums[CONV : CONV + 1, cols] = jnp.sum(drun, axis=0, keepdims=True)
        return carry

    lax.fori_loop(0, XBC // 128, channels, 0)
    for v in range(CONV + 1):
        for part in range(3):
            width = min(D, XBC - part * D)
            vec[3 * v + part : 3 * v + part + 1, 0:width] = sums[v : v + 1, part * D : part * D + width]
    dz = dz_in[...].astype(bf16)
    d_normed = dot(dgate[...], w_in[:INNER, :])
    d_normed = d_normed + dot(dproj[...], w_in[INNER : INNER + XBC, :])
    d_normed = d_normed + dot(dz[:, :HEADS], w_in[INNER + XBC :, :])
    src = blk[...].astype(f32)
    scale = lax.rsqrt(jnp.mean(src * src, axis=-1, keepdims=True) + EPS)
    vec[15:16, :] = jnp.sum(d_normed * src * scale, axis=0, keepdims=True)
    gate_gain = jnp.sum(ggain[...], axis=0, keepdims=True)
    vec[16:17, :] = gate_gain[:, :D]
    vec[17:18, :] = gate_gain[:, D:]
    vec[18:21, 0:128] = small_in[0:3, :]
    weighted = d_normed * gain[...]
    average = jnp.mean(weighted * src, axis=-1, keepdims=True)
    gin_out[...] = gout[...].astype(f32) + scale * weighted - src * (scale * scale * scale) * average
    grads_out[:XBC, :] = dot(dproj[...], normed[...], TN).astype(bf16)
    grads_out[XBC:VEC_ROW, :] = dot(dz, normed[...], TN).astype(bf16)
    grads_out[VEC_ROW : VEC_ROW + 32, :] = vec[...].astype(bf16)
    grads_out[VEC_ROW + 32 :, :] = jnp.zeros((REST_ROWS - VEC_ROW - 32, D), bf16)


def last(blk, gout, normed, gain, w_in, conv_w, pad, drun, edge, dz, dgate, ggain, small):
    t = blk.shape[0]
    outs = [((t, D), f32), ((REST_ROWS, D), bf16)]
    scratch = [pltpu.VMEM((t + 8, XBC), f32), pltpu.VMEM((t, XBC), bf16), pltpu.VMEM((32, D), f32), pltpu.VMEM((8, XBC), f32)]
    args = (blk, gout, normed, gain, w_in, conv_w, pad, drun, edge, dz, dgate, ggain, small)
    return call(last_kernel, outs, args, scratch)


class Refs:
    def __init__(self, names, refs):
        self.__dict__.update(zip(names, refs, strict=True))


def remote(src, dst, ssem, rsem, to):
    return pltpu.make_async_remote_copy(
        src_ref=src, dst_ref=dst, send_sem=ssem, recv_sem=rsem, device_id=to, device_id_type=MESH
    )


class Exchange:
    def __init__(self, reverse, state, decay, out, bufs, ssem, rsem):
        self.sib_state, self.sib_decay, self.mine, self.total, self.got, self.got_decay, self.back, self.back_got = bufs
        self.state, self.decay, self.out, self.reverse = state, decay, out, reverse
        self.ssem, self.rsem = ssem, rsem
        self.half = INNER // 2
        self.chips = lax.axis_size("seq") // SEQS
        self.rows = STATE // self.chips
        self.place, self.core = lax.axis_index("seq"), lax.axis_index("head")
        self.chip, self.which = self.place // SEQS, self.place % SEQS
        self.sibling = (self.place, 1 - self.core)
        self.later = (1 - self.core if reverse else self.core) == 1
        self.own_cols = lanes(self.core * self.half, self.half)
        self.sib_cols = lanes((1 - self.core) * self.half, self.half)
        self.flying = []

    def peer(self, k):
        return (lax.rem(self.chip + k, self.chips) * SEQS + self.which, self.core)

    def send(self, copies):
        self.flying = [remote(src, dst, self.ssem.at[n], self.rsem.at[n], to) for src, dst, n, to in copies]
        for c in self.flying:
            c.start()

    def arrive(self):
        for c in self.flying:
            c.wait()

    def begin(self):
        self.send(
            [
                (self.state.at[:, self.sib_cols], self.sib_state, 0, self.sibling),
                (self.decay.at[0:8, self.sib_cols], self.sib_decay, 1, self.sibling),
            ]
        )

    def ordered(self):
        own, other = self.state[:, self.own_cols], self.sib_state[...]
        own_decay, other_decay = self.decay[0:1, self.own_cols], self.sib_decay[0:1, :]
        later = self.later
        return (
            jnp.where(later, other, own),
            jnp.where(later, own, other),
            jnp.where(later, other_decay, own_decay),
            jnp.where(later, own_decay, other_decay),
        )

    def deal(self):
        self.arrive()
        early, late, early_decay, late_decay = self.ordered()
        self.mine[...] = (late_decay * early + late).astype(bf16)
        self.total[...] = jnp.broadcast_to(early_decay * late_decay, self.total.shape)
        copies = []
        for k in range(1, self.chips):
            to = lax.rem(self.chip + k, self.chips)
            piece = pl.ds(pl.multiple_of(to * self.rows, self.rows), self.rows)
            copies.append((self.mine.at[piece], self.got.at[k], 2 * k, self.peer(k)))
            copies.append((self.total, self.got_decay.at[k], 2 * k + 1, self.peer(k)))
        self.send(copies)
        self.got[0] = self.mine[pl.ds(pl.multiple_of(self.chip * self.rows, self.rows), self.rows), :]
        self.got_decay[0] = self.total[...]

    def scan(self):
        self.arrive()
        chips, chip = self.chips, self.chip

        def one(i, carry):
            source = chips - 1 - i if self.reverse else i
            slot = lax.rem(chip - source + chips, chips)
            to = lax.rem(source - chip + chips, chips)
            self.back[pl.ds(to, 1)] = carry.astype(bf16)[None]
            return self.got_decay[pl.ds(slot, 1)][0, 0:1, :] * carry + self.got[pl.ds(slot, 1)][0].astype(f32)

        lax.fori_loop(0, chips, one, jnp.zeros((self.rows, self.half), f32))
        here = pl.ds(pl.multiple_of(chip * self.rows, self.rows), self.rows)
        self.send([(self.back.at[k], self.back_got.at[here], 2 * chips + k, self.peer(k)) for k in range(1, chips)])
        self.back_got[here, :] = self.back[0]

    def hand(self):
        self.arrive()
        early, _, early_decay, _ = self.ordered()
        enter = self.back_got[...].astype(f32)
        second = early_decay * enter + early
        self.out[:, self.own_cols] = jnp.where(self.later, second, enter).astype(bf16)
        self.mine[...] = jnp.where(self.later, enter, second).astype(bf16)
        self.send([(self.mine, self.out.at[:, self.own_cols], 2 * self.chips, self.sibling)])


def exchange_scratch(chips):
    half, rows, n = INNER // 2, STATE // chips, 3 * chips
    return [
        pltpu.VMEM((STATE, half), f32),
        pltpu.VMEM((8, half), f32),
        pltpu.VMEM((STATE, half), bf16),
        pltpu.VMEM((8, half), f32),
        pltpu.VMEM((chips, rows, half), bf16),
        pltpu.VMEM((chips, 8, half), f32),
        pltpu.VMEM((chips, rows, half), bf16),
        pltpu.VMEM((STATE, half), bf16),
        pltpu.SemaphoreType.DMA((n,)),
        pltpu.SemaphoreType.DMA((n,)),
    ]


ORDERS = (("x", "y", "z1", "z2"), ("y", "x", "z1", "z2"), ("z1", "z2", "x", "y"))
STEPS = {"x": 1, "y": 2, "z1": 4, "z2": 8}
STAGES = 9


def bits_of():
    place = lax.axis_index("seq")
    return {
        "c": lax.axis_index("head"),
        "x": place % 2,
        "y": place // 2 % 2,
        "z1": place // 4 % 2,
        "z2": place // 8,
    }


def partner(d):
    place, core = lax.axis_index("seq"), lax.axis_index("head")
    if d == "c":
        return (place, 1 - core)
    return (place + STEPS[d] * (1 - 2 * bits_of()[d]), core)


class Sum:
    def __init__(self, held, got, out, ssem, rsem, lsem):
        self.streams = [self.stream(held, got, out, ssem, rsem, lsem, s) for s in range(3)]
        self.stage = -1

    def stream(self, held, got, out, ssem, rsem, lsem, s):
        rows = held.shape[0]
        bits = bits_of()
        cols = slice(s * 256, (s + 1) * 256)
        order = ("c",) + ORDERS[s]
        keeps, sends = [], []
        off, size = 0, rows
        for d in order[:4]:
            size //= 2
            keeps.append(off + bits[d] * size)
            sends.append(off + (1 - bits[d]) * size)
            off = keeps[-1]
        unit = rows // 16
        sizes = [rows // 2, rows // 4, rows // 8, unit, unit]
        slots = [0, rows // 2, rows // 2 + rows // 4, rows - 2 * unit, rows - unit]

        def at(start, size):
            return pl.ds(pl.multiple_of(start, 16), size)

        def copy(stage):
            if stage < 5:
                d = order[stage]
                where = at(sends[stage] if stage < 4 else off, sizes[stage])
                src, dst = held.at[where, cols], got.at[slice(slots[stage], slots[stage] + sizes[stage]), cols]
            else:
                d = order[8 - stage]
                where = at(keeps[8 - stage], sizes[8 - stage])
                src, dst = (held if stage == 5 else out).at[where, cols], out.at[where, cols]
            return remote(src, dst, ssem.at[s, stage], rsem.at[s, stage], partner(d))

        def add(stage):
            where = keeps[stage] if stage < 4 else off

            @pl.loop(0, sizes[stage] // unit)
            def _(i):
                here = at(where + i * unit, unit)
                held[here, cols] = held[here, cols] + got[at(slots[stage] + i * unit, unit), cols]

        def place():
            return pltpu.make_async_copy(held.at[at(off, unit), cols], out.at[at(off, unit), cols], lsem.at[s])

        return copy, add, place

    def tick(self):
        for copy, add, place in self.streams:
            if 0 <= self.stage < STAGES:
                copy(self.stage).wait()
                if self.stage < 5:
                    add(self.stage)
            if self.stage == 4:
                place().start()
            if self.stage == 5:
                place().wait()
            if self.stage + 1 < STAGES:
                copy(self.stage + 1).start()
        self.stage += 1


def greet():
    place, core = lax.axis_index("seq"), lax.axis_index("head")
    pieces = lax.axis_size("seq")
    chips = pieces // SEQS
    barrier = pltpu.get_barrier_semaphore()
    peers = [partner(d) for d in ("c", "x", "y", "z1", "z2")]
    peers += [((place // SEQS + k) % chips * SEQS + place % SEQS, core) for k in range(1, chips)]
    peers += [block_at(1), block_at(-1)]
    for to in peers:
        pl.semaphore_signal(barrier, inc=1, device_id=to, device_id_type=MESH)
    pl.semaphore_wait(barrier, len(peers))


def block_at(ahead):
    place, core = lax.axis_index("seq"), lax.axis_index("head")
    pieces = lax.axis_size("seq")
    block = (place // SEQS * 2 + core + ahead + pieces) % pieces
    return (block // 2 * SEQS + place % SEQS, block % 2)


def whole_kernel(names, *refs):
    r = Refs(names, refs)
    rows = r.blk.shape[0]
    place, core = lax.axis_index("seq"), lax.axis_index("head")
    chips = lax.axis_size("seq") // SEQS
    block = place // SEQS * 2 + core
    loads = [
        pltpu.make_async_copy(r.w_in_hbm.at[INNER:], r.w_in.at[INNER:], r.load_sem.at[0]),
        pltpu.make_async_copy(r.w_in_hbm.at[:INNER], r.w_in.at[:INNER], r.load_sem.at[1]),
        pltpu.make_async_copy(r.w_out_hbm, r.w_out, r.load_sem.at[2]),
    ]
    for c in loads:
        c.start()
    greet()
    edge = remote(r.blk.at[rows - 16 :], r.edge, r.edge_sem.at[0], r.edge_sem.at[1], block_at(1))
    edge.start()

    def norm(v):
        v = v.astype(f32)
        scale = lax.rsqrt(jnp.mean(v * v, axis=-1, keepdims=True) + EPS)
        return (v * scale * r.gain[...]).astype(bf16)

    r.normed[16:, :] = norm(r.blk[...])
    lane = iota((rows, 128), 1)
    keep = valid_rows(r.lengths, rows, 128)
    pick_lane = iota((128, 256), 1)
    pick_head = iota((128, 256), 0)
    left = one_hot(iota((1, 128), 1) < HEAD_DIM)
    right = one_hot(iota((1, 128), 1) >= HEAD_DIM)
    own_rows = slice(16, 16 + rows)

    loads[0].wait()
    r.head[3] = jnp.zeros((rows, 128), f32)
    r.head[3, :, 0:HEADS] = dot(r.normed[own_rows, :], r.w_in[INNER + XBC :, :], NT).astype(bf16).astype(f32)
    moved = r.head[3] + r.heads[0:1, :]
    soft = jnp.maximum(moved, 0.0) + jnp.log1p(jnp.exp(-jnp.abs(moved)))
    dt = jnp.where(lane < HEADS, soft * keep, 0.0)
    rates = -jnp.exp(r.heads[1:2, :])
    below = one_hot(iota((rows, rows), 0) >= iota((rows, rows), 1))
    cum = split_dot_left(below, dt) * rates
    cum2 = cum * LOG2E
    r.head[0] = dt
    r.head[1] = cum
    r.head[2] = sigmoid(moved) * keep
    r.head[3] = cum2
    r.cumt[...] = cum2.T

    def spread(i, carry):
        r.cumb[:, lanes(i * 256, 256)] = split_dot(r.head[3], one_hot((pick_lane >> 7) + 2 * i == pick_head))
        return carry

    lax.fori_loop(0, PAIRS, spread, 0)

    edge.wait()
    r.normed[0:16, :] = jnp.where(block == 0, 0.0, norm(r.edge[...]).astype(f32)).astype(bf16)

    def convolve(i):
        cols = lanes(i * 256, 256)
        part = dot(r.normed[...], r.w_in[pl.ds(pl.multiple_of(INNER + i * 256, 256), 256), :], NT)
        r.pad[:, cols] = part.astype(bf16).astype(f32)
        running = r.conv_b[:, cols] + r.pad[13 : 13 + rows, cols] * r.conv_w[0:1, cols]
        for tap in range(1, CONV):
            running = running + r.pad[13 + tap : 13 + tap + rows, cols] * r.conv_w[tap : tap + 1, cols]
        r.run[:, cols] = running
        return running * sigmoid(running)

    act = convolve(INNER // 256)
    r.b[...] = act[:, :STATE].astype(bf16)
    r.c[...] = act[:, STATE:].astype(bf16)
    keep2 = valid_rows(r.lengths, rows, 256)

    def channels(i, carry):
        cols = lanes(i * 256, 256)
        pick = one_hot((pick_lane >> 6) + 4 * i == pick_head)
        x = convolve(i) * keep2
        r.x[:, cols] = x
        xd = x * split_dot(r.head[0], pick)
        r.xd[:, cols] = xd.astype(bf16)
        wide = split_dot(r.head[3], pick)
        last = wide[rows - 1 : rows, :]
        r.xde[:, cols] = (xd * jnp.exp2(last - wide)).astype(bf16)
        r.spread[0:8, cols] = jnp.broadcast_to(jnp.exp2(last), (8, 256))
        r.spread[8:16, cols] = split_dot(jnp.broadcast_to(r.heads[2:3, :], (8, 128)), pick)
        return carry

    lax.fori_loop(0, INNER // 256, channels, 0)
    r.own[...] = dot(r.b[...], r.xde[...], TN)
    bufs = 8
    enter = Exchange(False, r.own, r.spread, r.enter, [getattr(r, f"f{k}") for k in range(bufs)], r.fs, r.fr)
    leave = Exchange(True, r.adj, r.spread, r.leave, [getattr(r, f"g{k}") for k in range(bufs)], r.gs, r.gr)
    enter.begin()

    causal = iota((rows, rows), 0) >= iota((rows, rows), 1)
    r.scores[...] = jnp.where(causal, dot(r.c[...], r.b[...], NT), 0.0)
    r.scores_t[...] = jnp.where(
        iota((rows, rows), 1) >= iota((rows, rows), 0), dot(r.b[...], r.c[...], NT), 0.0
    )
    loads[1].wait()
    enter.deal()

    def gates(i, carry):
        part = dot(r.normed[own_rows, :], r.w_in[pl.ds(pl.multiple_of(i * 256, 256), 256), :], NT)
        r.gate[:, lanes(i * 256, 256)] = part.astype(bf16)
        return carry

    def columns(i):
        c0 = r.cumb[:, lanes(i * 256, 128)]
        c1 = r.cumb[:, lanes(i * 256 + 128, 128)]
        return c0, c1

    def pair(i, carry):
        cols = lanes(i * 128, 128)
        xd = r.xd[:, cols]
        y = None
        for cc, part, mask in zip(columns(i), (0, 1), (left, right), strict=True):
            row = r.cumt[pl.ds(2 * i + part, 1), :]
            decay = jnp.exp2(jnp.minimum(jnp.concatenate([cc] * (rows // 128), axis=1) - row, 0.0))
            term = dot((decay * r.scores[...]).astype(bf16), xd * mask)
            y = term if y is None else y + term
        r.y[:, cols] = y
        return carry

    lax.fori_loop(0, INNER // 256, gates, 0)
    lax.fori_loop(0, PAIRS // 2, pair, 0)
    enter.scan()
    lax.fori_loop(PAIRS // 2, PAIRS, pair, 0)
    enter.hand()
    keep_d = valid_rows(r.lengths, rows, D)
    r.db[...] = (r.gout[...].astype(f32) * keep_d).astype(bf16)
    loads[2].wait()
    r.wide[...] = dot(r.db[...], r.w_out[...], NT)
    enter.arrive()

    def carried(i, carry):
        cols = lanes(i * 128, 128)
        c0, c1 = columns(i)
        y = r.y[:, cols] + jnp.exp2(jnp.where(lane < HEAD_DIM, c0, c1)) * dot(r.c[...], r.enter[:, cols])
        r.y[:, cols] = y
        r.mixed[:, cols] = (y + r.spread[8:9, cols] * r.x[:, cols]).astype(bf16)
        return carry

    lax.fori_loop(0, PAIRS, carried, 0)

    r.ggain[...] = jnp.zeros_like(r.ggain)
    step = 32

    def gating(i, carry):
        at = pl.ds(pl.multiple_of(i * step, step), step)
        g = r.gate[at, :].astype(f32)
        sg = sigmoid(g)
        mixed = r.mixed[at, :].astype(f32)
        gated = mixed * g * sg
        scale = lax.rsqrt(jnp.mean(gated * gated, axis=-1, keepdims=True) + EPS)
        r.gn[at, :] = (gated * scale * r.gate_gain[...]).astype(bf16)
        dgn = r.wide[at, :]
        r.ggain[...] += jnp.sum((dgn * gated * scale).reshape(step // 8, 8, INNER), axis=0)
        weighted = dgn * r.gate_gain[...]
        average = jnp.mean(weighted * gated, axis=-1, keepdims=True)
        d_gated = scale * weighted - gated * (scale * scale * scale) * average
        r.dy[at, :] = (d_gated * g * sg).astype(bf16)
        r.dgate[at, :] = (d_gated * mixed * sg * (1.0 + g * (1.0 - sg))).astype(bf16)
        return carry

    lax.fori_loop(0, rows // step, gating, 0)

    def weigh(i, carry):
        cols = lanes(i * 128, 128)
        c0, c1 = columns(i)
        grow = jnp.exp2(jnp.where(lane < HEAD_DIM, c0, c1))
        r.dye[:, cols] = (r.dy[:, cols].astype(f32) * grow).astype(bf16)
        return carry

    lax.fori_loop(0, PAIRS, weigh, 0)
    r.adj[...] = dot(r.c[...], r.dye[...], TN)
    leave.begin()

    def gate_grads(i, carry):
        at = pl.ds(pl.multiple_of(i * 256, 256), 256)
        r.first[at, :] = dot(r.dgate[:, lanes(i * 256, 256)], r.normed[own_rows, :], TN).astype(bf16)
        return carry

    def out_grads(i, carry):
        at = pl.ds(pl.multiple_of(INNER + i * 256, 256), 256)
        r.first[at, :] = dot(r.gn[:, lanes(i * 256, 256)], r.db[...], TN).astype(bf16)
        return carry

    def part(k, held, got, out, at):
        return Sum(held.at[at], got.at[at], out.at[at], r.ss.at[k], r.rs.at[k], r.ls.at[k])

    half = REST_ROWS // 2
    sums = [
        part(0, r.first, r.got_first, r.first_out, slice(0, INNER)),
        part(1, r.first, r.got_first, r.first_out, slice(INNER, FIRST_ROWS)),
        part(2, r.rest, r.got_rest, r.rest_out, slice(0, half)),
        part(3, r.rest, r.got_rest, r.rest_out, slice(half, REST_ROWS)),
    ]
    lax.fori_loop(0, INNER // 256, gate_grads, 0)
    leave.deal()
    sums[0].tick()
    lax.fori_loop(0, INNER // 256, out_grads, 0)
    r.block_out[...] = (r.blk[...].astype(f32) + keep_d * dot(r.gn[...], r.w_out[...])).astype(bf16)
    sums[1].tick()

    r.dscores[...] = jnp.zeros_like(r.dscores)
    r.q[...] = jnp.zeros_like(r.q)
    r.ry[...] = jnp.zeros_like(r.ry)
    row_head = iota((128, 128), 0)
    col_head = iota((128, 128), 1)

    def dsilu(cols):
        running = r.run[:, cols]
        sg = sigmoid(running)
        return sg * (1.0 + running * (1.0 - sg))

    def pair_back(i, carry):
        cols = lanes(i * 128, 128)
        xd, dy = r.xd[:, cols], r.dy[:, cols]
        v = None
        for cc, part, mask in zip(columns(i), (0, 1), (left, right), strict=True):
            row = r.cumt[pl.ds(2 * i + part, 1), :]
            decay = jnp.exp2(jnp.minimum(row - jnp.concatenate([cc] * (rows // 128), axis=1), 0.0))
            masked = dy * mask
            term = dot((decay * r.scores_t[...]).astype(bf16), masked)
            v = term if v is None else v + term
            r.dscores[...] += decay * dot(xd, masked, NT)
        r.wide[:, cols] = v
        r.ry[...] += split_dot(dy.astype(f32) * r.y[:, cols], one_hot((row_head >> 6) + 2 * i == col_head))
        return carry

    lax.fori_loop(0, PAIRS // 2, pair_back, 0)
    leave.scan()
    sums[0].tick()
    lax.fori_loop(PAIRS // 2, PAIRS, pair_back, 0)
    leave.hand()
    sums[1].tick()
    dsc = jnp.where(iota((rows, rows), 1) >= iota((rows, rows), 0), r.dscores[...], 0.0).astype(bf16)
    d_b = dot(dsc, r.c[...])
    d_c = dot(dsc, r.b[...], TN) + dot(r.dye[...], r.enter[...], NT)
    leave.arrive()

    def channels_back(i, carry):
        cols = lanes(i * 128, 128)
        c0, c1 = columns(i)
        c01 = jnp.where(lane < HEAD_DIM, c0, c1)
        v = r.wide[:, cols] + jnp.exp2(c01[rows - 1 : rows, :] - c01) * dot(r.b[...], r.leave[:, cols])
        dtw = split_dot(r.head[0], one_hot((col_head >> 6) + 2 * i == row_head))
        x = r.x[:, cols]
        dy = r.dy[:, cols].astype(f32)
        r.q[...] += split_dot(x * v, one_hot((row_head >> 6) + 2 * i == col_head))
        r.skip[:, cols] = jnp.sum((dy * x).reshape(rows // 8, 8, 128), axis=0)
        r.ext[0:rows, cols] = (dtw * v + r.spread[8:9, cols] * dy) * keep * dsilu(cols)
        return carry

    lax.fori_loop(0, PAIRS, channels_back, 0)
    d_b = d_b + dot(r.xde[...], r.leave[...], NT)
    r.ext[0:rows, INNER : INNER + STATE] = d_b * dsilu(slice(INNER, INNER + STATE))
    r.ext[0:rows, INNER + STATE :] = d_c * dsilu(slice(INNER + STATE, XBC))
    edge_back = remote(r.ext.at[0:8], r.edge_grad, r.edge_sem.at[2], r.edge_sem.at[3], block_at(-1))
    edge_back.start()
    sums[0].tick()
    full_pick = one_hot((iota((INNER, 128), 0) >> 6) == iota((INNER, 128), 1))
    out_state = r.spread[0:1, :] * r.enter[...].astype(f32) + r.own[...]
    d_last = split_dot(
        jnp.sum((r.leave[...].astype(f32) * out_state).reshape(STATE // 8, 8, INNER), axis=0), full_pick
    )
    d_last = jnp.sum(d_last, axis=0, keepdims=True)
    q = r.q[...]
    d_cum = r.ry[...] - r.head[0] * q + jnp.where(iota((rows, 128), 0) == rows - 1, d_last, 0.0)
    above = one_hot(iota((rows, rows), 0) <= iota((rows, rows), 1))
    dz = (q + split_dot_left(above, d_cum * -jnp.exp(r.heads[1:2, :]))) * r.head[2]
    r.vec[...] = jnp.zeros_like(r.vec)
    r.vec[18:19, 0:128] = jnp.sum(dz, axis=0, keepdims=True)
    r.vec[19:20, 0:128] = jnp.sum(d_cum * r.head[1], axis=0, keepdims=True)
    r.vec[20:21, 0:128] = jnp.sum(split_dot(r.skip[...], full_pick), axis=0, keepdims=True)
    dz = dz.astype(bf16)
    d_normed = dot(r.dgate[...], r.w_in[:INNER, :])
    d_normed = d_normed + dot(dz[:, :HEADS], r.w_in[INNER + XBC :, :])
    edge_back.wait()
    r.ext[rows : rows + 8, :] = jnp.where(block == chips * 2 - 1, 0.0, r.edge_grad[...])
    sums[1].tick()

    def conv_back(i, carry):
        cols = lanes(i * 128, 128)
        drun = r.ext[0:rows, cols]
        total = drun * r.conv_w[CONV - 1 : CONV, cols]
        for tap in range(CONV - 1):
            ahead = CONV - 1 - tap
            total = total + r.ext[ahead : ahead + rows, cols] * r.conv_w[tap : tap + 1, cols]
        r.dproj[:, cols] = total.astype(bf16)
        for tap in range(CONV):
            r.tap_sums[tap : tap + 1, cols] = jnp.sum(
                drun * r.pad[13 + tap : 13 + tap + rows, cols], axis=0, keepdims=True
            )
        r.tap_sums[CONV : CONV + 1, cols] = jnp.sum(drun, axis=0, keepdims=True)
        return carry

    lax.fori_loop(0, XBC // 128, conv_back, 0)

    def rest_grads(i, carry):
        at = pl.ds(pl.multiple_of(i * 256, 256), 256)
        r.rest[at, :] = dot(r.dproj[:, lanes(i * 256, 256)], r.normed[own_rows, :], TN).astype(bf16)
        return carry

    lax.fori_loop(0, 4, rest_grads, 0)
    sums[2].tick()
    sums[0].tick()
    lax.fori_loop(4, XBC // 256, rest_grads, 0)
    for v in range(CONV + 1):
        for part in range(3):
            width = min(D, XBC - part * D)
            r.vec[3 * v + part : 3 * v + part + 1, 0:width] = r.tap_sums[v : v + 1, part * D : part * D + width]
    d_normed = d_normed + dot(r.dproj[...], r.w_in[INNER : INNER + XBC, :])
    src = r.blk[...].astype(f32)
    scale = lax.rsqrt(jnp.mean(src * src, axis=-1, keepdims=True) + EPS)
    r.vec[15:16, :] = jnp.sum(d_normed * src * scale, axis=0, keepdims=True)
    gate_gain = jnp.sum(r.ggain[...], axis=0, keepdims=True)
    r.vec[16:17, :] = gate_gain[:, :D]
    r.vec[17:18, :] = gate_gain[:, D:]
    r.rest[XBC:VEC_ROW, :] = dot(dz, r.normed[own_rows, :], TN).astype(bf16)
    r.rest[VEC_ROW : VEC_ROW + 32, :] = r.vec[...].astype(bf16)
    r.rest[VEC_ROW + 32 :, :] = jnp.zeros((REST_ROWS - VEC_ROW - 32, D), bf16)
    sums[3].tick()
    sums[1].tick()
    weighted = d_normed * r.gain[...]
    average = jnp.mean(weighted * src, axis=-1, keepdims=True)
    r.grad_in[...] = r.gout[...].astype(f32) + scale * weighted - src * (scale * scale * scale) * average
    for _ in range(STAGES + 1):
        for total in (sums[2], sums[0], sums[3], sums[1]):
            if total.stage < STAGES:
                total.tick()


def whole(lengths, blk, gout, gain, w_in, conv_w, conv_b, heads, gate_gain, w_out):
    t = blk.shape[0]
    chips = lax.axis_size("seq") // SEQS
    ins = ["lengths", "blk", "gout", "gain", "w_in_hbm", "conv_w", "conv_b", "heads", "gate_gain", "w_out_hbm"]
    outs = {
        "block_out": ((t, D), bf16),
        "grad_in": ((t, D), f32),
        "first_out": ((FIRST_ROWS, D), bf16),
        "rest_out": ((REST_ROWS, D), bf16),
    }
    held = {
        "first": ((FIRST_ROWS, D), bf16),
        "rest": ((REST_ROWS, D), bf16),
        "w_in": ((PROJ, D), bf16),
        "w_out": ((INNER, D), bf16),
        "edge": ((16, D), bf16),
        "edge_grad": ((8, XBC), f32),
        "normed": ((t + 16, D), bf16),
        "gate": ((t, INNER), bf16),
        "pad": ((t + 16, XBC), f32),
        "run": ((t, XBC), f32),
        "x": ((t, INNER), f32),
        "xd": ((t, INNER), bf16),
        "xde": ((t, INNER), bf16),
        "b": ((t, STATE), bf16),
        "c": ((t, STATE), bf16),
        "head": ((4, t, 128), f32),
        "cumt": ((128, t), f32),
        "cumb": ((t, HEADS * 128), f32),
        "spread": ((16, INNER), f32),
        "own": ((STATE, INNER), f32),
        "enter": ((STATE, INNER), bf16),
        "y": ((t, INNER), f32),
        "mixed": ((t, INNER), bf16),
        "gn": ((t, INNER), bf16),
        "wide": ((t, INNER), f32),
        "db": ((t, D), bf16),
        "dy": ((t, INNER), bf16),
        "dye": ((t, INNER), bf16),
        "dgate": ((t, INNER), bf16),
        "ggain": ((8, INNER), f32),
        "adj": ((STATE, INNER), f32),
        "leave": ((STATE, INNER), bf16),
        "scores": ((t, t), f32),
        "scores_t": ((t, t), f32),
        "dscores": ((t, t), f32),
        "skip": ((8, INNER), f32),
        "q": ((t, 128), f32),
        "ry": ((t, 128), f32),
        "ext": ((t + 8, XBC), f32),
        "dproj": ((t, XBC), bf16),
        "vec": ((32, D), f32),
        "tap_sums": ((8, XBC), f32),
        "got_first": ((FIRST_ROWS, D), bf16),
        "got_rest": ((REST_ROWS, D), bf16),
    }
    names = ins + list(outs) + list(held)
    scratch = [pltpu.VMEM(s, d) for s, d in held.values()]
    for tag in ("f", "g"):
        scratch += exchange_scratch(chips)
        names += [f"{tag}{k}" for k in range(8)] + [f"{tag}s", f"{tag}r"]
    semaphores = {
        "ss": (WAVES, 3, STAGES),
        "rs": (WAVES, 3, STAGES),
        "ls": (WAVES, 3),
        "edge_sem": (4,),
        "load_sem": (3,),
    }
    for name, shape in semaphores.items():
        scratch.append(pltpu.SemaphoreType.DMA(shape))
        names.append(name)
    any_space = pl.BlockSpec(memory_space=pl.ANY)
    specs = {"lengths": SMEM, "w_in_hbm": any_space, "w_out_hbm": any_space, "first_out": any_space, "rest_out": any_space}
    return pl.pallas_call(
        partial(whole_kernel, names),
        out_shape=[jax.ShapeDtypeStruct(s, d) for s, d in outs.values()],
        in_specs=[specs.get(n, VMEM) for n in ins],
        out_specs=[specs.get(n, VMEM) for n in outs],
        scratch_shapes=scratch,
        compiler_params=pltpu.CompilerParams(vmem_limit_bytes=60 << 20, collective_id=0, has_side_effects=True),
    )(lengths, blk, gout, gain, w_in, conv_w, conv_b, heads, gate_gain, w_out)


def shifted(value, ahead):
    groups = lax.axis_size("head")
    count = lax.axis_size("seq") * groups
    moves = []
    for source in range(count):
        piece, half = source // groups, source % groups
        half += ahead
        if half == groups:
            half, piece = 0, piece + SEQS
        elif half < 0:
            half, piece = groups - 1, piece - SEQS
        if 0 <= piece * groups + half < count:
            moves.append((source, piece * groups + half))
    return lax.ppermute(value, ("seq", "head"), moves)


def by_parts(lengths, block_in, grad_out, gain, w_in, conv_w, conv_b, heads, gate_gain, w_out):
    edge = shifted(block_in[-16:], 1)
    (normed, gate, pad, run, x, xd, xde, b, c, head, cumt, cumb, rows, own) = front(
        lengths, block_in, edge, gain, w_in, conv_w, conv_b, heads
    )
    enter = exchange_plain(own, rows[0:8], False)
    (y, block_out, dy, dye, dgate, ggain, adj, grads_a) = middle(
        lengths, block_in, grad_out, normed, gate, x, xd, b, c, cumt, cumb, rows, enter, gate_gain, w_out
    )
    leave = exchange_plain(adj, rows[0:8], True)
    drun, dz, small = back(
        lengths, y, dy, dye, x, xd, xde, b, c, run, cumt, cumb, head, rows, heads, enter, own, leave
    )
    edge_back = shifted(drun[0:8], -1)
    grad_in, grads_b = last(
        block_in, grad_out, normed, gain, w_in, conv_w, pad, drun, edge_back, dz, dgate, ggain, small
    )
    grads_a, grads_b = lax.psum((grads_a, grads_b), ("seq", "head"))
    return block_out, grad_in, grads_a, grads_b


def local(block_in, grad_out, lengths, norm_gain, w_in, conv_w, conv_b, dt_bias, a_log, d_skip, gate_gain, w_out):
    run = whole if lax.axis_size("seq") == 16 and lax.axis_size("head") == 2 else by_parts
    heads = jnp.pad(jnp.stack([dt_bias, a_log, d_skip]), ((0, 5), (0, 128 - HEADS)))
    block_out, grad_in, grads_a, grads_b = run(
        lengths,
        block_in,
        grad_out,
        norm_gain.reshape(1, D),
        w_in.T,
        conv_w,
        conv_b.reshape(1, XBC),
        heads,
        gate_gain.reshape(1, INNER),
        w_out,
    )
    grad_w_in = jnp.concatenate([grads_a[:INNER], grads_b[: PROJ - INNER]], axis=0).astype(f32).T
    grad_w_out = grads_a[INNER:].astype(f32)
    vec = grads_b[VEC_ROW : VEC_ROW + 32].astype(f32)
    grad_conv = vec[0:12].reshape(CONV, 3 * D)[:, :XBC]
    grad_bias = vec[12:15].reshape(3 * D)[:XBC]
    grad_norm = vec[15]
    grad_gate = vec[16:18].reshape(INNER)
    grad_dt = vec[18, :HEADS]
    grad_alog = vec[19, :HEADS]
    grad_skip = vec[20, :HEADS]
    return (
        block_out,
        grad_in,
        grad_norm,
        grad_w_in,
        grad_conv,
        grad_bias,
        grad_dt,
        grad_alog,
        grad_skip,
        grad_gate,
        grad_w_out,
    )


def solution(mesh):
    rows = P(("seq", "head"), None)
    return jax.shard_map(
        local,
        mesh=mesh,
        in_specs=(rows, rows) + (P(),) * 10,
        out_specs=(rows, rows) + (P(),) * 9,
        check_vma=False,
    )
```

```python
from functools import partial

import jax
import jax.numpy as jnp
from jax import lax
from jax.experimental import pallas as pl
from jax.experimental.pallas import tpu as pltpu
from jax.sharding import PartitionSpec as P

D = 768
INNER = 1536
HEADS = 24
HEAD_DIM = 64
STATE = 128
CONV = 4
SEQS = 2
XBC = INNER + 2 * STATE
PROJ = 2 * INNER + 2 * STATE + HEADS
PAIRS = HEADS // 2
EPS = 1e-05
LOG2E = 1.4426950408889634

f32 = jnp.float32
bf16 = jnp.bfloat16
MESH = pl.DeviceIdType.MESH
VMEM = pl.BlockSpec(memory_space=pltpu.VMEM)
SMEM = pl.BlockSpec(memory_space=pltpu.SMEM)
NN = ((1,), (0,))
NT = ((1,), (1,))
TN = ((0,), (0,))


def dot(a, b, dims=NN):
    return lax.dot_general(a, b, (dims, ((), ())), preferred_element_type=f32)


def split_dot(a, pick, terms=3):
    total = None
    for _ in range(terms):
        part = a.astype(bf16)
        a = a - part.astype(f32)
        term = dot(part, pick)
        total = term if total is None else total + term
    return total


def split_dot_left(pick, a, terms=3):
    total = None
    for _ in range(terms):
        part = a.astype(bf16)
        a = a - part.astype(f32)
        term = dot(pick, part)
        total = term if total is None else total + term
    return total


def iota(shape, dim):
    return lax.broadcasted_iota(jnp.int32, shape, dim)


def one_hot(cond):
    return jnp.where(cond, 1.0, 0.0).astype(bf16)


def sigmoid(v):
    return 1.0 / (1.0 + jnp.exp(-v))


def lanes(start, size):
    return pl.ds(pl.multiple_of(start, 128), size)


def valid_rows(lengths_ref, rows, width):
    place = lax.axis_index("seq")
    first = (place // SEQS) * (rows * lax.axis_size("head")) + lax.axis_index("head") * rows
    limit = lengths_ref[place % SEQS]
    return jnp.where(iota((rows, width), 0) + first < limit, 1.0, 0.0)


def call(body, outs, args, scratch=(), smem=(), vmem=56 << 20, cost=None, **params):
    return pl.pallas_call(
        body,
        out_shape=[jax.ShapeDtypeStruct(s, d) for s, d in outs],
        in_specs=[SMEM if i in smem else VMEM for i in range(len(args))],
        out_specs=[VMEM] * len(outs),
        scratch_shapes=list(scratch),
        compiler_params=pltpu.CompilerParams(vmem_limit_bytes=vmem, **params),
    )(*args)


VEC_ROW = XBC + 128
REST_ROWS = 2048
FIRST_ROWS = 2 * INNER
WAVES = 4
SPLITS = 2


def front_kernel(
    lengths_ref,
    blk,
    edge,
    gain,
    w_in,
    conv_w,
    conv_b,
    heads_ref,
    normed_out,
    gate_out,
    pad_out,
    run_out,
    x_out,
    xd_out,
    xde_out,
    b_out,
    c_out,
    head_out,
    cumt_out,
    cumb_out,
    rows_out,
    state_out,
):
    rows = blk.shape[0]

    def norm(v):
        v = v.astype(f32)
        scale = lax.rsqrt(jnp.mean(v * v, axis=-1, keepdims=True) + EPS)
        return (v * scale * gain[...]).astype(bf16)

    normed = norm(blk[...])
    normed_out[...] = normed
    gate_out[...] = dot(normed, w_in[:INNER, :], NT).astype(bf16)
    ahead = norm(edge[...])
    pad_out[0:16, :] = dot(ahead, w_in[INNER : INNER + XBC, :], NT).astype(bf16).astype(f32)
    pad_out[16 : 16 + rows, :] = dot(normed, w_in[INNER : INNER + XBC, :], NT).astype(bf16).astype(f32)
    keep = valid_rows(lengths_ref, rows, 128)
    head_out[3] = jnp.zeros((rows, 128), f32)
    head_out[3, :, 0:HEADS] = dot(normed, w_in[INNER + XBC :, :], NT).astype(bf16).astype(f32)
    lane = iota((rows, 128), 1)
    shifted = head_out[3] + heads_ref[0:1, :]
    soft = jnp.maximum(shifted, 0.0) + jnp.log1p(jnp.exp(-jnp.abs(shifted)))
    dt = jnp.where(lane < HEADS, soft * keep, 0.0)
    rates = -jnp.exp(heads_ref[1:2, :])
    below = one_hot(iota((rows, rows), 0) >= iota((rows, rows), 1))
    cum = split_dot_left(below, dt) * rates
    cum2 = cum * LOG2E
    head_out[0] = dt
    head_out[1] = cum
    head_out[2] = sigmoid(shifted) * keep
    head_out[3] = cum2
    cumt_out[...] = cum2.T
    pick_lane = iota((128, 256), 1)
    pick_head = iota((128, 256), 0)

    def spread(i, carry):
        cumb_out[:, lanes(i * 256, 256)] = split_dot(
            head_out[3], one_hot((pick_lane >> 7) + 2 * i == pick_head)
        )
        return carry

    lax.fori_loop(0, PAIRS, spread, 0)

    def convolve(i):
        cols = lanes(i * 256, 256)
        running = conv_b[:, cols] + pad_out[13 : 13 + rows, cols] * conv_w[0:1, cols]
        for tap in range(1, CONV):
            running = running + pad_out[13 + tap : 13 + tap + rows, cols] * conv_w[tap : tap + 1, cols]
        run_out[:, cols] = running
        return running * sigmoid(running)

    act = convolve(INNER // 256)
    b_out[...] = act[:, :STATE].astype(bf16)
    c_out[...] = act[:, STATE:].astype(bf16)
    keep2 = valid_rows(lengths_ref, rows, 256)

    def channels(i, carry):
        cols = lanes(i * 256, 256)
        pick = one_hot((pick_lane >> 6) + 4 * i == pick_head)
        x = convolve(i) * keep2
        x_out[:, cols] = x
        xd = x * split_dot(head_out[0], pick)
        xd_out[:, cols] = xd.astype(bf16)
        wide = split_dot(head_out[3], pick)
        last = wide[rows - 1 : rows, :]
        xde_out[:, cols] = (xd * jnp.exp2(last - wide)).astype(bf16)
        rows_out[0:8, cols] = jnp.broadcast_to(jnp.exp2(last), (8, 256))
        rows_out[8:16, cols] = split_dot(jnp.broadcast_to(heads_ref[2:3, :], (8, 128)), pick)
        return carry

    lax.fori_loop(0, INNER // 256, channels, 0)
    state_out[...] = dot(b_out[...], xde_out[...], TN)


def front(lengths, blk, edge, gain, w_in, conv_w, conv_b, heads):
    t = blk.shape[0]
    outs = [
        ((t, D), bf16),
        ((t, INNER), bf16),
        ((t + 16, XBC), f32),
        ((t, XBC), f32),
        ((t, INNER), f32),
        ((t, INNER), bf16),
        ((t, INNER), bf16),
        ((t, STATE), bf16),
        ((t, STATE), bf16),
        ((4, t, 128), f32),
        ((128, t), f32),
        ((t, HEADS * 128), f32),
        ((16, INNER), f32),
        ((STATE, INNER), f32),
    ]
    return call(front_kernel, outs, (lengths, blk, edge, gain, w_in, conv_w, conv_b, heads), smem=(0,))


def exchange_plain(state, decay, reverse):
    groups = lax.axis_size("head")
    count = lax.axis_size("seq") * groups
    place = lax.axis_index("seq")
    states = lax.all_gather(state.astype(bf16), ("seq", "head"), axis=0)
    decays = lax.all_gather(decay[0:1], ("seq", "head"), axis=0)
    blocks = count // SEQS
    block = place // SEQS * groups + lax.axis_index("head")

    def one(i, carry):
        source = blocks - 1 - i if reverse else i
        index = (source // groups * SEQS + place % SEQS) * groups + source % groups
        new = lax.dynamic_index_in_dim(decays, index, 0, False) * carry
        return new + lax.dynamic_index_in_dim(states, index, 0, False).astype(f32)

    ahead = blocks - 1 - block if reverse else block
    return lax.fori_loop(0, ahead, one, jnp.zeros(state.shape, f32)).astype(bf16)


def middle_kernel(
    lengths_ref,
    blk,
    gout,
    normed,
    gate,
    x_in,
    xd_in,
    b_in,
    c_in,
    cumt,
    cumb,
    rows_in,
    enter,
    gain,
    w_out,
    y_out,
    block_out,
    dy_out,
    dye_out,
    dgate_out,
    ggain_out,
    adj_out,
    grads_out,
    scores,
    mixed,
    gated_s,
    gn_s,
    scale_s,
    dgn_s,
    db_s,
):
    rows = blk.shape[0]
    causal = iota((rows, rows), 0) >= iota((rows, rows), 1)
    scores[...] = jnp.where(causal, dot(c_in[...], b_in[...], NT), 0.0)
    lane = iota((rows, 128), 1)
    left = one_hot(iota((1, 128), 1) < HEAD_DIM)
    right = one_hot(iota((1, 128), 1) >= HEAD_DIM)

    def pair(i, carry):
        cols = lanes(i * 128, 128)
        c0 = cumb[:, lanes(i * 256, 128)]
        c1 = cumb[:, lanes(i * 256 + 128, 128)]
        xd = xd_in[:, cols]
        y = None
        for cc, part, mask in ((c0, 0, left), (c1, 1, right)):
            row = cumt[pl.ds(2 * i + part, 1), :]
            decay = jnp.exp2(jnp.minimum(jnp.concatenate([cc] * (rows // 128), axis=1) - row, 0.0))
            term = dot((decay * scores[...]).astype(bf16), xd * mask)
            y = term if y is None else y + term
        grow = jnp.exp2(jnp.where(lane < HEAD_DIM, c0, c1))
        y = y + grow * dot(c_in[...], enter[:, cols])
        y_out[:, cols] = y
        mixed[:, cols] = (y + rows_in[8:9, cols] * x_in[:, cols]).astype(bf16).astype(f32)
        return carry

    lax.fori_loop(0, PAIRS, pair, 0)
    step = 32

    def gating(i, carry):
        r = pl.ds(pl.multiple_of(i * step, step), step)
        g = gate[r, :].astype(f32)
        gated = mixed[r, :] * g * sigmoid(g)
        scale = lax.rsqrt(jnp.mean(gated * gated, axis=-1, keepdims=True) + EPS)
        gated_s[r, :] = gated
        scale_s[r, :] = jnp.broadcast_to(scale, (step, 128))
        gn_s[r, :] = (gated * scale * gain[...]).astype(bf16)
        return carry

    lax.fori_loop(0, rows // step, gating, 0)
    keep = valid_rows(lengths_ref, rows, D)
    db_s[...] = (gout[...].astype(f32) * keep).astype(bf16)
    dgn_s[...] = dot(db_s[...], w_out[...], NT)
    block_out[...] = (blk[...].astype(f32) + keep * dot(gn_s[...], w_out[...])).astype(bf16)
    ggain_out[...] = jnp.zeros_like(ggain_out)

    def ungating(i, carry):
        r = pl.ds(pl.multiple_of(i * step, step), step)
        g = gate[r, :].astype(f32)
        sg = sigmoid(g)
        gated = gated_s[r, :]
        scale = scale_s[r, 0:1]
        dgn = dgn_s[r, :]
        ggain_out[...] += jnp.sum((dgn * gated * scale).reshape(step // 8, 8, INNER), axis=0)
        weighted = dgn * gain[...]
        average = jnp.mean(weighted * gated, axis=-1, keepdims=True)
        d_gated = scale * weighted - gated * (scale * scale * scale) * average
        dy_out[r, :] = (d_gated * g * sg).astype(bf16)
        dgate_out[r, :] = (d_gated * mixed[r, :] * sg * (1.0 + g * (1.0 - sg))).astype(bf16)
        return carry

    lax.fori_loop(0, rows // step, ungating, 0)

    def weigh(i, carry):
        cols = lanes(i * 128, 128)
        grow = jnp.exp2(jnp.where(lane < HEAD_DIM, cumb[:, lanes(i * 256, 128)], cumb[:, lanes(i * 256 + 128, 128)]))
        dye_out[:, cols] = (dy_out[:, cols].astype(f32) * grow).astype(bf16)
        return carry

    lax.fori_loop(0, PAIRS, weigh, 0)
    adj_out[...] = dot(c_in[...], dye_out[...], TN)
    grads_out[:INNER, :] = dot(dgate_out[...], normed[...], TN).astype(bf16)
    grads_out[INNER:, :] = dot(gn_s[...], db_s[...], TN).astype(bf16)


def middle(lengths, blk, gout, normed, gate, x, xd, b, c, cumt, cumb, rows_in, enter, gain, w_out):
    t = blk.shape[0]
    outs = [
        ((t, INNER), f32),
        ((t, D), bf16),
        ((t, INNER), bf16),
        ((t, INNER), bf16),
        ((t, INNER), bf16),
        ((8, INNER), f32),
        ((STATE, INNER), f32),
        ((2 * INNER, D), bf16),
    ]
    scratch = [
        pltpu.VMEM((t, t), f32),
        pltpu.VMEM((t, INNER), f32),
        pltpu.VMEM((t, INNER), f32),
        pltpu.VMEM((t, INNER), bf16),
        pltpu.VMEM((t, 128), f32),
        pltpu.VMEM((t, INNER), f32),
        pltpu.VMEM((t, D), bf16),
    ]
    args = (lengths, blk, gout, normed, gate, x, xd, b, c, cumt, cumb, rows_in, enter, gain, w_out)
    return call(middle_kernel, outs, args, scratch, smem=(0,))


def back_kernel(
    lengths_ref,
    y_in,
    dy_in,
    dye_in,
    x_in,
    xd_in,
    xde_in,
    b_in,
    c_in,
    run_in,
    cumt,
    cumb,
    head_in,
    rows_in,
    heads_ref,
    enter,
    own,
    leave,
    drun_out,
    dz_out,
    small_out,
    scores,
    dscores,
    skip_s,
    q_s,
    ry_s,
):
    rows = y_in.shape[0]
    causal = iota((rows, rows), 1) >= iota((rows, rows), 0)
    scores[...] = jnp.where(causal, dot(b_in[...], c_in[...], NT), 0.0)
    dscores[...] = jnp.zeros_like(dscores)
    q_s[...] = jnp.zeros_like(q_s)
    ry_s[...] = jnp.zeros_like(ry_s)
    lane = iota((rows, 128), 1)
    keep = valid_rows(lengths_ref, rows, 128)
    left = one_hot(iota((1, 128), 1) < HEAD_DIM)
    right = one_hot(iota((1, 128), 1) >= HEAD_DIM)
    pick_lane = iota((128, 128), 0)
    pick_head = iota((128, 128), 1)

    def dsilu(cols):
        running = run_in[:, cols]
        sg = sigmoid(running)
        return sg * (1.0 + running * (1.0 - sg))

    def pair(i, carry):
        cols = lanes(i * 128, 128)
        c0 = cumb[:, lanes(i * 256, 128)]
        c1 = cumb[:, lanes(i * 256 + 128, 128)]
        xd = xd_in[:, cols]
        dy = dy_in[:, cols]
        v = None
        for cc, part, mask in ((c0, 0, left), (c1, 1, right)):
            row = cumt[pl.ds(2 * i + part, 1), :]
            decay = jnp.exp2(jnp.minimum(row - jnp.concatenate([cc] * (rows // 128), axis=1), 0.0))
            masked = dy * mask
            term = dot((decay * scores[...]).astype(bf16), masked)
            v = term if v is None else v + term
            dscores[...] += decay * dot(xd, masked, NT)
        c01 = jnp.where(lane < HEAD_DIM, c0, c1)
        v = v + jnp.exp2(c01[rows - 1 : rows, :] - c01) * dot(b_in[...], leave[:, cols])
        pick = one_hot((pick_lane >> 6) + 2 * i == pick_head)
        dtw = split_dot(head_in[0], one_hot((pick_head >> 6) + 2 * i == pick_lane))
        x = x_in[:, cols]
        dyf = dy.astype(f32)
        q_s[...] += split_dot(x * v, pick)
        ry_s[...] += split_dot(dyf * y_in[:, cols], pick)
        skip_s[:, cols] = jnp.sum((dyf * x).reshape(rows // 8, 8, 128), axis=0)
        dx = dtw * v + rows_in[8:9, cols] * dyf
        drun_out[:, cols] = dx * keep * dsilu(cols)
        return carry

    lax.fori_loop(0, PAIRS, pair, 0)
    dsc = jnp.where(causal, dscores[...], 0.0).astype(bf16)
    d_b = dot(dsc, c_in[...]) + dot(xde_in[...], leave[...], NT)
    d_c = dot(dsc, b_in[...], TN) + dot(dye_in[...], enter[...], NT)
    drun_out[:, INNER : INNER + STATE] = d_b * dsilu(slice(INNER, INNER + STATE))
    drun_out[:, INNER + STATE :] = d_c * dsilu(slice(INNER + STATE, XBC))
    full_pick = one_hot((iota((INNER, 128), 0) >> 6) == iota((INNER, 128), 1))
    out_state = rows_in[0:1, :] * enter[...].astype(f32) + own[...]
    d_last = split_dot(
        jnp.sum((leave[...].astype(f32) * out_state).reshape(STATE // 8, 8, INNER), axis=0), full_pick
    )
    d_last = jnp.sum(d_last, axis=0, keepdims=True)
    dt = head_in[0]
    q = q_s[...]
    d_cum = ry_s[...] - dt * q + jnp.where(iota((rows, 128), 0) == rows - 1, d_last, 0.0)
    rates = -jnp.exp(heads_ref[1:2, :])
    above = one_hot(iota((rows, rows), 0) <= iota((rows, rows), 1))
    d_dt = q + split_dot_left(above, d_cum * rates)
    dz = d_dt * head_in[2]
    dz_out[...] = dz
    small_out[0:1, :] = jnp.sum(dz, axis=0, keepdims=True)
    small_out[1:2, :] = jnp.sum(d_cum * head_in[1], axis=0, keepdims=True)
    small_out[2:3, :] = jnp.sum(split_dot(skip_s[...], full_pick), axis=0, keepdims=True)
    small_out[3:8, :] = jnp.zeros((5, 128), f32)


def back(lengths, y, dy, dye, x, xd, xde, b, c, run, cumt, cumb, head, rows_in, heads, enter, own, leave):
    t = y.shape[0]
    outs = [((t, XBC), f32), ((t, 128), f32), ((8, 128), f32)]
    scratch = [
        pltpu.VMEM((t, t), f32),
        pltpu.VMEM((t, t), f32),
        pltpu.VMEM((8, INNER), f32),
        pltpu.VMEM((t, 128), f32),
        pltpu.VMEM((t, 128), f32),
    ]
    args = (lengths, y, dy, dye, x, xd, xde, b, c, run, cumt, cumb, head, rows_in, heads, enter, own, leave)
    return call(back_kernel, outs, args, scratch, smem=(0,))


def last_kernel(
    blk,
    gout,
    normed,
    gain,
    w_in,
    conv_w,
    pad_in,
    drun_in,
    edge,
    dz_in,
    dgate,
    ggain,
    small_in,
    gin_out,
    grads_out,
    ext,
    dproj,
    vec,
    sums,
):
    rows = blk.shape[0]
    ext[0:rows, :] = drun_in[...]
    ext[rows : rows + 8, :] = edge[...]
    vec[...] = jnp.zeros_like(vec)

    def channels(i, carry):
        cols = lanes(i * 128, 128)
        drun = ext[0:rows, cols]
        total = drun * conv_w[CONV - 1 : CONV, cols]
        for tap in range(CONV - 1):
            ahead = CONV - 1 - tap
            total = total + ext[ahead : ahead + rows, cols] * conv_w[tap : tap + 1, cols]
        dproj[:, cols] = total.astype(bf16)
        for tap in range(CONV):
            sums[tap : tap + 1, cols] = jnp.sum(
                drun * pad_in[13 + tap : 13 + tap + rows, cols], axis=0, keepdims=True
            )
        sums[CONV : CONV + 1, cols] = jnp.sum(drun, axis=0, keepdims=True)
        return carry

    lax.fori_loop(0, XBC // 128, channels, 0)
    for v in range(CONV + 1):
        for part in range(3):
            width = min(D, XBC - part * D)
            vec[3 * v + part : 3 * v + part + 1, 0:width] = sums[v : v + 1, part * D : part * D + width]
    dz = dz_in[...].astype(bf16)
    d_normed = dot(dgate[...], w_in[:INNER, :])
    d_normed = d_normed + dot(dproj[...], w_in[INNER : INNER + XBC, :])
    d_normed = d_normed + dot(dz[:, :HEADS], w_in[INNER + XBC :, :])
    src = blk[...].astype(f32)
    scale = lax.rsqrt(jnp.mean(src * src, axis=-1, keepdims=True) + EPS)
    vec[15:16, :] = jnp.sum(d_normed * src * scale, axis=0, keepdims=True)
    gate_gain = jnp.sum(ggain[...], axis=0, keepdims=True)
    vec[16:17, :] = gate_gain[:, :D]
    vec[17:18, :] = gate_gain[:, D:]
    vec[18:21, 0:128] = small_in[0:3, :]
    weighted = d_normed * gain[...]
    average = jnp.mean(weighted * src, axis=-1, keepdims=True)
    gin_out[...] = gout[...].astype(f32) + scale * weighted - src * (scale * scale * scale) * average
    grads_out[:XBC, :] = dot(dproj[...], normed[...], TN).astype(bf16)
    grads_out[XBC:VEC_ROW, :] = dot(dz, normed[...], TN).astype(bf16)
    grads_out[VEC_ROW : VEC_ROW + 32, :] = vec[...].astype(bf16)
    grads_out[VEC_ROW + 32 :, :] = jnp.zeros((REST_ROWS - VEC_ROW - 32, D), bf16)


def last(blk, gout, normed, gain, w_in, conv_w, pad, drun, edge, dz, dgate, ggain, small):
    t = blk.shape[0]
    outs = [((t, D), f32), ((REST_ROWS, D), bf16)]
    scratch = [pltpu.VMEM((t + 8, XBC), f32), pltpu.VMEM((t, XBC), bf16), pltpu.VMEM((32, D), f32), pltpu.VMEM((8, XBC), f32)]
    args = (blk, gout, normed, gain, w_in, conv_w, pad, drun, edge, dz, dgate, ggain, small)
    return call(last_kernel, outs, args, scratch)


class Refs:
    def __init__(self, names, refs):
        self.__dict__.update(zip(names, refs, strict=True))


def remote(src, dst, ssem, rsem, to):
    return pltpu.make_async_remote_copy(
        src_ref=src, dst_ref=dst, send_sem=ssem, recv_sem=rsem, device_id=to, device_id_type=MESH
    )


class Exchange:
    def __init__(self, reverse, state, decay, out, bufs, decays, ssem, rsem, start, width):
        self.sib_state, self.mine, self.got, self.back, self.back_got = bufs
        self.sib_decay, self.total, self.got_decay = decays
        self.state, self.decay, self.out, self.reverse = state, decay, out, reverse
        self.ssem, self.rsem = ssem, rsem
        self.chips = lax.axis_size("seq") // SEQS
        self.rows = STATE // self.chips
        self.width = width
        place, core = lax.axis_index("seq"), lax.axis_index("head")
        self.core = core
        self.chip, self.which = place // SEQS, place % SEQS
        self.sibling = (place, 1 - core)
        self.later = (1 - core if reverse else core) == 1
        self.own_cols = lanes(core * (INNER // 2) + start, width)
        self.sib_cols = lanes((1 - core) * (INNER // 2) + start, width)
        self.flying = []

    def peer(self, k):
        return (lax.rem(self.chip + k, self.chips) * SEQS + self.which, self.core)

    def send(self, copies):
        self.flying = [remote(src, dst, self.ssem.at[n], self.rsem.at[n], to) for src, dst, n, to in copies]
        for c in self.flying:
            c.start()

    def arrive(self):
        for c in self.flying:
            c.wait()

    def begin(self):
        copies = [(self.state.at[:, self.sib_cols], self.sib_state, 0, self.sibling)]
        if not self.reverse:
            copies.append((self.decay.at[0:8, self.sib_cols], self.sib_decay, 1, self.sibling))
        self.send(copies)

    def ordered(self):
        own, other = self.state[:, self.own_cols], self.sib_state[...]
        own_decay, other_decay = self.decay[0:1, self.own_cols], self.sib_decay[0:1, :]
        later = self.later
        return (
            jnp.where(later, other, own),
            jnp.where(later, own, other),
            jnp.where(later, other_decay, own_decay),
            jnp.where(later, own_decay, other_decay),
        )

    def deal(self):
        self.arrive()
        early, late, early_decay, late_decay = self.ordered()
        self.mine[...] = (late_decay * early + late).astype(bf16)
        if not self.reverse:
            self.total[...] = jnp.broadcast_to(early_decay * late_decay, self.total.shape)
        copies = []
        for k in range(1, self.chips):
            to = lax.rem(self.chip + k, self.chips)
            piece = pl.ds(pl.multiple_of(to * self.rows, self.rows), self.rows)
            copies.append((self.mine.at[piece], self.got.at[k], 2 * k, self.peer(k)))
            if not self.reverse:
                copies.append((self.total, self.got_decay.at[k], 2 * k + 1, self.peer(k)))
        self.send(copies)
        self.got[0] = self.mine[pl.ds(pl.multiple_of(self.chip * self.rows, self.rows), self.rows), :]
        if not self.reverse:
            self.got_decay[0] = self.total[...]

    def scan(self):
        self.arrive()
        chips, chip = self.chips, self.chip

        def one(i, carry):
            source = chips - 1 - i if self.reverse else i
            slot = lax.rem(chip - source + chips, chips)
            to = lax.rem(source - chip + chips, chips)
            self.back[pl.ds(to, 1)] = carry.astype(bf16)[None]
            return self.got_decay[pl.ds(slot, 1)][0, 0:1, :] * carry + self.got[pl.ds(slot, 1)][0].astype(f32)

        lax.fori_loop(0, chips, one, jnp.zeros((self.rows, self.width), f32))
        here = pl.ds(pl.multiple_of(chip * self.rows, self.rows), self.rows)
        self.send([(self.back.at[k], self.back_got.at[here], 2 * chips + k, self.peer(k)) for k in range(1, chips)])
        self.back_got[here, :] = self.back[0]

    def hand(self):
        self.arrive()
        early, _, early_decay, _ = self.ordered()
        enter = self.back_got[...].astype(f32)
        second = early_decay * enter + early
        self.out[:, self.own_cols] = jnp.where(self.later, second, enter).astype(bf16)
        self.mine[...] = jnp.where(self.later, enter, second).astype(bf16)
        self.send([(self.mine, self.out.at[:, self.own_cols], 2 * self.chips, self.sibling)])


def exchange_scratch(chips, width):
    rows = STATE // chips
    states = [((STATE, width), f32), ((STATE, width), bf16), ((chips, rows, width), bf16)]
    states += [((chips, rows, width), bf16), ((STATE, width), bf16)]
    decays = [((8, width), f32), ((8, width), f32), ((chips, 8, width), f32)]
    return states, decays


ORDERS = (("x", "y", "z1", "z2"), ("y", "x", "z1", "z2"), ("z1", "z2", "x", "y"))
STEPS = {"x": 1, "y": 2, "z1": 4, "z2": 8}
STAGES = 9


def bits_of():
    place = lax.axis_index("seq")
    return {
        "c": lax.axis_index("head"),
        "x": place % 2,
        "y": place // 2 % 2,
        "z1": place // 4 % 2,
        "z2": place // 8,
    }


def partner(d):
    place, core = lax.axis_index("seq"), lax.axis_index("head")
    if d == "c":
        return (place, 1 - core)
    return (place + STEPS[d] * (1 - 2 * bits_of()[d]), core)


class Sum:
    def __init__(self, held, got, out, ssem, rsem, lsem):
        self.streams = [self.stream(held, got, out, ssem, rsem, lsem, s) for s in range(3)]
        self.stage = -1

    def stream(self, held, got, out, ssem, rsem, lsem, s):
        rows = held.shape[0]
        bits = bits_of()
        cols = slice(s * 256, (s + 1) * 256)
        order = ("c",) + ORDERS[s]
        keeps, sends = [], []
        off, size = 0, rows
        for d in order[:4]:
            size //= 2
            keeps.append(off + bits[d] * size)
            sends.append(off + (1 - bits[d]) * size)
            off = keeps[-1]
        unit = rows // 16
        sizes = [rows // 2, rows // 4, rows // 8, unit, unit]
        slots = [0, rows // 2, rows // 2 + rows // 4, rows - 2 * unit, rows - unit]

        def at(start, size):
            return pl.ds(pl.multiple_of(start, 16), size)

        def copy(stage):
            if stage < 5:
                d = order[stage]
                where = at(sends[stage] if stage < 4 else off, sizes[stage])
                src, dst = held.at[where, cols], got.at[slice(slots[stage], slots[stage] + sizes[stage]), cols]
            else:
                d = order[8 - stage]
                where = at(keeps[8 - stage], sizes[8 - stage])
                src, dst = (held if stage == 5 else out).at[where, cols], out.at[where, cols]
            return remote(src, dst, ssem.at[s, stage], rsem.at[s, stage], partner(d))

        def add(stage):
            where = keeps[stage] if stage < 4 else off

            @pl.loop(0, sizes[stage] // unit)
            def _(i):
                here = at(where + i * unit, unit)
                held[here, cols] = held[here, cols] + got[at(slots[stage] + i * unit, unit), cols]

        def place():
            return pltpu.make_async_copy(held.at[at(off, unit), cols], out.at[at(off, unit), cols], lsem.at[s])

        return copy, add, place

    def tick(self):
        for copy, add, place in self.streams:
            if 0 <= self.stage < STAGES:
                copy(self.stage).wait()
                if self.stage < 5:
                    add(self.stage)
            if self.stage == 4:
                place().start()
            if self.stage == 5:
                place().wait()
            if self.stage + 1 < STAGES:
                copy(self.stage + 1).start()
        self.stage += 1


def greet():
    place, core = lax.axis_index("seq"), lax.axis_index("head")
    pieces = lax.axis_size("seq")
    chips = pieces // SEQS
    barrier = pltpu.get_barrier_semaphore()
    peers = [partner(d) for d in ("c", "x", "y", "z1", "z2")]
    peers += [((place // SEQS + k) % chips * SEQS + place % SEQS, core) for k in range(1, chips)]
    peers += [block_at(1), block_at(-1)]
    for to in peers:
        pl.semaphore_signal(barrier, inc=1, device_id=to, device_id_type=MESH)
    pl.semaphore_wait(barrier, len(peers))


def block_at(ahead):
    place, core = lax.axis_index("seq"), lax.axis_index("head")
    pieces = lax.axis_size("seq")
    block = (place // SEQS * 2 + core + ahead + pieces) % pieces
    return (block // 2 * SEQS + place % SEQS, block % 2)


def whole_kernel(names, *refs):
    r = Refs(names, refs)
    rows = r.blk.shape[0]
    r.gain[...] = r.norm_gain[...].reshape(1, D)
    r.conv_b[...] = r.conv_bias[...].reshape(1, XBC)
    r.gate_gain[...] = r.gated_gain[...].reshape(1, INNER)
    r.heads[...] = jnp.zeros((8, 128), f32)
    for k, one in enumerate((r.dt_bias, r.a_log, r.d_skip)):
        r.heads[k : k + 1, 0:HEADS] = one[...].reshape(1, HEADS)
    place, core = lax.axis_index("seq"), lax.axis_index("head")
    chips = lax.axis_size("seq") // SEQS
    block = place // SEQS * 2 + core
    loads = [
        pltpu.make_async_copy(r.w_in_hbm.at[INNER:], r.w_in.at[INNER:], r.load_sem.at[0]),
        pltpu.make_async_copy(r.w_in_hbm.at[:INNER], r.w_in.at[:INNER], r.load_sem.at[1]),
        pltpu.make_async_copy(r.w_out_hbm, r.w_out, r.load_sem.at[2]),
    ]
    for c in loads:
        c.start()
    greet()
    edge = remote(r.blk.at[rows - 16 :], r.edge, r.edge_sem.at[0], r.edge_sem.at[1], block_at(1))
    edge.start()

    def norm(v):
        v = v.astype(f32)
        scale = lax.rsqrt(jnp.mean(v * v, axis=-1, keepdims=True) + EPS)
        return (v * scale * r.gain[...]).astype(bf16)

    r.normed[16:, :] = norm(r.blk[...])
    lane = iota((rows, 128), 1)
    keep = valid_rows(r.lengths, rows, 128)
    pick_lane = iota((128, 256), 1)
    pick_head = iota((128, 256), 0)
    left = one_hot(iota((1, 128), 1) < HEAD_DIM)
    right = one_hot(iota((1, 128), 1) >= HEAD_DIM)
    own_rows = slice(16, 16 + rows)

    loads[0].wait()
    r.head[3] = jnp.zeros((rows, 128), f32)
    r.head[3, :, 0:HEADS] = dot(r.normed[own_rows, :], r.w_in[INNER + XBC :, :], NT).astype(bf16).astype(f32)
    moved = r.head[3] + r.heads[0:1, :]
    soft = jnp.maximum(moved, 0.0) + jnp.log1p(jnp.exp(-jnp.abs(moved)))
    dt = jnp.where(lane < HEADS, soft * keep, 0.0)
    rates = -jnp.exp(r.heads[1:2, :])
    below = one_hot(iota((rows, rows), 0) >= iota((rows, rows), 1))
    cum = split_dot_left(below, dt) * rates
    cum2 = cum * LOG2E
    r.head[0] = dt
    r.head[1] = cum
    r.head[2] = sigmoid(moved) * keep
    r.head[3] = cum2
    r.cumt[...] = cum2.T

    edge.wait()
    r.normed[0:16, :] = jnp.where(block == 0, 0.0, norm(r.edge[...]).astype(f32)).astype(bf16)

    def project(start, width):
        part = dot(r.normed[...], r.w_in[pl.ds(pl.multiple_of(INNER + start, 128), width), :], NT)
        r.pad[:, lanes(start, width)] = part.astype(bf16).astype(f32)

    def convolve(start, width):
        cols = lanes(start, width)
        running = r.conv_b[:, cols] + r.pad[13 : 13 + rows, cols] * r.conv_w[0:1, cols]
        for tap in range(1, CONV):
            running = running + r.pad[13 + tap : 13 + tap + rows, cols] * r.conv_w[tap : tap + 1, cols]
        r.run[:, cols] = running
        return running * sigmoid(running)

    project(INNER, 2 * STATE)
    act = convolve(INNER, 2 * STATE)
    r.b[...] = act[:, :STATE].astype(bf16)
    r.c[...] = act[:, STATE:].astype(bf16)
    third = 3 * 128

    def channels(start):
        project(start, third)

        def one(i, carry):
            at = start + i * 128
            cols = lanes(at, 128)
            pick = one_hot((iota((128, 128), 1) >> 6) + at // HEAD_DIM == iota((128, 128), 0))
            x = convolve(at, 128) * keep
            r.x[:, cols] = x
            xd = x * split_dot(r.head[0], pick)
            r.xd[:, cols] = xd.astype(bf16)
            wide = split_dot(r.head[3], pick)
            last = wide[rows - 1 : rows, :]
            xde = (xd * jnp.exp2(last - wide)).astype(bf16)
            r.xde[:, cols] = xde
            r.spread[0:8, cols] = jnp.broadcast_to(jnp.exp2(last), (8, 128))
            r.spread[8:16, cols] = split_dot(jnp.broadcast_to(r.heads[2:3, :], (8, 128)), pick)
            return carry

        lax.fori_loop(0, third // 128, one, 0, unroll=3)
        r.own[:, start : start + third] = dot(r.b[...], r.xde[:, start : start + third], TN)

    def exchanges(reverse, state, out, tag):
        made = []
        for k in range(SPLITS):
            bufs = [getattr(r, f"{tag}{k}_{n}") for n in range(5)]
            decays = [getattr(r, f"d{k}_{n}") for n in range(3)]
            sems = getattr(r, f"{tag}s").at[k], getattr(r, f"{tag}r").at[k]
            width = INNER // 2 // SPLITS
            made.append(Exchange(reverse, state, r.spread, out, bufs, decays, *sems, k * width, width))
        return made

    enters = exchanges(False, r.own, r.enter, "f")
    leaves = exchanges(True, r.adj, r.leave, "g")
    channels(0)
    channels(INNER // 2)
    enters[0].begin()
    channels(third)
    enters[0].deal()
    channels(INNER // 2 + third)
    enters[1].begin()

    def spread(i, carry):
        r.cumb[:, lanes(i * 256, 256)] = split_dot(r.head[3], one_hot((pick_lane >> 7) + 2 * i == pick_head))
        return carry

    lax.fori_loop(0, PAIRS, spread, 0, unroll=2)

    causal = iota((rows, rows), 0) >= iota((rows, rows), 1)
    r.scores[...] = jnp.where(causal, dot(r.c[...], r.b[...], NT), 0.0)
    r.scores_t[...] = jnp.where(
        iota((rows, rows), 1) >= iota((rows, rows), 0), dot(r.b[...], r.c[...], NT), 0.0
    )
    loads[1].wait()
    enters[1].deal()

    def gates(i, carry):
        part = dot(r.normed[own_rows, :], r.w_in[pl.ds(pl.multiple_of(i * 256, 256), 256), :], NT)
        r.gate[:, lanes(i * 256, 256)] = part.astype(bf16)
        return carry

    def columns(i):
        c0 = r.cumb[:, lanes(i * 256, 128)]
        c1 = r.cumb[:, lanes(i * 256 + 128, 128)]
        return c0, c1

    def pair(i, carry):
        cols = lanes(i * 128, 128)
        xd = r.xd[:, cols]
        y = None
        for cc, part, mask in zip(columns(i), (0, 1), (left, right), strict=True):
            row = r.cumt[pl.ds(2 * i + part, 1), :]
            decay = jnp.exp2(jnp.minimum(jnp.concatenate([cc] * (rows // 128), axis=1) - row, 0.0))
            term = dot((decay * r.scores[...]).astype(bf16), xd * mask)
            y = term if y is None else y + term
        r.y[:, cols] = y
        return carry

    lax.fori_loop(0, INNER // 256, gates, 0, unroll=2)
    lax.fori_loop(0, 4, pair, 0, unroll=2)
    enters[0].scan()
    lax.fori_loop(4, 8, pair, 0, unroll=2)
    enters[1].scan()
    lax.fori_loop(8, PAIRS, pair, 0, unroll=2)
    enters[0].hand()
    keep_d = valid_rows(r.lengths, rows, D)
    r.db[...] = (r.gout[...].astype(f32) * keep_d).astype(bf16)
    loads[2].wait()
    r.wide[...] = dot(r.db[...], r.w_out[...], NT)
    enters[1].hand()
    for one in enters:
        one.arrive()

    def carried(i, carry):
        cols = lanes(i * 128, 128)
        c0, c1 = columns(i)
        y = r.y[:, cols] + jnp.exp2(jnp.where(lane < HEAD_DIM, c0, c1)) * dot(r.c[...], r.enter[:, cols])
        r.y[:, cols] = y
        r.mixed[:, cols] = (y + r.spread[8:9, cols] * r.x[:, cols]).astype(bf16)
        return carry

    lax.fori_loop(0, PAIRS, carried, 0, unroll=2)

    r.ggain[...] = jnp.zeros_like(r.ggain)
    step = 32

    def gating(i, carry):
        at = pl.ds(pl.multiple_of(i * step, step), step)
        g = r.gate[at, :].astype(f32)
        sg = sigmoid(g)
        mixed = r.mixed[at, :].astype(f32)
        gated = mixed * g * sg
        scale = lax.rsqrt(jnp.mean(gated * gated, axis=-1, keepdims=True) + EPS)
        r.gn[at, :] = (gated * scale * r.gate_gain[...]).astype(bf16)
        dgn = r.wide[at, :]
        r.ggain[...] += jnp.sum((dgn * gated * scale).reshape(step // 8, 8, INNER), axis=0)
        weighted = dgn * r.gate_gain[...]
        average = jnp.mean(weighted * gated, axis=-1, keepdims=True)
        d_gated = scale * weighted - gated * (scale * scale * scale) * average
        r.dy[at, :] = (d_gated * g * sg).astype(bf16)
        r.dgate[at, :] = (d_gated * mixed * sg * (1.0 + g * (1.0 - sg))).astype(bf16)
        return carry

    lax.fori_loop(0, rows // step, gating, 0)

    def weigh(i, carry):
        cols = lanes(i * 128, 128)
        c0, c1 = columns(i)
        grow = jnp.exp2(jnp.where(lane < HEAD_DIM, c0, c1))
        r.dye[:, cols] = (r.dy[:, cols].astype(f32) * grow).astype(bf16)
        return carry

    lax.fori_loop(0, PAIRS, weigh, 0, unroll=2)
    r.adj[...] = dot(r.c[...], r.dye[...], TN)
    for one in leaves:
        one.begin()

    def gate_grads(i, carry):
        at = pl.ds(pl.multiple_of(i * 256, 256), 256)
        r.first[at, :] = dot(r.dgate[:, lanes(i * 256, 256)], r.normed[own_rows, :], TN).astype(bf16)
        return carry

    def out_grads(i, carry):
        at = pl.ds(pl.multiple_of(INNER + i * 256, 256), 256)
        r.first[at, :] = dot(r.gn[:, lanes(i * 256, 256)], r.db[...], TN).astype(bf16)
        return carry

    def part(k, held, got, out, at):
        return Sum(held.at[at], got.at[at], out.at[at], r.ss.at[k], r.rs.at[k], r.ls.at[k])

    half = REST_ROWS // 2
    sums = [
        part(0, r.first, r.got_first, r.first_out, slice(0, INNER)),
        part(1, r.first, r.got_first, r.first_out, slice(INNER, FIRST_ROWS)),
        part(2, r.rest, r.got_rest, r.rest_out, slice(0, half)),
        part(3, r.rest, r.got_rest, r.rest_out, slice(half, REST_ROWS)),
    ]
    lax.fori_loop(0, INNER // 256, gate_grads, 0, unroll=2)
    for one in leaves:
        one.deal()
    sums[0].tick()
    lax.fori_loop(0, INNER // 256, out_grads, 0, unroll=2)
    r.block_out[...] = (r.blk[...].astype(f32) + keep_d * dot(r.gn[...], r.w_out[...])).astype(bf16)
    sums[1].tick()

    r.dscores[...] = jnp.zeros_like(r.dscores)
    r.q[...] = jnp.zeros_like(r.q)
    r.ry[...] = jnp.zeros_like(r.ry)
    row_head = iota((128, 128), 0)
    col_head = iota((128, 128), 1)

    def dsilu(cols):
        running = r.run[:, cols]
        sg = sigmoid(running)
        return sg * (1.0 + running * (1.0 - sg))

    def pair_back(i, carry):
        cols = lanes(i * 128, 128)
        xd, dy = r.xd[:, cols], r.dy[:, cols]
        v = None
        for cc, part, mask in zip(columns(i), (0, 1), (left, right), strict=True):
            row = r.cumt[pl.ds(2 * i + part, 1), :]
            decay = jnp.exp2(jnp.minimum(row - jnp.concatenate([cc] * (rows // 128), axis=1), 0.0))
            masked = dy * mask
            term = dot((decay * r.scores_t[...]).astype(bf16), masked)
            v = term if v is None else v + term
            r.dscores[...] += decay * dot(xd, masked, NT)
        r.wide[:, cols] = v
        r.ry[...] += split_dot(dy.astype(f32) * r.y[:, cols], one_hot((row_head >> 6) + 2 * i == col_head))
        return carry

    lax.fori_loop(0, PAIRS // 2, pair_back, 0, unroll=2)
    for one in leaves:
        one.scan()
    sums[0].tick()
    lax.fori_loop(PAIRS // 2, PAIRS, pair_back, 0, unroll=2)
    for one in leaves:
        one.hand()
    sums[1].tick()
    dsc = jnp.where(iota((rows, rows), 1) >= iota((rows, rows), 0), r.dscores[...], 0.0).astype(bf16)
    d_b = dot(dsc, r.c[...])
    d_c = dot(dsc, r.b[...], TN) + dot(r.dye[...], r.enter[...], NT)
    for one in leaves:
        one.arrive()

    def channels_back(i, carry):
        cols = lanes(i * 128, 128)
        c0, c1 = columns(i)
        c01 = jnp.where(lane < HEAD_DIM, c0, c1)
        v = r.wide[:, cols] + jnp.exp2(c01[rows - 1 : rows, :] - c01) * dot(r.b[...], r.leave[:, cols])
        dtw = split_dot(r.head[0], one_hot((col_head >> 6) + 2 * i == row_head))
        x = r.x[:, cols]
        dy = r.dy[:, cols].astype(f32)
        r.q[...] += split_dot(x * v, one_hot((row_head >> 6) + 2 * i == col_head))
        r.skip[:, cols] = jnp.sum((dy * x).reshape(rows // 8, 8, 128), axis=0)
        r.ext[0:rows, cols] = (dtw * v + r.spread[8:9, cols] * dy) * keep * dsilu(cols)
        return carry

    lax.fori_loop(0, PAIRS, channels_back, 0, unroll=2)
    d_b = d_b + dot(r.xde[...], r.leave[...], NT)
    r.ext[0:rows, INNER : INNER + STATE] = d_b * dsilu(slice(INNER, INNER + STATE))
    r.ext[0:rows, INNER + STATE :] = d_c * dsilu(slice(INNER + STATE, XBC))
    edge_back = remote(r.ext.at[0:8], r.edge_grad, r.edge_sem.at[2], r.edge_sem.at[3], block_at(-1))
    edge_back.start()
    sums[0].tick()
    full_pick = one_hot((iota((INNER, 128), 0) >> 6) == iota((INNER, 128), 1))
    out_state = r.spread[0:1, :] * r.enter[...].astype(f32) + r.own[...]
    d_last = split_dot(
        jnp.sum((r.leave[...].astype(f32) * out_state).reshape(STATE // 8, 8, INNER), axis=0), full_pick
    )
    d_last = jnp.sum(d_last, axis=0, keepdims=True)
    q = r.q[...]
    d_cum = r.ry[...] - r.head[0] * q + jnp.where(iota((rows, 128), 0) == rows - 1, d_last, 0.0)
    above = one_hot(iota((rows, rows), 0) <= iota((rows, rows), 1))
    dz = (q + split_dot_left(above, d_cum * -jnp.exp(r.heads[1:2, :]))) * r.head[2]
    r.vec[...] = jnp.zeros_like(r.vec)
    r.vec[18:19, 0:128] = jnp.sum(dz, axis=0, keepdims=True)
    r.vec[19:20, 0:128] = jnp.sum(d_cum * r.head[1], axis=0, keepdims=True)
    r.vec[20:21, 0:128] = jnp.sum(split_dot(r.skip[...], full_pick), axis=0, keepdims=True)
    dz = dz.astype(bf16)
    d_normed = dot(r.dgate[...], r.w_in[:INNER, :])
    d_normed = d_normed + dot(dz[:, :HEADS], r.w_in[INNER + XBC :, :])
    edge_back.wait()
    r.ext[rows : rows + 8, :] = jnp.where(block == chips * 2 - 1, 0.0, r.edge_grad[...])
    sums[1].tick()

    def conv_back(i, carry):
        cols = lanes(i * 128, 128)
        drun = r.ext[0:rows, cols]
        total = drun * r.conv_w[CONV - 1 : CONV, cols]
        for tap in range(CONV - 1):
            ahead = CONV - 1 - tap
            total = total + r.ext[ahead : ahead + rows, cols] * r.conv_w[tap : tap + 1, cols]
        r.dproj[:, cols] = total.astype(bf16)
        for tap in range(CONV):
            r.tap_sums[tap : tap + 1, cols] = jnp.sum(
                drun * r.pad[13 + tap : 13 + tap + rows, cols], axis=0, keepdims=True
            )
        r.tap_sums[CONV : CONV + 1, cols] = jnp.sum(drun, axis=0, keepdims=True)
        return carry

    lax.fori_loop(0, XBC // 128, conv_back, 0, unroll=2)

    def rest_grads(i, carry):
        at = pl.ds(pl.multiple_of(i * 256, 256), 256)
        r.rest[at, :] = dot(r.dproj[:, lanes(i * 256, 256)], r.normed[own_rows, :], TN).astype(bf16)
        return carry

    lax.fori_loop(0, 4, rest_grads, 0, unroll=2)
    sums[2].tick()
    sums[0].tick()
    lax.fori_loop(4, XBC // 256, rest_grads, 0)
    for v in range(CONV + 1):
        for part in range(3):
            width = min(D, XBC - part * D)
            r.vec[3 * v + part : 3 * v + part + 1, 0:width] = r.tap_sums[v : v + 1, part * D : part * D + width]
    d_normed = d_normed + dot(r.dproj[...], r.w_in[INNER : INNER + XBC, :])
    src = r.blk[...].astype(f32)
    scale = lax.rsqrt(jnp.mean(src * src, axis=-1, keepdims=True) + EPS)
    r.vec[15:16, :] = jnp.sum(d_normed * src * scale, axis=0, keepdims=True)
    gate_gain = jnp.sum(r.ggain[...], axis=0, keepdims=True)
    r.vec[16:17, :] = gate_gain[:, :D]
    r.vec[17:18, :] = gate_gain[:, D:]
    r.rest[XBC:VEC_ROW, :] = dot(dz, r.normed[own_rows, :], TN).astype(bf16)
    r.rest[VEC_ROW : VEC_ROW + 32, :] = r.vec[...].astype(bf16)
    r.rest[VEC_ROW + 32 :, :] = jnp.zeros((REST_ROWS - VEC_ROW - 32, D), bf16)
    sums[3].tick()
    sums[1].tick()
    weighted = d_normed * r.gain[...]
    average = jnp.mean(weighted * src, axis=-1, keepdims=True)
    r.grad_in[...] = r.gout[...].astype(f32) + scale * weighted - src * (scale * scale * scale) * average
    for _ in range(STAGES + 1):
        for total in (sums[2], sums[0], sums[3], sums[1]):
            if total.stage < STAGES:
                total.tick()


def whole(*args):
    t = args[0].shape[0]
    chips = lax.axis_size("seq") // SEQS
    ins = ["blk", "gout", "lengths", "norm_gain", "w_in_hbm", "conv_w", "conv_bias", "dt_bias", "a_log", "d_skip"]
    ins += ["gated_gain", "w_out_hbm"]
    outs = {
        "block_out": ((t, D), bf16),
        "grad_in": ((t, D), f32),
        "first_out": ((FIRST_ROWS, D), bf16),
        "rest_out": ((REST_ROWS, D), bf16),
    }
    held = {
        "first": ((FIRST_ROWS, D), bf16),
        "rest": ((REST_ROWS, D), bf16),
        "gain": ((1, D), f32),
        "conv_b": ((1, XBC), f32),
        "gate_gain": ((1, INNER), f32),
        "heads": ((8, 128), f32),
        "w_in": ((PROJ, D), bf16),
        "w_out": ((INNER, D), bf16),
        "edge": ((16, D), bf16),
        "edge_grad": ((8, XBC), f32),
        "normed": ((t + 16, D), bf16),
        "gate": ((t, INNER), bf16),
        "pad": ((t + 16, XBC), f32),
        "run": ((t, XBC), f32),
        "x": ((t, INNER), f32),
        "xd": ((t, INNER), bf16),
        "xde": ((t, INNER), bf16),
        "b": ((t, STATE), bf16),
        "c": ((t, STATE), bf16),
        "head": ((4, t, 128), f32),
        "cumt": ((128, t), f32),
        "cumb": ((t, HEADS * 128), f32),
        "spread": ((16, INNER), f32),
        "own": ((STATE, INNER), f32),
        "enter": ((STATE, INNER), bf16),
        "y": ((t, INNER), f32),
        "mixed": ((t, INNER), bf16),
        "gn": ((t, INNER), bf16),
        "wide": ((t, INNER), f32),
        "db": ((t, D), bf16),
        "dy": ((t, INNER), bf16),
        "dye": ((t, INNER), bf16),
        "dgate": ((t, INNER), bf16),
        "ggain": ((8, INNER), f32),
        "adj": ((STATE, INNER), f32),
        "leave": ((STATE, INNER), bf16),
        "scores": ((t, t), f32),
        "scores_t": ((t, t), f32),
        "dscores": ((t, t), f32),
        "skip": ((8, INNER), f32),
        "q": ((t, 128), f32),
        "ry": ((t, 128), f32),
        "ext": ((t + 8, XBC), f32),
        "dproj": ((t, XBC), bf16),
        "vec": ((32, D), f32),
        "tap_sums": ((8, XBC), f32),
        "got_first": ((FIRST_ROWS, D), bf16),
        "got_rest": ((REST_ROWS, D), bf16),
    }
    names = ins + list(outs) + list(held)
    scratch = [pltpu.VMEM(s, d) for s, d in held.values()]
    states, decays = exchange_scratch(chips, INNER // 2 // SPLITS)
    for tag, shapes in (("f", states), ("g", states), ("d", decays)):
        for k in range(SPLITS):
            scratch += [pltpu.VMEM(s, d) for s, d in shapes]
            names += [f"{tag}{k}_{n}" for n in range(len(shapes))]
    semaphores = {
        "ss": (WAVES, 3, STAGES),
        "rs": (WAVES, 3, STAGES),
        "ls": (WAVES, 3),
        "fs": (SPLITS, 3 * chips),
        "fr": (SPLITS, 3 * chips),
        "gs": (SPLITS, 3 * chips),
        "gr": (SPLITS, 3 * chips),
        "edge_sem": (4,),
        "load_sem": (3,),
    }
    for name, shape in semaphores.items():
        scratch.append(pltpu.SemaphoreType.DMA(shape))
        names.append(name)
    any_space = pl.BlockSpec(memory_space=pl.ANY)
    specs = {"lengths": SMEM, "w_in_hbm": any_space, "w_out_hbm": any_space, "first_out": any_space, "rest_out": any_space}
    return pl.pallas_call(
        partial(whole_kernel, names),
        out_shape=[jax.ShapeDtypeStruct(s, d) for s, d in outs.values()],
        in_specs=[specs.get(n, VMEM) for n in ins],
        out_specs=[specs.get(n, VMEM) for n in outs],
        scratch_shapes=scratch,
        compiler_params=pltpu.CompilerParams(vmem_limit_bytes=60 << 20, collective_id=0, has_side_effects=True),
    )(*args)


def finish_kernel(
    block_in,
    grad_in,
    first,
    rest,
    block_out,
    grad_out,
    norm_out,
    w_in_out,
    conv_out,
    bias_out,
    dt_out,
    alog_out,
    skip_out,
    gate_out,
    w_out_out,
    held_first,
    held_rest,
    held_block,
    held_grad,
    wide_in,
    wide_out,
    in_sem,
    out_sem,
    pass_sem,
):
    passed = [
        (pltpu.make_async_copy(src, by, pass_sem.at[n, 0]), pltpu.make_async_copy(by, dst, pass_sem.at[n, 1]))
        for n, (src, by, dst) in enumerate(((block_in, held_block, block_out), (grad_in, held_grad, grad_out)))
    ]
    chunks = [(first, held_first, k * 256, 256) for k in range(FIRST_ROWS // 256)]
    chunks += [(rest, held_rest, k * 256, 256) for k in range(REST_ROWS // 256)]
    loads = [
        pltpu.make_async_copy(src.at[start : start + size], dst.at[start : start + size], in_sem.at[n])
        for n, (src, dst, start, size) in enumerate(chunks)
    ]
    ahead = 4
    for c in loads[:ahead] + [load for load, _ in passed]:
        c.start()
    stores = [store for _, store in passed]
    for n, (src, held, start, size) in enumerate(chunks):
        loads[n].wait()
        if n == ahead:
            for load, store in passed:
                load.wait()
                store.start()
        if n + ahead < len(loads):
            loads[n + ahead].start()
        if src is first and start >= INNER:
            wide, out, at = wide_out, w_out_out, start - INNER
        else:
            wide, out, at = wide_in, w_in_out, start if src is first else INNER + start
        kept = min(size, out.shape[0] - at)
        if kept <= 0:
            continue
        wide[at : at + kept, :] = held[start : start + kept, :].astype(f32)
        c = pltpu.make_async_copy(wide.at[at : at + kept], out.at[at : at + kept], out_sem.at[n])
        c.start()
        stores.append(c)
    vec = held_rest[VEC_ROW : VEC_ROW + 32, :].astype(f32)

    def row(v):
        return jnp.concatenate([vec[3 * v + k : 3 * v + k + 1, : min(D, XBC - k * D)] for k in range(3)], axis=1)

    for v in range(CONV):
        conv_out[v : v + 1, :] = row(v)
    bias_out[...] = row(CONV).reshape(XBC)
    norm_out[...] = vec[15:16, :].reshape(D)
    gate_out[...] = jnp.concatenate([vec[16:17, :], vec[17:18, :]], axis=1).reshape(INNER)
    for k, out in enumerate((dt_out, alog_out, skip_out)):
        out[...] = vec[18 + k : 19 + k, 0:HEADS].reshape(HEADS)
    for c in stores:
        c.wait()


def finish(block_out, grad_in, first, rest):
    shapes = [block_out.shape, grad_in.shape, (D,), (PROJ, D), (CONV, XBC), (XBC,), (HEADS,), (HEADS,), (HEADS,), (INNER,)]
    shapes += [(INNER, D)]
    any_space = pl.BlockSpec(memory_space=pltpu.HBM)
    away = (0, 1, 3, 10)
    chunks = (FIRST_ROWS + REST_ROWS) // 256
    return pl.pallas_call(
        finish_kernel,
        out_shape=[jax.ShapeDtypeStruct(s, bf16 if k == 0 else f32) for k, s in enumerate(shapes)],
        in_specs=[any_space] * 4,
        out_specs=[any_space if k in away else VMEM for k in range(len(shapes))],
        scratch_shapes=[
            pltpu.VMEM((FIRST_ROWS, D), bf16),
            pltpu.VMEM((REST_ROWS, D), bf16),
            pltpu.VMEM(block_out.shape, bf16),
            pltpu.VMEM(grad_in.shape, f32),
            pltpu.VMEM((PROJ, D), f32),
            pltpu.VMEM((INNER, D), f32),
            pltpu.SemaphoreType.DMA((chunks,)),
            pltpu.SemaphoreType.DMA((chunks,)),
            pltpu.SemaphoreType.DMA((2, 2)),
        ],
        compiler_params=pltpu.CompilerParams(vmem_limit_bytes=60 << 20),
    )(block_out, grad_in, first, rest)


def shifted(value, ahead):
    groups = lax.axis_size("head")
    count = lax.axis_size("seq") * groups
    moves = []
    for source in range(count):
        piece, half = source // groups, source % groups
        half += ahead
        if half == groups:
            half, piece = 0, piece + SEQS
        elif half < 0:
            half, piece = groups - 1, piece - SEQS
        if 0 <= piece * groups + half < count:
            moves.append((source, piece * groups + half))
    return lax.ppermute(value, ("seq", "head"), moves)


def by_parts(block_in, grad_out, lengths, norm_gain, w_in, conv_w, conv_b, dt_bias, a_log, d_skip, gate_gain, w_out):
    heads = jnp.pad(jnp.stack([dt_bias, a_log, d_skip]), ((0, 5), (0, 128 - HEADS)))
    gain, conv_b, gate_gain = norm_gain.reshape(1, D), conv_b.reshape(1, XBC), gate_gain.reshape(1, INNER)
    edge = shifted(block_in[-16:], 1)
    (normed, gate, pad, run, x, xd, xde, b, c, head, cumt, cumb, rows, own) = front(
        lengths, block_in, edge, gain, w_in, conv_w, conv_b, heads
    )
    enter = exchange_plain(own, rows[0:8], False)
    (y, block_out, dy, dye, dgate, ggain, adj, grads_a) = middle(
        lengths, block_in, grad_out, normed, gate, x, xd, b, c, cumt, cumb, rows, enter, gate_gain, w_out
    )
    leave = exchange_plain(adj, rows[0:8], True)
    drun, dz, small = back(
        lengths, y, dy, dye, x, xd, xde, b, c, run, cumt, cumb, head, rows, heads, enter, own, leave
    )
    edge_back = shifted(drun[0:8], -1)
    grad_in, grads_b = last(
        block_in, grad_out, normed, gain, w_in, conv_w, pad, drun, edge_back, dz, dgate, ggain, small
    )
    grads_a, grads_b = lax.psum((grads_a, grads_b), ("seq", "head"))
    return block_out, grad_in, grads_a, grads_b


def local(block_in, grad_out, lengths, norm_gain, w_in, *others):
    run = whole if lax.axis_size("seq") == 16 and lax.axis_size("head") == 2 else by_parts
    outs = finish(*run(block_in, grad_out, lengths, norm_gain, w_in.T, *others))
    return (*outs[:3], outs[3].T, *outs[4:])


def solution(mesh):
    rows = P(("seq", "head"), None)
    return jax.shard_map(
        local,
        mesh=mesh,
        in_specs=(rows, rows) + (P(),) * 10,
        out_specs=(rows, rows) + (P(),) * 9,
        check_vma=False,
    )
```

```python
from functools import partial

import jax
import jax.numpy as jnp
from jax import lax
from jax.experimental import pallas as pl
from jax.experimental.pallas import tpu as pltpu
from jax.sharding import PartitionSpec as P

D = 768
INNER = 1536
HEADS = 24
HEAD_DIM = 64
STATE = 128
CONV = 4
SEQS = 2
XBC = INNER + 2 * STATE
PROJ = 2 * INNER + 2 * STATE + HEADS
PAIRS = HEADS // 2
EPS = 1e-05
LOG2E = 1.4426950408889634

f32 = jnp.float32
bf16 = jnp.bfloat16
MESH = pl.DeviceIdType.MESH
VMEM = pl.BlockSpec(memory_space=pltpu.VMEM)
SMEM = pl.BlockSpec(memory_space=pltpu.SMEM)
NN = ((1,), (0,))
NT = ((1,), (1,))
TN = ((0,), (0,))


def dot(a, b, dims=NN):
    return lax.dot_general(a, b, (dims, ((), ())), preferred_element_type=f32)


def split_dot(a, pick, terms=3):
    total = None
    for _ in range(terms):
        part = a.astype(bf16)
        a = a - part.astype(f32)
        term = dot(part, pick)
        total = term if total is None else total + term
    return total


def split_dot_left(pick, a, terms=3):
    total = None
    for _ in range(terms):
        part = a.astype(bf16)
        a = a - part.astype(f32)
        term = dot(pick, part)
        total = term if total is None else total + term
    return total


def iota(shape, dim):
    return lax.broadcasted_iota(jnp.int32, shape, dim)


def one_hot(cond):
    return jnp.where(cond, 1.0, 0.0).astype(bf16)


def sigmoid(v):
    return 1.0 / (1.0 + jnp.exp(-v))


def lanes(start, size):
    return pl.ds(pl.multiple_of(start, 128), size)


def valid_rows(lengths_ref, rows, width):
    place = lax.axis_index("seq")
    first = (place // SEQS) * (rows * lax.axis_size("head")) + lax.axis_index("head") * rows
    limit = lengths_ref[place % SEQS]
    return jnp.where(iota((rows, width), 0) + first < limit, 1.0, 0.0)


def call(body, outs, args, scratch=(), smem=(), vmem=56 << 20, cost=None, **params):
    return pl.pallas_call(
        body,
        out_shape=[jax.ShapeDtypeStruct(s, d) for s, d in outs],
        in_specs=[SMEM if i in smem else VMEM for i in range(len(args))],
        out_specs=[VMEM] * len(outs),
        scratch_shapes=list(scratch),
        compiler_params=pltpu.CompilerParams(vmem_limit_bytes=vmem, **params),
    )(*args)


VEC_ROW = XBC + 128
REST_ROWS = 2048
FIRST_ROWS = 2 * INNER
WAVES = 5
SPLITS = 2


def front_kernel(
    lengths_ref,
    blk,
    edge,
    gain,
    w_in,
    conv_w,
    conv_b,
    heads_ref,
    normed_out,
    gate_out,
    pad_out,
    run_out,
    x_out,
    xd_out,
    xde_out,
    b_out,
    c_out,
    head_out,
    cumt_out,
    cumb_out,
    rows_out,
    state_out,
):
    rows = blk.shape[0]

    def norm(v):
        v = v.astype(f32)
        scale = lax.rsqrt(jnp.mean(v * v, axis=-1, keepdims=True) + EPS)
        return (v * scale * gain[...]).astype(bf16)

    normed = norm(blk[...])
    normed_out[...] = normed
    gate_out[...] = dot(normed, w_in[:INNER, :], NT).astype(bf16)
    ahead = norm(edge[...])
    pad_out[0:16, :] = dot(ahead, w_in[INNER : INNER + XBC, :], NT).astype(bf16).astype(f32)
    pad_out[16 : 16 + rows, :] = dot(normed, w_in[INNER : INNER + XBC, :], NT).astype(bf16).astype(f32)
    keep = valid_rows(lengths_ref, rows, 128)
    head_out[3] = jnp.zeros((rows, 128), f32)
    head_out[3, :, 0:HEADS] = dot(normed, w_in[INNER + XBC :, :], NT).astype(bf16).astype(f32)
    lane = iota((rows, 128), 1)
    shifted = head_out[3] + heads_ref[0:1, :]
    soft = jnp.maximum(shifted, 0.0) + jnp.log1p(jnp.exp(-jnp.abs(shifted)))
    dt = jnp.where(lane < HEADS, soft * keep, 0.0)
    rates = -jnp.exp(heads_ref[1:2, :])
    below = one_hot(iota((rows, rows), 0) >= iota((rows, rows), 1))
    cum = split_dot_left(below, dt) * rates
    cum2 = cum * LOG2E
    head_out[0] = dt
    head_out[1] = cum
    head_out[2] = sigmoid(shifted) * keep
    head_out[3] = cum2
    cumt_out[...] = cum2.T
    pick_lane = iota((128, 256), 1)
    pick_head = iota((128, 256), 0)

    def spread(i, carry):
        cumb_out[:, lanes(i * 256, 256)] = split_dot(
            head_out[3], one_hot((pick_lane >> 7) + 2 * i == pick_head)
        )
        return carry

    lax.fori_loop(0, PAIRS, spread, 0)

    def convolve(i):
        cols = lanes(i * 256, 256)
        running = conv_b[:, cols] + pad_out[13 : 13 + rows, cols] * conv_w[0:1, cols]
        for tap in range(1, CONV):
            running = running + pad_out[13 + tap : 13 + tap + rows, cols] * conv_w[tap : tap + 1, cols]
        run_out[:, cols] = running
        return running * sigmoid(running)

    act = convolve(INNER // 256)
    b_out[...] = act[:, :STATE].astype(bf16)
    c_out[...] = act[:, STATE:].astype(bf16)
    keep2 = valid_rows(lengths_ref, rows, 256)

    def channels(i, carry):
        cols = lanes(i * 256, 256)
        pick = one_hot((pick_lane >> 6) + 4 * i == pick_head)
        x = convolve(i) * keep2
        x_out[:, cols] = x
        xd = x * split_dot(head_out[0], pick)
        xd_out[:, cols] = xd.astype(bf16)
        wide = split_dot(head_out[3], pick)
        last = wide[rows - 1 : rows, :]
        xde_out[:, cols] = (xd * jnp.exp2(last - wide)).astype(bf16)
        rows_out[0:8, cols] = jnp.broadcast_to(jnp.exp2(last), (8, 256))
        rows_out[8:16, cols] = split_dot(jnp.broadcast_to(heads_ref[2:3, :], (8, 128)), pick)
        return carry

    lax.fori_loop(0, INNER // 256, channels, 0)
    state_out[...] = dot(b_out[...], xde_out[...], TN)


def front(lengths, blk, edge, gain, w_in, conv_w, conv_b, heads):
    t = blk.shape[0]
    outs = [
        ((t, D), bf16),
        ((t, INNER), bf16),
        ((t + 16, XBC), f32),
        ((t, XBC), f32),
        ((t, INNER), f32),
        ((t, INNER), bf16),
        ((t, INNER), bf16),
        ((t, STATE), bf16),
        ((t, STATE), bf16),
        ((4, t, 128), f32),
        ((128, t), f32),
        ((t, HEADS * 128), f32),
        ((16, INNER), f32),
        ((STATE, INNER), f32),
    ]
    return call(front_kernel, outs, (lengths, blk, edge, gain, w_in, conv_w, conv_b, heads), smem=(0,))


def exchange_plain(state, decay, reverse):
    groups = lax.axis_size("head")
    count = lax.axis_size("seq") * groups
    place = lax.axis_index("seq")
    states = lax.all_gather(state.astype(bf16), ("seq", "head"), axis=0)
    decays = lax.all_gather(decay[0:1], ("seq", "head"), axis=0)
    blocks = count // SEQS
    block = place // SEQS * groups + lax.axis_index("head")

    def one(i, carry):
        source = blocks - 1 - i if reverse else i
        index = (source // groups * SEQS + place % SEQS) * groups + source % groups
        new = lax.dynamic_index_in_dim(decays, index, 0, False) * carry
        return new + lax.dynamic_index_in_dim(states, index, 0, False).astype(f32)

    ahead = blocks - 1 - block if reverse else block
    return lax.fori_loop(0, ahead, one, jnp.zeros(state.shape, f32)).astype(bf16)


def middle_kernel(
    lengths_ref,
    blk,
    gout,
    normed,
    gate,
    x_in,
    xd_in,
    b_in,
    c_in,
    cumt,
    cumb,
    rows_in,
    enter,
    gain,
    w_out,
    y_out,
    block_out,
    dy_out,
    dye_out,
    dgate_out,
    ggain_out,
    adj_out,
    grads_out,
    scores,
    mixed,
    gated_s,
    gn_s,
    scale_s,
    dgn_s,
    db_s,
):
    rows = blk.shape[0]
    causal = iota((rows, rows), 0) >= iota((rows, rows), 1)
    scores[...] = jnp.where(causal, dot(c_in[...], b_in[...], NT), 0.0)
    lane = iota((rows, 128), 1)
    left = one_hot(iota((1, 128), 1) < HEAD_DIM)
    right = one_hot(iota((1, 128), 1) >= HEAD_DIM)

    def pair(i, carry):
        cols = lanes(i * 128, 128)
        c0 = cumb[:, lanes(i * 256, 128)]
        c1 = cumb[:, lanes(i * 256 + 128, 128)]
        xd = xd_in[:, cols]
        y = None
        for cc, part, mask in ((c0, 0, left), (c1, 1, right)):
            row = cumt[pl.ds(2 * i + part, 1), :]
            decay = jnp.exp2(jnp.minimum(jnp.concatenate([cc] * (rows // 128), axis=1) - row, 0.0))
            term = dot((decay * scores[...]).astype(bf16), xd * mask)
            y = term if y is None else y + term
        grow = jnp.exp2(jnp.where(lane < HEAD_DIM, c0, c1))
        y = y + grow * dot(c_in[...], enter[:, cols])
        y_out[:, cols] = y
        mixed[:, cols] = (y + rows_in[8:9, cols] * x_in[:, cols]).astype(bf16).astype(f32)
        return carry

    lax.fori_loop(0, PAIRS, pair, 0)
    step = 32

    def gating(i, carry):
        r = pl.ds(pl.multiple_of(i * step, step), step)
        g = gate[r, :].astype(f32)
        gated = mixed[r, :] * g * sigmoid(g)
        scale = lax.rsqrt(jnp.mean(gated * gated, axis=-1, keepdims=True) + EPS)
        gated_s[r, :] = gated
        scale_s[r, :] = jnp.broadcast_to(scale, (step, 128))
        gn_s[r, :] = (gated * scale * gain[...]).astype(bf16)
        return carry

    lax.fori_loop(0, rows // step, gating, 0)
    keep = valid_rows(lengths_ref, rows, D)
    db_s[...] = (gout[...].astype(f32) * keep).astype(bf16)
    dgn_s[...] = dot(db_s[...], w_out[...], NT)
    block_out[...] = (blk[...].astype(f32) + keep * dot(gn_s[...], w_out[...])).astype(bf16)
    ggain_out[...] = jnp.zeros_like(ggain_out)

    def ungating(i, carry):
        r = pl.ds(pl.multiple_of(i * step, step), step)
        g = gate[r, :].astype(f32)
        sg = sigmoid(g)
        gated = gated_s[r, :]
        scale = scale_s[r, 0:1]
        dgn = dgn_s[r, :]
        ggain_out[...] += jnp.sum((dgn * gated * scale).reshape(step // 8, 8, INNER), axis=0)
        weighted = dgn * gain[...]
        average = jnp.mean(weighted * gated, axis=-1, keepdims=True)
        d_gated = scale * weighted - gated * (scale * scale * scale) * average
        dy_out[r, :] = (d_gated * g * sg).astype(bf16)
        dgate_out[r, :] = (d_gated * mixed[r, :] * sg * (1.0 + g * (1.0 - sg))).astype(bf16)
        return carry

    lax.fori_loop(0, rows // step, ungating, 0)

    def weigh(i, carry):
        cols = lanes(i * 128, 128)
        grow = jnp.exp2(jnp.where(lane < HEAD_DIM, cumb[:, lanes(i * 256, 128)], cumb[:, lanes(i * 256 + 128, 128)]))
        dye_out[:, cols] = (dy_out[:, cols].astype(f32) * grow).astype(bf16)
        return carry

    lax.fori_loop(0, PAIRS, weigh, 0)
    adj_out[...] = dot(c_in[...], dye_out[...], TN)
    grads_out[:INNER, :] = dot(dgate_out[...], normed[...], TN).astype(bf16)
    grads_out[INNER:, :] = dot(gn_s[...], db_s[...], TN).astype(bf16)


def middle(lengths, blk, gout, normed, gate, x, xd, b, c, cumt, cumb, rows_in, enter, gain, w_out):
    t = blk.shape[0]
    outs = [
        ((t, INNER), f32),
        ((t, D), bf16),
        ((t, INNER), bf16),
        ((t, INNER), bf16),
        ((t, INNER), bf16),
        ((8, INNER), f32),
        ((STATE, INNER), f32),
        ((2 * INNER, D), bf16),
    ]
    scratch = [
        pltpu.VMEM((t, t), f32),
        pltpu.VMEM((t, INNER), f32),
        pltpu.VMEM((t, INNER), f32),
        pltpu.VMEM((t, INNER), bf16),
        pltpu.VMEM((t, 128), f32),
        pltpu.VMEM((t, INNER), f32),
        pltpu.VMEM((t, D), bf16),
    ]
    args = (lengths, blk, gout, normed, gate, x, xd, b, c, cumt, cumb, rows_in, enter, gain, w_out)
    return call(middle_kernel, outs, args, scratch, smem=(0,))


def back_kernel(
    lengths_ref,
    y_in,
    dy_in,
    dye_in,
    x_in,
    xd_in,
    xde_in,
    b_in,
    c_in,
    run_in,
    cumt,
    cumb,
    head_in,
    rows_in,
    heads_ref,
    enter,
    own,
    leave,
    drun_out,
    dz_out,
    small_out,
    scores,
    dscores,
    skip_s,
    q_s,
    ry_s,
):
    rows = y_in.shape[0]
    causal = iota((rows, rows), 1) >= iota((rows, rows), 0)
    scores[...] = jnp.where(causal, dot(b_in[...], c_in[...], NT), 0.0)
    dscores[...] = jnp.zeros_like(dscores)
    q_s[...] = jnp.zeros_like(q_s)
    ry_s[...] = jnp.zeros_like(ry_s)
    lane = iota((rows, 128), 1)
    keep = valid_rows(lengths_ref, rows, 128)
    left = one_hot(iota((1, 128), 1) < HEAD_DIM)
    right = one_hot(iota((1, 128), 1) >= HEAD_DIM)
    pick_lane = iota((128, 128), 0)
    pick_head = iota((128, 128), 1)

    def dsilu(cols):
        running = run_in[:, cols]
        sg = sigmoid(running)
        return sg * (1.0 + running * (1.0 - sg))

    def pair(i, carry):
        cols = lanes(i * 128, 128)
        c0 = cumb[:, lanes(i * 256, 128)]
        c1 = cumb[:, lanes(i * 256 + 128, 128)]
        xd = xd_in[:, cols]
        dy = dy_in[:, cols]
        v = None
        for cc, part, mask in ((c0, 0, left), (c1, 1, right)):
            row = cumt[pl.ds(2 * i + part, 1), :]
            decay = jnp.exp2(jnp.minimum(row - jnp.concatenate([cc] * (rows // 128), axis=1), 0.0))
            masked = dy * mask
            term = dot((decay * scores[...]).astype(bf16), masked)
            v = term if v is None else v + term
            dscores[...] += decay * dot(xd, masked, NT)
        c01 = jnp.where(lane < HEAD_DIM, c0, c1)
        v = v + jnp.exp2(c01[rows - 1 : rows, :] - c01) * dot(b_in[...], leave[:, cols])
        pick = one_hot((pick_lane >> 6) + 2 * i == pick_head)
        dtw = split_dot(head_in[0], one_hot((pick_head >> 6) + 2 * i == pick_lane))
        x = x_in[:, cols]
        dyf = dy.astype(f32)
        q_s[...] += split_dot(x * v, pick)
        ry_s[...] += split_dot(dyf * y_in[:, cols], pick)
        skip_s[:, cols] = jnp.sum((dyf * x).reshape(rows // 8, 8, 128), axis=0)
        dx = dtw * v + rows_in[8:9, cols] * dyf
        drun_out[:, cols] = dx * keep * dsilu(cols)
        return carry

    lax.fori_loop(0, PAIRS, pair, 0)
    dsc = jnp.where(causal, dscores[...], 0.0).astype(bf16)
    d_b = dot(dsc, c_in[...]) + dot(xde_in[...], leave[...], NT)
    d_c = dot(dsc, b_in[...], TN) + dot(dye_in[...], enter[...], NT)
    drun_out[:, INNER : INNER + STATE] = d_b * dsilu(slice(INNER, INNER + STATE))
    drun_out[:, INNER + STATE :] = d_c * dsilu(slice(INNER + STATE, XBC))
    full_pick = one_hot((iota((INNER, 128), 0) >> 6) == iota((INNER, 128), 1))
    out_state = rows_in[0:1, :] * enter[...].astype(f32) + own[...]
    d_last = split_dot(
        jnp.sum((leave[...].astype(f32) * out_state).reshape(STATE // 8, 8, INNER), axis=0), full_pick
    )
    d_last = jnp.sum(d_last, axis=0, keepdims=True)
    dt = head_in[0]
    q = q_s[...]
    d_cum = ry_s[...] - dt * q + jnp.where(iota((rows, 128), 0) == rows - 1, d_last, 0.0)
    rates = -jnp.exp(heads_ref[1:2, :])
    above = one_hot(iota((rows, rows), 0) <= iota((rows, rows), 1))
    d_dt = q + split_dot_left(above, d_cum * rates)
    dz = d_dt * head_in[2]
    dz_out[...] = dz
    small_out[0:1, :] = jnp.sum(dz, axis=0, keepdims=True)
    small_out[1:2, :] = jnp.sum(d_cum * head_in[1], axis=0, keepdims=True)
    small_out[2:3, :] = jnp.sum(split_dot(skip_s[...], full_pick), axis=0, keepdims=True)
    small_out[3:8, :] = jnp.zeros((5, 128), f32)


def back(lengths, y, dy, dye, x, xd, xde, b, c, run, cumt, cumb, head, rows_in, heads, enter, own, leave):
    t = y.shape[0]
    outs = [((t, XBC), f32), ((t, 128), f32), ((8, 128), f32)]
    scratch = [
        pltpu.VMEM((t, t), f32),
        pltpu.VMEM((t, t), f32),
        pltpu.VMEM((8, INNER), f32),
        pltpu.VMEM((t, 128), f32),
        pltpu.VMEM((t, 128), f32),
    ]
    args = (lengths, y, dy, dye, x, xd, xde, b, c, run, cumt, cumb, head, rows_in, heads, enter, own, leave)
    return call(back_kernel, outs, args, scratch, smem=(0,))


def last_kernel(
    blk,
    gout,
    normed,
    gain,
    w_in,
    conv_w,
    pad_in,
    drun_in,
    edge,
    dz_in,
    dgate,
    ggain,
    small_in,
    gin_out,
    grads_out,
    ext,
    dproj,
    vec,
    sums,
):
    rows = blk.shape[0]
    ext[0:rows, :] = drun_in[...]
    ext[rows : rows + 8, :] = edge[...]
    vec[...] = jnp.zeros_like(vec)

    def channels(i, carry):
        cols = lanes(i * 128, 128)
        drun = ext[0:rows, cols]
        total = drun * conv_w[CONV - 1 : CONV, cols]
        for tap in range(CONV - 1):
            ahead = CONV - 1 - tap
            total = total + ext[ahead : ahead + rows, cols] * conv_w[tap : tap + 1, cols]
        dproj[:, cols] = total.astype(bf16)
        for tap in range(CONV):
            sums[tap : tap + 1, cols] = jnp.sum(
                drun * pad_in[13 + tap : 13 + tap + rows, cols], axis=0, keepdims=True
            )
        sums[CONV : CONV + 1, cols] = jnp.sum(drun, axis=0, keepdims=True)
        return carry

    lax.fori_loop(0, XBC // 128, channels, 0)
    for v in range(CONV + 1):
        for part in range(3):
            width = min(D, XBC - part * D)
            vec[3 * v + part : 3 * v + part + 1, 0:width] = sums[v : v + 1, part * D : part * D + width]
    dz = dz_in[...].astype(bf16)
    d_normed = dot(dgate[...], w_in[:INNER, :])
    d_normed = d_normed + dot(dproj[...], w_in[INNER : INNER + XBC, :])
    d_normed = d_normed + dot(dz[:, :HEADS], w_in[INNER + XBC :, :])
    src = blk[...].astype(f32)
    scale = lax.rsqrt(jnp.mean(src * src, axis=-1, keepdims=True) + EPS)
    vec[15:16, :] = jnp.sum(d_normed * src * scale, axis=0, keepdims=True)
    gate_gain = jnp.sum(ggain[...], axis=0, keepdims=True)
    vec[16:17, :] = gate_gain[:, :D]
    vec[17:18, :] = gate_gain[:, D:]
    vec[18:21, 0:128] = small_in[0:3, :]
    weighted = d_normed * gain[...]
    average = jnp.mean(weighted * src, axis=-1, keepdims=True)
    gin_out[...] = gout[...].astype(f32) + scale * weighted - src * (scale * scale * scale) * average
    grads_out[:XBC, :] = dot(dproj[...], normed[...], TN).astype(bf16)
    grads_out[XBC:VEC_ROW, :] = dot(dz, normed[...], TN).astype(bf16)
    grads_out[VEC_ROW : VEC_ROW + 32, :] = vec[...].astype(bf16)
    grads_out[VEC_ROW + 32 :, :] = jnp.zeros((REST_ROWS - VEC_ROW - 32, D), bf16)


def last(blk, gout, normed, gain, w_in, conv_w, pad, drun, edge, dz, dgate, ggain, small):
    t = blk.shape[0]
    outs = [((t, D), f32), ((REST_ROWS, D), bf16)]
    scratch = [pltpu.VMEM((t + 8, XBC), f32), pltpu.VMEM((t, XBC), bf16), pltpu.VMEM((32, D), f32), pltpu.VMEM((8, XBC), f32)]
    args = (blk, gout, normed, gain, w_in, conv_w, pad, drun, edge, dz, dgate, ggain, small)
    return call(last_kernel, outs, args, scratch)


class Refs:
    def __init__(self, names, refs):
        self.__dict__.update(zip(names, refs, strict=True))


def remote(src, dst, ssem, rsem, to):
    return pltpu.make_async_remote_copy(
        src_ref=src, dst_ref=dst, send_sem=ssem, recv_sem=rsem, device_id=to, device_id_type=MESH
    )


class Exchange:
    def __init__(self, reverse, state, decay, out, bufs, decays, ssem, rsem, start, width):
        self.sib_state, self.mine, self.got, self.back, self.back_got = bufs
        self.sib_decay, self.total, self.got_decay = decays
        self.state, self.decay, self.out, self.reverse = state, decay, out, reverse
        self.ssem, self.rsem = ssem, rsem
        self.chips = lax.axis_size("seq") // SEQS
        self.rows = STATE // self.chips
        self.width = width
        place, core = lax.axis_index("seq"), lax.axis_index("head")
        self.core = core
        self.chip, self.which = place // SEQS, place % SEQS
        self.sibling = (place, 1 - core)
        self.later = (1 - core if reverse else core) == 1
        self.own_cols = lanes(core * (INNER // 2) + start, width)
        self.sib_cols = lanes((1 - core) * (INNER // 2) + start, width)

    def peer(self, k):
        return (lax.rem(self.chip + k, self.chips) * SEQS + self.which, self.core)

    def send(self, copies):
        for src, dst, n, to in copies:
            remote(src, dst, self.ssem.at[n % 2], self.rsem.at[n], to).start()

    def arrive(self, *whole):
        for src, dst, n in whole:
            remote(src, dst, self.ssem.at[n % 2], self.rsem.at[n], self.sibling).wait()

    def begin(self):
        copies = [(self.state.at[:, self.sib_cols], self.sib_state, 0, self.sibling)]
        if not self.reverse:
            copies.append((self.decay.at[0:8, self.sib_cols], self.sib_decay, 1, self.sibling))
        self.send(copies)

    def ordered(self):
        own, other = self.state[:, self.own_cols], self.sib_state[...]
        own_decay, other_decay = self.decay[0:1, self.own_cols], self.sib_decay[0:1, :]
        later = self.later
        return (
            jnp.where(later, other, own),
            jnp.where(later, own, other),
            jnp.where(later, other_decay, own_decay),
            jnp.where(later, own_decay, other_decay),
        )

    def deal(self):
        whole = [(self.state.at[:, self.sib_cols], self.sib_state, 0)]
        if not self.reverse:
            whole.append((self.decay.at[0:8, self.sib_cols], self.sib_decay, 1))
        self.arrive(*whole)
        early, late, early_decay, late_decay = self.ordered()
        self.mine[...] = (late_decay * early + late).astype(bf16)
        if not self.reverse:
            self.total[...] = jnp.broadcast_to(early_decay * late_decay, self.total.shape)
        copies = []
        for k in range(1, self.chips):
            to = lax.rem(self.chip + k, self.chips)
            piece = pl.ds(pl.multiple_of(to * self.rows, self.rows), self.rows)
            copies.append((self.mine.at[piece], self.got.at[k], 2, self.peer(k)))
            if not self.reverse:
                copies.append((self.total, self.got_decay.at[k], 3, self.peer(k)))
        self.send(copies)
        self.got[0] = self.mine[pl.ds(pl.multiple_of(self.chip * self.rows, self.rows), self.rows), :]
        if not self.reverse:
            self.got_decay[0] = self.total[...]

    def scan(self):
        others = slice(1, self.chips)
        whole = [(self.got.at[others], self.got.at[others], 2)]
        if not self.reverse:
            whole.append((self.got_decay.at[others], self.got_decay.at[others], 3))
        self.arrive(*whole)
        chips, chip = self.chips, self.chip

        def one(i, carry):
            source = chips - 1 - i if self.reverse else i
            slot = lax.rem(chip - source + chips, chips)
            to = lax.rem(source - chip + chips, chips)
            self.back[pl.ds(to, 1)] = carry.astype(bf16)[None]
            return self.got_decay[pl.ds(slot, 1)][0, 0:1, :] * carry + self.got[pl.ds(slot, 1)][0].astype(f32)

        lax.fori_loop(0, chips, one, jnp.zeros((self.rows, self.width), f32))
        here = pl.ds(pl.multiple_of(chip * self.rows, self.rows), self.rows)
        self.send([(self.back.at[k], self.back_got.at[here], 4, self.peer(k)) for k in range(1, chips)])
        self.back_got[here, :] = self.back[0]

    def hand(self):
        self.arrive((self.back.at[1 : self.chips], self.back.at[1 : self.chips], 4))
        early, _, early_decay, _ = self.ordered()
        enter = self.back_got[...].astype(f32)
        second = early_decay * enter + early
        self.out[:, self.own_cols] = jnp.where(self.later, second, enter).astype(bf16)
        self.mine[...] = jnp.where(self.later, enter, second).astype(bf16)
        self.send([(self.mine, self.out.at[:, self.own_cols], 6, self.sibling)])

    def end(self):
        self.arrive((self.mine, self.mine, 6))


def exchange_scratch(chips, width):
    rows = STATE // chips
    states = [((STATE, width), f32), ((STATE, width), bf16), ((chips, rows, width), bf16)]
    states += [((chips, rows, width), bf16), ((STATE, width), bf16)]
    decays = [((8, width), f32), ((8, width), f32), ((chips, 8, width), f32)]
    return states, decays


ORDERS = (
    ("x", "z1", "y", "z2"),
    ("x", "y", "z2", "z1"),
    ("z1", "x", "y", "z2"),
    ("y", "x", "z1", "z2"),
    ("x", "z1", "y", "z2"),
    ("y", "x", "z1", "z2"),
    ("z1", "z2", "y", "x"),
    ("y", "x", "z2", "z1"),
    ("x", "y", "z1", "z2"),
    ("y", "x", "z1", "z2"),
    ("x", "y", "z2", "z1"),
    ("z1", "x", "y", "z2"),
    ("y", "x", "z1", "z2"),
    ("z1", "x", "y", "z2"),
    ("x", "y", "z2", "z1"),
)
SCHEDULE = {
    "g2": (
        2, 0,
    ),
    "o2": (
        0, 5, 2,
    ),
    "b0": (
        1,
    ),
    "b1": (
        5,
    ),
    "b2": (
        1, 4, 3,
    ),
    "s": (
        2, 5, 4,
    ),
    "e": (
        1, 2, 3, 0,
    ),
    "h": (
        1, 5,
    ),
    "c1": (
        2, 4, 0,
    ),
    "c3": (
        1, 5,
    ),
    "r1": (
        8, 7, 6, 0, 4,
    ),
    "v2": (
        3, 2,
    ),
    "v3": (
        6, 8, 1,
    ),
    "r2": (
        11, 9, 7, 2, 11, 5,
    ),
    "e1": (
        8, 3, 6, 9, 1, 0, 10, 7, 4, 11, 8,
    ),
    "e2": (
        10, 7, 2, 11,
    ),
    "r3": (
        12, 9, 1, 12, 11, 13, 7, 3, 0, 6, 10, 4, 14, 14,
    ),
    "z": (
        12, 6, 10, 7, 5, 11, 13, 14, 2, 9, 1, 8, 0, 12, 10, 11, 14, 4, 3, 6, 5, 10, 13, 9, 14, 12, 7, 6, 4,
        13, 8, 2, 10, 7, 14, 3, 13, 9, 12, 8, 6, 5, 10, 14, 11, 13, 0, 1, 3, 12, 4, 9, 13, 14, 8, 12, 11, 10,
        6, 9, 7, 13, 3, 14, 14, 11, 12, 10, 8, 0, 5, 13, 9, 6, 7, 8, 4, 13, 12, 3, 9,
    ),
}
STEPS = {"x": 1, "y": 2, "z1": 4, "z2": 8}
STAGES = 9


def bits_of():
    place = lax.axis_index("seq")
    return {
        "c": lax.axis_index("head"),
        "x": place % 2,
        "y": place // 2 % 2,
        "z1": place // 4 % 2,
        "z2": place // 8,
    }


def partner(d):
    place, core = lax.axis_index("seq"), lax.axis_index("head")
    if d == "c":
        return (place, 1 - core)
    return (place + STEPS[d] * (1 - 2 * bits_of()[d]), core)


class Sum:
    def __init__(self, held, got, out, ssem, rsem, lsem, orders):
        self.streams = [self.stream(held, got, out, ssem, rsem, lsem, s, order) for s, order in enumerate(orders)]
        self.stages = [-1] * len(orders)

    def stream(self, held, got, out, ssem, rsem, lsem, s, order):
        rows = held.shape[0]
        bits = bits_of()
        cols = slice(s * 256, (s + 1) * 256)
        order = ("c",) + order
        keeps, sends = [], []
        off, size = 0, rows
        for d in order[:4]:
            size //= 2
            keeps.append(off + bits[d] * size)
            sends.append(off + (1 - bits[d]) * size)
            off = keeps[-1]
        unit = rows // 16
        sizes = [rows // 2, rows // 4, rows // 8, unit, unit]
        slots = [0, rows // 2, rows // 2 + rows // 4, rows - 2 * unit, rows - unit]

        def at(start, size):
            return pl.ds(pl.multiple_of(start, 16), size)

        def copy(stage):
            if stage < 5:
                d = order[stage]
                where = at(sends[stage] if stage < 4 else off, sizes[stage])
                src, dst = held.at[where, cols], got.at[slice(slots[stage], slots[stage] + sizes[stage]), cols]
            else:
                d = order[8 - stage]
                where = at(keeps[8 - stage], sizes[8 - stage])
                src, dst = (held if stage == 5 else out).at[where, cols], out.at[where, cols]
            return remote(src, dst, ssem.at[s], rsem.at[s, stage], partner(d))

        def add(stage):
            where = keeps[stage] if stage < 4 else off

            @pl.loop(0, sizes[stage] // unit)
            def _(i):
                here = at(where + i * unit, unit)
                held[here, cols] = held[here, cols] + got[at(slots[stage] + i * unit, unit), cols]

        def place():
            return pltpu.make_async_copy(held.at[at(off, unit), cols], out.at[at(off, unit), cols], lsem.at[s])

        return copy, add, place

    def tick(self, s):
        copy, add, place = self.streams[s]
        stage = self.stages[s]
        if 0 <= stage < STAGES:
            copy(stage).wait()
            if stage < 5:
                add(stage)
        if stage == 4:
            place().start()
        if stage == 5:
            place().wait()
        if stage + 1 < STAGES:
            copy(stage + 1).start()
        self.stages[s] = stage + 1


def greet():
    place, core = lax.axis_index("seq"), lax.axis_index("head")
    pieces = lax.axis_size("seq")
    chips = pieces // SEQS
    barrier = pltpu.get_barrier_semaphore()
    peers = [partner(d) for d in ("c", "x", "y", "z1", "z2")]
    peers += [((place // SEQS + k) % chips * SEQS + place % SEQS, core) for k in range(1, chips)]
    peers += [block_at(1), block_at(-1)]
    for to in peers:
        pl.semaphore_signal(barrier, inc=1, device_id=to, device_id_type=MESH)
    return barrier, len(peers)


def block_at(ahead):
    place, core = lax.axis_index("seq"), lax.axis_index("head")
    pieces = lax.axis_size("seq")
    block = (place // SEQS * 2 + core + ahead + pieces) % pieces
    return (block // 2 * SEQS + place % SEQS, block % 2)


def whole_kernel(names, *refs):
    r = Refs(names, refs)
    rows = r.blk.shape[0]
    greeted = greet()
    loads = [
        pltpu.make_async_copy(r.w_in_hbm.at[INNER:], r.w_in.at[INNER:], r.load_sem.at[0]),
        pltpu.make_async_copy(r.w_in_hbm.at[:INNER], r.w_in.at[:INNER], r.load_sem.at[1]),
        pltpu.make_async_copy(r.w_out_hbm, r.w_out, r.load_sem.at[2]),
    ]
    for c in loads:
        c.start()
    r.gain[...] = r.norm_gain[...].reshape(1, D)
    r.conv_b[...] = r.conv_bias[...].reshape(1, XBC)
    r.gate_gain[...] = r.gated_gain[...].reshape(1, INNER)
    r.heads[...] = jnp.zeros((8, 128), f32)
    for k, one in enumerate((r.dt_bias, r.a_log, r.d_skip)):
        r.heads[k : k + 1, 0:HEADS] = one[...].reshape(1, HEADS)
    place, core = lax.axis_index("seq"), lax.axis_index("head")
    chips = lax.axis_size("seq") // SEQS
    block = place // SEQS * 2 + core

    def norm(v):
        v = v.astype(f32)
        scale = lax.rsqrt(jnp.mean(v * v, axis=-1, keepdims=True) + EPS)
        return (v * scale * r.gain[...]).astype(bf16)

    r.normed[...] = norm(r.blk[...])
    lane = iota((rows, 128), 1)
    keep = valid_rows(r.lengths, rows, 128)
    pick_lane = iota((128, 256), 1)
    pick_head = iota((128, 256), 0)
    left = one_hot(iota((1, 128), 1) < HEAD_DIM)
    right = one_hot(iota((1, 128), 1) >= HEAD_DIM)

    loads[0].wait()

    def project(i, carry):
        part = dot(r.normed[...], r.w_in[pl.ds(pl.multiple_of(INNER + i * 256, 256), 256), :], NT)
        r.pad[16:, lanes(i * 256, 256)] = part.astype(bf16).astype(f32)
        return carry

    lax.fori_loop(0, XBC // 256, project, 0, unroll=7)
    pl.semaphore_wait(*greeted)
    edge = remote(r.pad.at[rows + 8 :], r.pad.at[8:16], r.edge_sem.at[0], r.edge_sem.at[1], block_at(1))
    edge.start()

    r.head[3] = jnp.zeros((rows, 128), f32)
    r.head[3, :, 0:HEADS] = dot(r.normed[...], r.w_in[INNER + XBC :, :], NT).astype(bf16).astype(f32)
    moved = r.head[3] + r.heads[0:1, :]
    soft = jnp.maximum(moved, 0.0) + jnp.log1p(jnp.exp(-jnp.abs(moved)))
    dt = jnp.where(lane < HEADS, soft * keep, 0.0)
    rates = -jnp.exp(r.heads[1:2, :])
    below = one_hot(iota((rows, rows), 0) >= iota((rows, rows), 1))
    cum = split_dot_left(below, dt) * rates
    cum2 = cum * LOG2E
    r.head[0] = dt
    r.head[1] = cum
    r.head[2] = sigmoid(moved) * keep
    r.head[3] = cum2
    r.cumt[...] = cum2.T

    edge.wait()
    r.pad[8:16, :] = jnp.where(block == 0, 0.0, r.pad[8:16, :])

    def convolve(start, width):
        cols = lanes(start, width)
        running = r.conv_b[:, cols] + r.pad[13 : 13 + rows, cols] * r.conv_w[0:1, cols]
        for tap in range(1, CONV):
            running = running + r.pad[13 + tap : 13 + tap + rows, cols] * r.conv_w[tap : tap + 1, cols]
        r.run[:, cols] = running
        return running * sigmoid(running)

    act = convolve(INNER, 2 * STATE)
    r.b[...] = act[:, :STATE].astype(bf16)
    r.c[...] = act[:, STATE:].astype(bf16)
    third = 3 * 128

    def channels(start):
        def one(i, carry):
            at = start + i * 128
            cols = lanes(at, 128)
            pick = one_hot((iota((128, 128), 1) >> 6) + at // HEAD_DIM == iota((128, 128), 0))
            x = convolve(at, 128) * keep
            r.x[:, cols] = x
            xd = x * split_dot(r.head[0], pick)
            r.xd[:, cols] = xd.astype(bf16)
            wide = split_dot(r.head[3], pick)
            last = wide[rows - 1 : rows, :]
            xde = (xd * jnp.exp2(last - wide)).astype(bf16)
            r.xde[:, cols] = xde
            r.spread[0:8, cols] = jnp.broadcast_to(jnp.exp2(last), (8, 128))
            r.spread[8:16, cols] = split_dot(jnp.broadcast_to(r.heads[2:3, :], (8, 128)), pick)
            return carry

        lax.fori_loop(0, third // 128, one, 0, unroll=3)
        r.own[:, start : start + third] = dot(r.b[...], r.xde[:, start : start + third], TN)

    def exchanges(reverse, state, out, tag):
        made = []
        for k in range(SPLITS):
            bufs = [getattr(r, f"{tag}{k}_{n}") for n in range(5)]
            decays = [getattr(r, f"d{k}_{n}") for n in range(3)]
            sems = getattr(r, f"{tag}s").at[k], getattr(r, f"{tag}r").at[k]
            width = INNER // 2 // SPLITS
            made.append(Exchange(reverse, state, r.spread, out, bufs, decays, *sems, k * width, width))
        return made

    enters = exchanges(False, r.own, r.enter, "f")
    leaves = exchanges(True, r.adj, r.leave, "g")
    channels(0)
    channels(INNER // 2)
    enters[0].begin()
    channels(third)
    enters[0].deal()
    channels(INNER // 2 + third)
    enters[1].begin()

    def spread(i, carry):
        r.cumb[:, lanes(i * 256, 256)] = split_dot(r.head[3], one_hot((pick_lane >> 7) + 2 * i == pick_head))
        return carry

    lax.fori_loop(0, PAIRS, spread, 0, unroll=2)

    causal = iota((rows, rows), 0) >= iota((rows, rows), 1)
    r.scores[...] = jnp.where(causal, dot(r.c[...], r.b[...], NT), 0.0)
    loads[1].wait()
    enters[1].deal()

    def gates(i, carry):
        part = dot(r.normed[...], r.w_in[pl.ds(pl.multiple_of(i * 256, 256), 256), :], NT)
        r.gate[:, lanes(i * 256, 256)] = part.astype(bf16)
        return carry

    def columns(i):
        c0 = r.cumb[:, lanes(i * 256, 128)]
        c1 = r.cumb[:, lanes(i * 256 + 128, 128)]
        return c0, c1

    def pair(i, carry):
        cols = lanes(i * 128, 128)
        xd = r.xd[:, cols]
        y = None
        for cc, part, mask in zip(columns(i), (0, 1), (left, right), strict=True):
            row = r.cumt[pl.ds(2 * i + part, 1), :]
            decay = jnp.exp2(jnp.minimum(jnp.concatenate([cc] * (rows // 128), axis=1) - row, 0.0))
            term = dot((decay * r.scores[...]).astype(bf16), xd * mask)
            y = term if y is None else y + term
        r.y[:, cols] = y
        return carry

    lax.fori_loop(0, INNER // 256, gates, 0, unroll=2)
    lax.fori_loop(0, 4, pair, 0, unroll=2)
    enters[0].scan()
    lax.fori_loop(4, 8, pair, 0, unroll=2)
    enters[1].scan()
    lax.fori_loop(8, PAIRS, pair, 0, unroll=2)
    enters[0].hand()
    keep_d = valid_rows(r.lengths, rows, D)
    r.db[...] = (r.gout[...].astype(f32) * keep_d).astype(bf16)
    loads[2].wait()
    r.wide[...] = dot(r.db[...], r.w_out[...], NT)
    enters[1].hand()
    for one in enters:
        one.end()

    def carried(i, carry):
        cols = lanes(i * 128, 128)
        c0, c1 = columns(i)
        y = r.y[:, cols] + jnp.exp2(jnp.where(lane < HEAD_DIM, c0, c1)) * dot(r.c[...], r.enter[:, cols])
        r.y[:, cols] = y
        r.mixed[:, cols] = (y + r.spread[8:9, cols] * r.x[:, cols]).astype(bf16)
        return carry

    lax.fori_loop(0, PAIRS, carried, 0, unroll=2)

    r.ggain[...] = jnp.zeros_like(r.ggain)
    step = 32

    def gating(i, carry):
        at = pl.ds(pl.multiple_of(i * step, step), step)
        g = r.gate[at, :].astype(f32)
        sg = sigmoid(g)
        mixed = r.mixed[at, :].astype(f32)
        gated = mixed * g * sg
        scale = lax.rsqrt(jnp.mean(gated * gated, axis=-1, keepdims=True) + EPS)
        r.gn[at, :] = (gated * scale * r.gate_gain[...]).astype(bf16)
        dgn = r.wide[at, :]
        r.ggain[...] += jnp.sum((dgn * gated * scale).reshape(step // 8, 8, INNER), axis=0)
        weighted = dgn * r.gate_gain[...]
        average = jnp.mean(weighted * gated, axis=-1, keepdims=True)
        d_gated = scale * weighted - gated * (scale * scale * scale) * average
        r.dy[at, :] = (d_gated * g * sg).astype(bf16)
        r.dgate[at, :] = (d_gated * mixed * sg * (1.0 + g * (1.0 - sg))).astype(bf16)
        return carry

    lax.fori_loop(0, rows // step, gating, 0)

    def weigh(i, carry):
        cols = lanes(i * 128, 128)
        c0, c1 = columns(i)
        grow = jnp.exp2(jnp.where(lane < HEAD_DIM, c0, c1))
        r.dye[:, cols] = (r.dy[:, cols].astype(f32) * grow).astype(bf16)
        return carry

    lax.fori_loop(0, PAIRS, weigh, 0, unroll=2)
    r.adj[...] = dot(r.c[...], r.dye[...], TN)
    for one in leaves:
        one.begin()

    def gate_grads(i, carry):
        at = pl.ds(pl.multiple_of(i * 256, 256), 256)
        r.first[at, :] = dot(r.dgate[:, lanes(i * 256, 256)], r.normed[...], TN).astype(bf16)
        return carry

    def out_grads(i, carry):
        at = pl.ds(pl.multiple_of(INNER + i * 256, 256), 256)
        r.first[at, :] = dot(r.gn[:, lanes(i * 256, 256)], r.db[...], TN).astype(bf16)
        return carry

    def part(k, held, got, out, at):
        return Sum(held.at[at], got.at[at], out.at[at], r.ss.at[k], r.rs.at[k], r.ls.at[k], ORDERS[3 * k : 3 * k + 3])

    sums = [
        part(0, r.first, r.got_first, r.first_out, slice(0, INNER)),
        part(1, r.first, r.got_first, r.first_out, slice(INNER, FIRST_ROWS)),
        part(2, r.rest, r.got_rest, r.rest_out, slice(0, D)),
        part(3, r.rest, r.got_rest, r.rest_out, slice(D, INNER)),
        part(4, r.rest, r.got_rest, r.rest_out, slice(INNER, REST_ROWS)),
    ]
    def slot(name):
        for n in SCHEDULE.get(name, ()):
            sums[n // 3].tick(n % 3)

    lax.fori_loop(0, INNER // 256, gate_grads, 0, unroll=2)
    slot("g2")
    for one in leaves:
        one.deal()
    slot("d")
    lax.fori_loop(0, INNER // 256, out_grads, 0, unroll=2)
    slot("o2")
    r.block_out[...] = (r.blk[...].astype(f32) + keep_d * dot(r.gn[...], r.w_out[...])).astype(bf16)
    stores = [
        pltpu.make_async_copy(r.block_out, r.block_out_hbm, r.store_sem.at[0]),
        pltpu.make_async_copy(r.grad_in, r.grad_in_hbm, r.store_sem.at[1]),
    ]
    stores[0].start()
    slot("b0")

    r.scores_t[...] = jnp.where(
        iota((rows, rows), 1) >= iota((rows, rows), 0), dot(r.b[...], r.c[...], NT), 0.0
    )

    r.dscores[...] = jnp.zeros_like(r.dscores)
    r.q[...] = jnp.zeros_like(r.q)
    r.ry[...] = jnp.zeros_like(r.ry)
    row_head = iota((128, 128), 0)
    col_head = iota((128, 128), 1)

    def dsilu(cols):
        running = r.run[:, cols]
        sg = sigmoid(running)
        return sg * (1.0 + running * (1.0 - sg))

    def pair_back(i, carry):
        cols = lanes(i * 128, 128)
        xd, dy = r.xd[:, cols], r.dy[:, cols]
        v = None
        for cc, part, mask in zip(columns(i), (0, 1), (left, right), strict=True):
            row = r.cumt[pl.ds(2 * i + part, 1), :]
            decay = jnp.exp2(jnp.minimum(row - jnp.concatenate([cc] * (rows // 128), axis=1), 0.0))
            masked = dy * mask
            term = dot((decay * r.scores_t[...]).astype(bf16), masked)
            v = term if v is None else v + term
            r.dscores[...] += decay * dot(xd, masked, NT)
        r.wide[:, cols] = v
        r.ry[...] += split_dot(dy.astype(f32) * r.y[:, cols], one_hot((row_head >> 6) + 2 * i == col_head))
        return carry

    lax.fori_loop(0, 4, pair_back, 0, unroll=2)
    slot("b1")
    lax.fori_loop(4, 8, pair_back, 0, unroll=2)
    slot("b2")
    lax.fori_loop(8, PAIRS, pair_back, 0, unroll=2)
    slot("b3")
    for one in leaves:
        one.scan()
    slot("s")
    dsc = jnp.where(iota((rows, rows), 1) >= iota((rows, rows), 0), r.dscores[...], 0.0).astype(bf16)
    d_b = dot(dsc, r.c[...])
    d_c = dot(dsc, r.b[...], TN) + dot(r.dye[...], r.enter[...], NT)
    slot("e")
    for one in leaves:
        one.hand()
    slot("h")
    for one in leaves:
        one.end()
    slot("l")

    def channels_back(i, carry):
        cols = lanes(i * 128, 128)
        c0, c1 = columns(i)
        c01 = jnp.where(lane < HEAD_DIM, c0, c1)
        v = r.wide[:, cols] + jnp.exp2(c01[rows - 1 : rows, :] - c01) * dot(r.b[...], r.leave[:, cols])
        dtw = split_dot(r.head[0], one_hot((col_head >> 6) + 2 * i == row_head))
        x = r.x[:, cols]
        dy = r.dy[:, cols].astype(f32)
        r.q[...] += split_dot(x * v, one_hot((row_head >> 6) + 2 * i == col_head))
        r.skip[:, cols] = jnp.sum((dy * x).reshape(rows // 8, 8, 128), axis=0)
        r.ext[0:rows, cols] = (dtw * v + r.spread[8:9, cols] * dy) * keep * dsilu(cols)
        return carry

    def conv_back(i, carry):
        cols = lanes(i * 128, 128)
        drun = r.ext[0:rows, cols]
        total = drun * r.conv_w[CONV - 1 : CONV, cols]
        for tap in range(CONV - 1):
            ahead = CONV - 1 - tap
            total = total + r.ext[ahead : ahead + rows, cols] * r.conv_w[tap : tap + 1, cols]
        r.dproj[:, cols] = total.astype(bf16)
        for tap in range(CONV):
            r.tap_sums[tap : tap + 1, cols] = jnp.sum(
                drun * r.pad[13 + tap : 13 + tap + rows, cols], axis=0, keepdims=True
            )
        r.tap_sums[CONV : CONV + 1, cols] = jnp.sum(drun, axis=0, keepdims=True)
        return carry

    def rest_grads(i, carry):
        at = pl.ds(pl.multiple_of(i * 256, 256), 256)
        r.rest[at, :] = dot(r.dproj[:, lanes(i * 256, 256)], r.normed[...], TN).astype(bf16)
        return carry

    halves = (slice(0, INNER // 2), slice(INNER // 2, XBC))

    def edges(k):
        cols = halves[k]
        sems = r.edge_sem.at[2 + 2 * k], r.edge_sem.at[3 + 2 * k]
        return remote(r.ext.at[0:8, cols], r.edge_grad.at[:, cols], *sems, block_at(-1))

    def edge_in(k):
        edges(k).wait()
        r.ext[rows : rows + 8, halves[k]] = jnp.where(block == chips * 2 - 1, 0.0, r.edge_grad[:, halves[k]])

    lax.fori_loop(0, PAIRS // 2, channels_back, 0, unroll=2)
    edges(0).start()
    slot("c1")
    lax.fori_loop(PAIRS // 2, PAIRS, channels_back, 0, unroll=2)
    d_b = d_b + dot(r.xde[...], r.leave[...], NT)
    r.ext[0:rows, INNER : INNER + STATE] = d_b * dsilu(slice(INNER, INNER + STATE))
    r.ext[0:rows, INNER + STATE :] = d_c * dsilu(slice(INNER + STATE, XBC))
    edges(1).start()
    slot("c2")

    edge_in(0)
    slot("c3")
    lax.fori_loop(0, 6, conv_back, 0, unroll=2)
    slot("v1")
    lax.fori_loop(0, 3, rest_grads, 0, unroll=3)
    slot("r1")
    edge_in(1)
    slot("v2")
    lax.fori_loop(6, XBC // 128, conv_back, 0, unroll=2)
    slot("v3")
    lax.fori_loop(3, XBC // 256, rest_grads, 0, unroll=2)
    slot("r2")
    full_pick = one_hot((iota((INNER, 128), 0) >> 6) == iota((INNER, 128), 1))
    out_state = r.spread[0:1, :] * r.enter[...].astype(f32) + r.own[...]
    d_last = split_dot(
        jnp.sum((r.leave[...].astype(f32) * out_state).reshape(STATE // 8, 8, INNER), axis=0), full_pick
    )
    d_last = jnp.sum(d_last, axis=0, keepdims=True)
    q = r.q[...]
    d_cum = r.ry[...] - r.head[0] * q + jnp.where(iota((rows, 128), 0) == rows - 1, d_last, 0.0)
    above = one_hot(iota((rows, rows), 0) <= iota((rows, rows), 1))
    dz = (q + split_dot_left(above, d_cum * -jnp.exp(r.heads[1:2, :]))) * r.head[2]
    r.vec[...] = jnp.zeros_like(r.vec)
    r.vec[18:19, 0:128] = jnp.sum(dz, axis=0, keepdims=True)
    r.vec[19:20, 0:128] = jnp.sum(d_cum * r.head[1], axis=0, keepdims=True)
    r.vec[20:21, 0:128] = jnp.sum(split_dot(r.skip[...], full_pick), axis=0, keepdims=True)
    dz = dz.astype(bf16)
    slot("e1")
    d_normed = dot(r.dgate[...], r.w_in[:INNER, :])
    d_normed = d_normed + dot(dz[:, :HEADS], r.w_in[INNER + XBC :, :])
    d_normed = d_normed + dot(r.dproj[...], r.w_in[INNER : INNER + XBC, :])
    slot("e2")
    for v in range(CONV + 1):
        for part in range(3):
            width = min(D, XBC - part * D)
            r.vec[3 * v + part : 3 * v + part + 1, 0:width] = r.tap_sums[v : v + 1, part * D : part * D + width]
    src = r.blk[...].astype(f32)
    scale = lax.rsqrt(jnp.mean(src * src, axis=-1, keepdims=True) + EPS)
    r.vec[15:16, :] = jnp.sum(d_normed * src * scale, axis=0, keepdims=True)
    gate_gain = jnp.sum(r.ggain[...], axis=0, keepdims=True)
    r.vec[16:17, :] = gate_gain[:, :D]
    r.vec[17:18, :] = gate_gain[:, D:]
    r.rest[XBC:VEC_ROW, :] = dot(dz, r.normed[...], TN).astype(bf16)
    r.rest[VEC_ROW : VEC_ROW + 32, :] = r.vec[...].astype(bf16)
    r.rest[VEC_ROW + 32 :, :] = jnp.zeros((REST_ROWS - VEC_ROW - 32, D), bf16)
    slot("r3")
    weighted = d_normed * r.gain[...]
    average = jnp.mean(weighted * src, axis=-1, keepdims=True)
    r.grad_in[...] = r.gout[...].astype(f32) + scale * weighted - src * (scale * scale * scale) * average
    stores[1].start()
    slot("z")
    for c in stores:
        c.wait()


def whole(*args):
    t = args[0].shape[0]
    chips = lax.axis_size("seq") // SEQS
    ins = ["blk", "gout", "lengths", "norm_gain", "w_in_hbm", "conv_w", "conv_bias", "dt_bias", "a_log", "d_skip"]
    ins += ["gated_gain", "w_out_hbm"]
    outs = {
        "block_out_hbm": ((t, D), bf16),
        "grad_in_hbm": ((t, D), f32),
        "first_out": ((FIRST_ROWS, D), bf16),
        "rest_out": ((REST_ROWS, D), bf16),
    }
    held = {
        "block_out": ((t, D), bf16),
        "grad_in": ((t, D), f32),
        "first": ((FIRST_ROWS, D), bf16),
        "rest": ((REST_ROWS, D), bf16),
        "gain": ((1, D), f32),
        "conv_b": ((1, XBC), f32),
        "gate_gain": ((1, INNER), f32),
        "heads": ((8, 128), f32),
        "w_in": ((PROJ, D), bf16),
        "w_out": ((INNER, D), bf16),
        "edge_grad": ((8, XBC), f32),
        "normed": ((t, D), bf16),
        "gate": ((t, INNER), bf16),
        "pad": ((t + 16, XBC), f32),
        "run": ((t, XBC), f32),
        "x": ((t, INNER), f32),
        "xd": ((t, INNER), bf16),
        "xde": ((t, INNER), bf16),
        "b": ((t, STATE), bf16),
        "c": ((t, STATE), bf16),
        "head": ((4, t, 128), f32),
        "cumt": ((128, t), f32),
        "cumb": ((t, HEADS * 128), f32),
        "spread": ((16, INNER), f32),
        "own": ((STATE, INNER), f32),
        "enter": ((STATE, INNER), bf16),
        "y": ((t, INNER), f32),
        "mixed": ((t, INNER), bf16),
        "gn": ((t, INNER), bf16),
        "wide": ((t, INNER), f32),
        "db": ((t, D), bf16),
        "dy": ((t, INNER), bf16),
        "dye": ((t, INNER), bf16),
        "dgate": ((t, INNER), bf16),
        "ggain": ((8, INNER), f32),
        "adj": ((STATE, INNER), f32),
        "leave": ((STATE, INNER), bf16),
        "scores": ((t, t), f32),
        "scores_t": ((t, t), f32),
        "dscores": ((t, t), f32),
        "skip": ((8, INNER), f32),
        "q": ((t, 128), f32),
        "ry": ((t, 128), f32),
        "ext": ((t + 8, XBC), f32),
        "dproj": ((t, XBC), bf16),
        "vec": ((32, D), f32),
        "tap_sums": ((8, XBC), f32),
        "got_first": ((FIRST_ROWS, D), bf16),
        "got_rest": ((REST_ROWS, D), bf16),
    }
    names = ins + list(outs) + list(held)
    scratch = [pltpu.VMEM(s, d) for s, d in held.values()]
    states, decays = exchange_scratch(chips, INNER // 2 // SPLITS)
    for tag, shapes in (("f", states), ("g", states), ("d", decays)):
        for k in range(SPLITS):
            scratch += [pltpu.VMEM(s, d) for s, d in shapes]
            names += [f"{tag}{k}_{n}" for n in range(len(shapes))]
    semaphores = {
        "ss": (WAVES, 3),
        "rs": (WAVES, 3, STAGES),
        "ls": (WAVES, 3),
        "fs": (SPLITS, 2),
        "fr": (SPLITS, 7),
        "gs": (SPLITS, 2),
        "gr": (SPLITS, 7),
        "edge_sem": (6,),
        "load_sem": (3,),
        "store_sem": (2,),
    }
    for name, shape in semaphores.items():
        scratch.append(pltpu.SemaphoreType.DMA(shape))
        names.append(name)
    any_space = pl.BlockSpec(memory_space=pl.ANY)
    specs = {n: any_space for n in ("w_in_hbm", "w_out_hbm", *outs)} | {"lengths": SMEM}
    return pl.pallas_call(
        partial(whole_kernel, names),
        out_shape=[jax.ShapeDtypeStruct(s, d) for s, d in outs.values()],
        in_specs=[specs.get(n, VMEM) for n in ins],
        out_specs=[specs.get(n, VMEM) for n in outs],
        scratch_shapes=scratch,
        compiler_params=pltpu.CompilerParams(vmem_limit_bytes=60 << 20, collective_id=0, has_side_effects=True),
    )(*args)


def finish_kernel(
    block_in,
    grad_in,
    first,
    rest,
    block_out,
    grad_out,
    norm_out,
    w_in_out,
    conv_out,
    bias_out,
    dt_out,
    alog_out,
    skip_out,
    gate_out,
    w_out_out,
    held_first,
    held_rest,
    held_block,
    held_grad,
    wide_in,
    wide_out,
    in_sem,
    out_sem,
    pass_sem,
):
    passed = [
        (pltpu.make_async_copy(src, by, pass_sem.at[n, 0]), pltpu.make_async_copy(by, dst, pass_sem.at[n, 1]))
        for n, (src, by, dst) in enumerate(((block_in, held_block, block_out), (grad_in, held_grad, grad_out)))
    ]
    chunks = [(first, held_first, k * 256, 256) for k in range(FIRST_ROWS // 256)]
    chunks += [(rest, held_rest, k * 256, 256) for k in range(REST_ROWS // 256)]
    loads = [
        pltpu.make_async_copy(src.at[start : start + size], dst.at[start : start + size], in_sem.at[n])
        for n, (src, dst, start, size) in enumerate(chunks)
    ]
    ahead = 8
    for c in loads[:ahead] + [load for load, _ in passed]:
        c.start()
    stores = [store for _, store in passed]
    for n, (src, held, start, size) in enumerate(chunks):
        loads[n].wait()
        if n == ahead:
            for load, store in passed:
                load.wait()
                store.start()
        if n + ahead < len(loads):
            loads[n + ahead].start()
        if src is first and start >= INNER:
            wide, out, at = wide_out, w_out_out, start - INNER
        else:
            wide, out, at = wide_in, w_in_out, start if src is first else INNER + start
        kept = min(size, out.shape[0] - at)
        if kept <= 0:
            continue
        wide[at : at + kept, :] = held[start : start + kept, :].astype(f32)
        c = pltpu.make_async_copy(wide.at[at : at + kept], out.at[at : at + kept], out_sem.at[n])
        c.start()
        stores.append(c)
    vec = held_rest[VEC_ROW : VEC_ROW + 32, :].astype(f32)

    def row(v):
        return jnp.concatenate([vec[3 * v + k : 3 * v + k + 1, : min(D, XBC - k * D)] for k in range(3)], axis=1)

    for v in range(CONV):
        conv_out[v : v + 1, :] = row(v)
    bias_out[...] = row(CONV).reshape(XBC)
    norm_out[...] = vec[15:16, :].reshape(D)
    gate_out[...] = jnp.concatenate([vec[16:17, :], vec[17:18, :]], axis=1).reshape(INNER)
    for k, out in enumerate((dt_out, alog_out, skip_out)):
        out[...] = vec[18 + k : 19 + k, 0:HEADS].reshape(HEADS)
    for c in stores:
        c.wait()


def finish(block_out, grad_in, first, rest):
    shapes = [block_out.shape, grad_in.shape, (D,), (PROJ, D), (CONV, XBC), (XBC,), (HEADS,), (HEADS,), (HEADS,), (INNER,)]
    shapes += [(INNER, D)]
    any_space = pl.BlockSpec(memory_space=pltpu.HBM)
    away = (0, 1, 3, 10)
    chunks = (FIRST_ROWS + REST_ROWS) // 256
    return pl.pallas_call(
        finish_kernel,
        out_shape=[jax.ShapeDtypeStruct(s, bf16 if k == 0 else f32) for k, s in enumerate(shapes)],
        in_specs=[any_space] * 4,
        out_specs=[any_space if k in away else VMEM for k in range(len(shapes))],
        scratch_shapes=[
            pltpu.VMEM((FIRST_ROWS, D), bf16),
            pltpu.VMEM((REST_ROWS, D), bf16),
            pltpu.VMEM(block_out.shape, bf16),
            pltpu.VMEM(grad_in.shape, f32),
            pltpu.VMEM((PROJ, D), f32),
            pltpu.VMEM((INNER, D), f32),
            pltpu.SemaphoreType.DMA((chunks,)),
            pltpu.SemaphoreType.DMA((chunks,)),
            pltpu.SemaphoreType.DMA((2, 2)),
        ],
        compiler_params=pltpu.CompilerParams(vmem_limit_bytes=60 << 20),
    )(block_out, grad_in, first, rest)


def shifted(value, ahead):
    groups = lax.axis_size("head")
    count = lax.axis_size("seq") * groups
    moves = []
    for source in range(count):
        piece, half = source // groups, source % groups
        half += ahead
        if half == groups:
            half, piece = 0, piece + SEQS
        elif half < 0:
            half, piece = groups - 1, piece - SEQS
        if 0 <= piece * groups + half < count:
            moves.append((source, piece * groups + half))
    return lax.ppermute(value, ("seq", "head"), moves)


def by_parts(block_in, grad_out, lengths, norm_gain, w_in, conv_w, conv_b, dt_bias, a_log, d_skip, gate_gain, w_out):
    heads = jnp.pad(jnp.stack([dt_bias, a_log, d_skip]), ((0, 5), (0, 128 - HEADS)))
    gain, conv_b, gate_gain = norm_gain.reshape(1, D), conv_b.reshape(1, XBC), gate_gain.reshape(1, INNER)
    edge = shifted(block_in[-16:], 1)
    (normed, gate, pad, run, x, xd, xde, b, c, head, cumt, cumb, rows, own) = front(
        lengths, block_in, edge, gain, w_in, conv_w, conv_b, heads
    )
    enter = exchange_plain(own, rows[0:8], False)
    (y, block_out, dy, dye, dgate, ggain, adj, grads_a) = middle(
        lengths, block_in, grad_out, normed, gate, x, xd, b, c, cumt, cumb, rows, enter, gate_gain, w_out
    )
    leave = exchange_plain(adj, rows[0:8], True)
    drun, dz, small = back(
        lengths, y, dy, dye, x, xd, xde, b, c, run, cumt, cumb, head, rows, heads, enter, own, leave
    )
    edge_back = shifted(drun[0:8], -1)
    grad_in, grads_b = last(
        block_in, grad_out, normed, gain, w_in, conv_w, pad, drun, edge_back, dz, dgate, ggain, small
    )
    grads_a, grads_b = lax.psum((grads_a, grads_b), ("seq", "head"))
    return block_out, grad_in, grads_a, grads_b


def local(block_in, grad_out, lengths, norm_gain, w_in, *others):
    run = whole if lax.axis_size("seq") == 16 and lax.axis_size("head") == 2 else by_parts
    outs = finish(*run(block_in, grad_out, lengths, norm_gain, w_in.T, *others))
    return (*outs[:3], outs[3].T, *outs[4:])


def solution(mesh):
    rows = P(("seq", "head"), None)
    return jax.shard_map(
        local,
        mesh=mesh,
        in_specs=(rows, rows) + (P(),) * 10,
        out_specs=(rows, rows) + (P(),) * 9,
        check_vma=False,
    )
```

```python
from functools import partial

import jax
import jax.numpy as jnp
from jax import lax
from jax.experimental import pallas as pl
from jax.experimental.pallas import tpu as pltpu
from jax.sharding import PartitionSpec as P

D = 768
INNER = 1536
HEADS = 24
HEAD_DIM = 64
STATE = 128
CONV = 4
SEQS = 2
XBC = INNER + 2 * STATE
PROJ = 2 * INNER + 2 * STATE + HEADS
PAIRS = HEADS // 2
EPS = 1e-05
LOG2E = 1.4426950408889634

f32 = jnp.float32
bf16 = jnp.bfloat16
MESH = pl.DeviceIdType.MESH
VMEM = pl.BlockSpec(memory_space=pltpu.VMEM)
SMEM = pl.BlockSpec(memory_space=pltpu.SMEM)
NN = ((1,), (0,))
NT = ((1,), (1,))
TN = ((0,), (0,))


def dot(a, b, dims=NN):
    return lax.dot_general(a, b, (dims, ((), ())), preferred_element_type=f32)


def split_dot(a, pick, terms=3):
    total = None
    for _ in range(terms):
        part = a.astype(bf16)
        a = a - part.astype(f32)
        term = dot(part, pick)
        total = term if total is None else total + term
    return total


def split_dot_left(pick, a, terms=3):
    total = None
    for _ in range(terms):
        part = a.astype(bf16)
        a = a - part.astype(f32)
        term = dot(pick, part)
        total = term if total is None else total + term
    return total


def iota(shape, dim):
    return lax.broadcasted_iota(jnp.int32, shape, dim)


def one_hot(cond):
    return jnp.where(cond, 1.0, 0.0).astype(bf16)


def sigmoid(v):
    return 1.0 / (1.0 + jnp.exp(-v))


def lanes(start, size):
    return pl.ds(pl.multiple_of(start, 128), size)


def valid_rows(lengths_ref, rows, width):
    place = lax.axis_index("seq")
    first = (place // SEQS) * (rows * lax.axis_size("head")) + lax.axis_index("head") * rows
    limit = lengths_ref[place % SEQS]
    return jnp.where(iota((rows, width), 0) + first < limit, 1.0, 0.0)


def call(body, outs, args, scratch=(), smem=(), vmem=56 << 20, cost=None, **params):
    return pl.pallas_call(
        body,
        out_shape=[jax.ShapeDtypeStruct(s, d) for s, d in outs],
        in_specs=[SMEM if i in smem else VMEM for i in range(len(args))],
        out_specs=[VMEM] * len(outs),
        scratch_shapes=list(scratch),
        compiler_params=pltpu.CompilerParams(vmem_limit_bytes=vmem, **params),
    )(*args)


REST_ROWS = XBC
VEC_ROWS = 48
FIRST_ROWS = 2 * INNER
WAVES = 4
SPLITS = 2


def front_kernel(
    lengths_ref,
    blk,
    edge,
    gain,
    w_in,
    conv_w,
    conv_b,
    heads_ref,
    normed_out,
    gate_out,
    pad_out,
    run_out,
    x_out,
    xd_out,
    xde_out,
    b_out,
    c_out,
    head_out,
    cumt_out,
    cumb_out,
    rows_out,
    state_out,
):
    rows = blk.shape[0]

    def norm(v):
        v = v.astype(f32)
        scale = lax.rsqrt(jnp.mean(v * v, axis=-1, keepdims=True) + EPS)
        return (v * scale * gain[...]).astype(bf16)

    normed = norm(blk[...])
    normed_out[...] = normed
    gate_out[...] = dot(normed, w_in[:INNER, :], NT).astype(bf16)
    ahead = norm(edge[...])
    pad_out[0:16, :] = dot(ahead, w_in[INNER : INNER + XBC, :], NT).astype(bf16).astype(f32)
    pad_out[16 : 16 + rows, :] = dot(normed, w_in[INNER : INNER + XBC, :], NT).astype(bf16).astype(f32)
    keep = valid_rows(lengths_ref, rows, 128)
    head_out[3] = jnp.zeros((rows, 128), f32)
    head_out[3, :, 0:HEADS] = dot(normed, w_in[INNER + XBC :, :], NT).astype(bf16).astype(f32)
    lane = iota((rows, 128), 1)
    shifted = head_out[3] + heads_ref[0:1, :]
    soft = jnp.maximum(shifted, 0.0) + jnp.log1p(jnp.exp(-jnp.abs(shifted)))
    dt = jnp.where(lane < HEADS, soft * keep, 0.0)
    rates = -jnp.exp(heads_ref[1:2, :])
    below = one_hot(iota((rows, rows), 0) >= iota((rows, rows), 1))
    cum = split_dot_left(below, dt) * rates
    cum2 = cum * LOG2E
    head_out[0] = dt
    head_out[1] = cum
    head_out[2] = sigmoid(shifted) * keep
    head_out[3] = cum2
    cumt_out[...] = cum2.T
    pick_lane = iota((128, 256), 1)
    pick_head = iota((128, 256), 0)

    def spread(i, carry):
        cumb_out[:, lanes(i * 256, 256)] = split_dot(
            head_out[3], one_hot((pick_lane >> 7) + 2 * i == pick_head)
        )
        return carry

    lax.fori_loop(0, PAIRS, spread, 0)

    def convolve(i):
        cols = lanes(i * 256, 256)
        running = conv_b[:, cols] + pad_out[13 : 13 + rows, cols] * conv_w[0:1, cols]
        for tap in range(1, CONV):
            running = running + pad_out[13 + tap : 13 + tap + rows, cols] * conv_w[tap : tap + 1, cols]
        run_out[:, cols] = running
        return running * sigmoid(running)

    act = convolve(INNER // 256)
    b_out[...] = act[:, :STATE].astype(bf16)
    c_out[...] = act[:, STATE:].astype(bf16)
    keep2 = valid_rows(lengths_ref, rows, 256)

    def channels(i, carry):
        cols = lanes(i * 256, 256)
        pick = one_hot((pick_lane >> 6) + 4 * i == pick_head)
        x = convolve(i) * keep2
        x_out[:, cols] = x
        xd = x * split_dot(head_out[0], pick)
        xd_out[:, cols] = xd.astype(bf16)
        wide = split_dot(head_out[3], pick)
        last = wide[rows - 1 : rows, :]
        xde_out[:, cols] = (xd * jnp.exp2(last - wide)).astype(bf16)
        rows_out[0:8, cols] = jnp.broadcast_to(jnp.exp2(last), (8, 256))
        rows_out[8:16, cols] = split_dot(jnp.broadcast_to(heads_ref[2:3, :], (8, 128)), pick)
        return carry

    lax.fori_loop(0, INNER // 256, channels, 0)
    state_out[...] = dot(b_out[...], xde_out[...], TN)


def front(lengths, blk, edge, gain, w_in, conv_w, conv_b, heads):
    t = blk.shape[0]
    outs = [
        ((t, D), bf16),
        ((t, INNER), bf16),
        ((t + 16, XBC), f32),
        ((t, XBC), f32),
        ((t, INNER), f32),
        ((t, INNER), bf16),
        ((t, INNER), bf16),
        ((t, STATE), bf16),
        ((t, STATE), bf16),
        ((4, t, 128), f32),
        ((128, t), f32),
        ((t, HEADS * 128), f32),
        ((16, INNER), f32),
        ((STATE, INNER), f32),
    ]
    return call(front_kernel, outs, (lengths, blk, edge, gain, w_in, conv_w, conv_b, heads), smem=(0,))


def exchange_plain(state, decay, reverse):
    groups = lax.axis_size("head")
    count = lax.axis_size("seq") * groups
    place = lax.axis_index("seq")
    states = lax.all_gather(state.astype(bf16), ("seq", "head"), axis=0)
    decays = lax.all_gather(decay[0:1], ("seq", "head"), axis=0)
    blocks = count // SEQS
    block = place // SEQS * groups + lax.axis_index("head")

    def one(i, carry):
        source = blocks - 1 - i if reverse else i
        index = (source // groups * SEQS + place % SEQS) * groups + source % groups
        new = lax.dynamic_index_in_dim(decays, index, 0, False) * carry
        return new + lax.dynamic_index_in_dim(states, index, 0, False).astype(f32)

    ahead = blocks - 1 - block if reverse else block
    return lax.fori_loop(0, ahead, one, jnp.zeros(state.shape, f32)).astype(bf16)


def middle_kernel(
    lengths_ref,
    blk,
    gout,
    normed,
    gate,
    x_in,
    xd_in,
    b_in,
    c_in,
    cumt,
    cumb,
    rows_in,
    enter,
    gain,
    w_out,
    y_out,
    block_out,
    dy_out,
    dye_out,
    dgate_out,
    ggain_out,
    adj_out,
    grads_out,
    scores,
    mixed,
    gated_s,
    gn_s,
    scale_s,
    dgn_s,
    db_s,
):
    rows = blk.shape[0]
    causal = iota((rows, rows), 0) >= iota((rows, rows), 1)
    scores[...] = jnp.where(causal, dot(c_in[...], b_in[...], NT), 0.0)
    lane = iota((rows, 128), 1)
    left = one_hot(iota((1, 128), 1) < HEAD_DIM)
    right = one_hot(iota((1, 128), 1) >= HEAD_DIM)

    def pair(i, carry):
        cols = lanes(i * 128, 128)
        c0 = cumb[:, lanes(i * 256, 128)]
        c1 = cumb[:, lanes(i * 256 + 128, 128)]
        xd = xd_in[:, cols]
        y = None
        for cc, part, mask in ((c0, 0, left), (c1, 1, right)):
            row = cumt[pl.ds(2 * i + part, 1), :]
            decay = jnp.exp2(jnp.minimum(jnp.concatenate([cc] * (rows // 128), axis=1) - row, 0.0))
            term = dot((decay * scores[...]).astype(bf16), xd * mask)
            y = term if y is None else y + term
        grow = jnp.exp2(jnp.where(lane < HEAD_DIM, c0, c1))
        y = y + grow * dot(c_in[...], enter[:, cols])
        y_out[:, cols] = y
        mixed[:, cols] = (y + rows_in[8:9, cols] * x_in[:, cols]).astype(bf16).astype(f32)
        return carry

    lax.fori_loop(0, PAIRS, pair, 0)
    step = 32

    def gating(i, carry):
        r = pl.ds(pl.multiple_of(i * step, step), step)
        g = gate[r, :].astype(f32)
        gated = mixed[r, :] * g * sigmoid(g)
        scale = lax.rsqrt(jnp.mean(gated * gated, axis=-1, keepdims=True) + EPS)
        gated_s[r, :] = gated
        scale_s[r, :] = jnp.broadcast_to(scale, (step, 128))
        gn_s[r, :] = (gated * scale * gain[...]).astype(bf16)
        return carry

    lax.fori_loop(0, rows // step, gating, 0)
    keep = valid_rows(lengths_ref, rows, D)
    db_s[...] = (gout[...].astype(f32) * keep).astype(bf16)
    dgn_s[...] = dot(db_s[...], w_out[...], NT)
    block_out[...] = (blk[...].astype(f32) + keep * dot(gn_s[...], w_out[...])).astype(bf16)
    ggain_out[...] = jnp.zeros_like(ggain_out)

    def ungating(i, carry):
        r = pl.ds(pl.multiple_of(i * step, step), step)
        g = gate[r, :].astype(f32)
        sg = sigmoid(g)
        gated = gated_s[r, :]
        scale = scale_s[r, 0:1]
        dgn = dgn_s[r, :]
        ggain_out[...] += jnp.sum((dgn * gated * scale).reshape(step // 8, 8, INNER), axis=0)
        weighted = dgn * gain[...]
        average = jnp.mean(weighted * gated, axis=-1, keepdims=True)
        d_gated = scale * weighted - gated * (scale * scale * scale) * average
        dy_out[r, :] = (d_gated * g * sg).astype(bf16)
        dgate_out[r, :] = (d_gated * mixed[r, :] * sg * (1.0 + g * (1.0 - sg))).astype(bf16)
        return carry

    lax.fori_loop(0, rows // step, ungating, 0)

    def weigh(i, carry):
        cols = lanes(i * 128, 128)
        grow = jnp.exp2(jnp.where(lane < HEAD_DIM, cumb[:, lanes(i * 256, 128)], cumb[:, lanes(i * 256 + 128, 128)]))
        dye_out[:, cols] = (dy_out[:, cols].astype(f32) * grow).astype(bf16)
        return carry

    lax.fori_loop(0, PAIRS, weigh, 0)
    adj_out[...] = dot(c_in[...], dye_out[...], TN)
    grads_out[:INNER, :] = dot(dgate_out[...], normed[...], TN).astype(bf16)
    grads_out[INNER:, :] = dot(gn_s[...], db_s[...], TN).astype(bf16)


def middle(lengths, blk, gout, normed, gate, x, xd, b, c, cumt, cumb, rows_in, enter, gain, w_out):
    t = blk.shape[0]
    outs = [
        ((t, INNER), f32),
        ((t, D), bf16),
        ((t, INNER), bf16),
        ((t, INNER), bf16),
        ((t, INNER), bf16),
        ((8, INNER), f32),
        ((STATE, INNER), f32),
        ((2 * INNER, D), bf16),
    ]
    scratch = [
        pltpu.VMEM((t, t), f32),
        pltpu.VMEM((t, INNER), f32),
        pltpu.VMEM((t, INNER), f32),
        pltpu.VMEM((t, INNER), bf16),
        pltpu.VMEM((t, 128), f32),
        pltpu.VMEM((t, INNER), f32),
        pltpu.VMEM((t, D), bf16),
    ]
    args = (lengths, blk, gout, normed, gate, x, xd, b, c, cumt, cumb, rows_in, enter, gain, w_out)
    return call(middle_kernel, outs, args, scratch, smem=(0,))


def back_kernel(
    lengths_ref,
    y_in,
    dy_in,
    dye_in,
    x_in,
    xd_in,
    xde_in,
    b_in,
    c_in,
    run_in,
    cumt,
    cumb,
    head_in,
    rows_in,
    heads_ref,
    enter,
    own,
    leave,
    drun_out,
    dz_out,
    small_out,
    scores,
    dscores,
    skip_s,
    q_s,
    ry_s,
):
    rows = y_in.shape[0]
    causal = iota((rows, rows), 1) >= iota((rows, rows), 0)
    scores[...] = jnp.where(causal, dot(b_in[...], c_in[...], NT), 0.0)
    dscores[...] = jnp.zeros_like(dscores)
    q_s[...] = jnp.zeros_like(q_s)
    ry_s[...] = jnp.zeros_like(ry_s)
    lane = iota((rows, 128), 1)
    keep = valid_rows(lengths_ref, rows, 128)
    left = one_hot(iota((1, 128), 1) < HEAD_DIM)
    right = one_hot(iota((1, 128), 1) >= HEAD_DIM)
    pick_lane = iota((128, 128), 0)
    pick_head = iota((128, 128), 1)

    def dsilu(cols):
        running = run_in[:, cols]
        sg = sigmoid(running)
        return sg * (1.0 + running * (1.0 - sg))

    def pair(i, carry):
        cols = lanes(i * 128, 128)
        c0 = cumb[:, lanes(i * 256, 128)]
        c1 = cumb[:, lanes(i * 256 + 128, 128)]
        xd = xd_in[:, cols]
        dy = dy_in[:, cols]
        v = None
        for cc, part, mask in ((c0, 0, left), (c1, 1, right)):
            row = cumt[pl.ds(2 * i + part, 1), :]
            decay = jnp.exp2(jnp.minimum(row - jnp.concatenate([cc] * (rows // 128), axis=1), 0.0))
            masked = dy * mask
            term = dot((decay * scores[...]).astype(bf16), masked)
            v = term if v is None else v + term
            dscores[...] += decay * dot(xd, masked, NT)
        c01 = jnp.where(lane < HEAD_DIM, c0, c1)
        v = v + jnp.exp2(c01[rows - 1 : rows, :] - c01) * dot(b_in[...], leave[:, cols])
        pick = one_hot((pick_lane >> 6) + 2 * i == pick_head)
        dtw = split_dot(head_in[0], one_hot((pick_head >> 6) + 2 * i == pick_lane))
        x = x_in[:, cols]
        dyf = dy.astype(f32)
        q_s[...] += split_dot(x * v, pick)
        ry_s[...] += split_dot(dyf * y_in[:, cols], pick)
        skip_s[:, cols] = jnp.sum((dyf * x).reshape(rows // 8, 8, 128), axis=0)
        dx = dtw * v + rows_in[8:9, cols] * dyf
        drun_out[:, cols] = dx * keep * dsilu(cols)
        return carry

    lax.fori_loop(0, PAIRS, pair, 0)
    dsc = jnp.where(causal, dscores[...], 0.0).astype(bf16)
    d_b = dot(dsc, c_in[...]) + dot(xde_in[...], leave[...], NT)
    d_c = dot(dsc, b_in[...], TN) + dot(dye_in[...], enter[...], NT)
    drun_out[:, INNER : INNER + STATE] = d_b * dsilu(slice(INNER, INNER + STATE))
    drun_out[:, INNER + STATE :] = d_c * dsilu(slice(INNER + STATE, XBC))
    full_pick = one_hot((iota((INNER, 128), 0) >> 6) == iota((INNER, 128), 1))
    out_state = rows_in[0:1, :] * enter[...].astype(f32) + own[...]
    d_last = split_dot(
        jnp.sum((leave[...].astype(f32) * out_state).reshape(STATE // 8, 8, INNER), axis=0), full_pick
    )
    d_last = jnp.sum(d_last, axis=0, keepdims=True)
    dt = head_in[0]
    q = q_s[...]
    d_cum = ry_s[...] - dt * q + jnp.where(iota((rows, 128), 0) == rows - 1, d_last, 0.0)
    rates = -jnp.exp(heads_ref[1:2, :])
    above = one_hot(iota((rows, rows), 0) <= iota((rows, rows), 1))
    d_dt = q + split_dot_left(above, d_cum * rates)
    dz = d_dt * head_in[2]
    dz_out[...] = dz
    small_out[0:1, :] = jnp.sum(dz, axis=0, keepdims=True)
    small_out[1:2, :] = jnp.sum(d_cum * head_in[1], axis=0, keepdims=True)
    small_out[2:3, :] = jnp.sum(split_dot(skip_s[...], full_pick), axis=0, keepdims=True)
    small_out[3:8, :] = jnp.zeros((5, 128), f32)


def back(lengths, y, dy, dye, x, xd, xde, b, c, run, cumt, cumb, head, rows_in, heads, enter, own, leave):
    t = y.shape[0]
    outs = [((t, XBC), f32), ((t, 128), f32), ((8, 128), f32)]
    scratch = [
        pltpu.VMEM((t, t), f32),
        pltpu.VMEM((t, t), f32),
        pltpu.VMEM((8, INNER), f32),
        pltpu.VMEM((t, 128), f32),
        pltpu.VMEM((t, 128), f32),
    ]
    args = (lengths, y, dy, dye, x, xd, xde, b, c, run, cumt, cumb, head, rows_in, heads, enter, own, leave)
    return call(back_kernel, outs, args, scratch, smem=(0,))


def last_kernel(
    blk,
    gout,
    normed,
    gain,
    w_in,
    conv_w,
    pad_in,
    drun_in,
    edge,
    dz_in,
    dgate,
    ggain,
    small_in,
    gin_out,
    grads_out,
    vec_out,
    ext,
    dproj,
    sums,
):
    rows = blk.shape[0]
    ext[0:rows, :] = drun_in[...]
    ext[rows : rows + 8, :] = edge[...]
    vec_out[...] = jnp.zeros_like(vec_out)

    def channels(i, carry):
        cols = lanes(i * 128, 128)
        drun = ext[0:rows, cols]
        total = drun * conv_w[CONV - 1 : CONV, cols]
        for tap in range(CONV - 1):
            ahead = CONV - 1 - tap
            total = total + ext[ahead : ahead + rows, cols] * conv_w[tap : tap + 1, cols]
        dproj[:, cols] = total.astype(bf16)
        for tap in range(CONV):
            sums[tap : tap + 1, cols] = jnp.sum(
                drun * pad_in[13 + tap : 13 + tap + rows, cols], axis=0, keepdims=True
            )
        sums[CONV : CONV + 1, cols] = jnp.sum(drun, axis=0, keepdims=True)
        return carry

    lax.fori_loop(0, XBC // 128, channels, 0)
    for v in range(CONV + 1):
        for part in range(3):
            width = min(D, XBC - part * D)
            vec_out[HEADS + 3 * v + part : HEADS + 3 * v + part + 1, 0:width] = sums[v : v + 1, part * D : part * D + width]
    dz = dz_in[...].astype(bf16)
    d_normed = dot(dgate[...], w_in[:INNER, :])
    d_normed = d_normed + dot(dproj[...], w_in[INNER : INNER + XBC, :])
    d_normed = d_normed + dot(dz[:, :HEADS], w_in[INNER + XBC :, :])
    src = blk[...].astype(f32)
    scale = lax.rsqrt(jnp.mean(src * src, axis=-1, keepdims=True) + EPS)
    vec_out[39:40, :] = jnp.sum(d_normed * src * scale, axis=0, keepdims=True)
    gate_gain = jnp.sum(ggain[...], axis=0, keepdims=True)
    vec_out[40:41, :] = gate_gain[:, :D]
    vec_out[41:42, :] = gate_gain[:, D:]
    vec_out[42:45, 0:128] = small_in[0:3, :]
    weighted = d_normed * gain[...]
    average = jnp.mean(weighted * src, axis=-1, keepdims=True)
    gin_out[...] = gout[...].astype(f32) + scale * weighted - src * (scale * scale * scale) * average
    grads_out[...] = dot(dproj[...], normed[...], TN).astype(bf16)
    vec_out[0:HEADS, :] = dot(dz, normed[...], TN)[0:HEADS, :]


def last(blk, gout, normed, gain, w_in, conv_w, pad, drun, edge, dz, dgate, ggain, small):
    t = blk.shape[0]
    outs = [((t, D), f32), ((REST_ROWS, D), bf16), ((VEC_ROWS, D), f32)]
    scratch = [pltpu.VMEM((t + 8, XBC), f32), pltpu.VMEM((t, XBC), bf16), pltpu.VMEM((8, XBC), f32)]
    args = (blk, gout, normed, gain, w_in, conv_w, pad, drun, edge, dz, dgate, ggain, small)
    return call(last_kernel, outs, args, scratch)


class Refs:
    def __init__(self, names, refs):
        self.__dict__.update(zip(names, refs, strict=True))


def remote(src, dst, ssem, rsem, to):
    return pltpu.make_async_remote_copy(
        src_ref=src, dst_ref=dst, send_sem=ssem, recv_sem=rsem, device_id=to, device_id_type=MESH
    )


class Exchange:
    def __init__(self, reverse, state, decay, out, bufs, decays, ssem, rsem, start, width):
        self.sib_state, self.mine, self.got, self.back, self.back_got = bufs
        self.sib_decay, self.total, self.got_decay = decays
        self.state, self.decay, self.out, self.reverse = state, decay, out, reverse
        self.ssem, self.rsem = ssem, rsem
        self.chips = lax.axis_size("seq") // SEQS
        self.rows = STATE // self.chips
        self.width = width
        place, core = lax.axis_index("seq"), lax.axis_index("head")
        self.core = core
        self.chip, self.which = place // SEQS, place % SEQS
        self.sibling = (place, 1 - core)
        self.later = (1 - core if reverse else core) == 1
        self.own_cols = lanes(core * (INNER // 2) + start, width)
        self.sib_cols = lanes((1 - core) * (INNER // 2) + start, width)

    def peer(self, k):
        return (lax.rem(self.chip + k, self.chips) * SEQS + self.which, self.core)

    def send(self, copies):
        for src, dst, n, to in copies:
            remote(src, dst, self.ssem.at[n % 2], self.rsem.at[n], to).start()

    def arrive(self, *whole):
        for src, dst, n in whole:
            remote(src, dst, self.ssem.at[n % 2], self.rsem.at[n], self.sibling).wait()

    def begin(self):
        copies = [(self.state.at[:, self.sib_cols], self.sib_state, 0, self.sibling)]
        if not self.reverse:
            copies.append((self.decay.at[0:8, self.sib_cols], self.sib_decay, 1, self.sibling))
        self.send(copies)

    def ordered(self):
        own, other = self.state[:, self.own_cols], self.sib_state[...]
        own_decay, other_decay = self.decay[0:1, self.own_cols], self.sib_decay[0:1, :]
        later = self.later
        return (
            jnp.where(later, other, own),
            jnp.where(later, own, other),
            jnp.where(later, other_decay, own_decay),
            jnp.where(later, own_decay, other_decay),
        )

    def deal(self):
        whole = [(self.state.at[:, self.sib_cols], self.sib_state, 0)]
        if not self.reverse:
            whole.append((self.decay.at[0:8, self.sib_cols], self.sib_decay, 1))
        self.arrive(*whole)
        early, late, early_decay, late_decay = self.ordered()
        self.mine[...] = (late_decay * early + late).astype(bf16)
        if not self.reverse:
            self.total[...] = jnp.broadcast_to(early_decay * late_decay, self.total.shape)
        copies = []
        for k in range(1, self.chips):
            to = lax.rem(self.chip + k, self.chips)
            piece = pl.ds(pl.multiple_of(to * self.rows, self.rows), self.rows)
            copies.append((self.mine.at[piece], self.got.at[k], 2, self.peer(k)))
            if not self.reverse:
                copies.append((self.total, self.got_decay.at[k], 3, self.peer(k)))
        self.send(copies)
        self.got[0] = self.mine[pl.ds(pl.multiple_of(self.chip * self.rows, self.rows), self.rows), :]
        if not self.reverse:
            self.got_decay[0] = self.total[...]

    def scan(self):
        others = slice(1, self.chips)
        whole = [(self.got.at[others], self.got.at[others], 2)]
        if not self.reverse:
            whole.append((self.got_decay.at[others], self.got_decay.at[others], 3))
        self.arrive(*whole)
        chips, chip = self.chips, self.chip

        def one(i, carry):
            source = chips - 1 - i if self.reverse else i
            slot = lax.rem(chip - source + chips, chips)
            to = lax.rem(source - chip + chips, chips)
            self.back[pl.ds(to, 1)] = carry.astype(bf16)[None]
            return self.got_decay[pl.ds(slot, 1)][0, 0:1, :] * carry + self.got[pl.ds(slot, 1)][0].astype(f32)

        lax.fori_loop(0, chips, one, jnp.zeros((self.rows, self.width), f32))
        here = pl.ds(pl.multiple_of(chip * self.rows, self.rows), self.rows)
        self.send([(self.back.at[k], self.back_got.at[here], 4, self.peer(k)) for k in range(1, chips)])
        self.back_got[here, :] = self.back[0]

    def hand(self):
        self.arrive((self.back.at[1 : self.chips], self.back.at[1 : self.chips], 4))
        early, _, early_decay, _ = self.ordered()
        enter = self.back_got[...].astype(f32)
        second = early_decay * enter + early
        self.out[:, self.own_cols] = jnp.where(self.later, second, enter).astype(bf16)
        self.mine[...] = jnp.where(self.later, enter, second).astype(bf16)
        self.send([(self.mine, self.out.at[:, self.own_cols], 6, self.sibling)])

    def end(self):
        self.arrive((self.mine, self.mine, 6))


def exchange_scratch(chips, width):
    rows = STATE // chips
    states = [((STATE, width), f32), ((STATE, width), bf16), ((chips, rows, width), bf16)]
    states += [((chips, rows, width), bf16), ((STATE, width), bf16)]
    decays = [((8, width), f32), ((8, width), f32), ((chips, 8, width), f32)]
    return states, decays


ORDERS = (
    ("x", "y", "z1", "z2"),
    ("z1", "y", "x", "z2"),
    ("x", "z1", "y", "z2"),
    ("x", "y", "z2", "z1"),
    ("x", "y", "z1", "z2"),
    ("y", "x", "z2", "z1"),
    ("z1", "y", "x", "z2"),
    ("y", "x", "z1", "z2"),
    ("x", "y", "z1", "z2"),
    ("z1", "y", "x", "z2"),
    ("y", "z1", "x", "z2"),
    ("x", "y", "z1", "z2"),
    ("y", "z1", "z2", "x"),
    ("x", "z2", "y", "z1"),
    ("y", "z2", "x", "z1"),
)
SCHEDULE = {
    "g2": (
        2, 1,
    ),
    "o2": (
        2, 5,
    ),
    "b1": (
        1, 5, 0,
    ),
    "b2": (
        3,
    ),
    "b3": (
        4, 0,
    ),
    "s": (
        2,
    ),
    "e": (
        5, 1, 3, 0,
    ),
    "h": (
        4, 2,
    ),
    "c1": (
        5, 1, 0,
    ),
    "c2": (
        2, 3,
    ),
    "r1": (
        6, 8, 1, 5, 7, 4, 8, 7, 0,
    ),
    "v2": (
        2, 6,
    ),
    "v3": (
        5,
    ),
    "r2": (
        9, 1, 11, 4, 10, 9, 11, 8, 6, 7, 2, 10, 3, 6, 8, 9, 7, 0, 11, 1, 5, 4, 10,
    ),
    "e1": (
        2, 7,
    ),
    "e2": (
        0, 11, 6, 3, 9, 10, 8, 5, 4,
    ),
    "r3": (
        11, 7, 0, 12, 2, 6, 3, 4, 13,
    ),
    "z": (
        14, 8, 10, 12, 9, 1, 13, 7, 14, 11, 4, 3, 10, 12, 6, 2, 13, 14, 9, 7, 5, 8, 3, 0, 11, 1, 10, 6, 9, 8,
        0, 13, 12, 7, 4, 14, 10, 11, 9, 3, 13, 3, 5, 14, 12, 8, 10, 6, 11, 9, 1, 4, 13, 8, 6, 12, 7, 10, 11,
        14, 9,
    ),
}
STEPS = {"x": 1, "y": 2, "z1": 4, "z2": 8}
STAGES = 9


def bits_of():
    place = lax.axis_index("seq")
    return {
        "c": lax.axis_index("head"),
        "x": place % 2,
        "y": place // 2 % 2,
        "z1": place // 4 % 2,
        "z2": place // 8,
    }


def partner(d):
    place, core = lax.axis_index("seq"), lax.axis_index("head")
    if d == "c":
        return (place, 1 - core)
    return (place + STEPS[d] * (1 - 2 * bits_of()[d]), core)


class Sum:
    def __init__(self, held, got, out, ssem, rsem, lsem, orders):
        self.streams = [self.stream(held, got, out, ssem, rsem, lsem, s, order) for s, order in enumerate(orders)]
        self.stages = [-1] * len(orders)

    def stream(self, held, got, out, ssem, rsem, lsem, s, order):
        rows = held.shape[0]
        bits = bits_of()
        cols = slice(s * 256, (s + 1) * 256)
        order = ("c",) + order
        keeps, sends = [], []
        off, size = 0, rows
        for d in order[:4]:
            size //= 2
            keeps.append(off + bits[d] * size)
            sends.append(off + (1 - bits[d]) * size)
            off = keeps[-1]
        unit = rows // 16
        sizes = [rows // 2, rows // 4, rows // 8, unit, unit]
        slots = [0, rows // 2, rows // 2 + rows // 4, rows - 2 * unit, rows - unit]

        def at(start, size):
            return pl.ds(pl.multiple_of(start, 16), size)

        def copy(stage):
            if stage < 5:
                d = order[stage]
                where = at(sends[stage] if stage < 4 else off, sizes[stage])
                src, dst = held.at[where, cols], got.at[slice(slots[stage], slots[stage] + sizes[stage]), cols]
            else:
                d = order[8 - stage]
                where = at(keeps[8 - stage], sizes[8 - stage])
                src, dst = (held if stage == 5 else out).at[where, cols], out.at[where, cols]
            return remote(src, dst, ssem.at[s], rsem.at[s, stage], partner(d))

        def add(stage):
            where = keeps[stage] if stage < 4 else off

            @pl.loop(0, sizes[stage] // unit)
            def _(i):
                here = at(where + i * unit, unit)
                held[here, cols] = held[here, cols] + got[at(slots[stage] + i * unit, unit), cols]

        def place():
            return pltpu.make_async_copy(held.at[at(off, unit), cols], out.at[at(off, unit), cols], lsem.at[s])

        return copy, add, place

    def tick(self, s):
        copy, add, place = self.streams[s]
        stage = self.stages[s]
        if 0 <= stage < STAGES:
            copy(stage).wait()
            if stage < 5:
                add(stage)
        if stage == 4:
            place().start()
        if stage == 5:
            place().wait()
        if stage + 1 < STAGES:
            copy(stage + 1).start()
        self.stages[s] = stage + 1


class Swap:
    def __init__(self, held, got, ssem, rsem, orders):
        self.held, self.got, self.ssem, self.rsem = held, got, ssem, rsem
        self.orders = [("c",) + order for order in orders]
        self.stages = [-1] * len(orders)

    def tick(self, s):
        cols = slice(s * 256, (s + 1) * 256)
        order, stage = self.orders[s], self.stages[s]

        def copy(k):
            return remote(
                self.held.at[:, cols], self.got.at[k, :, cols], self.ssem.at[s], self.rsem.at[s, k], partner(order[k])
            )

        if 0 <= stage < len(order):
            copy(stage).wait()
            self.held[:, cols] = self.held[:, cols] + self.got[stage, :, cols]
        if stage + 1 < len(order):
            copy(stage + 1).start()
        self.stages[s] = stage + 1


def greet():
    place, core = lax.axis_index("seq"), lax.axis_index("head")
    pieces = lax.axis_size("seq")
    chips = pieces // SEQS
    barrier = pltpu.get_barrier_semaphore()
    peers = [partner(d) for d in ("c", "x", "y", "z1", "z2")]
    peers += [((place // SEQS + k) % chips * SEQS + place % SEQS, core) for k in range(1, chips)]
    peers += [block_at(1), block_at(-1)]
    for to in peers:
        pl.semaphore_signal(barrier, inc=1, device_id=to, device_id_type=MESH)
    return barrier, len(peers)


def block_at(ahead):
    place, core = lax.axis_index("seq"), lax.axis_index("head")
    pieces = lax.axis_size("seq")
    block = (place // SEQS * 2 + core + ahead + pieces) % pieces
    return (block // 2 * SEQS + place % SEQS, block % 2)


def whole_kernel(names, *refs):
    r = Refs(names, refs)
    rows = r.blk.shape[0]
    greeted = greet()
    loads = [
        pltpu.make_async_copy(r.w_in_hbm.at[INNER:], r.w_in.at[INNER:], r.load_sem.at[0]),
        pltpu.make_async_copy(r.w_in_hbm.at[:INNER], r.w_in.at[:INNER], r.load_sem.at[1]),
        pltpu.make_async_copy(r.w_out_hbm, r.w_out, r.load_sem.at[2]),
    ]
    for c in loads:
        c.start()
    r.gain[...] = r.norm_gain[...].reshape(1, D)
    r.conv_b[...] = r.conv_bias[...].reshape(1, XBC)
    r.gate_gain[...] = r.gated_gain[...].reshape(1, INNER)
    r.heads[...] = jnp.zeros((8, 128), f32)
    for k, one in enumerate((r.dt_bias, r.a_log, r.d_skip)):
        r.heads[k : k + 1, 0:HEADS] = one[...].reshape(1, HEADS)
    place, core = lax.axis_index("seq"), lax.axis_index("head")
    chips = lax.axis_size("seq") // SEQS
    block = place // SEQS * 2 + core

    def norm(v):
        v = v.astype(f32)
        scale = lax.rsqrt(jnp.mean(v * v, axis=-1, keepdims=True) + EPS)
        return (v * scale * r.gain[...]).astype(bf16)

    r.normed[...] = norm(r.blk[...])
    lane = iota((rows, 128), 1)
    keep = valid_rows(r.lengths, rows, 128)
    pick_lane = iota((128, 256), 1)
    pick_head = iota((128, 256), 0)
    left = one_hot(iota((1, 128), 1) < HEAD_DIM)
    right = one_hot(iota((1, 128), 1) >= HEAD_DIM)

    loads[0].wait()

    def project(i, carry):
        part = dot(r.normed[...], r.w_in[pl.ds(pl.multiple_of(INNER + i * 256, 256), 256), :], NT)
        r.pad[16:, lanes(i * 256, 256)] = part.astype(bf16).astype(f32)
        return carry

    lax.fori_loop(0, XBC // 256, project, 0, unroll=7)
    pl.semaphore_wait(*greeted)
    edge = remote(r.pad.at[rows + 8 :], r.pad.at[8:16], r.edge_sem.at[0], r.edge_sem.at[1], block_at(1))
    edge.start()

    r.head[3] = jnp.zeros((rows, 128), f32)
    r.head[3, :, 0:HEADS] = dot(r.normed[...], r.w_in[INNER + XBC :, :], NT).astype(bf16).astype(f32)
    moved = r.head[3] + r.heads[0:1, :]
    soft = jnp.maximum(moved, 0.0) + jnp.log1p(jnp.exp(-jnp.abs(moved)))
    dt = jnp.where(lane < HEADS, soft * keep, 0.0)
    rates = -jnp.exp(r.heads[1:2, :])
    below = one_hot(iota((rows, rows), 0) >= iota((rows, rows), 1))
    cum = split_dot_left(below, dt) * rates
    cum2 = cum * LOG2E
    r.head[0] = dt
    r.head[1] = cum
    r.head[2] = sigmoid(moved) * keep
    r.head[3] = cum2
    r.cumt[...] = cum2.T

    def widen(i, carry):
        cols = lanes(i * 128, 128)
        pick = one_hot((iota((128, 128), 1) >> 6) + 2 * i == iota((128, 128), 0))
        r.dt_wide[:, cols] = split_dot(r.head[0], pick)
        wide = split_dot(r.head[3], pick)
        last = wide[rows - 1 : rows, :]
        r.grow[:, cols] = jnp.exp2(wide)
        r.fall[:, cols] = jnp.exp2(last - wide)
        r.spread[0:8, cols] = jnp.broadcast_to(jnp.exp2(last), (8, 128))
        r.spread[8:16, cols] = split_dot(jnp.broadcast_to(r.heads[2:3, :], (8, 128)), pick)
        return carry

    lax.fori_loop(0, PAIRS, widen, 0, unroll=2)

    edge.wait()
    r.pad[8:16, :] = jnp.where(block == 0, 0.0, r.pad[8:16, :])

    def convolve(start, width):
        cols = lanes(start, width)
        running = r.conv_b[:, cols] + r.pad[13 : 13 + rows, cols] * r.conv_w[0:1, cols]
        for tap in range(1, CONV):
            running = running + r.pad[13 + tap : 13 + tap + rows, cols] * r.conv_w[tap : tap + 1, cols]
        r.run[:, cols] = running
        return running * sigmoid(running)

    act = convolve(INNER, 2 * STATE)
    r.b[...] = act[:, :STATE].astype(bf16)
    r.c[...] = act[:, STATE:].astype(bf16)
    third = 3 * 128

    def channels(start):
        def one(i, carry):
            at = start + i * 128
            cols = lanes(at, 128)
            x = convolve(at, 128) * keep
            r.x[:, cols] = x
            xd = x * r.dt_wide[:, cols]
            r.xd[:, cols] = xd.astype(bf16)
            r.xde[:, cols] = (xd * r.fall[:, cols]).astype(bf16)
            return carry

        lax.fori_loop(0, third // 128, one, 0, unroll=3)
        r.own[:, start : start + third] = dot(r.b[...], r.xde[:, start : start + third], TN)

    def exchanges(reverse, state, out, tag):
        made = []
        for k in range(SPLITS):
            bufs = [getattr(r, f"{tag}{k}_{n}") for n in range(5)]
            decays = [getattr(r, f"d{k}_{n}") for n in range(3)]
            sems = getattr(r, f"{tag}s").at[k], getattr(r, f"{tag}r").at[k]
            width = INNER // 2 // SPLITS
            made.append(Exchange(reverse, state, r.spread, out, bufs, decays, *sems, k * width, width))
        return made

    enters = exchanges(False, r.own, r.enter, "f")
    leaves = exchanges(True, r.adj, r.leave, "g")
    channels(0)
    channels(INNER // 2)
    enters[0].begin()
    channels(third)
    enters[0].deal()
    channels(INNER // 2 + third)
    enters[1].begin()

    def spread(i, carry):
        r.cumb[:, lanes(i * 256, 256)] = split_dot(r.head[3], one_hot((pick_lane >> 7) + 2 * i == pick_head))
        return carry


    causal = iota((rows, rows), 0) >= iota((rows, rows), 1)
    r.scores[...] = jnp.where(causal, dot(r.c[...], r.b[...], NT), 0.0)
    lax.fori_loop(0, 4, spread, 0, unroll=2)
    enters[1].deal()
    lax.fori_loop(4, PAIRS, spread, 0, unroll=2)
    loads[1].wait()

    def gates(i, carry):
        part = dot(r.normed[...], r.w_in[pl.ds(pl.multiple_of(i * 256, 256), 256), :], NT)
        r.gate[:, lanes(i * 256, 256)] = part.astype(bf16)
        return carry

    def columns(i):
        c0 = r.cumb[:, lanes(i * 256, 128)]
        c1 = r.cumb[:, lanes(i * 256 + 128, 128)]
        return c0, c1

    def pair(i, carry):
        cols = lanes(i * 128, 128)
        xd = r.xd[:, cols]
        y = None
        for cc, part, mask in zip(columns(i), (0, 1), (left, right), strict=True):
            row = r.cumt[pl.ds(2 * i + part, 1), :]
            decay = jnp.exp2(jnp.minimum(jnp.concatenate([cc] * (rows // 128), axis=1) - row, 0.0))
            term = dot((decay * r.scores[...]).astype(bf16), xd * mask)
            y = term if y is None else y + term
        r.y[:, cols] = y
        return carry

    lax.fori_loop(0, INNER // 256, gates, 0, unroll=2)
    enters[0].scan()
    lax.fori_loop(0, 6, pair, 0, unroll=2)
    enters[1].scan()
    lax.fori_loop(6, PAIRS, pair, 0, unroll=2)

    def slopes(i, carry):
        cols = lanes(i * 128, 128)
        running = r.run[:, cols]
        sg = sigmoid(running)
        r.run[:, cols] = sg * (1.0 + running * (1.0 - sg))
        return carry

    lax.fori_loop(0, XBC // 128, slopes, 0, unroll=2)
    keep_d = valid_rows(r.lengths, rows, D)
    r.db[...] = (r.gout[...].astype(f32) * keep_d).astype(bf16)
    loads[2].wait()
    r.wide[...] = dot(r.db[...], r.w_out[...], NT)
    for one in enters:
        one.hand()
    for one in enters:
        one.end()

    def carried(i, carry):
        cols = lanes(i * 128, 128)
        y = r.y[:, cols] + r.grow[:, cols] * dot(r.c[...], r.enter[:, cols])
        r.y[:, cols] = y
        r.mixed[:, cols] = (y + r.spread[8:9, cols] * r.x[:, cols]).astype(bf16)
        return carry

    lax.fori_loop(0, PAIRS, carried, 0, unroll=2)

    r.ggain[...] = jnp.zeros_like(r.ggain)
    step = 32

    def gating(i, carry):
        at = pl.ds(pl.multiple_of(i * step, step), step)
        g = r.gate[at, :].astype(f32)
        sg = sigmoid(g)
        mixed = r.mixed[at, :].astype(f32)
        gated = mixed * g * sg
        scale = lax.rsqrt(jnp.mean(gated * gated, axis=-1, keepdims=True) + EPS)
        r.gn[at, :] = (gated * scale * r.gate_gain[...]).astype(bf16)
        dgn = r.wide[at, :]
        r.ggain[...] += jnp.sum((dgn * gated * scale).reshape(step // 8, 8, INNER), axis=0)
        weighted = dgn * r.gate_gain[...]
        average = jnp.mean(weighted * gated, axis=-1, keepdims=True)
        d_gated = scale * weighted - gated * (scale * scale * scale) * average
        r.dy[at, :] = (d_gated * g * sg).astype(bf16)
        r.dgate[at, :] = (d_gated * mixed * sg * (1.0 + g * (1.0 - sg))).astype(bf16)
        return carry

    lax.fori_loop(0, rows // step, gating, 0)

    def weigh(i, carry):
        cols = lanes(i * 128, 128)
        r.dye[:, cols] = (r.dy[:, cols].astype(f32) * r.grow[:, cols]).astype(bf16)
        return carry

    lax.fori_loop(0, PAIRS, weigh, 0, unroll=2)
    r.adj[...] = dot(r.c[...], r.dye[...], TN)
    for one in leaves:
        one.begin()

    def gate_grads(i, carry):
        at = pl.ds(pl.multiple_of(i * 256, 256), 256)
        r.first[at, :] = dot(r.dgate[:, lanes(i * 256, 256)], r.normed[...], TN).astype(bf16)
        return carry

    def out_grads(i, carry):
        at = pl.ds(pl.multiple_of(INNER + i * 256, 256), 256)
        r.first[at, :] = dot(r.gn[:, lanes(i * 256, 256)], r.db[...], TN).astype(bf16)
        return carry

    def part(k, held, got, out, at):
        return Sum(held.at[at], got.at[at], out.at[at], r.ss.at[k], r.rs.at[k], r.ls.at[k], ORDERS[3 * k : 3 * k + 3])

    sums = [
        part(0, r.first, r.got_first, r.first_out, slice(0, INNER)),
        part(1, r.first, r.got_first, r.first_out, slice(INNER, FIRST_ROWS)),
        part(2, r.rest, r.got_rest, r.rest_out, slice(0, D)),
        part(3, r.rest, r.got_rest, r.rest_out, slice(D, REST_ROWS)),
        Swap(r.vec, r.got_vec, r.vs, r.vr, ORDERS[12:15]),
    ]
    def slot(name):
        for n in SCHEDULE.get(name, ()):
            sums[n // 3].tick(n % 3)

    lax.fori_loop(0, INNER // 256, gate_grads, 0, unroll=2)
    slot("g2")
    for one in leaves:
        one.deal()
    slot("d")
    lax.fori_loop(0, INNER // 256, out_grads, 0, unroll=2)
    slot("o2")
    r.block_out[...] = (r.blk[...].astype(f32) + keep_d * dot(r.gn[...], r.w_out[...])).astype(bf16)
    stores = [
        pltpu.make_async_copy(r.block_out, r.block_out_hbm, r.store_sem.at[0]),
        pltpu.make_async_copy(r.grad_in, r.grad_in_hbm, r.store_sem.at[1]),
    ]
    stores[0].start()
    slot("b0")

    r.scores_t[...] = jnp.where(
        iota((rows, rows), 1) >= iota((rows, rows), 0), dot(r.b[...], r.c[...], NT), 0.0
    )

    r.dscores[...] = jnp.zeros_like(r.dscores)
    r.q[...] = jnp.zeros_like(r.q)
    r.ry[...] = jnp.zeros_like(r.ry)
    row_head = iota((128, 128), 0)
    col_head = iota((128, 128), 1)

    def pair_back(i, carry):
        cols = lanes(i * 128, 128)
        xd, dy = r.xd[:, cols], r.dy[:, cols]
        v = None
        for cc, part, mask in zip(columns(i), (0, 1), (left, right), strict=True):
            row = r.cumt[pl.ds(2 * i + part, 1), :]
            decay = jnp.exp2(jnp.minimum(row - jnp.concatenate([cc] * (rows // 128), axis=1), 0.0))
            masked = dy * mask
            term = dot((decay * r.scores_t[...]).astype(bf16), masked)
            v = term if v is None else v + term
            r.dscores[...] += decay * dot(xd, masked, NT)
        r.wide[:, cols] = v
        r.ry[...] += split_dot(dy.astype(f32) * r.y[:, cols], one_hot((row_head >> 6) + 2 * i == col_head))
        return carry

    lax.fori_loop(0, 4, pair_back, 0, unroll=2)
    slot("b1")
    lax.fori_loop(4, 8, pair_back, 0, unroll=2)
    slot("b2")
    lax.fori_loop(8, PAIRS, pair_back, 0, unroll=2)
    slot("b3")
    for one in leaves:
        one.scan()
    slot("s")
    dsc = jnp.where(iota((rows, rows), 1) >= iota((rows, rows), 0), r.dscores[...], 0.0).astype(bf16)
    d_b = dot(dsc, r.c[...])
    d_c = dot(dsc, r.b[...], TN) + dot(r.dye[...], r.enter[...], NT)
    slot("e")
    for one in leaves:
        one.hand()
    slot("h")
    for one in leaves:
        one.end()
    slot("l")

    def channels_back(i, carry):
        cols = lanes(i * 128, 128)
        v = r.wide[:, cols] + r.fall[:, cols] * dot(r.b[...], r.leave[:, cols])
        x = r.x[:, cols]
        dy = r.dy[:, cols].astype(f32)
        r.q[...] += split_dot(x * v, one_hot((row_head >> 6) + 2 * i == col_head))
        r.skip[:, cols] = jnp.sum((dy * x).reshape(rows // 8, 8, 128), axis=0)
        r.ext[0:rows, cols] = (r.dt_wide[:, cols] * v + r.spread[8:9, cols] * dy) * keep * r.run[:, cols]
        return carry

    def conv_back(i, carry):
        cols = lanes(i * 128, 128)
        drun = r.ext[0:rows, cols]
        total = drun * r.conv_w[CONV - 1 : CONV, cols]
        for tap in range(CONV - 1):
            ahead = CONV - 1 - tap
            total = total + r.ext[ahead : ahead + rows, cols] * r.conv_w[tap : tap + 1, cols]
        r.dproj[:, cols] = total.astype(bf16)
        for tap in range(CONV):
            r.tap_sums[tap : tap + 1, cols] = jnp.sum(
                drun * r.pad[13 + tap : 13 + tap + rows, cols], axis=0, keepdims=True
            )
        r.tap_sums[CONV : CONV + 1, cols] = jnp.sum(drun, axis=0, keepdims=True)
        return carry

    def rest_grads(i, carry):
        at = pl.ds(pl.multiple_of(i * 256, 256), 256)
        r.rest[at, :] = dot(r.dproj[:, lanes(i * 256, 256)], r.normed[...], TN).astype(bf16)
        return carry

    halves = (slice(0, INNER // 2), slice(INNER // 2, XBC))

    def edges(k):
        cols = halves[k]
        sems = r.edge_sem.at[2 + 2 * k], r.edge_sem.at[3 + 2 * k]
        return remote(r.ext.at[0:8, cols], r.edge_grad.at[:, cols], *sems, block_at(-1))

    def edge_in(k):
        edges(k).wait()
        r.ext[rows : rows + 8, halves[k]] = jnp.where(block == chips * 2 - 1, 0.0, r.edge_grad[:, halves[k]])

    lax.fori_loop(0, PAIRS // 2, channels_back, 0, unroll=2)
    edges(0).start()
    slot("c1")
    lax.fori_loop(PAIRS // 2, PAIRS, channels_back, 0, unroll=2)
    d_b = d_b + dot(r.xde[...], r.leave[...], NT)
    r.ext[0:rows, INNER : INNER + STATE] = d_b * r.run[:, INNER : INNER + STATE]
    r.ext[0:rows, INNER + STATE :] = d_c * r.run[:, INNER + STATE :]
    edges(1).start()
    slot("c2")

    edge_in(0)
    slot("c3")
    lax.fori_loop(0, 6, conv_back, 0, unroll=2)
    slot("v1")
    lax.fori_loop(0, 3, rest_grads, 0, unroll=3)
    slot("r1")
    edge_in(1)
    slot("v2")
    lax.fori_loop(6, XBC // 128, conv_back, 0, unroll=2)
    slot("v3")
    lax.fori_loop(3, XBC // 256, rest_grads, 0, unroll=2)
    slot("r2")
    full_pick = one_hot((iota((INNER, 128), 0) >> 6) == iota((INNER, 128), 1))
    out_state = r.spread[0:1, :] * r.enter[...].astype(f32) + r.own[...]
    d_last = split_dot(
        jnp.sum((r.leave[...].astype(f32) * out_state).reshape(STATE // 8, 8, INNER), axis=0), full_pick
    )
    d_last = jnp.sum(d_last, axis=0, keepdims=True)
    q = r.q[...]
    d_cum = r.ry[...] - r.head[0] * q + jnp.where(iota((rows, 128), 0) == rows - 1, d_last, 0.0)
    above = one_hot(iota((rows, rows), 0) <= iota((rows, rows), 1))
    dz = (q + split_dot_left(above, d_cum * -jnp.exp(r.heads[1:2, :]))) * r.head[2]
    r.vec[...] = jnp.zeros_like(r.vec)
    r.vec[42:43, 0:128] = jnp.sum(dz, axis=0, keepdims=True)
    r.vec[43:44, 0:128] = jnp.sum(d_cum * r.head[1], axis=0, keepdims=True)
    r.vec[44:45, 0:128] = jnp.sum(split_dot(r.skip[...], full_pick), axis=0, keepdims=True)
    dz = dz.astype(bf16)
    slot("e1")
    d_normed = dot(r.dgate[...], r.w_in[:INNER, :])
    d_normed = d_normed + dot(dz[:, :HEADS], r.w_in[INNER + XBC :, :])
    d_normed = d_normed + dot(r.dproj[...], r.w_in[INNER : INNER + XBC, :])
    slot("e2")
    for v in range(CONV + 1):
        for part in range(3):
            width = min(D, XBC - part * D)
            r.vec[HEADS + 3 * v + part : HEADS + 3 * v + part + 1, 0:width] = r.tap_sums[v : v + 1, part * D : part * D + width]
    src = r.blk[...].astype(f32)
    scale = lax.rsqrt(jnp.mean(src * src, axis=-1, keepdims=True) + EPS)
    r.vec[39:40, :] = jnp.sum(d_normed * src * scale, axis=0, keepdims=True)
    gate_gain = jnp.sum(r.ggain[...], axis=0, keepdims=True)
    r.vec[40:41, :] = gate_gain[:, :D]
    r.vec[41:42, :] = gate_gain[:, D:]
    r.vec[0:HEADS, :] = dot(dz, r.normed[...], TN)[0:HEADS, :]
    slot("r3")
    weighted = d_normed * r.gain[...]
    average = jnp.mean(weighted * src, axis=-1, keepdims=True)
    r.grad_in[...] = r.gout[...].astype(f32) + scale * weighted - src * (scale * scale * scale) * average
    stores[1].start()
    slot("z")
    out = pltpu.make_async_copy(r.vec, r.vec_out, r.store_sem.at[2])
    out.start()
    for c in (*stores, out):
        c.wait()


def whole(*args):
    t = args[0].shape[0]
    chips = lax.axis_size("seq") // SEQS
    ins = ["blk", "gout", "lengths", "norm_gain", "w_in_hbm", "conv_w", "conv_bias", "dt_bias", "a_log", "d_skip"]
    ins += ["gated_gain", "w_out_hbm"]
    outs = {
        "block_out_hbm": ((t, D), bf16),
        "grad_in_hbm": ((t, D), f32),
        "first_out": ((FIRST_ROWS, D), bf16),
        "rest_out": ((REST_ROWS, D), bf16),
        "vec_out": ((VEC_ROWS, D), f32),
    }
    held = {
        "block_out": ((t, D), bf16),
        "grad_in": ((t, D), f32),
        "first": ((FIRST_ROWS, D), bf16),
        "rest": ((REST_ROWS, D), bf16),
        "gain": ((1, D), f32),
        "conv_b": ((1, XBC), f32),
        "gate_gain": ((1, INNER), f32),
        "heads": ((8, 128), f32),
        "w_in": ((PROJ, D), bf16),
        "w_out": ((INNER, D), bf16),
        "edge_grad": ((8, XBC), f32),
        "normed": ((t, D), bf16),
        "gate": ((t, INNER), bf16),
        "pad": ((t + 16, XBC), f32),
        "run": ((t, XBC), f32),
        "x": ((t, INNER), f32),
        "xd": ((t, INNER), bf16),
        "xde": ((t, INNER), bf16),
        "b": ((t, STATE), bf16),
        "c": ((t, STATE), bf16),
        "head": ((4, t, 128), f32),
        "cumt": ((128, t), f32),
        "cumb": ((t, HEADS * 128), f32),
        "spread": ((16, INNER), f32),
        "own": ((STATE, INNER), f32),
        "enter": ((STATE, INNER), bf16),
        "y": ((t, INNER), f32),
        "grow": ((t, INNER), f32),
        "fall": ((t, INNER), f32),
        "dt_wide": ((t, INNER), f32),
        "mixed": ((t, INNER), bf16),
        "gn": ((t, INNER), bf16),
        "wide": ((t, INNER), f32),
        "db": ((t, D), bf16),
        "dy": ((t, INNER), bf16),
        "dye": ((t, INNER), bf16),
        "dgate": ((t, INNER), bf16),
        "ggain": ((8, INNER), f32),
        "adj": ((STATE, INNER), f32),
        "leave": ((STATE, INNER), bf16),
        "scores": ((t, t), f32),
        "scores_t": ((t, t), f32),
        "dscores": ((t, t), f32),
        "skip": ((8, INNER), f32),
        "q": ((t, 128), f32),
        "ry": ((t, 128), f32),
        "ext": ((t + 8, XBC), f32),
        "dproj": ((t, XBC), bf16),
        "vec": ((VEC_ROWS, D), f32),
        "got_vec": ((5, VEC_ROWS, D), f32),
        "tap_sums": ((8, XBC), f32),
        "got_first": ((FIRST_ROWS, D), bf16),
        "got_rest": ((REST_ROWS, D), bf16),
    }
    names = ins + list(outs) + list(held)
    scratch = [pltpu.VMEM(s, d) for s, d in held.values()]
    states, decays = exchange_scratch(chips, INNER // 2 // SPLITS)
    for tag, shapes in (("f", states), ("g", states), ("d", decays)):
        for k in range(SPLITS):
            scratch += [pltpu.VMEM(s, d) for s, d in shapes]
            names += [f"{tag}{k}_{n}" for n in range(len(shapes))]
    semaphores = {
        "ss": (WAVES, 3),
        "rs": (WAVES, 3, STAGES),
        "ls": (WAVES, 3),
        "fs": (SPLITS, 2),
        "fr": (SPLITS, 7),
        "gs": (SPLITS, 2),
        "gr": (SPLITS, 7),
        "edge_sem": (6,),
        "load_sem": (3,),
        "store_sem": (3,),
        "vs": (3,),
        "vr": (3, 5),
    }
    for name, shape in semaphores.items():
        scratch.append(pltpu.SemaphoreType.DMA(shape))
        names.append(name)
    any_space = pl.BlockSpec(memory_space=pl.ANY)
    specs = {n: any_space for n in ("w_in_hbm", "w_out_hbm", *outs)} | {"lengths": SMEM}
    return pl.pallas_call(
        partial(whole_kernel, names),
        out_shape=[jax.ShapeDtypeStruct(s, d) for s, d in outs.values()],
        in_specs=[specs.get(n, VMEM) for n in ins],
        out_specs=[specs.get(n, VMEM) for n in outs],
        scratch_shapes=scratch,
        compiler_params=pltpu.CompilerParams(vmem_limit_bytes=60 << 20, collective_id=0, has_side_effects=True),
    )(*args)


def finish_kernel(
    block_in,
    grad_in,
    first,
    rest,
    vec_in,
    block_out,
    grad_out,
    norm_out,
    w_in_out,
    conv_out,
    bias_out,
    dt_out,
    alog_out,
    skip_out,
    gate_out,
    w_out_out,
    held_first,
    held_rest,
    held_block,
    held_grad,
    vec,
    wide_in,
    wide_out,
    in_sem,
    out_sem,
    pass_sem,
):
    passed = [
        (pltpu.make_async_copy(src, by, pass_sem.at[n, 0]), pltpu.make_async_copy(by, dst, pass_sem.at[n, 1]))
        for n, (src, by, dst) in enumerate(((block_in, held_block, block_out), (grad_in, held_grad, grad_out)))
    ]
    chunks = [(first, held_first, k * 256, 256) for k in range(FIRST_ROWS // 256)]
    chunks += [(rest, held_rest, k * 256, 256) for k in range(REST_ROWS // 256)]
    loads = [
        pltpu.make_async_copy(src.at[start : start + size], dst.at[start : start + size], in_sem.at[n])
        for n, (src, dst, start, size) in enumerate(chunks)
    ]
    ahead = 8
    small = pltpu.make_async_copy(vec_in, vec, pass_sem.at[1, 2])
    for c in loads[:ahead] + [small] + [load for load, _ in passed]:
        c.start()
    stores = [store for _, store in passed]
    for n, (src, held, start, size) in enumerate(chunks):
        loads[n].wait()
        if n == ahead:
            for load, store in passed:
                load.wait()
                store.start()
        if n + ahead < len(loads):
            loads[n + ahead].start()
        if src is first and start >= INNER:
            wide, out, at = wide_out, w_out_out, start - INNER
        else:
            wide, out, at = wide_in, w_in_out, start if src is first else INNER + start
        wide[at : at + size, :] = held[start : start + size, :].astype(f32)
        c = pltpu.make_async_copy(wide.at[at : at + size], out.at[at : at + size], out_sem.at[n])
        c.start()
        stores.append(c)
    small.wait()
    wide_in[INNER + XBC :, :] = vec[0:HEADS, :]
    c = pltpu.make_async_copy(wide_in.at[INNER + XBC :], w_in_out.at[INNER + XBC :], pass_sem.at[0, 2])
    c.start()
    stores.append(c)

    def row(v):
        return jnp.concatenate([vec[HEADS + 3 * v + k : HEADS + 3 * v + k + 1, : min(D, XBC - k * D)] for k in range(3)], axis=1)

    for v in range(CONV):
        conv_out[v : v + 1, :] = row(v)
    bias_out[...] = row(CONV).reshape(XBC)
    norm_out[...] = vec[39:40, :].reshape(D)
    gate_out[...] = jnp.concatenate([vec[40:41, :], vec[41:42, :]], axis=1).reshape(INNER)
    for k, out in enumerate((dt_out, alog_out, skip_out)):
        out[...] = vec[42 + k : 43 + k, 0:HEADS].reshape(HEADS)
    for c in stores:
        c.wait()


def finish(block_out, grad_in, first, rest, vec):
    shapes = [block_out.shape, grad_in.shape, (D,), (PROJ, D), (CONV, XBC), (XBC,), (HEADS,), (HEADS,), (HEADS,), (INNER,)]
    shapes += [(INNER, D)]
    any_space = pl.BlockSpec(memory_space=pltpu.HBM)
    away = (0, 1, 3, 10)
    chunks = (FIRST_ROWS + REST_ROWS) // 256
    return pl.pallas_call(
        finish_kernel,
        out_shape=[jax.ShapeDtypeStruct(s, bf16 if k == 0 else f32) for k, s in enumerate(shapes)],
        in_specs=[any_space] * 5,
        out_specs=[any_space if k in away else VMEM for k in range(len(shapes))],
        scratch_shapes=[
            pltpu.VMEM((FIRST_ROWS, D), bf16),
            pltpu.VMEM((REST_ROWS, D), bf16),
            pltpu.VMEM(block_out.shape, bf16),
            pltpu.VMEM(grad_in.shape, f32),
            pltpu.VMEM((VEC_ROWS, D), f32),
            pltpu.VMEM((PROJ, D), f32),
            pltpu.VMEM((INNER, D), f32),
            pltpu.SemaphoreType.DMA((chunks,)),
            pltpu.SemaphoreType.DMA((chunks,)),
            pltpu.SemaphoreType.DMA((2, 3)),
        ],
        compiler_params=pltpu.CompilerParams(vmem_limit_bytes=60 << 20),
    )(block_out, grad_in, first, rest, vec)


def shifted(value, ahead):
    groups = lax.axis_size("head")
    count = lax.axis_size("seq") * groups
    moves = []
    for source in range(count):
        piece, half = source // groups, source % groups
        half += ahead
        if half == groups:
            half, piece = 0, piece + SEQS
        elif half < 0:
            half, piece = groups - 1, piece - SEQS
        if 0 <= piece * groups + half < count:
            moves.append((source, piece * groups + half))
    return lax.ppermute(value, ("seq", "head"), moves)


def by_parts(block_in, grad_out, lengths, norm_gain, w_in, conv_w, conv_b, dt_bias, a_log, d_skip, gate_gain, w_out):
    heads = jnp.pad(jnp.stack([dt_bias, a_log, d_skip]), ((0, 5), (0, 128 - HEADS)))
    gain, conv_b, gate_gain = norm_gain.reshape(1, D), conv_b.reshape(1, XBC), gate_gain.reshape(1, INNER)
    edge = shifted(block_in[-16:], 1)
    (normed, gate, pad, run, x, xd, xde, b, c, head, cumt, cumb, rows, own) = front(
        lengths, block_in, edge, gain, w_in, conv_w, conv_b, heads
    )
    enter = exchange_plain(own, rows[0:8], False)
    (y, block_out, dy, dye, dgate, ggain, adj, grads_a) = middle(
        lengths, block_in, grad_out, normed, gate, x, xd, b, c, cumt, cumb, rows, enter, gate_gain, w_out
    )
    leave = exchange_plain(adj, rows[0:8], True)
    drun, dz, small = back(
        lengths, y, dy, dye, x, xd, xde, b, c, run, cumt, cumb, head, rows, heads, enter, own, leave
    )
    edge_back = shifted(drun[0:8], -1)
    grad_in, grads_b, vec = last(
        block_in, grad_out, normed, gain, w_in, conv_w, pad, drun, edge_back, dz, dgate, ggain, small
    )
    grads_a, grads_b, vec = lax.psum((grads_a, grads_b, vec), ("seq", "head"))
    return block_out, grad_in, grads_a, grads_b, vec


def local(block_in, grad_out, lengths, norm_gain, w_in, *others):
    run = whole if lax.axis_size("seq") == 16 and lax.axis_size("head") == 2 else by_parts
    outs = finish(*run(block_in, grad_out, lengths, norm_gain, w_in.T, *others))
    return (*outs[:3], outs[3].T, *outs[4:])


def solution(mesh):
    rows = P(("seq", "head"), None)
    return jax.shard_map(
        local,
        mesh=mesh,
        in_specs=(rows, rows) + (P(),) * 10,
        out_specs=(rows, rows) + (P(),) * 9,
        check_vma=False,
    )
```

```python
from functools import partial

import jax
import jax.numpy as jnp
from jax import lax
from jax.experimental import pallas as pl
from jax.experimental.pallas import tpu as pltpu
from jax.sharding import PartitionSpec as P

D = 768
INNER = 1536
HEADS = 24
HEAD_DIM = 64
STATE = 128
CONV = 4
SEQS = 2
XBC = INNER + 2 * STATE
PROJ = 2 * INNER + 2 * STATE + HEADS
PAIRS = HEADS // 2
EPS = 1e-05
LOG2E = 1.4426950408889634

f32 = jnp.float32
bf16 = jnp.bfloat16
MESH = pl.DeviceIdType.MESH
VMEM = pl.BlockSpec(memory_space=pltpu.VMEM)
SMEM = pl.BlockSpec(memory_space=pltpu.SMEM)
NN = ((1,), (0,))
NT = ((1,), (1,))
TN = ((0,), (0,))


def dot(a, b, dims=NN):
    return lax.dot_general(a, b, (dims, ((), ())), preferred_element_type=f32)


def split_dot(a, pick, terms=3):
    total = None
    for _ in range(terms):
        part = a.astype(bf16)
        a = a - part.astype(f32)
        term = dot(part, pick)
        total = term if total is None else total + term
    return total


def split_dot_left(pick, a, terms=3):
    total = None
    for _ in range(terms):
        part = a.astype(bf16)
        a = a - part.astype(f32)
        term = dot(pick, part)
        total = term if total is None else total + term
    return total


def iota(shape, dim):
    return lax.broadcasted_iota(jnp.int32, shape, dim)


def one_hot(cond):
    return jnp.where(cond, 1.0, 0.0).astype(bf16)


def sigmoid(v):
    return 1.0 / (1.0 + jnp.exp(-v))


def lanes(start, size):
    return pl.ds(pl.multiple_of(start, 128), size)


def valid_rows(lengths_ref, rows, width):
    place = lax.axis_index("seq")
    first = (place // SEQS) * (rows * lax.axis_size("head")) + lax.axis_index("head") * rows
    limit = lengths_ref[place % SEQS]
    return jnp.where(iota((rows, width), 0) + first < limit, 1.0, 0.0)


def call(body, outs, args, scratch=(), smem=(), vmem=56 << 20, cost=None, **params):
    return pl.pallas_call(
        body,
        out_shape=[jax.ShapeDtypeStruct(s, d) for s, d in outs],
        in_specs=[SMEM if i in smem else VMEM for i in range(len(args))],
        out_specs=[VMEM] * len(outs),
        scratch_shapes=list(scratch),
        compiler_params=pltpu.CompilerParams(vmem_limit_bytes=vmem, **params),
    )(*args)


REST_ROWS = XBC
VEC_ROWS = 48
FIRST_ROWS = 2 * INNER
WAVES = 4
SPLITS = 2


def front_kernel(
    lengths_ref,
    blk,
    edge,
    gain,
    w_in,
    conv_w,
    conv_b,
    heads_ref,
    normed_out,
    gate_out,
    pad_out,
    run_out,
    x_out,
    xd_out,
    xde_out,
    b_out,
    c_out,
    head_out,
    cumt_out,
    cumb_out,
    rows_out,
    state_out,
):
    rows = blk.shape[0]

    def norm(v):
        v = v.astype(f32)
        scale = lax.rsqrt(jnp.mean(v * v, axis=-1, keepdims=True) + EPS)
        return (v * scale * gain[...]).astype(bf16)

    normed = norm(blk[...])
    normed_out[...] = normed
    gate_out[...] = dot(normed, w_in[:INNER, :], NT).astype(bf16)
    ahead = norm(edge[...])
    pad_out[0:16, :] = dot(ahead, w_in[INNER : INNER + XBC, :], NT).astype(bf16).astype(f32)
    pad_out[16 : 16 + rows, :] = dot(normed, w_in[INNER : INNER + XBC, :], NT).astype(bf16).astype(f32)
    keep = valid_rows(lengths_ref, rows, 128)
    head_out[3] = jnp.zeros((rows, 128), f32)
    head_out[3, :, 0:HEADS] = dot(normed, w_in[INNER + XBC :, :], NT).astype(bf16).astype(f32)
    lane = iota((rows, 128), 1)
    shifted = head_out[3] + heads_ref[0:1, :]
    soft = jnp.maximum(shifted, 0.0) + jnp.log1p(jnp.exp(-jnp.abs(shifted)))
    dt = jnp.where(lane < HEADS, soft * keep, 0.0)
    rates = -jnp.exp(heads_ref[1:2, :])
    below = one_hot(iota((rows, rows), 0) >= iota((rows, rows), 1))
    cum = split_dot_left(below, dt) * rates
    cum2 = cum * LOG2E
    head_out[0] = dt
    head_out[1] = cum
    head_out[2] = sigmoid(shifted) * keep
    head_out[3] = cum2
    cumt_out[...] = cum2.T
    pick_lane = iota((128, 256), 1)
    pick_head = iota((128, 256), 0)

    def spread(i, carry):
        cumb_out[:, lanes(i * 256, 256)] = split_dot(
            head_out[3], one_hot((pick_lane >> 7) + 2 * i == pick_head)
        )
        return carry

    lax.fori_loop(0, PAIRS, spread, 0)

    def convolve(i):
        cols = lanes(i * 256, 256)
        running = conv_b[:, cols] + pad_out[13 : 13 + rows, cols] * conv_w[0:1, cols]
        for tap in range(1, CONV):
            running = running + pad_out[13 + tap : 13 + tap + rows, cols] * conv_w[tap : tap + 1, cols]
        run_out[:, cols] = running
        return running * sigmoid(running)

    act = convolve(INNER // 256)
    b_out[...] = act[:, :STATE].astype(bf16)
    c_out[...] = act[:, STATE:].astype(bf16)
    keep2 = valid_rows(lengths_ref, rows, 256)

    def channels(i, carry):
        cols = lanes(i * 256, 256)
        pick = one_hot((pick_lane >> 6) + 4 * i == pick_head)
        x = convolve(i) * keep2
        x_out[:, cols] = x
        xd = x * split_dot(head_out[0], pick)
        xd_out[:, cols] = xd.astype(bf16)
        wide = split_dot(head_out[3], pick)
        last = wide[rows - 1 : rows, :]
        xde_out[:, cols] = (xd * jnp.exp2(last - wide)).astype(bf16)
        rows_out[0:8, cols] = jnp.broadcast_to(jnp.exp2(last), (8, 256))
        rows_out[8:16, cols] = split_dot(jnp.broadcast_to(heads_ref[2:3, :], (8, 128)), pick)
        return carry

    lax.fori_loop(0, INNER // 256, channels, 0)
    state_out[...] = dot(b_out[...], xde_out[...], TN)


def front(lengths, blk, edge, gain, w_in, conv_w, conv_b, heads):
    t = blk.shape[0]
    outs = [
        ((t, D), bf16),
        ((t, INNER), bf16),
        ((t + 16, XBC), f32),
        ((t, XBC), f32),
        ((t, INNER), f32),
        ((t, INNER), bf16),
        ((t, INNER), bf16),
        ((t, STATE), bf16),
        ((t, STATE), bf16),
        ((4, t, 128), f32),
        ((128, t), f32),
        ((t, HEADS * 128), f32),
        ((16, INNER), f32),
        ((STATE, INNER), f32),
    ]
    return call(front_kernel, outs, (lengths, blk, edge, gain, w_in, conv_w, conv_b, heads), smem=(0,))


def exchange_plain(state, decay, reverse):
    groups = lax.axis_size("head")
    count = lax.axis_size("seq") * groups
    place = lax.axis_index("seq")
    states = lax.all_gather(state.astype(bf16), ("seq", "head"), axis=0)
    decays = lax.all_gather(decay[0:1], ("seq", "head"), axis=0)
    blocks = count // SEQS
    block = place // SEQS * groups + lax.axis_index("head")

    def one(i, carry):
        source = blocks - 1 - i if reverse else i
        index = (source // groups * SEQS + place % SEQS) * groups + source % groups
        new = lax.dynamic_index_in_dim(decays, index, 0, False) * carry
        return new + lax.dynamic_index_in_dim(states, index, 0, False).astype(f32)

    ahead = blocks - 1 - block if reverse else block
    return lax.fori_loop(0, ahead, one, jnp.zeros(state.shape, f32)).astype(bf16)


def middle_kernel(
    lengths_ref,
    blk,
    gout,
    normed,
    gate,
    x_in,
    xd_in,
    b_in,
    c_in,
    cumt,
    cumb,
    rows_in,
    enter,
    gain,
    w_out,
    y_out,
    block_out,
    dy_out,
    dye_out,
    dgate_out,
    ggain_out,
    adj_out,
    grads_out,
    scores,
    mixed,
    gated_s,
    gn_s,
    scale_s,
    dgn_s,
    db_s,
):
    rows = blk.shape[0]
    causal = iota((rows, rows), 0) >= iota((rows, rows), 1)
    scores[...] = jnp.where(causal, dot(c_in[...], b_in[...], NT), 0.0)
    lane = iota((rows, 128), 1)
    left = one_hot(iota((1, 128), 1) < HEAD_DIM)
    right = one_hot(iota((1, 128), 1) >= HEAD_DIM)

    def pair(i, carry):
        cols = lanes(i * 128, 128)
        c0 = cumb[:, lanes(i * 256, 128)]
        c1 = cumb[:, lanes(i * 256 + 128, 128)]
        xd = xd_in[:, cols]
        y = None
        for cc, part, mask in ((c0, 0, left), (c1, 1, right)):
            row = cumt[pl.ds(2 * i + part, 1), :]
            decay = jnp.exp2(jnp.minimum(jnp.concatenate([cc] * (rows // 128), axis=1) - row, 0.0))
            term = dot((decay * scores[...]).astype(bf16), xd * mask)
            y = term if y is None else y + term
        grow = jnp.exp2(jnp.where(lane < HEAD_DIM, c0, c1))
        y = y + grow * dot(c_in[...], enter[:, cols])
        y_out[:, cols] = y
        mixed[:, cols] = (y + rows_in[8:9, cols] * x_in[:, cols]).astype(bf16).astype(f32)
        return carry

    lax.fori_loop(0, PAIRS, pair, 0)
    step = 32

    def gating(i, carry):
        r = pl.ds(pl.multiple_of(i * step, step), step)
        g = gate[r, :].astype(f32)
        gated = mixed[r, :] * g * sigmoid(g)
        scale = lax.rsqrt(jnp.mean(gated * gated, axis=-1, keepdims=True) + EPS)
        gated_s[r, :] = gated
        scale_s[r, :] = jnp.broadcast_to(scale, (step, 128))
        gn_s[r, :] = (gated * scale * gain[...]).astype(bf16)
        return carry

    lax.fori_loop(0, rows // step, gating, 0)
    keep = valid_rows(lengths_ref, rows, D)
    db_s[...] = (gout[...].astype(f32) * keep).astype(bf16)
    dgn_s[...] = dot(db_s[...], w_out[...], NT)
    block_out[...] = (blk[...].astype(f32) + keep * dot(gn_s[...], w_out[...])).astype(bf16)
    ggain_out[...] = jnp.zeros_like(ggain_out)

    def ungating(i, carry):
        r = pl.ds(pl.multiple_of(i * step, step), step)
        g = gate[r, :].astype(f32)
        sg = sigmoid(g)
        gated = gated_s[r, :]
        scale = scale_s[r, 0:1]
        dgn = dgn_s[r, :]
        ggain_out[...] += jnp.sum((dgn * gated * scale).reshape(step // 8, 8, INNER), axis=0)
        weighted = dgn * gain[...]
        average = jnp.mean(weighted * gated, axis=-1, keepdims=True)
        d_gated = scale * weighted - gated * (scale * scale * scale) * average
        dy_out[r, :] = (d_gated * g * sg).astype(bf16)
        dgate_out[r, :] = (d_gated * mixed[r, :] * sg * (1.0 + g * (1.0 - sg))).astype(bf16)
        return carry

    lax.fori_loop(0, rows // step, ungating, 0)

    def weigh(i, carry):
        cols = lanes(i * 128, 128)
        grow = jnp.exp2(jnp.where(lane < HEAD_DIM, cumb[:, lanes(i * 256, 128)], cumb[:, lanes(i * 256 + 128, 128)]))
        dye_out[:, cols] = (dy_out[:, cols].astype(f32) * grow).astype(bf16)
        return carry

    lax.fori_loop(0, PAIRS, weigh, 0)
    adj_out[...] = dot(c_in[...], dye_out[...], TN)
    grads_out[:INNER, :] = dot(dgate_out[...], normed[...], TN).astype(bf16)
    grads_out[INNER:, :] = dot(gn_s[...], db_s[...], TN).astype(bf16)


def middle(lengths, blk, gout, normed, gate, x, xd, b, c, cumt, cumb, rows_in, enter, gain, w_out):
    t = blk.shape[0]
    outs = [
        ((t, INNER), f32),
        ((t, D), bf16),
        ((t, INNER), bf16),
        ((t, INNER), bf16),
        ((t, INNER), bf16),
        ((8, INNER), f32),
        ((STATE, INNER), f32),
        ((2 * INNER, D), bf16),
    ]
    scratch = [
        pltpu.VMEM((t, t), f32),
        pltpu.VMEM((t, INNER), f32),
        pltpu.VMEM((t, INNER), f32),
        pltpu.VMEM((t, INNER), bf16),
        pltpu.VMEM((t, 128), f32),
        pltpu.VMEM((t, INNER), f32),
        pltpu.VMEM((t, D), bf16),
    ]
    args = (lengths, blk, gout, normed, gate, x, xd, b, c, cumt, cumb, rows_in, enter, gain, w_out)
    return call(middle_kernel, outs, args, scratch, smem=(0,))


def back_kernel(
    lengths_ref,
    y_in,
    dy_in,
    dye_in,
    x_in,
    xd_in,
    xde_in,
    b_in,
    c_in,
    run_in,
    cumt,
    cumb,
    head_in,
    rows_in,
    heads_ref,
    enter,
    own,
    leave,
    drun_out,
    dz_out,
    small_out,
    scores,
    dscores,
    skip_s,
    q_s,
    ry_s,
):
    rows = y_in.shape[0]
    causal = iota((rows, rows), 1) >= iota((rows, rows), 0)
    scores[...] = jnp.where(causal, dot(b_in[...], c_in[...], NT), 0.0)
    dscores[...] = jnp.zeros_like(dscores)
    q_s[...] = jnp.zeros_like(q_s)
    ry_s[...] = jnp.zeros_like(ry_s)
    lane = iota((rows, 128), 1)
    keep = valid_rows(lengths_ref, rows, 128)
    left = one_hot(iota((1, 128), 1) < HEAD_DIM)
    right = one_hot(iota((1, 128), 1) >= HEAD_DIM)
    pick_lane = iota((128, 128), 0)
    pick_head = iota((128, 128), 1)

    def dsilu(cols):
        running = run_in[:, cols]
        sg = sigmoid(running)
        return sg * (1.0 + running * (1.0 - sg))

    def pair(i, carry):
        cols = lanes(i * 128, 128)
        c0 = cumb[:, lanes(i * 256, 128)]
        c1 = cumb[:, lanes(i * 256 + 128, 128)]
        xd = xd_in[:, cols]
        dy = dy_in[:, cols]
        v = None
        for cc, part, mask in ((c0, 0, left), (c1, 1, right)):
            row = cumt[pl.ds(2 * i + part, 1), :]
            decay = jnp.exp2(jnp.minimum(row - jnp.concatenate([cc] * (rows // 128), axis=1), 0.0))
            masked = dy * mask
            term = dot((decay * scores[...]).astype(bf16), masked)
            v = term if v is None else v + term
            dscores[...] += decay * dot(xd, masked, NT)
        c01 = jnp.where(lane < HEAD_DIM, c0, c1)
        v = v + jnp.exp2(c01[rows - 1 : rows, :] - c01) * dot(b_in[...], leave[:, cols])
        pick = one_hot((pick_lane >> 6) + 2 * i == pick_head)
        dtw = split_dot(head_in[0], one_hot((pick_head >> 6) + 2 * i == pick_lane))
        x = x_in[:, cols]
        dyf = dy.astype(f32)
        q_s[...] += split_dot(x * v, pick)
        ry_s[...] += split_dot(dyf * y_in[:, cols], pick)
        skip_s[:, cols] = jnp.sum((dyf * x).reshape(rows // 8, 8, 128), axis=0)
        dx = dtw * v + rows_in[8:9, cols] * dyf
        drun_out[:, cols] = dx * keep * dsilu(cols)
        return carry

    lax.fori_loop(0, PAIRS, pair, 0)
    dsc = jnp.where(causal, dscores[...], 0.0).astype(bf16)
    d_b = dot(dsc, c_in[...]) + dot(xde_in[...], leave[...], NT)
    d_c = dot(dsc, b_in[...], TN) + dot(dye_in[...], enter[...], NT)
    drun_out[:, INNER : INNER + STATE] = d_b * dsilu(slice(INNER, INNER + STATE))
    drun_out[:, INNER + STATE :] = d_c * dsilu(slice(INNER + STATE, XBC))
    full_pick = one_hot((iota((INNER, 128), 0) >> 6) == iota((INNER, 128), 1))
    out_state = rows_in[0:1, :] * enter[...].astype(f32) + own[...]
    d_last = split_dot(
        jnp.sum((leave[...].astype(f32) * out_state).reshape(STATE // 8, 8, INNER), axis=0), full_pick
    )
    d_last = jnp.sum(d_last, axis=0, keepdims=True)
    dt = head_in[0]
    q = q_s[...]
    d_cum = ry_s[...] - dt * q + jnp.where(iota((rows, 128), 0) == rows - 1, d_last, 0.0)
    rates = -jnp.exp(heads_ref[1:2, :])
    above = one_hot(iota((rows, rows), 0) <= iota((rows, rows), 1))
    d_dt = q + split_dot_left(above, d_cum * rates)
    dz = d_dt * head_in[2]
    dz_out[...] = dz
    small_out[0:1, :] = jnp.sum(dz, axis=0, keepdims=True)
    small_out[1:2, :] = jnp.sum(d_cum * head_in[1], axis=0, keepdims=True)
    small_out[2:3, :] = jnp.sum(split_dot(skip_s[...], full_pick), axis=0, keepdims=True)
    small_out[3:8, :] = jnp.zeros((5, 128), f32)


def back(lengths, y, dy, dye, x, xd, xde, b, c, run, cumt, cumb, head, rows_in, heads, enter, own, leave):
    t = y.shape[0]
    outs = [((t, XBC), f32), ((t, 128), f32), ((8, 128), f32)]
    scratch = [
        pltpu.VMEM((t, t), f32),
        pltpu.VMEM((t, t), f32),
        pltpu.VMEM((8, INNER), f32),
        pltpu.VMEM((t, 128), f32),
        pltpu.VMEM((t, 128), f32),
    ]
    args = (lengths, y, dy, dye, x, xd, xde, b, c, run, cumt, cumb, head, rows_in, heads, enter, own, leave)
    return call(back_kernel, outs, args, scratch, smem=(0,))


def last_kernel(
    blk,
    gout,
    normed,
    gain,
    w_in,
    conv_w,
    pad_in,
    drun_in,
    edge,
    dz_in,
    dgate,
    ggain,
    small_in,
    gin_out,
    grads_out,
    vec_out,
    ext,
    dproj,
    sums,
):
    rows = blk.shape[0]
    ext[0:rows, :] = drun_in[...]
    ext[rows : rows + 8, :] = edge[...]
    vec_out[...] = jnp.zeros_like(vec_out)

    def channels(i, carry):
        cols = lanes(i * 128, 128)
        drun = ext[0:rows, cols]
        total = drun * conv_w[CONV - 1 : CONV, cols]
        for tap in range(CONV - 1):
            ahead = CONV - 1 - tap
            total = total + ext[ahead : ahead + rows, cols] * conv_w[tap : tap + 1, cols]
        dproj[:, cols] = total.astype(bf16)
        for tap in range(CONV):
            sums[tap : tap + 1, cols] = jnp.sum(
                drun * pad_in[13 + tap : 13 + tap + rows, cols], axis=0, keepdims=True
            )
        sums[CONV : CONV + 1, cols] = jnp.sum(drun, axis=0, keepdims=True)
        return carry

    lax.fori_loop(0, XBC // 128, channels, 0)
    for v in range(CONV + 1):
        for part in range(3):
            width = min(D, XBC - part * D)
            vec_out[HEADS + 3 * v + part : HEADS + 3 * v + part + 1, 0:width] = sums[v : v + 1, part * D : part * D + width]
    dz = dz_in[...].astype(bf16)
    d_normed = dot(dgate[...], w_in[:INNER, :])
    d_normed = d_normed + dot(dproj[...], w_in[INNER : INNER + XBC, :])
    d_normed = d_normed + dot(dz[:, :HEADS], w_in[INNER + XBC :, :])
    src = blk[...].astype(f32)
    scale = lax.rsqrt(jnp.mean(src * src, axis=-1, keepdims=True) + EPS)
    vec_out[39:40, :] = jnp.sum(d_normed * src * scale, axis=0, keepdims=True)
    gate_gain = jnp.sum(ggain[...], axis=0, keepdims=True)
    vec_out[40:41, :] = gate_gain[:, :D]
    vec_out[41:42, :] = gate_gain[:, D:]
    vec_out[42:45, 0:128] = small_in[0:3, :]
    weighted = d_normed * gain[...]
    average = jnp.mean(weighted * src, axis=-1, keepdims=True)
    gin_out[...] = gout[...].astype(f32) + scale * weighted - src * (scale * scale * scale) * average
    grads_out[...] = dot(dproj[...], normed[...], TN).astype(bf16)
    vec_out[0:HEADS, :] = dot(dz, normed[...], TN)[0:HEADS, :]


def last(blk, gout, normed, gain, w_in, conv_w, pad, drun, edge, dz, dgate, ggain, small):
    t = blk.shape[0]
    outs = [((t, D), f32), ((REST_ROWS, D), bf16), ((VEC_ROWS, D), f32)]
    scratch = [pltpu.VMEM((t + 8, XBC), f32), pltpu.VMEM((t, XBC), bf16), pltpu.VMEM((8, XBC), f32)]
    args = (blk, gout, normed, gain, w_in, conv_w, pad, drun, edge, dz, dgate, ggain, small)
    return call(last_kernel, outs, args, scratch)


class Refs:
    def __init__(self, names, refs):
        self.__dict__.update(zip(names, refs, strict=True))


def remote(src, dst, ssem, rsem, to):
    return pltpu.make_async_remote_copy(
        src_ref=src, dst_ref=dst, send_sem=ssem, recv_sem=rsem, device_id=to, device_id_type=MESH
    )


class Exchange:
    def __init__(self, reverse, state, decay, out, bufs, decays, ssem, rsem, start, width):
        self.sib_state, self.mine, self.got, self.back, self.back_got = bufs
        self.sib_decay, self.total, self.got_decay = decays
        self.state, self.decay, self.out, self.reverse = state, decay, out, reverse
        self.ssem, self.rsem = ssem, rsem
        self.chips = lax.axis_size("seq") // SEQS
        self.rows = STATE // self.chips
        self.width = width
        place, core = lax.axis_index("seq"), lax.axis_index("head")
        self.core = core
        self.chip, self.which = place // SEQS, place % SEQS
        self.sibling = (place, 1 - core)
        self.later = (1 - core if reverse else core) == 1
        self.own_cols = lanes(core * (INNER // 2) + start, width)
        self.sib_cols = lanes((1 - core) * (INNER // 2) + start, width)

    def peer(self, k):
        return (lax.rem(self.chip + k, self.chips) * SEQS + self.which, self.core)

    def send(self, copies):
        for src, dst, n, to in copies:
            remote(src, dst, self.ssem.at[n % 2], self.rsem.at[n], to).start()

    def arrive(self, *whole):
        for src, dst, n in whole:
            remote(src, dst, self.ssem.at[n % 2], self.rsem.at[n], self.sibling).wait()

    def begin(self):
        copies = [(self.state.at[:, self.sib_cols], self.sib_state, 0, self.sibling)]
        if not self.reverse:
            copies.append((self.decay.at[0:8, self.sib_cols], self.sib_decay, 1, self.sibling))
        self.send(copies)

    def ordered(self):
        own, other = self.state[:, self.own_cols], self.sib_state[...]
        own_decay, other_decay = self.decay[0:1, self.own_cols], self.sib_decay[0:1, :]
        later = self.later
        return (
            jnp.where(later, other, own),
            jnp.where(later, own, other),
            jnp.where(later, other_decay, own_decay),
            jnp.where(later, own_decay, other_decay),
        )

    def deal(self):
        whole = [(self.state.at[:, self.sib_cols], self.sib_state, 0)]
        if not self.reverse:
            whole.append((self.decay.at[0:8, self.sib_cols], self.sib_decay, 1))
        self.arrive(*whole)
        early, late, early_decay, late_decay = self.ordered()
        self.mine[...] = (late_decay * early + late).astype(bf16)
        if not self.reverse:
            self.total[...] = jnp.broadcast_to(early_decay * late_decay, self.total.shape)
        copies = []
        for k in range(1, self.chips):
            to = lax.rem(self.chip + k, self.chips)
            piece = pl.ds(pl.multiple_of(to * self.rows, self.rows), self.rows)
            copies.append((self.mine.at[piece], self.got.at[k], 2, self.peer(k)))
            if not self.reverse:
                copies.append((self.total, self.got_decay.at[k], 3, self.peer(k)))
        self.send(copies)
        self.got[0] = self.mine[pl.ds(pl.multiple_of(self.chip * self.rows, self.rows), self.rows), :]
        if not self.reverse:
            self.got_decay[0] = self.total[...]

    def scan(self):
        others = slice(1, self.chips)
        whole = [(self.got.at[others], self.got.at[others], 2)]
        if not self.reverse:
            whole.append((self.got_decay.at[others], self.got_decay.at[others], 3))
        self.arrive(*whole)
        chips, chip = self.chips, self.chip

        def one(i, carry):
            source = chips - 1 - i if self.reverse else i
            slot = lax.rem(chip - source + chips, chips)
            to = lax.rem(source - chip + chips, chips)
            self.back[pl.ds(to, 1)] = carry.astype(bf16)[None]
            return self.got_decay[pl.ds(slot, 1)][0, 0:1, :] * carry + self.got[pl.ds(slot, 1)][0].astype(f32)

        lax.fori_loop(0, chips, one, jnp.zeros((self.rows, self.width), f32))
        here = pl.ds(pl.multiple_of(chip * self.rows, self.rows), self.rows)
        self.send([(self.back.at[k], self.back_got.at[here], 4, self.peer(k)) for k in range(1, chips)])
        self.back_got[here, :] = self.back[0]

    def hand(self):
        self.arrive((self.back.at[1 : self.chips], self.back.at[1 : self.chips], 4))
        early, _, early_decay, _ = self.ordered()
        enter = self.back_got[...].astype(f32)
        second = early_decay * enter + early
        self.out[:, self.own_cols] = jnp.where(self.later, second, enter).astype(bf16)
        self.mine[...] = jnp.where(self.later, enter, second).astype(bf16)
        self.send([(self.mine, self.out.at[:, self.own_cols], 6, self.sibling)])

    def end(self):
        self.arrive((self.mine, self.mine, 6))


def exchange_scratch(chips, width):
    rows = STATE // chips
    states = [((STATE, width), f32), ((STATE, width), bf16), ((chips, rows, width), bf16)]
    states += [((chips, rows, width), bf16), ((STATE, width), bf16)]
    decays = [((8, width), f32), ((8, width), f32), ((chips, 8, width), f32)]
    return states, decays


ORDERS = (
    ("x", "y", "z1", "z2"),
    ("z1", "y", "x", "z2"),
    ("x", "z1", "y", "z2"),
    ("x", "y", "z2", "z1"),
    ("x", "y", "z1", "z2"),
    ("y", "x", "z2", "z1"),
    ("z1", "y", "x", "z2"),
    ("y", "x", "z1", "z2"),
    ("x", "y", "z1", "z2"),
    ("z1", "y", "x", "z2"),
    ("y", "z1", "x", "z2"),
    ("x", "y", "z1", "z2"),
    ("y", "z1", "z2", "x"),
    ("x", "z2", "y", "z1"),
    ("y", "z2", "x", "z1"),
)
SCHEDULE = {
    "g2": (
        2, 1,
    ),
    "o2": (
        2, 5,
    ),
    "b1": (
        1, 5, 0,
    ),
    "b2": (
        3,
    ),
    "b3": (
        4, 0,
    ),
    "s": (
        2,
    ),
    "e": (
        5, 1, 3, 0,
    ),
    "h": (
        4, 2,
    ),
    "c1": (
        5, 1, 0,
    ),
    "c2": (
        2, 3,
    ),
    "r1": (
        6, 8, 1, 5, 7, 4, 8, 7, 0,
    ),
    "v2": (
        2, 6,
    ),
    "v3": (
        5,
    ),
    "r2": (
        9, 1, 11, 4, 10, 9, 11, 8, 6, 7, 2, 10, 3, 6, 8, 9, 7, 0, 11, 1, 5, 4, 10,
    ),
    "e1": (
        2, 7,
    ),
    "e2": (
        0, 11, 6, 3, 9, 10, 8, 5, 4,
    ),
    "r3": (
        11, 7, 0, 12, 2, 6, 3, 4, 13,
    ),
    "z": (
        14, 8, 10, 12, 9, 1, 13, 7, 14, 11, 4, 3, 10, 12, 6, 2, 13, 14, 9, 7, 5, 8, 3, 0, 11, 1, 10, 6, 9, 8,
        0, 13, 12, 7, 4, 14, 10, 11, 9, 3, 13, 3, 5, 14, 12, 8, 10, 6, 11, 9, 1, 4, 13, 8, 6, 12, 7, 10, 11,
        14, 9,
    ),
}
STEPS = {"x": 1, "y": 2, "z1": 4, "z2": 8}
STAGES = 9


def bits_of():
    place = lax.axis_index("seq")
    return {
        "c": lax.axis_index("head"),
        "x": place % 2,
        "y": place // 2 % 2,
        "z1": place // 4 % 2,
        "z2": place // 8,
    }


def partner(d):
    place, core = lax.axis_index("seq"), lax.axis_index("head")
    if d == "c":
        return (place, 1 - core)
    return (place + STEPS[d] * (1 - 2 * bits_of()[d]), core)


class Sum:
    def __init__(self, held, got, out, ssem, rsem, lsem, orders):
        self.streams = [self.stream(held, got, out, ssem, rsem, lsem, s, order) for s, order in enumerate(orders)]
        self.stages = [-1] * len(orders)

    def stream(self, held, got, out, ssem, rsem, lsem, s, order):
        rows = held.shape[0]
        bits = bits_of()
        cols = slice(s * 256, (s + 1) * 256)
        order = ("c",) + order
        keeps, sends = [], []
        off, size = 0, rows
        for d in order[:4]:
            size //= 2
            keeps.append(off + bits[d] * size)
            sends.append(off + (1 - bits[d]) * size)
            off = keeps[-1]
        unit = rows // 16
        sizes = [rows // 2, rows // 4, rows // 8, unit, unit]
        slots = [0, rows // 2, rows // 2 + rows // 4, rows - 2 * unit, rows - unit]

        def at(start, size):
            return pl.ds(pl.multiple_of(start, 16), size)

        def copy(stage):
            if stage < 5:
                d = order[stage]
                where = at(sends[stage] if stage < 4 else off, sizes[stage])
                src, dst = held.at[where, cols], got.at[slice(slots[stage], slots[stage] + sizes[stage]), cols]
            else:
                d = order[8 - stage]
                where = at(keeps[8 - stage], sizes[8 - stage])
                src, dst = (held if stage == 5 else out).at[where, cols], out.at[where, cols]
            return remote(src, dst, ssem.at[s], rsem.at[s, stage], partner(d))

        def add(stage):
            where = keeps[stage] if stage < 4 else off

            @pl.loop(0, sizes[stage] // unit)
            def _(i):
                here = at(where + i * unit, unit)
                held[here, cols] = held[here, cols] + got[at(slots[stage] + i * unit, unit), cols]

        def place():
            return pltpu.make_async_copy(held.at[at(off, unit), cols], out.at[at(off, unit), cols], lsem.at[s])

        return copy, add, place

    def tick(self, s):
        copy, add, place = self.streams[s]
        stage = self.stages[s]
        if 0 <= stage < STAGES:
            copy(stage).wait()
            if stage < 5:
                add(stage)
        if stage == 4:
            place().start()
        if stage == 5:
            place().wait()
        if stage + 1 < STAGES:
            copy(stage + 1).start()
        self.stages[s] = stage + 1


class Swap:
    def __init__(self, held, got, ssem, rsem, orders):
        self.held, self.got, self.ssem, self.rsem = held, got, ssem, rsem
        self.orders = [("c",) + order for order in orders]
        self.stages = [-1] * len(orders)

    def tick(self, s):
        cols = slice(s * 256, (s + 1) * 256)
        order, stage = self.orders[s], self.stages[s]

        def copy(k):
            return remote(
                self.held.at[:, cols], self.got.at[k, :, cols], self.ssem.at[s], self.rsem.at[s, k], partner(order[k])
            )

        if 0 <= stage < len(order):
            copy(stage).wait()
            self.held[:, cols] = self.held[:, cols] + self.got[stage, :, cols]
        if stage + 1 < len(order):
            copy(stage + 1).start()
        self.stages[s] = stage + 1


def greet():
    place, core = lax.axis_index("seq"), lax.axis_index("head")
    pieces = lax.axis_size("seq")
    chips = pieces // SEQS
    barrier = pltpu.get_barrier_semaphore()
    peers = [partner(d) for d in ("c", "x", "y", "z1", "z2")]
    peers += [((place // SEQS + k) % chips * SEQS + place % SEQS, core) for k in range(1, chips)]
    peers += [block_at(1), block_at(-1)]
    for to in peers:
        pl.semaphore_signal(barrier, inc=1, device_id=to, device_id_type=MESH)
    return barrier, len(peers)


def block_at(ahead):
    place, core = lax.axis_index("seq"), lax.axis_index("head")
    pieces = lax.axis_size("seq")
    block = (place // SEQS * 2 + core + ahead + pieces) % pieces
    return (block // 2 * SEQS + place % SEQS, block % 2)


def whole_kernel(names, *refs):
    r = Refs(names, refs)
    rows = r.blk.shape[0]
    greeted = greet()
    loads = [
        pltpu.make_async_copy(r.w_in_hbm.at[INNER:], r.w_in.at[INNER:], r.load_sem.at[0]),
        pltpu.make_async_copy(r.w_in_hbm.at[:INNER], r.w_in.at[:INNER], r.load_sem.at[1]),
        pltpu.make_async_copy(r.w_out_hbm, r.w_out, r.load_sem.at[2]),
    ]
    for c in loads:
        c.start()
    r.gain[...] = r.norm_gain[...].reshape(1, D)
    r.conv_b[...] = r.conv_bias[...].reshape(1, XBC)
    r.gate_gain[...] = r.gated_gain[...].reshape(1, INNER)
    r.heads[...] = jnp.zeros((8, 128), f32)
    for k, one in enumerate((r.dt_bias, r.a_log, r.d_skip)):
        r.heads[k : k + 1, 0:HEADS] = one[...].reshape(1, HEADS)
    place, core = lax.axis_index("seq"), lax.axis_index("head")
    chips = lax.axis_size("seq") // SEQS
    block = place // SEQS * 2 + core

    def norm(v):
        v = v.astype(f32)
        scale = lax.rsqrt(jnp.mean(v * v, axis=-1, keepdims=True) + EPS)
        return (v * scale * r.gain[...]).astype(bf16)

    r.normed[...] = norm(r.blk[...])
    lane = iota((rows, 128), 1)
    keep = valid_rows(r.lengths, rows, 128)
    pick_lane = iota((128, 256), 1)
    pick_head = iota((128, 256), 0)
    left = one_hot(iota((1, 128), 1) < HEAD_DIM)
    right = one_hot(iota((1, 128), 1) >= HEAD_DIM)

    loads[0].wait()

    def project(i, carry):
        part = dot(r.normed[...], r.w_in[pl.ds(pl.multiple_of(INNER + i * 256, 256), 256), :], NT)
        r.pad[16:, lanes(i * 256, 256)] = part.astype(bf16).astype(f32)
        return carry

    lax.fori_loop(0, XBC // 256, project, 0, unroll=7)
    pl.semaphore_wait(*greeted)
    edge = remote(r.pad.at[rows + 8 :], r.pad.at[8:16], r.edge_sem.at[0], r.edge_sem.at[1], block_at(1))
    edge.start()

    r.head[3] = jnp.zeros((rows, 128), f32)
    r.head[3, :, 0:HEADS] = dot(r.normed[...], r.w_in[INNER + XBC :, :], NT).astype(bf16).astype(f32)
    moved = r.head[3] + r.heads[0:1, :]
    soft = jnp.maximum(moved, 0.0) + jnp.log1p(jnp.exp(-jnp.abs(moved)))
    dt = jnp.where(lane < HEADS, soft * keep, 0.0)
    rates = -jnp.exp(r.heads[1:2, :])
    below = one_hot(iota((rows, rows), 0) >= iota((rows, rows), 1))
    cum = split_dot_left(below, dt) * rates
    cum2 = cum * LOG2E
    r.head[0] = dt
    r.head[1] = cum
    r.head[2] = sigmoid(moved) * keep
    r.head[3] = cum2
    r.cumt[...] = cum2.T

    def widen(i, carry):
        cols = lanes(i * 128, 128)
        pick = one_hot((iota((128, 128), 1) >> 6) + 2 * i == iota((128, 128), 0))
        r.dt_wide[:, cols] = split_dot(r.head[0], pick)
        wide = split_dot(r.head[3], pick)
        last = wide[rows - 1 : rows, :]
        r.grow[:, cols] = jnp.exp2(wide)
        r.fall[:, cols] = jnp.exp2(last - wide)
        r.spread[0:8, cols] = jnp.broadcast_to(jnp.exp2(last), (8, 128))
        r.spread[8:16, cols] = split_dot(jnp.broadcast_to(r.heads[2:3, :], (8, 128)), pick)
        return carry

    lax.fori_loop(0, PAIRS, widen, 0, unroll=2)

    edge.wait()
    r.pad[8:16, :] = jnp.where(block == 0, 0.0, r.pad[8:16, :])

    def convolve(start, width):
        cols = lanes(start, width)
        running = r.conv_b[:, cols] + r.pad[13 : 13 + rows, cols] * r.conv_w[0:1, cols]
        for tap in range(1, CONV):
            running = running + r.pad[13 + tap : 13 + tap + rows, cols] * r.conv_w[tap : tap + 1, cols]
        r.run[:, cols] = running
        return running * sigmoid(running)

    act = convolve(INNER, 2 * STATE)
    r.b[...] = act[:, :STATE].astype(bf16)
    r.c[...] = act[:, STATE:].astype(bf16)
    third = 3 * 128

    def channels(start):
        def one(i, carry):
            at = start + i * 128
            cols = lanes(at, 128)
            x = convolve(at, 128) * keep
            r.x[:, cols] = x
            xd = x * r.dt_wide[:, cols]
            r.xd[:, cols] = xd.astype(bf16)
            r.xde[:, cols] = (xd * r.fall[:, cols]).astype(bf16)
            return carry

        lax.fori_loop(0, third // 128, one, 0, unroll=3)
        r.own[:, start : start + third] = dot(r.b[...], r.xde[:, start : start + third], TN)

    def exchanges(reverse, state, out, tag):
        made = []
        for k in range(SPLITS):
            bufs = [getattr(r, f"{tag}{k}_{n}") for n in range(5)]
            decays = [getattr(r, f"d{k}_{n}") for n in range(3)]
            sems = getattr(r, f"{tag}s").at[k], getattr(r, f"{tag}r").at[k]
            width = INNER // 2 // SPLITS
            made.append(Exchange(reverse, state, r.spread, out, bufs, decays, *sems, k * width, width))
        return made

    enters = exchanges(False, r.own, r.enter, "f")
    leaves = exchanges(True, r.adj, r.leave, "g")
    channels(0)
    channels(INNER // 2)
    enters[0].begin()
    channels(third)
    enters[0].deal()
    channels(INNER // 2 + third)
    enters[1].begin()

    def spread(i, carry):
        r.cumb[:, lanes(i * 256, 256)] = split_dot(r.head[3], one_hot((pick_lane >> 7) + 2 * i == pick_head))
        return carry


    causal = iota((rows, rows), 0) >= iota((rows, rows), 1)
    r.scores[...] = jnp.where(causal, dot(r.c[...], r.b[...], NT), 0.0)
    lax.fori_loop(0, 4, spread, 0, unroll=2)
    enters[1].deal()
    lax.fori_loop(4, PAIRS, spread, 0, unroll=2)
    loads[1].wait()

    def gates(i, carry):
        part = dot(r.normed[...], r.w_in[pl.ds(pl.multiple_of(i * 256, 256), 256), :], NT)
        r.gate[:, lanes(i * 256, 256)] = part.astype(bf16)
        return carry

    def columns(i):
        c0 = r.cumb[:, lanes(i * 256, 128)]
        c1 = r.cumb[:, lanes(i * 256 + 128, 128)]
        return c0, c1

    def pair(i, carry):
        cols = lanes(i * 128, 128)
        xd = r.xd[:, cols]
        y = None
        for cc, part, mask in zip(columns(i), (0, 1), (left, right), strict=True):
            row = r.cumt[pl.ds(2 * i + part, 1), :]
            decay = jnp.exp2(jnp.minimum(jnp.concatenate([cc] * (rows // 128), axis=1) - row, 0.0))
            term = dot((decay * r.scores[...]).astype(bf16), xd * mask)
            y = term if y is None else y + term
        r.y[:, cols] = y
        return carry

    lax.fori_loop(0, INNER // 256, gates, 0, unroll=2)
    enters[0].scan()
    lax.fori_loop(0, 6, pair, 0, unroll=2)
    enters[1].scan()
    lax.fori_loop(6, PAIRS, pair, 0, unroll=2)

    def slopes(i, carry):
        cols = lanes(i * 128, 128)
        running = r.run[:, cols]
        sg = sigmoid(running)
        r.run[:, cols] = sg * (1.0 + running * (1.0 - sg))
        return carry

    lax.fori_loop(0, XBC // 128, slopes, 0, unroll=2)
    keep_d = valid_rows(r.lengths, rows, D)
    r.db[...] = (r.gout[...].astype(f32) * keep_d).astype(bf16)
    loads[2].wait()
    r.wide[...] = dot(r.db[...], r.w_out[...], NT)
    for one in enters:
        one.hand()
    for one in enters:
        one.end()

    def carried(i, carry):
        cols = lanes(i * 128, 128)
        y = r.y[:, cols] + r.grow[:, cols] * dot(r.c[...], r.enter[:, cols])
        r.y[:, cols] = y
        r.mixed[:, cols] = (y + r.spread[8:9, cols] * r.x[:, cols]).astype(bf16)
        return carry

    lax.fori_loop(0, PAIRS, carried, 0, unroll=2)

    r.ggain[...] = jnp.zeros_like(r.ggain)
    step = 16

    def gating(i, carry):
        at = pl.ds(pl.multiple_of(i * step, step), step)
        g = r.gate[at, :].astype(f32)
        sg = sigmoid(g)
        mixed = r.mixed[at, :].astype(f32)
        gated = mixed * g * sg
        scale = lax.rsqrt(jnp.mean(gated * gated, axis=-1, keepdims=True) + EPS)
        r.gn[at, :] = (gated * scale * r.gate_gain[...]).astype(bf16)
        dgn = r.wide[at, :]
        r.ggain[...] += jnp.sum((dgn * gated * scale).reshape(step // 8, 8, INNER), axis=0)
        weighted = dgn * r.gate_gain[...]
        average = jnp.mean(weighted * gated, axis=-1, keepdims=True)
        d_gated = scale * weighted - gated * (scale * scale * scale) * average
        dy = (d_gated * g * sg).astype(bf16)
        r.dy[at, :] = dy
        r.dye[at, :] = (dy.astype(f32) * r.grow[at, :]).astype(bf16)
        r.dgate[at, :] = (d_gated * mixed * sg * (1.0 + g * (1.0 - sg))).astype(bf16)
        return carry

    lax.fori_loop(0, rows // step, gating, 0, unroll=2)

    r.adj[...] = dot(r.c[...], r.dye[...], TN)
    for one in leaves:
        one.begin()

    def gate_grads(i, carry):
        at = pl.ds(pl.multiple_of(i * 256, 256), 256)
        r.first[at, :] = dot(r.dgate[:, lanes(i * 256, 256)], r.normed[...], TN).astype(bf16)
        return carry

    def out_grads(i, carry):
        at = pl.ds(pl.multiple_of(INNER + i * 256, 256), 256)
        r.first[at, :] = dot(r.gn[:, lanes(i * 256, 256)], r.db[...], TN).astype(bf16)
        return carry

    def part(k, held, got, out, at):
        return Sum(held.at[at], got.at[at], out.at[at], r.ss.at[k], r.rs.at[k], r.ls.at[k], ORDERS[3 * k : 3 * k + 3])

    sums = [
        part(0, r.first, r.got_first, r.first_out, slice(0, INNER)),
        part(1, r.first, r.got_first, r.first_out, slice(INNER, FIRST_ROWS)),
        part(2, r.rest, r.got_rest, r.rest_out, slice(0, D)),
        part(3, r.rest, r.got_rest, r.rest_out, slice(D, REST_ROWS)),
        Swap(r.vec, r.got_vec, r.vs, r.vr, ORDERS[12:15]),
    ]
    def slot(name):
        for n in SCHEDULE.get(name, ()):
            sums[n // 3].tick(n % 3)

    lax.fori_loop(0, INNER // 256, gate_grads, 0, unroll=2)
    slot("g2")
    for one in leaves:
        one.deal()
    slot("d")
    lax.fori_loop(0, INNER // 256, out_grads, 0, unroll=2)
    slot("o2")
    r.block_out[...] = (r.blk[...].astype(f32) + keep_d * dot(r.gn[...], r.w_out[...])).astype(bf16)
    stores = [
        pltpu.make_async_copy(r.block_out, r.block_out_hbm, r.store_sem.at[0]),
        pltpu.make_async_copy(r.grad_in, r.grad_in_hbm, r.store_sem.at[1]),
    ]
    stores[0].start()
    slot("b0")

    r.scores_t[...] = jnp.where(
        iota((rows, rows), 1) >= iota((rows, rows), 0), dot(r.b[...], r.c[...], NT), 0.0
    )

    r.dscores[...] = jnp.zeros_like(r.dscores)
    r.q[...] = jnp.zeros_like(r.q)
    r.ry[...] = jnp.zeros_like(r.ry)
    row_head = iota((128, 128), 0)
    col_head = iota((128, 128), 1)

    def pair_back(i, carry):
        cols = lanes(i * 128, 128)
        xd, dy = r.xd[:, cols], r.dy[:, cols]
        v = None
        for cc, part, mask in zip(columns(i), (0, 1), (left, right), strict=True):
            row = r.cumt[pl.ds(2 * i + part, 1), :]
            decay = jnp.exp2(jnp.minimum(row - jnp.concatenate([cc] * (rows // 128), axis=1), 0.0))
            masked = dy * mask
            term = dot((decay * r.scores_t[...]).astype(bf16), masked)
            v = term if v is None else v + term
            r.dscores[...] += decay * dot(xd, masked, NT)
        r.wide[:, cols] = v
        r.ry[...] += split_dot(dy.astype(f32) * r.y[:, cols], one_hot((row_head >> 6) + 2 * i == col_head))
        return carry

    lax.fori_loop(0, 4, pair_back, 0, unroll=2)
    slot("b1")
    lax.fori_loop(4, 8, pair_back, 0, unroll=2)
    slot("b2")
    lax.fori_loop(8, PAIRS, pair_back, 0, unroll=2)
    slot("b3")
    for one in leaves:
        one.scan()
    slot("s")
    dsc = jnp.where(iota((rows, rows), 1) >= iota((rows, rows), 0), r.dscores[...], 0.0).astype(bf16)
    d_b = dot(dsc, r.c[...])
    d_c = dot(dsc, r.b[...], TN) + dot(r.dye[...], r.enter[...], NT)
    slot("e")
    for one in leaves:
        one.hand()
    slot("h")
    for one in leaves:
        one.end()
    slot("l")

    def channels_back(i, carry):
        cols = lanes(i * 128, 128)
        v = r.wide[:, cols] + r.fall[:, cols] * dot(r.b[...], r.leave[:, cols])
        x = r.x[:, cols]
        dy = r.dy[:, cols].astype(f32)
        r.q[...] += split_dot(x * v, one_hot((row_head >> 6) + 2 * i == col_head))
        r.skip[:, cols] = jnp.sum((dy * x).reshape(rows // 8, 8, 128), axis=0)
        r.ext[0:rows, cols] = (r.dt_wide[:, cols] * v + r.spread[8:9, cols] * dy) * keep * r.run[:, cols]
        return carry

    def conv_back(i, carry):
        cols = lanes(i * 128, 128)
        drun = r.ext[0:rows, cols]
        total = drun * r.conv_w[CONV - 1 : CONV, cols]
        for tap in range(CONV - 1):
            ahead = CONV - 1 - tap
            total = total + r.ext[ahead : ahead + rows, cols] * r.conv_w[tap : tap + 1, cols]
        r.dproj[:, cols] = total.astype(bf16)
        for tap in range(CONV):
            r.tap_sums[tap : tap + 1, cols] = jnp.sum(
                drun * r.pad[13 + tap : 13 + tap + rows, cols], axis=0, keepdims=True
            )
        r.tap_sums[CONV : CONV + 1, cols] = jnp.sum(drun, axis=0, keepdims=True)
        return carry

    def rest_grads(i, carry):
        at = pl.ds(pl.multiple_of(i * 256, 256), 256)
        r.rest[at, :] = dot(r.dproj[:, lanes(i * 256, 256)], r.normed[...], TN).astype(bf16)
        return carry

    halves = (slice(0, INNER // 2), slice(INNER // 2, XBC))

    def edges(k):
        cols = halves[k]
        sems = r.edge_sem.at[2 + 2 * k], r.edge_sem.at[3 + 2 * k]
        return remote(r.ext.at[0:8, cols], r.edge_grad.at[:, cols], *sems, block_at(-1))

    def edge_in(k):
        edges(k).wait()
        r.ext[rows : rows + 8, halves[k]] = jnp.where(block == chips * 2 - 1, 0.0, r.edge_grad[:, halves[k]])

    lax.fori_loop(0, PAIRS // 2, channels_back, 0, unroll=2)
    edges(0).start()
    slot("c1")
    lax.fori_loop(PAIRS // 2, PAIRS, channels_back, 0, unroll=2)
    d_b = d_b + dot(r.xde[...], r.leave[...], NT)
    r.ext[0:rows, INNER : INNER + STATE] = d_b * r.run[:, INNER : INNER + STATE]
    r.ext[0:rows, INNER + STATE :] = d_c * r.run[:, INNER + STATE :]
    edges(1).start()
    slot("c2")

    edge_in(0)
    slot("c3")
    lax.fori_loop(0, 6, conv_back, 0, unroll=2)
    slot("v1")
    lax.fori_loop(0, 3, rest_grads, 0, unroll=3)
    slot("r1")
    edge_in(1)
    slot("v2")
    lax.fori_loop(6, XBC // 128, conv_back, 0, unroll=2)
    slot("v3")
    lax.fori_loop(3, XBC // 256, rest_grads, 0, unroll=2)
    slot("r2")
    full_pick = one_hot((iota((INNER, 128), 0) >> 6) == iota((INNER, 128), 1))
    out_state = r.spread[0:1, :] * r.enter[...].astype(f32) + r.own[...]
    d_last = split_dot(
        jnp.sum((r.leave[...].astype(f32) * out_state).reshape(STATE // 8, 8, INNER), axis=0), full_pick
    )
    d_last = jnp.sum(d_last, axis=0, keepdims=True)
    q = r.q[...]
    d_cum = r.ry[...] - r.head[0] * q + jnp.where(iota((rows, 128), 0) == rows - 1, d_last, 0.0)
    above = one_hot(iota((rows, rows), 0) <= iota((rows, rows), 1))
    dz = (q + split_dot_left(above, d_cum * -jnp.exp(r.heads[1:2, :]))) * r.head[2]
    r.vec[...] = jnp.zeros_like(r.vec)
    r.vec[42:43, 0:128] = jnp.sum(dz, axis=0, keepdims=True)
    r.vec[43:44, 0:128] = jnp.sum(d_cum * r.head[1], axis=0, keepdims=True)
    r.vec[44:45, 0:128] = jnp.sum(split_dot(r.skip[...], full_pick), axis=0, keepdims=True)
    dz = dz.astype(bf16)
    slot("e1")
    d_normed = dot(r.dgate[...], r.w_in[:INNER, :])
    d_normed = d_normed + dot(dz[:, :HEADS], r.w_in[INNER + XBC :, :])
    d_normed = d_normed + dot(r.dproj[...], r.w_in[INNER : INNER + XBC, :])
    slot("e2")
    for v in range(CONV + 1):
        for part in range(3):
            width = min(D, XBC - part * D)
            r.vec[HEADS + 3 * v + part : HEADS + 3 * v + part + 1, 0:width] = r.tap_sums[v : v + 1, part * D : part * D + width]
    src = r.blk[...].astype(f32)
    scale = lax.rsqrt(jnp.mean(src * src, axis=-1, keepdims=True) + EPS)
    r.vec[39:40, :] = jnp.sum(d_normed * src * scale, axis=0, keepdims=True)
    gate_gain = jnp.sum(r.ggain[...], axis=0, keepdims=True)
    r.vec[40:41, :] = gate_gain[:, :D]
    r.vec[41:42, :] = gate_gain[:, D:]
    r.vec[0:HEADS, :] = dot(dz, r.normed[...], TN)[0:HEADS, :]
    slot("r3")
    weighted = d_normed * r.gain[...]
    average = jnp.mean(weighted * src, axis=-1, keepdims=True)
    r.grad_in[...] = r.gout[...].astype(f32) + scale * weighted - src * (scale * scale * scale) * average
    stores[1].start()
    slot("z")
    out = pltpu.make_async_copy(r.vec, r.vec_out, r.store_sem.at[2])
    out.start()
    for c in (*stores, out):
        c.wait()


def whole(*args):
    t = args[0].shape[0]
    chips = lax.axis_size("seq") // SEQS
    ins = ["blk", "gout", "lengths", "norm_gain", "w_in_hbm", "conv_w", "conv_bias", "dt_bias", "a_log", "d_skip"]
    ins += ["gated_gain", "w_out_hbm"]
    outs = {
        "block_out_hbm": ((t, D), bf16),
        "grad_in_hbm": ((t, D), f32),
        "first_out": ((FIRST_ROWS, D), bf16),
        "rest_out": ((REST_ROWS, D), bf16),
        "vec_out": ((VEC_ROWS, D), f32),
    }
    held = {
        "block_out": ((t, D), bf16),
        "grad_in": ((t, D), f32),
        "first": ((FIRST_ROWS, D), bf16),
        "rest": ((REST_ROWS, D), bf16),
        "gain": ((1, D), f32),
        "conv_b": ((1, XBC), f32),
        "gate_gain": ((1, INNER), f32),
        "heads": ((8, 128), f32),
        "w_in": ((PROJ, D), bf16),
        "w_out": ((INNER, D), bf16),
        "edge_grad": ((8, XBC), f32),
        "normed": ((t, D), bf16),
        "gate": ((t, INNER), bf16),
        "pad": ((t + 16, XBC), f32),
        "run": ((t, XBC), f32),
        "x": ((t, INNER), f32),
        "xd": ((t, INNER), bf16),
        "xde": ((t, INNER), bf16),
        "b": ((t, STATE), bf16),
        "c": ((t, STATE), bf16),
        "head": ((4, t, 128), f32),
        "cumt": ((128, t), f32),
        "cumb": ((t, HEADS * 128), f32),
        "spread": ((16, INNER), f32),
        "own": ((STATE, INNER), f32),
        "enter": ((STATE, INNER), bf16),
        "y": ((t, INNER), f32),
        "grow": ((t, INNER), f32),
        "fall": ((t, INNER), f32),
        "dt_wide": ((t, INNER), f32),
        "mixed": ((t, INNER), bf16),
        "gn": ((t, INNER), bf16),
        "wide": ((t, INNER), f32),
        "db": ((t, D), bf16),
        "dy": ((t, INNER), bf16),
        "dye": ((t, INNER), bf16),
        "dgate": ((t, INNER), bf16),
        "ggain": ((8, INNER), f32),
        "adj": ((STATE, INNER), f32),
        "leave": ((STATE, INNER), bf16),
        "scores": ((t, t), f32),
        "scores_t": ((t, t), f32),
        "dscores": ((t, t), f32),
        "skip": ((8, INNER), f32),
        "q": ((t, 128), f32),
        "ry": ((t, 128), f32),
        "ext": ((t + 8, XBC), f32),
        "dproj": ((t, XBC), bf16),
        "vec": ((VEC_ROWS, D), f32),
        "got_vec": ((5, VEC_ROWS, D), f32),
        "tap_sums": ((8, XBC), f32),
        "got_first": ((FIRST_ROWS, D), bf16),
        "got_rest": ((REST_ROWS, D), bf16),
    }
    names = ins + list(outs) + list(held)
    scratch = [pltpu.VMEM(s, d) for s, d in held.values()]
    states, decays = exchange_scratch(chips, INNER // 2 // SPLITS)
    for tag, shapes in (("f", states), ("g", states), ("d", decays)):
        for k in range(SPLITS):
            scratch += [pltpu.VMEM(s, d) for s, d in shapes]
            names += [f"{tag}{k}_{n}" for n in range(len(shapes))]
    semaphores = {
        "ss": (WAVES, 3),
        "rs": (WAVES, 3, STAGES),
        "ls": (WAVES, 3),
        "fs": (SPLITS, 2),
        "fr": (SPLITS, 7),
        "gs": (SPLITS, 2),
        "gr": (SPLITS, 7),
        "edge_sem": (6,),
        "load_sem": (3,),
        "store_sem": (3,),
        "vs": (3,),
        "vr": (3, 5),
    }
    for name, shape in semaphores.items():
        scratch.append(pltpu.SemaphoreType.DMA(shape))
        names.append(name)
    any_space = pl.BlockSpec(memory_space=pl.ANY)
    specs = {n: any_space for n in ("w_in_hbm", "w_out_hbm", *outs)} | {"lengths": SMEM}
    return pl.pallas_call(
        partial(whole_kernel, names),
        out_shape=[jax.ShapeDtypeStruct(s, d) for s, d in outs.values()],
        in_specs=[specs.get(n, VMEM) for n in ins],
        out_specs=[specs.get(n, VMEM) for n in outs],
        scratch_shapes=scratch,
        compiler_params=pltpu.CompilerParams(vmem_limit_bytes=60 << 20, collective_id=0, has_side_effects=True),
    )(*args)


def finish_kernel(
    block_in,
    grad_in,
    first,
    rest,
    vec_in,
    block_out,
    grad_out,
    norm_out,
    w_in_out,
    conv_out,
    bias_out,
    dt_out,
    alog_out,
    skip_out,
    gate_out,
    w_out_out,
    held_first,
    held_rest,
    held_block,
    held_grad,
    vec,
    wide_in,
    wide_out,
    in_sem,
    out_sem,
    pass_sem,
):
    passed = [
        (pltpu.make_async_copy(src, by, pass_sem.at[n, 0]), pltpu.make_async_copy(by, dst, pass_sem.at[n, 1]))
        for n, (src, by, dst) in enumerate(((block_in, held_block, block_out), (grad_in, held_grad, grad_out)))
    ]
    chunks = [(first, held_first, k * 256, 256) for k in range(FIRST_ROWS // 256)]
    chunks += [(rest, held_rest, k * 256, 256) for k in range(REST_ROWS // 256)]
    loads = [
        pltpu.make_async_copy(src.at[start : start + size], dst.at[start : start + size], in_sem.at[n])
        for n, (src, dst, start, size) in enumerate(chunks)
    ]
    ahead = 8
    small = pltpu.make_async_copy(vec_in, vec, pass_sem.at[1, 2])
    for c in loads[:ahead] + [small] + [load for load, _ in passed]:
        c.start()
    stores = [store for _, store in passed]
    for n, (src, held, start, size) in enumerate(chunks):
        loads[n].wait()
        if n == ahead:
            for load, store in passed:
                load.wait()
                store.start()
        if n + ahead < len(loads):
            loads[n + ahead].start()
        if src is first and start >= INNER:
            wide, out, at = wide_out, w_out_out, start - INNER
        else:
            wide, out, at = wide_in, w_in_out, start if src is first else INNER + start
        wide[at : at + size, :] = held[start : start + size, :].astype(f32)
        c = pltpu.make_async_copy(wide.at[at : at + size], out.at[at : at + size], out_sem.at[n])
        c.start()
        stores.append(c)
    small.wait()
    wide_in[INNER + XBC :, :] = vec[0:HEADS, :]
    c = pltpu.make_async_copy(wide_in.at[INNER + XBC :], w_in_out.at[INNER + XBC :], pass_sem.at[0, 2])
    c.start()
    stores.append(c)

    def row(v):
        return jnp.concatenate([vec[HEADS + 3 * v + k : HEADS + 3 * v + k + 1, : min(D, XBC - k * D)] for k in range(3)], axis=1)

    for v in range(CONV):
        conv_out[v : v + 1, :] = row(v)
    bias_out[...] = row(CONV).reshape(XBC)
    norm_out[...] = vec[39:40, :].reshape(D)
    gate_out[...] = jnp.concatenate([vec[40:41, :], vec[41:42, :]], axis=1).reshape(INNER)
    for k, out in enumerate((dt_out, alog_out, skip_out)):
        out[...] = vec[42 + k : 43 + k, 0:HEADS].reshape(HEADS)
    for c in stores:
        c.wait()


def finish(block_out, grad_in, first, rest, vec):
    shapes = [block_out.shape, grad_in.shape, (D,), (PROJ, D), (CONV, XBC), (XBC,), (HEADS,), (HEADS,), (HEADS,), (INNER,)]
    shapes += [(INNER, D)]
    any_space = pl.BlockSpec(memory_space=pltpu.HBM)
    away = (0, 1, 3, 10)
    chunks = (FIRST_ROWS + REST_ROWS) // 256
    return pl.pallas_call(
        finish_kernel,
        out_shape=[jax.ShapeDtypeStruct(s, bf16 if k == 0 else f32) for k, s in enumerate(shapes)],
        in_specs=[any_space] * 5,
        out_specs=[any_space if k in away else VMEM for k in range(len(shapes))],
        scratch_shapes=[
            pltpu.VMEM((FIRST_ROWS, D), bf16),
            pltpu.VMEM((REST_ROWS, D), bf16),
            pltpu.VMEM(block_out.shape, bf16),
            pltpu.VMEM(grad_in.shape, f32),
            pltpu.VMEM((VEC_ROWS, D), f32),
            pltpu.VMEM((PROJ, D), f32),
            pltpu.VMEM((INNER, D), f32),
            pltpu.SemaphoreType.DMA((chunks,)),
            pltpu.SemaphoreType.DMA((chunks,)),
            pltpu.SemaphoreType.DMA((2, 3)),
        ],
        compiler_params=pltpu.CompilerParams(vmem_limit_bytes=60 << 20),
    )(block_out, grad_in, first, rest, vec)


def shifted(value, ahead):
    groups = lax.axis_size("head")
    count = lax.axis_size("seq") * groups
    moves = []
    for source in range(count):
        piece, half = source // groups, source % groups
        half += ahead
        if half == groups:
            half, piece = 0, piece + SEQS
        elif half < 0:
            half, piece = groups - 1, piece - SEQS
        if 0 <= piece * groups + half < count:
            moves.append((source, piece * groups + half))
    return lax.ppermute(value, ("seq", "head"), moves)


def by_parts(block_in, grad_out, lengths, norm_gain, w_in, conv_w, conv_b, dt_bias, a_log, d_skip, gate_gain, w_out):
    heads = jnp.pad(jnp.stack([dt_bias, a_log, d_skip]), ((0, 5), (0, 128 - HEADS)))
    gain, conv_b, gate_gain = norm_gain.reshape(1, D), conv_b.reshape(1, XBC), gate_gain.reshape(1, INNER)
    edge = shifted(block_in[-16:], 1)
    (normed, gate, pad, run, x, xd, xde, b, c, head, cumt, cumb, rows, own) = front(
        lengths, block_in, edge, gain, w_in, conv_w, conv_b, heads
    )
    enter = exchange_plain(own, rows[0:8], False)
    (y, block_out, dy, dye, dgate, ggain, adj, grads_a) = middle(
        lengths, block_in, grad_out, normed, gate, x, xd, b, c, cumt, cumb, rows, enter, gate_gain, w_out
    )
    leave = exchange_plain(adj, rows[0:8], True)
    drun, dz, small = back(
        lengths, y, dy, dye, x, xd, xde, b, c, run, cumt, cumb, head, rows, heads, enter, own, leave
    )
    edge_back = shifted(drun[0:8], -1)
    grad_in, grads_b, vec = last(
        block_in, grad_out, normed, gain, w_in, conv_w, pad, drun, edge_back, dz, dgate, ggain, small
    )
    grads_a, grads_b, vec = lax.psum((grads_a, grads_b, vec), ("seq", "head"))
    return block_out, grad_in, grads_a, grads_b, vec


def local(block_in, grad_out, lengths, norm_gain, w_in, *others):
    run = whole if lax.axis_size("seq") == 16 and lax.axis_size("head") == 2 else by_parts
    outs = finish(*run(block_in, grad_out, lengths, norm_gain, w_in.T, *others))
    return (*outs[:3], outs[3].T, *outs[4:])


def solution(mesh):
    rows = P(("seq", "head"), None)
    return jax.shard_map(
        local,
        mesh=mesh,
        in_specs=(rows, rows) + (P(),) * 10,
        out_specs=(rows, rows) + (P(),) * 9,
        check_vma=False,
    )
```

```python
from functools import partial

import jax
import jax.numpy as jnp
from jax import lax
from jax.experimental import pallas as pl
from jax.experimental.pallas import tpu as pltpu
from jax.sharding import PartitionSpec as P

D = 768
INNER = 1536
HEADS = 24
HEAD_DIM = 64
STATE = 128
CONV = 4
SEQS = 2
XBC = INNER + 2 * STATE
PROJ = 2 * INNER + 2 * STATE + HEADS
PAIRS = HEADS // 2
EPS = 1e-05
LOG2E = 1.4426950408889634

f32 = jnp.float32
bf16 = jnp.bfloat16
MESH = pl.DeviceIdType.MESH
VMEM = pl.BlockSpec(memory_space=pltpu.VMEM)
SMEM = pl.BlockSpec(memory_space=pltpu.SMEM)
NN = ((1,), (0,))
NT = ((1,), (1,))
TN = ((0,), (0,))


def dot(a, b, dims=NN):
    return lax.dot_general(a, b, (dims, ((), ())), preferred_element_type=f32)


def split_dot(a, pick, terms=3):
    total = None
    for _ in range(terms):
        part = a.astype(bf16)
        a = a - part.astype(f32)
        term = dot(part, pick)
        total = term if total is None else total + term
    return total


def split_dot_left(pick, a, terms=3):
    total = None
    for _ in range(terms):
        part = a.astype(bf16)
        a = a - part.astype(f32)
        term = dot(pick, part)
        total = term if total is None else total + term
    return total


def iota(shape, dim):
    return lax.broadcasted_iota(jnp.int32, shape, dim)


def one_hot(cond):
    return jnp.where(cond, 1.0, 0.0).astype(bf16)


def sigmoid(v):
    return 1.0 / (1.0 + jnp.exp(-v))


def lanes(start, size):
    return pl.ds(pl.multiple_of(start, 128), size)


def valid_rows(lengths_ref, rows, width):
    place = lax.axis_index("seq")
    first = (place // SEQS) * (rows * lax.axis_size("head")) + lax.axis_index("head") * rows
    limit = lengths_ref[place % SEQS]
    return jnp.where(iota((rows, width), 0) + first < limit, 1.0, 0.0)


def call(body, outs, args, scratch=(), smem=(), vmem=56 << 20, cost=None, **params):
    return pl.pallas_call(
        body,
        out_shape=[jax.ShapeDtypeStruct(s, d) for s, d in outs],
        in_specs=[SMEM if i in smem else VMEM for i in range(len(args))],
        out_specs=[VMEM] * len(outs),
        scratch_shapes=list(scratch),
        compiler_params=pltpu.CompilerParams(vmem_limit_bytes=vmem, **params),
    )(*args)


REST_ROWS = XBC
VEC_ROWS = 48
FIRST_ROWS = 2 * INNER
WAVES = 4
SPLITS = 2


def front_kernel(
    lengths_ref,
    blk,
    edge,
    gain,
    w_in,
    conv_w,
    conv_b,
    heads_ref,
    normed_out,
    gate_out,
    pad_out,
    run_out,
    x_out,
    xd_out,
    xde_out,
    b_out,
    c_out,
    head_out,
    cumt_out,
    cumb_out,
    rows_out,
    state_out,
):
    rows = blk.shape[0]

    def norm(v):
        v = v.astype(f32)
        scale = lax.rsqrt(jnp.mean(v * v, axis=-1, keepdims=True) + EPS)
        return (v * scale * gain[...]).astype(bf16)

    normed = norm(blk[...])
    normed_out[...] = normed
    gate_out[...] = dot(normed, w_in[:INNER, :], NT).astype(bf16)
    ahead = norm(edge[...])
    pad_out[0:16, :] = dot(ahead, w_in[INNER : INNER + XBC, :], NT).astype(bf16).astype(f32)
    pad_out[16 : 16 + rows, :] = dot(normed, w_in[INNER : INNER + XBC, :], NT).astype(bf16).astype(f32)
    keep = valid_rows(lengths_ref, rows, 128)
    head_out[3] = jnp.zeros((rows, 128), f32)
    head_out[3, :, 0:HEADS] = dot(normed, w_in[INNER + XBC :, :], NT).astype(bf16).astype(f32)
    lane = iota((rows, 128), 1)
    shifted = head_out[3] + heads_ref[0:1, :]
    soft = jnp.maximum(shifted, 0.0) + jnp.log1p(jnp.exp(-jnp.abs(shifted)))
    dt = jnp.where(lane < HEADS, soft * keep, 0.0)
    rates = -jnp.exp(heads_ref[1:2, :])
    below = one_hot(iota((rows, rows), 0) >= iota((rows, rows), 1))
    cum = split_dot_left(below, dt) * rates
    cum2 = cum * LOG2E
    head_out[0] = dt
    head_out[1] = cum
    head_out[2] = sigmoid(shifted) * keep
    head_out[3] = cum2
    cumt_out[...] = cum2.T
    pick_lane = iota((128, 256), 1)
    pick_head = iota((128, 256), 0)

    def spread(i, carry):
        cumb_out[:, lanes(i * 256, 256)] = split_dot(
            head_out[3], one_hot((pick_lane >> 7) + 2 * i == pick_head)
        )
        return carry

    lax.fori_loop(0, PAIRS, spread, 0)

    def convolve(i):
        cols = lanes(i * 256, 256)
        running = conv_b[:, cols] + pad_out[13 : 13 + rows, cols] * conv_w[0:1, cols]
        for tap in range(1, CONV):
            running = running + pad_out[13 + tap : 13 + tap + rows, cols] * conv_w[tap : tap + 1, cols]
        run_out[:, cols] = running
        return running * sigmoid(running)

    act = convolve(INNER // 256)
    b_out[...] = act[:, :STATE].astype(bf16)
    c_out[...] = act[:, STATE:].astype(bf16)
    keep2 = valid_rows(lengths_ref, rows, 256)

    def channels(i, carry):
        cols = lanes(i * 256, 256)
        pick = one_hot((pick_lane >> 6) + 4 * i == pick_head)
        x = convolve(i) * keep2
        x_out[:, cols] = x
        xd = x * split_dot(head_out[0], pick)
        xd_out[:, cols] = xd.astype(bf16)
        wide = split_dot(head_out[3], pick)
        last = wide[rows - 1 : rows, :]
        xde_out[:, cols] = (xd * jnp.exp2(last - wide)).astype(bf16)
        rows_out[0:8, cols] = jnp.broadcast_to(jnp.exp2(last), (8, 256))
        rows_out[8:16, cols] = split_dot(jnp.broadcast_to(heads_ref[2:3, :], (8, 128)), pick)
        return carry

    lax.fori_loop(0, INNER // 256, channels, 0)
    state_out[...] = dot(b_out[...], xde_out[...], TN)


def front(lengths, blk, edge, gain, w_in, conv_w, conv_b, heads):
    t = blk.shape[0]
    outs = [
        ((t, D), bf16),
        ((t, INNER), bf16),
        ((t + 16, XBC), f32),
        ((t, XBC), f32),
        ((t, INNER), f32),
        ((t, INNER), bf16),
        ((t, INNER), bf16),
        ((t, STATE), bf16),
        ((t, STATE), bf16),
        ((4, t, 128), f32),
        ((128, t), f32),
        ((t, HEADS * 128), f32),
        ((16, INNER), f32),
        ((STATE, INNER), f32),
    ]
    return call(front_kernel, outs, (lengths, blk, edge, gain, w_in, conv_w, conv_b, heads), smem=(0,))


def exchange_plain(state, decay, reverse):
    groups = lax.axis_size("head")
    count = lax.axis_size("seq") * groups
    place = lax.axis_index("seq")
    states = lax.all_gather(state.astype(bf16), ("seq", "head"), axis=0)
    decays = lax.all_gather(decay[0:1], ("seq", "head"), axis=0)
    blocks = count // SEQS
    block = place // SEQS * groups + lax.axis_index("head")

    def one(i, carry):
        source = blocks - 1 - i if reverse else i
        index = (source // groups * SEQS + place % SEQS) * groups + source % groups
        new = lax.dynamic_index_in_dim(decays, index, 0, False) * carry
        return new + lax.dynamic_index_in_dim(states, index, 0, False).astype(f32)

    ahead = blocks - 1 - block if reverse else block
    return lax.fori_loop(0, ahead, one, jnp.zeros(state.shape, f32)).astype(bf16)


def middle_kernel(
    lengths_ref,
    blk,
    gout,
    normed,
    gate,
    x_in,
    xd_in,
    b_in,
    c_in,
    cumt,
    cumb,
    rows_in,
    enter,
    gain,
    w_out,
    y_out,
    block_out,
    dy_out,
    dye_out,
    dgate_out,
    ggain_out,
    adj_out,
    grads_out,
    scores,
    mixed,
    gated_s,
    gn_s,
    scale_s,
    dgn_s,
    db_s,
):
    rows = blk.shape[0]
    causal = iota((rows, rows), 0) >= iota((rows, rows), 1)
    scores[...] = jnp.where(causal, dot(c_in[...], b_in[...], NT), 0.0)
    lane = iota((rows, 128), 1)
    left = one_hot(iota((1, 128), 1) < HEAD_DIM)
    right = one_hot(iota((1, 128), 1) >= HEAD_DIM)

    def pair(i, carry):
        cols = lanes(i * 128, 128)
        c0 = cumb[:, lanes(i * 256, 128)]
        c1 = cumb[:, lanes(i * 256 + 128, 128)]
        xd = xd_in[:, cols]
        y = None
        for cc, part, mask in ((c0, 0, left), (c1, 1, right)):
            row = cumt[pl.ds(2 * i + part, 1), :]
            decay = jnp.exp2(jnp.minimum(jnp.concatenate([cc] * (rows // 128), axis=1) - row, 0.0))
            term = dot((decay * scores[...]).astype(bf16), xd * mask)
            y = term if y is None else y + term
        grow = jnp.exp2(jnp.where(lane < HEAD_DIM, c0, c1))
        y = y + grow * dot(c_in[...], enter[:, cols])
        y_out[:, cols] = y
        mixed[:, cols] = (y + rows_in[8:9, cols] * x_in[:, cols]).astype(bf16).astype(f32)
        return carry

    lax.fori_loop(0, PAIRS, pair, 0)
    step = 32

    def gating(i, carry):
        r = pl.ds(pl.multiple_of(i * step, step), step)
        g = gate[r, :].astype(f32)
        gated = mixed[r, :] * g * sigmoid(g)
        scale = lax.rsqrt(jnp.mean(gated * gated, axis=-1, keepdims=True) + EPS)
        gated_s[r, :] = gated
        scale_s[r, :] = jnp.broadcast_to(scale, (step, 128))
        gn_s[r, :] = (gated * scale * gain[...]).astype(bf16)
        return carry

    lax.fori_loop(0, rows // step, gating, 0)
    keep = valid_rows(lengths_ref, rows, D)
    db_s[...] = (gout[...].astype(f32) * keep).astype(bf16)
    dgn_s[...] = dot(db_s[...], w_out[...], NT)
    block_out[...] = (blk[...].astype(f32) + keep * dot(gn_s[...], w_out[...])).astype(bf16)
    ggain_out[...] = jnp.zeros_like(ggain_out)

    def ungating(i, carry):
        r = pl.ds(pl.multiple_of(i * step, step), step)
        g = gate[r, :].astype(f32)
        sg = sigmoid(g)
        gated = gated_s[r, :]
        scale = scale_s[r, 0:1]
        dgn = dgn_s[r, :]
        ggain_out[...] += jnp.sum((dgn * gated * scale).reshape(step // 8, 8, INNER), axis=0)
        weighted = dgn * gain[...]
        average = jnp.mean(weighted * gated, axis=-1, keepdims=True)
        d_gated = scale * weighted - gated * (scale * scale * scale) * average
        dy_out[r, :] = (d_gated * g * sg).astype(bf16)
        dgate_out[r, :] = (d_gated * mixed[r, :] * sg * (1.0 + g * (1.0 - sg))).astype(bf16)
        return carry

    lax.fori_loop(0, rows // step, ungating, 0)

    def weigh(i, carry):
        cols = lanes(i * 128, 128)
        grow = jnp.exp2(jnp.where(lane < HEAD_DIM, cumb[:, lanes(i * 256, 128)], cumb[:, lanes(i * 256 + 128, 128)]))
        dye_out[:, cols] = (dy_out[:, cols].astype(f32) * grow).astype(bf16)
        return carry

    lax.fori_loop(0, PAIRS, weigh, 0)
    adj_out[...] = dot(c_in[...], dye_out[...], TN)
    grads_out[:INNER, :] = dot(dgate_out[...], normed[...], TN).astype(bf16)
    grads_out[INNER:, :] = dot(gn_s[...], db_s[...], TN).astype(bf16)


def middle(lengths, blk, gout, normed, gate, x, xd, b, c, cumt, cumb, rows_in, enter, gain, w_out):
    t = blk.shape[0]
    outs = [
        ((t, INNER), f32),
        ((t, D), bf16),
        ((t, INNER), bf16),
        ((t, INNER), bf16),
        ((t, INNER), bf16),
        ((8, INNER), f32),
        ((STATE, INNER), f32),
        ((2 * INNER, D), bf16),
    ]
    scratch = [
        pltpu.VMEM((t, t), f32),
        pltpu.VMEM((t, INNER), f32),
        pltpu.VMEM((t, INNER), f32),
        pltpu.VMEM((t, INNER), bf16),
        pltpu.VMEM((t, 128), f32),
        pltpu.VMEM((t, INNER), f32),
        pltpu.VMEM((t, D), bf16),
    ]
    args = (lengths, blk, gout, normed, gate, x, xd, b, c, cumt, cumb, rows_in, enter, gain, w_out)
    return call(middle_kernel, outs, args, scratch, smem=(0,))


def back_kernel(
    lengths_ref,
    y_in,
    dy_in,
    dye_in,
    x_in,
    xd_in,
    xde_in,
    b_in,
    c_in,
    run_in,
    cumt,
    cumb,
    head_in,
    rows_in,
    heads_ref,
    enter,
    own,
    leave,
    drun_out,
    dz_out,
    small_out,
    scores,
    dscores,
    skip_s,
    q_s,
    ry_s,
):
    rows = y_in.shape[0]
    causal = iota((rows, rows), 1) >= iota((rows, rows), 0)
    scores[...] = jnp.where(causal, dot(b_in[...], c_in[...], NT), 0.0)
    dscores[...] = jnp.zeros_like(dscores)
    q_s[...] = jnp.zeros_like(q_s)
    ry_s[...] = jnp.zeros_like(ry_s)
    lane = iota((rows, 128), 1)
    keep = valid_rows(lengths_ref, rows, 128)
    left = one_hot(iota((1, 128), 1) < HEAD_DIM)
    right = one_hot(iota((1, 128), 1) >= HEAD_DIM)
    pick_lane = iota((128, 128), 0)
    pick_head = iota((128, 128), 1)

    def dsilu(cols):
        running = run_in[:, cols]
        sg = sigmoid(running)
        return sg * (1.0 + running * (1.0 - sg))

    def pair(i, carry):
        cols = lanes(i * 128, 128)
        c0 = cumb[:, lanes(i * 256, 128)]
        c1 = cumb[:, lanes(i * 256 + 128, 128)]
        xd = xd_in[:, cols]
        dy = dy_in[:, cols]
        v = None
        for cc, part, mask in ((c0, 0, left), (c1, 1, right)):
            row = cumt[pl.ds(2 * i + part, 1), :]
            decay = jnp.exp2(jnp.minimum(row - jnp.concatenate([cc] * (rows // 128), axis=1), 0.0))
            masked = dy * mask
            term = dot((decay * scores[...]).astype(bf16), masked)
            v = term if v is None else v + term
            dscores[...] += decay * dot(xd, masked, NT)
        c01 = jnp.where(lane < HEAD_DIM, c0, c1)
        v = v + jnp.exp2(c01[rows - 1 : rows, :] - c01) * dot(b_in[...], leave[:, cols])
        pick = one_hot((pick_lane >> 6) + 2 * i == pick_head)
        dtw = split_dot(head_in[0], one_hot((pick_head >> 6) + 2 * i == pick_lane))
        x = x_in[:, cols]
        dyf = dy.astype(f32)
        q_s[...] += split_dot(x * v, pick)
        ry_s[...] += split_dot(dyf * y_in[:, cols], pick)
        skip_s[:, cols] = jnp.sum((dyf * x).reshape(rows // 8, 8, 128), axis=0)
        dx = dtw * v + rows_in[8:9, cols] * dyf
        drun_out[:, cols] = dx * keep * dsilu(cols)
        return carry

    lax.fori_loop(0, PAIRS, pair, 0)
    dsc = jnp.where(causal, dscores[...], 0.0).astype(bf16)
    d_b = dot(dsc, c_in[...]) + dot(xde_in[...], leave[...], NT)
    d_c = dot(dsc, b_in[...], TN) + dot(dye_in[...], enter[...], NT)
    drun_out[:, INNER : INNER + STATE] = d_b * dsilu(slice(INNER, INNER + STATE))
    drun_out[:, INNER + STATE :] = d_c * dsilu(slice(INNER + STATE, XBC))
    full_pick = one_hot((iota((INNER, 128), 0) >> 6) == iota((INNER, 128), 1))
    out_state = rows_in[0:1, :] * enter[...].astype(f32) + own[...]
    d_last = split_dot(
        jnp.sum((leave[...].astype(f32) * out_state).reshape(STATE // 8, 8, INNER), axis=0), full_pick
    )
    d_last = jnp.sum(d_last, axis=0, keepdims=True)
    dt = head_in[0]
    q = q_s[...]
    d_cum = ry_s[...] - dt * q + jnp.where(iota((rows, 128), 0) == rows - 1, d_last, 0.0)
    rates = -jnp.exp(heads_ref[1:2, :])
    above = one_hot(iota((rows, rows), 0) <= iota((rows, rows), 1))
    d_dt = q + split_dot_left(above, d_cum * rates)
    dz = d_dt * head_in[2]
    dz_out[...] = dz
    small_out[0:1, :] = jnp.sum(dz, axis=0, keepdims=True)
    small_out[1:2, :] = jnp.sum(d_cum * head_in[1], axis=0, keepdims=True)
    small_out[2:3, :] = jnp.sum(split_dot(skip_s[...], full_pick), axis=0, keepdims=True)
    small_out[3:8, :] = jnp.zeros((5, 128), f32)


def back(lengths, y, dy, dye, x, xd, xde, b, c, run, cumt, cumb, head, rows_in, heads, enter, own, leave):
    t = y.shape[0]
    outs = [((t, XBC), f32), ((t, 128), f32), ((8, 128), f32)]
    scratch = [
        pltpu.VMEM((t, t), f32),
        pltpu.VMEM((t, t), f32),
        pltpu.VMEM((8, INNER), f32),
        pltpu.VMEM((t, 128), f32),
        pltpu.VMEM((t, 128), f32),
    ]
    args = (lengths, y, dy, dye, x, xd, xde, b, c, run, cumt, cumb, head, rows_in, heads, enter, own, leave)
    return call(back_kernel, outs, args, scratch, smem=(0,))


def last_kernel(
    blk,
    gout,
    normed,
    gain,
    w_in,
    conv_w,
    pad_in,
    drun_in,
    edge,
    dz_in,
    dgate,
    ggain,
    small_in,
    gin_out,
    grads_out,
    vec_out,
    ext,
    dproj,
    sums,
):
    rows = blk.shape[0]
    ext[0:rows, :] = drun_in[...]
    ext[rows : rows + 8, :] = edge[...]
    vec_out[...] = jnp.zeros_like(vec_out)

    def channels(i, carry):
        cols = lanes(i * 128, 128)
        drun = ext[0:rows, cols]
        total = drun * conv_w[CONV - 1 : CONV, cols]
        for tap in range(CONV - 1):
            ahead = CONV - 1 - tap
            total = total + ext[ahead : ahead + rows, cols] * conv_w[tap : tap + 1, cols]
        dproj[:, cols] = total.astype(bf16)
        for tap in range(CONV):
            sums[tap : tap + 1, cols] = jnp.sum(
                drun * pad_in[13 + tap : 13 + tap + rows, cols], axis=0, keepdims=True
            )
        sums[CONV : CONV + 1, cols] = jnp.sum(drun, axis=0, keepdims=True)
        return carry

    lax.fori_loop(0, XBC // 128, channels, 0)
    for v in range(CONV + 1):
        for part in range(3):
            width = min(D, XBC - part * D)
            vec_out[HEADS + 3 * v + part : HEADS + 3 * v + part + 1, 0:width] = sums[v : v + 1, part * D : part * D + width]
    dz = dz_in[...].astype(bf16)
    d_normed = dot(dgate[...], w_in[:INNER, :])
    d_normed = d_normed + dot(dproj[...], w_in[INNER : INNER + XBC, :])
    d_normed = d_normed + dot(dz[:, :HEADS], w_in[INNER + XBC :, :])
    src = blk[...].astype(f32)
    scale = lax.rsqrt(jnp.mean(src * src, axis=-1, keepdims=True) + EPS)
    vec_out[39:40, :] = jnp.sum(d_normed * src * scale, axis=0, keepdims=True)
    gate_gain = jnp.sum(ggain[...], axis=0, keepdims=True)
    vec_out[40:41, :] = gate_gain[:, :D]
    vec_out[41:42, :] = gate_gain[:, D:]
    vec_out[42:45, 0:128] = small_in[0:3, :]
    weighted = d_normed * gain[...]
    average = jnp.mean(weighted * src, axis=-1, keepdims=True)
    gin_out[...] = gout[...].astype(f32) + scale * weighted - src * (scale * scale * scale) * average
    grads_out[...] = dot(dproj[...], normed[...], TN).astype(bf16)
    vec_out[0:HEADS, :] = dot(dz, normed[...], TN)[0:HEADS, :]


def last(blk, gout, normed, gain, w_in, conv_w, pad, drun, edge, dz, dgate, ggain, small):
    t = blk.shape[0]
    outs = [((t, D), f32), ((REST_ROWS, D), bf16), ((VEC_ROWS, D), f32)]
    scratch = [pltpu.VMEM((t + 8, XBC), f32), pltpu.VMEM((t, XBC), bf16), pltpu.VMEM((8, XBC), f32)]
    args = (blk, gout, normed, gain, w_in, conv_w, pad, drun, edge, dz, dgate, ggain, small)
    return call(last_kernel, outs, args, scratch)


class Refs:
    def __init__(self, names, refs):
        self.__dict__.update(zip(names, refs, strict=True))


def remote(src, dst, ssem, rsem, to):
    return pltpu.make_async_remote_copy(
        src_ref=src, dst_ref=dst, send_sem=ssem, recv_sem=rsem, device_id=to, device_id_type=MESH
    )


class Exchange:
    def __init__(self, reverse, state, decay, out, bufs, decays, ssem, rsem, start, width):
        self.sib_state, self.mine, self.got, self.back, self.back_got = bufs
        self.sib_decay, self.total, self.got_decay = decays
        self.state, self.decay, self.out, self.reverse = state, decay, out, reverse
        self.ssem, self.rsem = ssem, rsem
        self.chips = lax.axis_size("seq") // SEQS
        self.rows = STATE // self.chips
        self.width = width
        place, core = lax.axis_index("seq"), lax.axis_index("head")
        self.core = core
        self.chip, self.which = place // SEQS, place % SEQS
        self.sibling = (place, 1 - core)
        self.later = (1 - core if reverse else core) == 1
        self.own_cols = lanes(core * (INNER // 2) + start, width)
        self.sib_cols = lanes((1 - core) * (INNER // 2) + start, width)

    def peer(self, k):
        return (lax.rem(self.chip + k, self.chips) * SEQS + self.which, self.core)

    def send(self, copies):
        for src, dst, n, to in copies:
            remote(src, dst, self.ssem.at[n % 2], self.rsem.at[n], to).start()

    def arrive(self, *whole):
        for src, dst, n in whole:
            remote(src, dst, self.ssem.at[n % 2], self.rsem.at[n], self.sibling).wait()

    def begin(self):
        copies = [(self.state.at[:, self.sib_cols], self.sib_state, 0, self.sibling)]
        if not self.reverse:
            copies.append((self.decay.at[0:8, self.sib_cols], self.sib_decay, 1, self.sibling))
        self.send(copies)

    def ordered(self):
        own, other = self.state[:, self.own_cols], self.sib_state[...]
        own_decay, other_decay = self.decay[0:1, self.own_cols], self.sib_decay[0:1, :]
        later = self.later
        return (
            jnp.where(later, other, own),
            jnp.where(later, own, other),
            jnp.where(later, other_decay, own_decay),
            jnp.where(later, own_decay, other_decay),
        )

    def deal(self):
        whole = [(self.state.at[:, self.sib_cols], self.sib_state, 0)]
        if not self.reverse:
            whole.append((self.decay.at[0:8, self.sib_cols], self.sib_decay, 1))
        self.arrive(*whole)
        early, late, early_decay, late_decay = self.ordered()
        self.mine[...] = (late_decay * early + late).astype(bf16)
        if not self.reverse:
            self.total[...] = jnp.broadcast_to(early_decay * late_decay, self.total.shape)
        copies = []
        for k in range(1, self.chips):
            to = lax.rem(self.chip + k, self.chips)
            piece = pl.ds(pl.multiple_of(to * self.rows, self.rows), self.rows)
            copies.append((self.mine.at[piece], self.got.at[k], 2, self.peer(k)))
            if not self.reverse:
                copies.append((self.total, self.got_decay.at[k], 3, self.peer(k)))
        self.send(copies)
        self.got[0] = self.mine[pl.ds(pl.multiple_of(self.chip * self.rows, self.rows), self.rows), :]
        if not self.reverse:
            self.got_decay[0] = self.total[...]

    def scan(self):
        others = slice(1, self.chips)
        whole = [(self.got.at[others], self.got.at[others], 2)]
        if not self.reverse:
            whole.append((self.got_decay.at[others], self.got_decay.at[others], 3))
        self.arrive(*whole)
        chips, chip = self.chips, self.chip

        def one(i, carry):
            source = chips - 1 - i if self.reverse else i
            slot = lax.rem(chip - source + chips, chips)
            to = lax.rem(source - chip + chips, chips)
            self.back[pl.ds(to, 1)] = carry.astype(bf16)[None]
            return self.got_decay[pl.ds(slot, 1)][0, 0:1, :] * carry + self.got[pl.ds(slot, 1)][0].astype(f32)

        lax.fori_loop(0, chips, one, jnp.zeros((self.rows, self.width), f32))
        here = pl.ds(pl.multiple_of(chip * self.rows, self.rows), self.rows)
        self.send([(self.back.at[k], self.back_got.at[here], 4, self.peer(k)) for k in range(1, chips)])
        self.back_got[here, :] = self.back[0]

    def hand(self):
        self.arrive((self.back.at[1 : self.chips], self.back.at[1 : self.chips], 4))
        early, _, early_decay, _ = self.ordered()
        enter = self.back_got[...].astype(f32)
        second = early_decay * enter + early
        self.out[:, self.own_cols] = jnp.where(self.later, second, enter).astype(bf16)
        self.mine[...] = jnp.where(self.later, enter, second).astype(bf16)
        self.send([(self.mine, self.out.at[:, self.own_cols], 6, self.sibling)])

    def end(self):
        self.arrive((self.mine, self.mine, 6))


def exchange_scratch(chips, width):
    rows = STATE // chips
    states = [((STATE, width), f32), ((STATE, width), bf16), ((chips, rows, width), bf16)]
    states += [((chips, rows, width), bf16), ((STATE, width), bf16)]
    decays = [((8, width), f32), ((8, width), f32), ((chips, 8, width), f32)]
    return states, decays


ORDERS = (
    ("x", "y", "z1", "z2"),
    ("z1", "y", "x", "z2"),
    ("x", "z1", "y", "z2"),
    ("x", "y", "z2", "z1"),
    ("x", "y", "z1", "z2"),
    ("y", "x", "z2", "z1"),
    ("z1", "y", "x", "z2"),
    ("y", "x", "z1", "z2"),
    ("x", "y", "z1", "z2"),
    ("z1", "y", "x", "z2"),
    ("y", "z1", "x", "z2"),
    ("x", "y", "z1", "z2"),
    ("y", "z1", "z2", "x"),
    ("x", "z2", "y", "z1"),
    ("y", "z2", "x", "z1"),
)
SCHEDULE = {
    "g2": (
        2, 1,
    ),
    "o2": (
        2, 5,
    ),
    "b1": (
        1, 5, 0,
    ),
    "b2": (
        3,
    ),
    "b3": (
        4, 0,
    ),
    "s": (
        2,
    ),
    "e": (
        5, 1, 3, 0,
    ),
    "h": (
        4, 2,
    ),
    "c1": (
        5, 1, 0,
    ),
    "c2": (
        2, 3,
    ),
    "r1": (
        6, 8, 1, 5, 7, 4, 8, 7, 0,
    ),
    "v2": (
        2, 6,
    ),
    "v3": (
        5,
    ),
    "r2": (
        9, 1, 11, 4, 10, 9, 11, 8, 6, 7, 2, 10, 3, 6, 8, 9, 7, 0, 11, 1, 5, 4, 10,
    ),
    "e1": (
        2, 7,
    ),
    "e2": (
        0, 11, 6, 3, 9, 10, 8, 5, 4,
    ),
    "r3": (
        11, 7, 0, 12, 2, 6, 3, 4, 13,
    ),
    "z": (
        14, 8, 10, 12, 9, 1, 13, 7, 14, 11, 4, 3, 10, 12, 6, 2, 13, 14, 9, 7, 5, 8, 3, 0, 11, 1, 10, 6, 9, 8,
        0, 13, 12, 7, 4, 14, 10, 11, 9, 3, 13, 3, 5, 14, 12, 8, 10, 6, 11, 9, 1, 4, 13, 8, 6, 12, 7, 10, 11,
        14, 9,
    ),
}
STEPS = {"x": 1, "y": 2, "z1": 4, "z2": 8}
STAGES = 9


def bits_of():
    place = lax.axis_index("seq")
    return {
        "c": lax.axis_index("head"),
        "x": place % 2,
        "y": place // 2 % 2,
        "z1": place // 4 % 2,
        "z2": place // 8,
    }


def partner(d):
    place, core = lax.axis_index("seq"), lax.axis_index("head")
    if d == "c":
        return (place, 1 - core)
    return (place + STEPS[d] * (1 - 2 * bits_of()[d]), core)


class Sum:
    def __init__(self, held, got, out, ssem, rsem, lsem, orders):
        self.streams = [self.stream(held, got, out, ssem, rsem, lsem, s, order) for s, order in enumerate(orders)]
        self.stages = [-1] * len(orders)

    def stream(self, held, got, out, ssem, rsem, lsem, s, order):
        rows = held.shape[0]
        bits = bits_of()
        cols = slice(s * 256, (s + 1) * 256)
        order = ("c",) + order
        keeps, sends = [], []
        off, size = 0, rows
        for d in order[:4]:
            size //= 2
            keeps.append(off + bits[d] * size)
            sends.append(off + (1 - bits[d]) * size)
            off = keeps[-1]
        unit = rows // 16
        sizes = [rows // 2, rows // 4, rows // 8, unit, unit]
        slots = [0, rows // 2, rows // 2 + rows // 4, rows - 2 * unit, rows - unit]

        def at(start, size):
            return pl.ds(pl.multiple_of(start, 16), size)

        def copy(stage):
            if stage < 5:
                d = order[stage]
                where = at(sends[stage] if stage < 4 else off, sizes[stage])
                src, dst = held.at[where, cols], got.at[slice(slots[stage], slots[stage] + sizes[stage]), cols]
            else:
                d = order[8 - stage]
                where = at(keeps[8 - stage], sizes[8 - stage])
                src, dst = (held if stage == 5 else out).at[where, cols], out.at[where, cols]
            return remote(src, dst, ssem.at[s], rsem.at[s, stage], partner(d))

        def add(stage):
            where = keeps[stage] if stage < 4 else off

            @pl.loop(0, sizes[stage] // unit)
            def _(i):
                here = at(where + i * unit, unit)
                held[here, cols] = held[here, cols] + got[at(slots[stage] + i * unit, unit), cols]

        def place():
            return pltpu.make_async_copy(held.at[at(off, unit), cols], out.at[at(off, unit), cols], lsem.at[s])

        return copy, add, place

    def tick(self, s):
        copy, add, place = self.streams[s]
        stage = self.stages[s]
        if 0 <= stage < STAGES:
            copy(stage).wait()
            if stage < 5:
                add(stage)
        if stage == 4:
            place().start()
        if stage == 5:
            place().wait()
        if stage + 1 < STAGES:
            copy(stage + 1).start()
        self.stages[s] = stage + 1


class Swap:
    def __init__(self, held, got, ssem, rsem, orders):
        self.held, self.got, self.ssem, self.rsem = held, got, ssem, rsem
        self.orders = [("c",) + order for order in orders]
        self.stages = [-1] * len(orders)

    def tick(self, s):
        cols = slice(s * 256, (s + 1) * 256)
        order, stage = self.orders[s], self.stages[s]

        def copy(k):
            return remote(
                self.held.at[:, cols], self.got.at[k, :, cols], self.ssem.at[s], self.rsem.at[s, k], partner(order[k])
            )

        if 0 <= stage < len(order):
            copy(stage).wait()
            self.held[:, cols] = self.held[:, cols] + self.got[stage, :, cols]
        if stage + 1 < len(order):
            copy(stage + 1).start()
        self.stages[s] = stage + 1


def greet():
    place, core = lax.axis_index("seq"), lax.axis_index("head")
    pieces = lax.axis_size("seq")
    chips = pieces // SEQS
    barrier = pltpu.get_barrier_semaphore()
    peers = [partner("c"), partner("x")]
    peers += [((place // SEQS + k) % chips * SEQS + place % SEQS, core) for k in range(1, chips)]
    peers += [block_at(2 * core - 1)]
    for to in peers:
        pl.semaphore_signal(barrier, inc=1, device_id=to, device_id_type=MESH)
    return barrier, len(peers)


def block_at(ahead):
    place, core = lax.axis_index("seq"), lax.axis_index("head")
    pieces = lax.axis_size("seq")
    block = (place // SEQS * 2 + core + ahead + pieces) % pieces
    return (block // 2 * SEQS + place % SEQS, block % 2)


def whole_kernel(names, *refs):
    r = Refs(names, refs)
    rows = r.blk.shape[0]
    greeted = greet()
    loads = [
        pltpu.make_async_copy(r.w_in_hbm.at[INNER:], r.w_in.at[INNER:], r.load_sem.at[0]),
        pltpu.make_async_copy(r.w_in_hbm.at[:INNER], r.w_in.at[:INNER], r.load_sem.at[1]),
        pltpu.make_async_copy(r.w_out_hbm, r.w_out, r.load_sem.at[2]),
    ]
    for c in loads:
        c.start()
    r.gain[...] = r.norm_gain[...].reshape(1, D)
    r.conv_b[...] = r.conv_bias[...].reshape(1, XBC)
    r.gate_gain[...] = r.gated_gain[...].reshape(1, INNER)
    r.heads[...] = jnp.zeros((8, 128), f32)
    for k, one in enumerate((r.dt_bias, r.a_log, r.d_skip)):
        r.heads[k : k + 1, 0:HEADS] = one[...].reshape(1, HEADS)
    place, core = lax.axis_index("seq"), lax.axis_index("head")
    chips = lax.axis_size("seq") // SEQS
    block = place // SEQS * 2 + core

    def norm(v):
        v = v.astype(f32)
        scale = lax.rsqrt(jnp.mean(v * v, axis=-1, keepdims=True) + EPS)
        return (v * scale * r.gain[...]).astype(bf16)

    r.normed[...] = norm(r.blk[...])
    lane = iota((rows, 128), 1)
    keep = valid_rows(r.lengths, rows, 128)
    pick_lane = iota((128, 256), 1)
    pick_head = iota((128, 256), 0)
    left = one_hot(iota((1, 128), 1) < HEAD_DIM)
    right = one_hot(iota((1, 128), 1) >= HEAD_DIM)

    loads[0].wait()

    def project(i, carry):
        part = dot(r.normed[...], r.w_in[pl.ds(pl.multiple_of(INNER + i * 256, 256), 256), :], NT)
        r.pad[16:, lanes(i * 256, 256)] = part.astype(bf16).astype(f32)
        return carry

    lax.fori_loop(0, XBC // 256, project, 0, unroll=7)
    pl.semaphore_wait(*greeted)
    edge = remote(r.pad.at[rows + 8 :], r.pad.at[8:16], r.edge_sem.at[0], r.edge_sem.at[1], block_at(1))
    edge.start()

    r.head[3] = jnp.zeros((rows, 128), f32)
    r.head[3, :, 0:HEADS] = dot(r.normed[...], r.w_in[INNER + XBC :, :], NT).astype(bf16).astype(f32)
    moved = r.head[3] + r.heads[0:1, :]
    soft = jnp.maximum(moved, 0.0) + jnp.log1p(jnp.exp(-jnp.abs(moved)))
    dt = jnp.where(lane < HEADS, soft * keep, 0.0)
    rates = -jnp.exp(r.heads[1:2, :])
    below = one_hot(iota((rows, rows), 0) >= iota((rows, rows), 1))
    cum = split_dot_left(below, dt) * rates
    cum2 = cum * LOG2E
    r.head[0] = dt
    r.head[1] = cum
    r.head[2] = sigmoid(moved) * keep
    r.head[3] = cum2
    r.cumt[...] = cum2.T

    def widen(i, carry):
        cols = lanes(i * 128, 128)
        pick = one_hot((iota((128, 128), 1) >> 6) + 2 * i == iota((128, 128), 0))
        r.dt_wide[:, cols] = split_dot(r.head[0], pick)
        wide = split_dot(r.head[3], pick)
        last = wide[rows - 1 : rows, :]
        r.grow[:, cols] = jnp.exp2(wide)
        r.fall[:, cols] = jnp.exp2(last - wide)
        r.spread[0:8, cols] = jnp.broadcast_to(jnp.exp2(last), (8, 128))
        r.spread[8:16, cols] = split_dot(jnp.broadcast_to(r.heads[2:3, :], (8, 128)), pick)
        return carry

    lax.fori_loop(0, PAIRS, widen, 0, unroll=2)

    edge.wait()
    r.pad[8:16, :] = jnp.where(block == 0, 0.0, r.pad[8:16, :])

    def convolve(start, width):
        cols = lanes(start, width)
        running = r.conv_b[:, cols] + r.pad[13 : 13 + rows, cols] * r.conv_w[0:1, cols]
        for tap in range(1, CONV):
            running = running + r.pad[13 + tap : 13 + tap + rows, cols] * r.conv_w[tap : tap + 1, cols]
        r.run[:, cols] = running
        return running * sigmoid(running)

    act = convolve(INNER, 2 * STATE)
    r.b[...] = act[:, :STATE].astype(bf16)
    r.c[...] = act[:, STATE:].astype(bf16)
    third = 3 * 128

    def channels(start):
        def one(i, carry):
            at = start + i * 128
            cols = lanes(at, 128)
            x = convolve(at, 128) * keep
            r.x[:, cols] = x
            xd = x * r.dt_wide[:, cols]
            r.xd[:, cols] = xd.astype(bf16)
            r.xde[:, cols] = (xd * r.fall[:, cols]).astype(bf16)
            return carry

        lax.fori_loop(0, third // 128, one, 0, unroll=3)
        r.own[:, start : start + third] = dot(r.b[...], r.xde[:, start : start + third], TN)

    def exchanges(reverse, state, out, tag):
        made = []
        for k in range(SPLITS):
            bufs = [getattr(r, f"{tag}{k}_{n}") for n in range(5)]
            decays = [getattr(r, f"d{k}_{n}") for n in range(3)]
            sems = getattr(r, f"{tag}s").at[k], getattr(r, f"{tag}r").at[k]
            width = INNER // 2 // SPLITS
            made.append(Exchange(reverse, state, r.spread, out, bufs, decays, *sems, k * width, width))
        return made

    enters = exchanges(False, r.own, r.enter, "f")
    leaves = exchanges(True, r.adj, r.leave, "g")
    channels(0)
    channels(INNER // 2)
    enters[0].begin()
    channels(third)
    enters[0].deal()
    channels(INNER // 2 + third)
    enters[1].begin()

    def spread(i, carry):
        r.cumb[:, lanes(i * 256, 256)] = split_dot(r.head[3], one_hot((pick_lane >> 7) + 2 * i == pick_head))
        return carry


    causal = iota((rows, rows), 0) >= iota((rows, rows), 1)
    r.scores[...] = jnp.where(causal, dot(r.c[...], r.b[...], NT), 0.0)
    lax.fori_loop(0, 4, spread, 0, unroll=2)
    enters[1].deal()
    lax.fori_loop(4, PAIRS, spread, 0, unroll=2)
    loads[1].wait()

    def gates(i, carry):
        part = dot(r.normed[...], r.w_in[pl.ds(pl.multiple_of(i * 256, 256), 256), :], NT)
        r.gate[:, lanes(i * 256, 256)] = part.astype(bf16)
        return carry

    def columns(i):
        c0 = r.cumb[:, lanes(i * 256, 128)]
        c1 = r.cumb[:, lanes(i * 256 + 128, 128)]
        return c0, c1

    def pair(i, carry):
        cols = lanes(i * 128, 128)
        xd = r.xd[:, cols]
        y = None
        for cc, part, mask in zip(columns(i), (0, 1), (left, right), strict=True):
            row = r.cumt[pl.ds(2 * i + part, 1), :]
            decay = jnp.exp2(jnp.minimum(jnp.concatenate([cc] * (rows // 128), axis=1) - row, 0.0))
            term = dot((decay * r.scores[...]).astype(bf16), xd * mask)
            y = term if y is None else y + term
        r.y[:, cols] = y
        return carry

    lax.fori_loop(0, INNER // 256, gates, 0, unroll=2)
    enters[0].scan()
    lax.fori_loop(0, 6, pair, 0, unroll=2)
    enters[1].scan()
    lax.fori_loop(6, PAIRS, pair, 0, unroll=2)

    def slopes(i, carry):
        cols = lanes(i * 128, 128)
        running = r.run[:, cols]
        sg = sigmoid(running)
        r.run[:, cols] = sg * (1.0 + running * (1.0 - sg))
        return carry

    lax.fori_loop(0, XBC // 128, slopes, 0, unroll=2)
    keep_d = valid_rows(r.lengths, rows, D)
    r.db[...] = (r.gout[...].astype(f32) * keep_d).astype(bf16)
    loads[2].wait()
    r.wide[...] = dot(r.db[...], r.w_out[...], NT)
    for one in enters:
        one.hand()
    for one in enters:
        one.end()

    def carried(i, carry):
        cols = lanes(i * 128, 128)
        y = r.y[:, cols] + r.grow[:, cols] * dot(r.c[...], r.enter[:, cols])
        r.y[:, cols] = y
        r.mixed[:, cols] = (y + r.spread[8:9, cols] * r.x[:, cols]).astype(bf16)
        return carry

    lax.fori_loop(0, PAIRS, carried, 0, unroll=2)

    r.ggain[...] = jnp.zeros_like(r.ggain)
    step = 32

    def gating(i, carry):
        at = pl.ds(pl.multiple_of(i * step, step), step)
        g = r.gate[at, :].astype(f32)
        sg = sigmoid(g)
        mixed = r.mixed[at, :].astype(f32)
        gated = mixed * g * sg
        scale = lax.rsqrt(jnp.mean(gated * gated, axis=-1, keepdims=True) + EPS)
        r.gn[at, :] = (gated * scale * r.gate_gain[...]).astype(bf16)
        dgn = r.wide[at, :]
        r.ggain[...] += jnp.sum((dgn * gated * scale).reshape(step // 8, 8, INNER), axis=0)
        weighted = dgn * r.gate_gain[...]
        average = jnp.mean(weighted * gated, axis=-1, keepdims=True)
        d_gated = scale * weighted - gated * (scale * scale * scale) * average
        r.dy[at, :] = (d_gated * g * sg).astype(bf16)
        r.dgate[at, :] = (d_gated * mixed * sg * (1.0 + g * (1.0 - sg))).astype(bf16)
        return carry

    lax.fori_loop(0, rows // step, gating, 0)

    def weigh(i, carry):
        cols = lanes(i * 128, 128)
        r.dye[:, cols] = (r.dy[:, cols].astype(f32) * r.grow[:, cols]).astype(bf16)
        return carry

    lax.fori_loop(0, PAIRS, weigh, 0, unroll=2)
    r.adj[...] = dot(r.c[...], r.dye[...], TN)
    for one in leaves:
        one.begin()

    def gate_grads(i, carry):
        at = pl.ds(pl.multiple_of(i * 256, 256), 256)
        r.first[at, :] = dot(r.dgate[:, lanes(i * 256, 256)], r.normed[...], TN).astype(bf16)
        return carry

    def out_grads(i, carry):
        at = pl.ds(pl.multiple_of(INNER + i * 256, 256), 256)
        r.first[at, :] = dot(r.gn[:, lanes(i * 256, 256)], r.db[...], TN).astype(bf16)
        return carry

    def part(k, held, got, out, at):
        return Sum(held.at[at], got.at[at], out.at[at], r.ss.at[k], r.rs.at[k], r.ls.at[k], ORDERS[3 * k : 3 * k + 3])

    sums = [
        part(0, r.first, r.got_first, r.first_out, slice(0, INNER)),
        part(1, r.first, r.got_first, r.first_out, slice(INNER, FIRST_ROWS)),
        part(2, r.rest, r.got_rest, r.rest_out, slice(0, D)),
        part(3, r.rest, r.got_rest, r.rest_out, slice(D, REST_ROWS)),
        Swap(r.vec, r.got_vec, r.vs, r.vr, ORDERS[12:15]),
    ]
    def slot(name):
        for n in SCHEDULE.get(name, ()):
            sums[n // 3].tick(n % 3)

    lax.fori_loop(0, INNER // 256, gate_grads, 0, unroll=2)
    slot("g2")
    for one in leaves:
        one.deal()
    slot("d")
    lax.fori_loop(0, INNER // 256, out_grads, 0, unroll=2)
    slot("o2")
    r.block_out[...] = (r.blk[...].astype(f32) + keep_d * dot(r.gn[...], r.w_out[...])).astype(bf16)
    stores = [
        pltpu.make_async_copy(r.block_out, r.block_out_hbm, r.store_sem.at[0]),
        pltpu.make_async_copy(r.grad_in, r.grad_in_hbm, r.store_sem.at[1]),
    ]
    stores[0].start()
    slot("b0")

    r.scores_t[...] = jnp.where(
        iota((rows, rows), 1) >= iota((rows, rows), 0), dot(r.b[...], r.c[...], NT), 0.0
    )

    r.dscores[...] = jnp.zeros_like(r.dscores)
    r.q[...] = jnp.zeros_like(r.q)
    r.ry[...] = jnp.zeros_like(r.ry)
    row_head = iota((128, 128), 0)
    col_head = iota((128, 128), 1)

    def pair_back(i, carry):
        cols = lanes(i * 128, 128)
        xd, dy = r.xd[:, cols], r.dy[:, cols]
        v = None
        for cc, part, mask in zip(columns(i), (0, 1), (left, right), strict=True):
            row = r.cumt[pl.ds(2 * i + part, 1), :]
            decay = jnp.exp2(jnp.minimum(row - jnp.concatenate([cc] * (rows // 128), axis=1), 0.0))
            masked = dy * mask
            term = dot((decay * r.scores_t[...]).astype(bf16), masked)
            v = term if v is None else v + term
            r.dscores[...] += decay * dot(xd, masked, NT)
        r.wide[:, cols] = v
        r.ry[...] += split_dot(dy.astype(f32) * r.y[:, cols], one_hot((row_head >> 6) + 2 * i == col_head))
        return carry

    lax.fori_loop(0, 4, pair_back, 0, unroll=2)
    slot("b1")
    lax.fori_loop(4, 8, pair_back, 0, unroll=2)
    slot("b2")
    lax.fori_loop(8, PAIRS, pair_back, 0, unroll=2)
    slot("b3")
    for one in leaves:
        one.scan()
    slot("s")
    dsc = jnp.where(iota((rows, rows), 1) >= iota((rows, rows), 0), r.dscores[...], 0.0).astype(bf16)
    d_b = dot(dsc, r.c[...])
    d_c = dot(dsc, r.b[...], TN) + dot(r.dye[...], r.enter[...], NT)
    slot("e")
    for one in leaves:
        one.hand()
    slot("h")
    for one in leaves:
        one.end()
    slot("l")

    def channels_back(i, carry):
        cols = lanes(i * 128, 128)
        v = r.wide[:, cols] + r.fall[:, cols] * dot(r.b[...], r.leave[:, cols])
        x = r.x[:, cols]
        dy = r.dy[:, cols].astype(f32)
        r.q[...] += split_dot(x * v, one_hot((row_head >> 6) + 2 * i == col_head))
        r.skip[:, cols] = jnp.sum((dy * x).reshape(rows // 8, 8, 128), axis=0)
        r.ext[0:rows, cols] = (r.dt_wide[:, cols] * v + r.spread[8:9, cols] * dy) * keep * r.run[:, cols]
        return carry

    def conv_back(i, carry):
        cols = lanes(i * 128, 128)
        drun = r.ext[0:rows, cols]
        total = drun * r.conv_w[CONV - 1 : CONV, cols]
        for tap in range(CONV - 1):
            ahead = CONV - 1 - tap
            total = total + r.ext[ahead : ahead + rows, cols] * r.conv_w[tap : tap + 1, cols]
        r.dproj[:, cols] = total.astype(bf16)
        for tap in range(CONV):
            r.tap_sums[tap : tap + 1, cols] = jnp.sum(
                drun * r.pad[13 + tap : 13 + tap + rows, cols], axis=0, keepdims=True
            )
        r.tap_sums[CONV : CONV + 1, cols] = jnp.sum(drun, axis=0, keepdims=True)
        return carry

    def rest_grads(i, carry):
        at = pl.ds(pl.multiple_of(i * 256, 256), 256)
        r.rest[at, :] = dot(r.dproj[:, lanes(i * 256, 256)], r.normed[...], TN).astype(bf16)
        return carry

    halves = (slice(0, INNER // 2), slice(INNER // 2, XBC))

    def edges(k):
        cols = halves[k]
        sems = r.edge_sem.at[2 + 2 * k], r.edge_sem.at[3 + 2 * k]
        return remote(r.ext.at[0:8, cols], r.edge_grad.at[:, cols], *sems, block_at(-1))

    def edge_in(k):
        edges(k).wait()
        r.ext[rows : rows + 8, halves[k]] = jnp.where(block == chips * 2 - 1, 0.0, r.edge_grad[:, halves[k]])

    lax.fori_loop(0, PAIRS // 2, channels_back, 0, unroll=2)
    edges(0).start()
    slot("c1")
    lax.fori_loop(PAIRS // 2, PAIRS, channels_back, 0, unroll=2)
    d_b = d_b + dot(r.xde[...], r.leave[...], NT)
    r.ext[0:rows, INNER : INNER + STATE] = d_b * r.run[:, INNER : INNER + STATE]
    r.ext[0:rows, INNER + STATE :] = d_c * r.run[:, INNER + STATE :]
    edges(1).start()
    slot("c2")

    edge_in(0)
    slot("c3")
    lax.fori_loop(0, 6, conv_back, 0, unroll=2)
    slot("v1")
    lax.fori_loop(0, 3, rest_grads, 0, unroll=3)
    slot("r1")
    edge_in(1)
    slot("v2")
    lax.fori_loop(6, XBC // 128, conv_back, 0, unroll=2)
    slot("v3")
    lax.fori_loop(3, XBC // 256, rest_grads, 0, unroll=2)
    slot("r2")
    full_pick = one_hot((iota((INNER, 128), 0) >> 6) == iota((INNER, 128), 1))
    out_state = r.spread[0:1, :] * r.enter[...].astype(f32) + r.own[...]
    d_last = split_dot(
        jnp.sum((r.leave[...].astype(f32) * out_state).reshape(STATE // 8, 8, INNER), axis=0), full_pick
    )
    d_last = jnp.sum(d_last, axis=0, keepdims=True)
    q = r.q[...]
    d_cum = r.ry[...] - r.head[0] * q + jnp.where(iota((rows, 128), 0) == rows - 1, d_last, 0.0)
    above = one_hot(iota((rows, rows), 0) <= iota((rows, rows), 1))
    dz = (q + split_dot_left(above, d_cum * -jnp.exp(r.heads[1:2, :]))) * r.head[2]
    r.vec[...] = jnp.zeros_like(r.vec)
    r.vec[42:43, 0:128] = jnp.sum(dz, axis=0, keepdims=True)
    r.vec[43:44, 0:128] = jnp.sum(d_cum * r.head[1], axis=0, keepdims=True)
    r.vec[44:45, 0:128] = jnp.sum(split_dot(r.skip[...], full_pick), axis=0, keepdims=True)
    dz = dz.astype(bf16)
    slot("e1")
    d_normed = dot(r.dgate[...], r.w_in[:INNER, :])
    d_normed = d_normed + dot(dz[:, :HEADS], r.w_in[INNER + XBC :, :])
    d_normed = d_normed + dot(r.dproj[...], r.w_in[INNER : INNER + XBC, :])
    slot("e2")
    for v in range(CONV + 1):
        for part in range(3):
            width = min(D, XBC - part * D)
            r.vec[HEADS + 3 * v + part : HEADS + 3 * v + part + 1, 0:width] = r.tap_sums[v : v + 1, part * D : part * D + width]
    src = r.blk[...].astype(f32)
    scale = lax.rsqrt(jnp.mean(src * src, axis=-1, keepdims=True) + EPS)
    r.vec[39:40, :] = jnp.sum(d_normed * src * scale, axis=0, keepdims=True)
    gate_gain = jnp.sum(r.ggain[...], axis=0, keepdims=True)
    r.vec[40:41, :] = gate_gain[:, :D]
    r.vec[41:42, :] = gate_gain[:, D:]
    r.vec[0:HEADS, :] = dot(dz, r.normed[...], TN)[0:HEADS, :]
    slot("r3")
    weighted = d_normed * r.gain[...]
    average = jnp.mean(weighted * src, axis=-1, keepdims=True)
    r.grad_in[...] = r.gout[...].astype(f32) + scale * weighted - src * (scale * scale * scale) * average
    stores[1].start()
    slot("z")
    out = pltpu.make_async_copy(r.vec, r.vec_out, r.store_sem.at[2])
    out.start()
    for c in (*stores, out):
        c.wait()


def whole(*args):
    t = args[0].shape[0]
    chips = lax.axis_size("seq") // SEQS
    ins = ["blk", "gout", "lengths", "norm_gain", "w_in_hbm", "conv_w", "conv_bias", "dt_bias", "a_log", "d_skip"]
    ins += ["gated_gain", "w_out_hbm"]
    outs = {
        "block_out_hbm": ((t, D), bf16),
        "grad_in_hbm": ((t, D), f32),
        "first_out": ((FIRST_ROWS, D), bf16),
        "rest_out": ((REST_ROWS, D), bf16),
        "vec_out": ((VEC_ROWS, D), f32),
    }
    held = {
        "block_out": ((t, D), bf16),
        "grad_in": ((t, D), f32),
        "first": ((FIRST_ROWS, D), bf16),
        "rest": ((REST_ROWS, D), bf16),
        "gain": ((1, D), f32),
        "conv_b": ((1, XBC), f32),
        "gate_gain": ((1, INNER), f32),
        "heads": ((8, 128), f32),
        "w_in": ((PROJ, D), bf16),
        "w_out": ((INNER, D), bf16),
        "edge_grad": ((8, XBC), f32),
        "normed": ((t, D), bf16),
        "gate": ((t, INNER), bf16),
        "pad": ((t + 16, XBC), f32),
        "run": ((t, XBC), f32),
        "x": ((t, INNER), f32),
        "xd": ((t, INNER), bf16),
        "xde": ((t, INNER), bf16),
        "b": ((t, STATE), bf16),
        "c": ((t, STATE), bf16),
        "head": ((4, t, 128), f32),
        "cumt": ((128, t), f32),
        "cumb": ((t, HEADS * 128), f32),
        "spread": ((16, INNER), f32),
        "own": ((STATE, INNER), f32),
        "enter": ((STATE, INNER), bf16),
        "y": ((t, INNER), f32),
        "grow": ((t, INNER), f32),
        "fall": ((t, INNER), f32),
        "dt_wide": ((t, INNER), f32),
        "mixed": ((t, INNER), bf16),
        "gn": ((t, INNER), bf16),
        "wide": ((t, INNER), f32),
        "db": ((t, D), bf16),
        "dy": ((t, INNER), bf16),
        "dye": ((t, INNER), bf16),
        "dgate": ((t, INNER), bf16),
        "ggain": ((8, INNER), f32),
        "adj": ((STATE, INNER), f32),
        "leave": ((STATE, INNER), bf16),
        "scores": ((t, t), f32),
        "scores_t": ((t, t), f32),
        "dscores": ((t, t), f32),
        "skip": ((8, INNER), f32),
        "q": ((t, 128), f32),
        "ry": ((t, 128), f32),
        "ext": ((t + 8, XBC), f32),
        "dproj": ((t, XBC), bf16),
        "vec": ((VEC_ROWS, D), f32),
        "got_vec": ((5, VEC_ROWS, D), f32),
        "tap_sums": ((8, XBC), f32),
        "got_first": ((FIRST_ROWS, D), bf16),
        "got_rest": ((REST_ROWS, D), bf16),
    }
    names = ins + list(outs) + list(held)
    scratch = [pltpu.VMEM(s, d) for s, d in held.values()]
    states, decays = exchange_scratch(chips, INNER // 2 // SPLITS)
    for tag, shapes in (("f", states), ("g", states), ("d", decays)):
        for k in range(SPLITS):
            scratch += [pltpu.VMEM(s, d) for s, d in shapes]
            names += [f"{tag}{k}_{n}" for n in range(len(shapes))]
    semaphores = {
        "ss": (WAVES, 3),
        "rs": (WAVES, 3, STAGES),
        "ls": (WAVES, 3),
        "fs": (SPLITS, 2),
        "fr": (SPLITS, 7),
        "gs": (SPLITS, 2),
        "gr": (SPLITS, 7),
        "edge_sem": (6,),
        "load_sem": (3,),
        "store_sem": (3,),
        "vs": (3,),
        "vr": (3, 5),
    }
    for name, shape in semaphores.items():
        scratch.append(pltpu.SemaphoreType.DMA(shape))
        names.append(name)
    any_space = pl.BlockSpec(memory_space=pl.ANY)
    specs = {n: any_space for n in ("w_in_hbm", "w_out_hbm", *outs)} | {"lengths": SMEM}
    return pl.pallas_call(
        partial(whole_kernel, names),
        out_shape=[jax.ShapeDtypeStruct(s, d) for s, d in outs.values()],
        in_specs=[specs.get(n, VMEM) for n in ins],
        out_specs=[specs.get(n, VMEM) for n in outs],
        scratch_shapes=scratch,
        compiler_params=pltpu.CompilerParams(vmem_limit_bytes=60 << 20, collective_id=0, has_side_effects=True),
    )(*args)


def finish_kernel(
    block_in,
    grad_in,
    first,
    rest,
    vec_in,
    block_out,
    grad_out,
    norm_out,
    w_in_out,
    conv_out,
    bias_out,
    dt_out,
    alog_out,
    skip_out,
    gate_out,
    w_out_out,
    held_first,
    held_rest,
    held_block,
    held_grad,
    vec,
    wide_in,
    wide_out,
    in_sem,
    out_sem,
    pass_sem,
):
    passed = [
        (pltpu.make_async_copy(src, by, pass_sem.at[n, 0]), pltpu.make_async_copy(by, dst, pass_sem.at[n, 1]))
        for n, (src, by, dst) in enumerate(((block_in, held_block, block_out), (grad_in, held_grad, grad_out)))
    ]
    chunks = [(first, held_first, k * 256, 256) for k in range(FIRST_ROWS // 256)]
    chunks += [(rest, held_rest, k * 256, 256) for k in range(REST_ROWS // 256)]
    loads = [
        pltpu.make_async_copy(src.at[start : start + size], dst.at[start : start + size], in_sem.at[n])
        for n, (src, dst, start, size) in enumerate(chunks)
    ]
    ahead = 8
    small = pltpu.make_async_copy(vec_in, vec, pass_sem.at[1, 2])
    for c in loads[:ahead] + [small] + [load for load, _ in passed]:
        c.start()
    stores = [store for _, store in passed]
    for n, (src, held, start, size) in enumerate(chunks):
        loads[n].wait()
        if n == ahead:
            for load, store in passed:
                load.wait()
                store.start()
        if n + ahead < len(loads):
            loads[n + ahead].start()
        if src is first and start >= INNER:
            wide, out, at = wide_out, w_out_out, start - INNER
        else:
            wide, out, at = wide_in, w_in_out, start if src is first else INNER + start
        wide[at : at + size, :] = held[start : start + size, :].astype(f32)
        c = pltpu.make_async_copy(wide.at[at : at + size], out.at[at : at + size], out_sem.at[n])
        c.start()
        stores.append(c)
    small.wait()
    wide_in[INNER + XBC :, :] = vec[0:HEADS, :]
    c = pltpu.make_async_copy(wide_in.at[INNER + XBC :], w_in_out.at[INNER + XBC :], pass_sem.at[0, 2])
    c.start()
    stores.append(c)

    def row(v):
        return jnp.concatenate([vec[HEADS + 3 * v + k : HEADS + 3 * v + k + 1, : min(D, XBC - k * D)] for k in range(3)], axis=1)

    for v in range(CONV):
        conv_out[v : v + 1, :] = row(v)
    bias_out[...] = row(CONV).reshape(XBC)
    norm_out[...] = vec[39:40, :].reshape(D)
    gate_out[...] = jnp.concatenate([vec[40:41, :], vec[41:42, :]], axis=1).reshape(INNER)
    for k, out in enumerate((dt_out, alog_out, skip_out)):
        out[...] = vec[42 + k : 43 + k, 0:HEADS].reshape(HEADS)
    for c in stores:
        c.wait()


def finish(block_out, grad_in, first, rest, vec):
    shapes = [block_out.shape, grad_in.shape, (D,), (PROJ, D), (CONV, XBC), (XBC,), (HEADS,), (HEADS,), (HEADS,), (INNER,)]
    shapes += [(INNER, D)]
    any_space = pl.BlockSpec(memory_space=pltpu.HBM)
    away = (0, 1, 3, 10)
    chunks = (FIRST_ROWS + REST_ROWS) // 256
    return pl.pallas_call(
        finish_kernel,
        out_shape=[jax.ShapeDtypeStruct(s, bf16 if k == 0 else f32) for k, s in enumerate(shapes)],
        in_specs=[any_space] * 5,
        out_specs=[any_space if k in away else VMEM for k in range(len(shapes))],
        scratch_shapes=[
            pltpu.VMEM((FIRST_ROWS, D), bf16),
            pltpu.VMEM((REST_ROWS, D), bf16),
            pltpu.VMEM(block_out.shape, bf16),
            pltpu.VMEM(grad_in.shape, f32),
            pltpu.VMEM((VEC_ROWS, D), f32),
            pltpu.VMEM((PROJ, D), f32),
            pltpu.VMEM((INNER, D), f32),
            pltpu.SemaphoreType.DMA((chunks,)),
            pltpu.SemaphoreType.DMA((chunks,)),
            pltpu.SemaphoreType.DMA((2, 3)),
        ],
        compiler_params=pltpu.CompilerParams(vmem_limit_bytes=60 << 20),
    )(block_out, grad_in, first, rest, vec)


def shifted(value, ahead):
    groups = lax.axis_size("head")
    count = lax.axis_size("seq") * groups
    moves = []
    for source in range(count):
        piece, half = source // groups, source % groups
        half += ahead
        if half == groups:
            half, piece = 0, piece + SEQS
        elif half < 0:
            half, piece = groups - 1, piece - SEQS
        if 0 <= piece * groups + half < count:
            moves.append((source, piece * groups + half))
    return lax.ppermute(value, ("seq", "head"), moves)


def by_parts(block_in, grad_out, lengths, norm_gain, w_in, conv_w, conv_b, dt_bias, a_log, d_skip, gate_gain, w_out):
    heads = jnp.pad(jnp.stack([dt_bias, a_log, d_skip]), ((0, 5), (0, 128 - HEADS)))
    gain, conv_b, gate_gain = norm_gain.reshape(1, D), conv_b.reshape(1, XBC), gate_gain.reshape(1, INNER)
    edge = shifted(block_in[-16:], 1)
    (normed, gate, pad, run, x, xd, xde, b, c, head, cumt, cumb, rows, own) = front(
        lengths, block_in, edge, gain, w_in, conv_w, conv_b, heads
    )
    enter = exchange_plain(own, rows[0:8], False)
    (y, block_out, dy, dye, dgate, ggain, adj, grads_a) = middle(
        lengths, block_in, grad_out, normed, gate, x, xd, b, c, cumt, cumb, rows, enter, gate_gain, w_out
    )
    leave = exchange_plain(adj, rows[0:8], True)
    drun, dz, small = back(
        lengths, y, dy, dye, x, xd, xde, b, c, run, cumt, cumb, head, rows, heads, enter, own, leave
    )
    edge_back = shifted(drun[0:8], -1)
    grad_in, grads_b, vec = last(
        block_in, grad_out, normed, gain, w_in, conv_w, pad, drun, edge_back, dz, dgate, ggain, small
    )
    grads_a, grads_b, vec = lax.psum((grads_a, grads_b, vec), ("seq", "head"))
    return block_out, grad_in, grads_a, grads_b, vec


def local(block_in, grad_out, lengths, norm_gain, w_in, *others):
    run = whole if lax.axis_size("seq") == 16 and lax.axis_size("head") == 2 else by_parts
    outs = finish(*run(block_in, grad_out, lengths, norm_gain, w_in.T, *others))
    return (*outs[:3], outs[3].T, *outs[4:])


def solution(mesh):
    rows = P(("seq", "head"), None)
    return jax.shard_map(
        local,
        mesh=mesh,
        in_specs=(rows, rows) + (P(),) * 10,
        out_specs=(rows, rows) + (P(),) * 9,
        check_vma=False,
    )
```
